32 devices in a mesh: dp: 8 (over y, x, core), ctx: 4 (over z).
Axes of the slice: x: 2, y: 2, z: 4, core: 2. Of those that a mesh axis runs over, the one named last changes fastest.
Arguments:
- enc_in: bfloat16 [16, 1024, 768], P('dp', 'ctx'), may hold values from -6 to 6
- segments: int32 [16, 1024], P('dp'), may hold values from 0 to 3, never falling along the last dimension, each value on 1 to 682 neighbouring positions
- dec_in: bfloat16 [16, 1024, 768], P('dp', 'ctx'), may hold values from -6 to 6
- retrieved: int32 [16, 8, 512], P('dp'), may hold values from 0 to 1023, as said below
- enc_cot: bfloat16 [16, 1024, 768], P('dp', 'ctx'), may hold values from -6 to 6
- dec_cot: bfloat16 [16, 1024, 768], P('dp', 'ctx'), may hold values from -6 to 6
- enc_qkv: bfloat16 [768, 2304], P(('dp', 'ctx')), may hold values from -0.3125 to 0.3125
- enc_out: bfloat16 [768, 768], P(('dp', 'ctx')), may hold values from -1.75 to 1.75
- enc_up: bfloat16 [768, 3072], P(('dp', 'ctx')), may hold values from -0.21875 to 0.21875
- enc_down: bfloat16 [3072, 768], P(('dp', 'ctx')), may hold values from -0.109375 to 0.109375
- enc_bias: bfloat16 [768, 6], P(('dp', 'ctx')), may hold values from -1.25 to 1.25
- enc_up_bias: bfloat16 [3072], P(('dp', 'ctx')), may hold values from -1.25 to 1.25
- enc_gain: bfloat16 [768, 2], P(('dp', 'ctx')), may hold values from 0.5 to 1.5
- decoder_self_projections: bfloat16 [768, 2304], P(('dp', 'ctx')), may hold values from -0.3125 to 0.3125
- dec_out: bfloat16 [768, 768], P(('dp', 'ctx')), may hold values from -1.75 to 1.75
- cross_q: bfloat16 [768, 768], P(('dp', 'ctx')), may hold values from -0.3125 to 0.3125
- cross_kv: bfloat16 [768, 1536], P(('dp', 'ctx')), may hold values from -0.3125 to 0.3125
- cross_out: bfloat16 [768, 768], P(('dp', 'ctx')), may hold values from -1.75 to 1.75
- dec_up: bfloat16 [768, 3072], P(('dp', 'ctx')), may hold values from -0.21875 to 0.21875
- dec_down: bfloat16 [3072, 768], P(('dp', 'ctx')), may hold values from -0.109375 to 0.109375
- dec_bias: bfloat16 [768, 10], P(('dp', 'ctx')), may hold values from -1.25 to 1.25
- dec_up_bias: bfloat16 [3072], P(('dp', 'ctx')), may hold values from -1.25 to 1.25
- dec_gain: bfloat16 [768, 3], P(('dp', 'ctx')), may hold values from 0.5 to 1.5
Outputs:
- enc_hidden: bfloat16 [16, 1024, 768], P('dp', 'ctx')
- dec_hidden: bfloat16 [16, 1024, 768], P('dp', 'ctx')
- enc_in_grad: float32 [16, 1024, 768], P('dp', 'ctx')
- dec_in_grad: float32 [16, 1024, 768], P('dp', 'ctx')
- enc_qkv_grad: float32 [768, 2304], P(('dp', 'ctx'))
- enc_out_grad: float32 [768, 768], P(('dp', 'ctx'))
- enc_up_grad: float32 [768, 3072], P(('dp', 'ctx'))
- enc_down_grad: float32 [3072, 768], P(('dp', 'ctx'))
- enc_bias_grad: float32 [768, 6], P(('dp', 'ctx'))
- enc_up_bias_grad: float32 [3072], P(('dp', 'ctx'))
- enc_gain_grad: float32 [768, 2], P(('dp', 'ctx'))
- dec_qkv_grad: float32 [768, 2304], P(('dp', 'ctx'))
- dec_out_grad: float32 [768, 768], P(('dp', 'ctx'))
- cross_q_grad: float32 [768, 768], P(('dp', 'ctx'))
- mixed_pair_slope: float32 [768, 1536], P(('dp', 'ctx'))
- cross_out_grad: float32 [768, 768], P(('dp', 'ctx'))
- dec_up_grad: float32 [768, 3072], P(('dp', 'ctx'))
- dec_down_grad: float32 [3072, 768], P(('dp', 'ctx'))
- dec_bias_grad: float32 [768, 10], P(('dp', 'ctx'))
- dec_up_bias_grad: float32 [3072], P(('dp', 'ctx'))
- dec_gain_grad: float32 [768, 3], P(('dp', 'ctx'))
The draws below stay inside these ranges and needn't reach their ends.
Inputs may be any that keep to these rules, and one draw needn't show every extreme that they name: `segments`: segment numbers never fall along a sequence; a document holds at most 682 tokens. `retrieved`: the 512 positions of one decoder block are distinct encoder positions of its own sequence.
All inputs are finite; a program needn't handle non-finite values.
Results may differ from the reference program's by a relative error of at most 0.03.
Values may be sent and summed in bfloat16 or wider, within the bound.
A program may use at most 384 MiB of HBM per device.

```python
import math
import jax
import jax.numpy as jnp
import numpy as np
from jax import lax

D = 768
HEADS = 12
HEAD_DIM = 64
FF = 3072
BLOCK = 128
RETR = 512
SOURCE_TOKENS = 1024
DEC_LEN = 1024
SEQS = 16


def draw_retrieved(key, part):
    block_count = DEC_LEN // BLOCK
    row_count = SEQS * block_count
    noise_key = jax.random.fold_in(key, 11)
    favour_key = jax.random.fold_in(key, 23)
    random_whole_draws = jax.random.randint(noise_key, (row_count, SOURCE_TOKENS), 0, 1 << 16)
    preferred_lines = jax.random.randint(favour_key, (row_count, 8), 0, 2)
    logit_increment = jnp.repeat(preferred_lines, SOURCE_TOKENS // 8, axis=1) * (1 << 15)
    logit_sorted_order = (random_whole_draws - logit_increment) * SOURCE_TOKENS + jnp.arange(SOURCE_TOKENS, dtype=jnp.int32)[None, :]
    logit_sorted_order = logit_sorted_order.at[0, SOURCE_TOKENS - 1].set(-(1 << 30) + 1)
    logit_sorted_order = logit_sorted_order.at[0, 0].set(-(1 << 30))
    ordering = jnp.argsort(logit_sorted_order, axis=1)
    return ordering[:, :RETR].astype(jnp.int32).reshape(SEQS, block_count, RETR)


def block_scale(own_key, shape, shards, smallest, high):
    def one(position, shards_of):
        draws = jax.random.uniform(jax.random.fold_in(jax.random.fold_in(own_key, 6), position), (shards_of,), jnp.float32, smallest / len(shards), high / len(shards))
        return jnp.repeat(jnp.exp(draws), shape[position] // shards_of).reshape((-1,) + (1,) * (len(shape) - position - 1))

    gain = one(*shards[0])
    for cut in shards[1:]:
        gain = gain * one(*cut)
    return gain


def profile(count, total, bound, lean):
    portions = [(1 << 20) // math.isqrt(standing ** lean) + 1 for standing in range(2, count + 1)]
    surplus, given = total - bound - (count - 1), [1] * (count - 1)
    while surplus > 0:
        candidates = [i for i in range(count - 1) if given[i] < bound]
        mass, budget = sum([portions[i] for i in candidates]), surplus
        for i in candidates:
            extra = min(bound - given[i], max(1, budget * portions[i] // mass), surplus)
            given[i] = given[i] + extra
            surplus = surplus - extra
    return np.array([bound] + given)


def uneven(stream_key, number_of, total, most, lean):
    if number_of == 2:
        one = jax.random.randint(stream_key, (), max(1, total - most), min(most, total - 1) + 1)
        return jnp.stack([one, total - one])
    sizes = jnp.asarray(profile(number_of, total, most, lean), jnp.int32)
    couples = (number_of - 1) // 2
    donor, taker = sizes[1:1 + 2 * couples:2], sizes[2:2 + 2 * couples:2]
    room = jnp.minimum(donor - 1, most - taker)
    passed = jax.random.randint(jax.random.fold_in(stream_key, 1), (couples,), 0, 1 << 20) % (room + 1)
    sizes = sizes.at[1:1 + 2 * couples:2].set(donor - passed).at[2:2 + 2 * couples:2].set(taker + passed)
    return sizes[jax.random.permutation(jax.random.fold_in(stream_key, 2), number_of)]


def bell_draw(key, shape, deviation, bound, pieces=(), kind=jnp.bfloat16):
    loudness = block_scale(key, shape, pieces, -0.22, 0.18) if pieces else 1.0
    drawn = jax.random.normal(key, shape, jnp.float32) * deviation * loudness
    return jnp.minimum(jnp.maximum(drawn, -bound), bound).astype(kind)


def setup_inputs(seed: int = 0) -> dict:
    key_of = jax.random.split(jax.random.key(seed), 24)
    enc_in = bell_draw(key_of[0], (SEQS, SOURCE_TOKENS, D), 1.0, 6.0, ((0, 8), (1, 4)))
    segments = jax.vmap(lambda own: jnp.searchsorted(jnp.cumsum(uneven(own, SOURCE_TOKENS // 512 + 2, SOURCE_TOKENS, SOURCE_TOKENS * 2 // 3, 2)), jnp.arange(SOURCE_TOKENS), side="right"))(jax.random.split(key_of[1], SEQS)).reshape((SEQS, SOURCE_TOKENS)).astype(jnp.int32)
    dec_in = bell_draw(key_of[2], (SEQS, DEC_LEN, D), 1.0, 6.0, ((0, 8), (1, 4)))
    retrieved = draw_retrieved(jax.random.fold_in(key_of[23], 71), 0)
    enc_cot = bell_draw(key_of[4], (SEQS, SOURCE_TOKENS, D), 1.0, 6.0, ((0, 8), (1, 4)))
    dec_cot = bell_draw(key_of[5], (SEQS, DEC_LEN, D), 1.0, 6.0, ((0, 8), (1, 4)))
    enc_qkv = bell_draw(key_of[6], (D, 3 * D), (D // 2) ** -0.5, 0.3125, ((0, 32),))
    enc_out = bell_draw(key_of[7], (D, D), (D // 64) ** -0.5, 1.75, ((0, 32),))
    enc_up = bell_draw(key_of[8], (D, FF), D ** -0.5, 0.21875, ((0, 32),))
    enc_down = bell_draw(key_of[9], (FF, D), FF ** -0.5, 0.109375, ((0, 32),))
    enc_bias = bell_draw(key_of[10], (D, 6), 0.2, 1.25, ((0, 32),))
    enc_up_bias = bell_draw(key_of[11], (FF,), 0.2, 1.25, ((0, 32),))
    enc_gain = jnp.clip(1.0 + 0.1 * jax.random.normal(key_of[12], (D, 2), jnp.float32), 0.5, 1.5).astype(jnp.bfloat16)
    decoder_self_projections = bell_draw(key_of[13], (D, 3 * D), (D // 2) ** -0.5, 0.3125, ((0, 32),))
    dec_out = bell_draw(key_of[14], (D, D), (D // 64) ** -0.5, 1.75, ((0, 32),))
    cross_q = bell_draw(key_of[15], (D, D), (D // 2) ** -0.5, 0.3125, ((0, 32),))
    cross_kv = bell_draw(key_of[16], (D, 2 * D), (D // 2) ** -0.5, 0.3125, ((0, 32),))
    cross_out = bell_draw(key_of[17], (D, D), (D // 64) ** -0.5, 1.75, ((0, 32),))
    dec_up = bell_draw(key_of[18], (D, FF), D ** -0.5, 0.21875, ((0, 32),))
    dec_down = bell_draw(key_of[19], (FF, D), FF ** -0.5, 0.109375, ((0, 32),))
    dec_bias = bell_draw(key_of[20], (D, 10), 0.2, 1.25, ((0, 32),))
    dec_up_bias = bell_draw(key_of[21], (FF,), 0.2, 1.25, ((0, 32),))
    dec_gain = jnp.clip(1.0 + 0.1 * jax.random.normal(key_of[22], (D, 3), jnp.float32), 0.5, 1.5).astype(jnp.bfloat16)
    return {"enc_in": enc_in, "segments": segments, "dec_in": dec_in, "retrieved": retrieved, "enc_cot": enc_cot, "dec_cot": dec_cot, "enc_qkv": enc_qkv, "enc_out": enc_out, "enc_up": enc_up, "enc_down": enc_down, "enc_bias": enc_bias, "enc_up_bias": enc_up_bias, "enc_gain": enc_gain, "decoder_self_projections": decoder_self_projections, "dec_out": dec_out, "cross_q": cross_q, "cross_kv": cross_kv, "cross_out": cross_out, "dec_up": dec_up, "dec_down": dec_down, "dec_bias": dec_bias, "dec_up_bias": dec_up_bias, "dec_gain": dec_gain}


EPS = 1e-05
NEG = -1e+30
HIGH = lax.Precision.HIGHEST

@jax.custom_vjp
def low(v):
    return lax.optimization_barrier(v.astype(jnp.bfloat16)).astype(jnp.float32)

@jax.custom_vjp
def low_back(v):
    return v

def low_keep(v):
    return (low(v), None)

def low_pass(kept, grad):
    return (grad,)

def back_keep(v):
    return (v, None)

def back_low(kept, grad):
    return (low(grad),)
low.defvjp(low_keep, low_pass)
low_back.defvjp(back_keep, back_low)

def matmul(left_side, right_side):
    return jnp.dot(left_side, right_side, precision=HIGH, preferred_element_type=jnp.float32)

def layer_norm(hidden, gain_row, shift_row):
    center = hidden - lax.optimization_barrier(jnp.mean(hidden, axis=-1, keepdims=True))
    spread = lax.optimization_barrier(jnp.mean(center * center, axis=-1, keepdims=True))
    return center * lax.rsqrt(spread + EPS) * gain_row + shift_row

def gelu_exact(values):
    return jax.nn.gelu(values, approximate=False)

def attend_rows(queries, pairs, allowed):
    row_count = queries.shape[0]
    key_count = pairs.shape[0]
    query_heads = queries.reshape(row_count, HEADS, HEAD_DIM)
    key_heads = pairs[:, :D].reshape(key_count, HEADS, HEAD_DIM)
    value_heads = pairs[:, D:].reshape(key_count, HEADS, HEAD_DIM)
    scores = low_back(jnp.einsum('rhd,khd->hrk', query_heads, key_heads, precision=HIGH) * HEAD_DIM ** (-0.5))
    if allowed is not None:
        scores = jnp.where(allowed[None], scores, NEG)
    row_max = lax.optimization_barrier(jnp.max(scores, axis=-1, keepdims=True))
    lifted = jnp.exp(scores - row_max)
    attn_probs = low(lifted / lax.optimization_barrier(jnp.sum(lifted, axis=-1, keepdims=True)))
    output = jnp.einsum('hrk,khd->rhd', attn_probs, value_heads, precision=HIGH)
    return output.reshape(row_count, D)

def encoder_attention(queries, pairs, seg_row):
    block_size = min(512, SOURCE_TOKENS)
    block_count = SOURCE_TOKENS // block_size

    def one_block(inputs):
        query_block, seg_block = inputs
        return attend_rows(query_block, pairs, seg_block[:, None] == seg_row[None, :])
    output = lax.map(jax.checkpoint(one_block), (queries.reshape(block_count, block_size, D), seg_row.reshape(block_count, block_size)))
    return output.reshape(SOURCE_TOKENS, D)

def decoder_attention(queries, pairs):
    block_size = min(512, DEC_LEN)
    block_count = DEC_LEN // block_size
    key_pos = jnp.arange(DEC_LEN, dtype=jnp.int32)

    def one_block(inputs):
        query_block, query_pos = inputs
        return attend_rows(query_block, pairs, query_pos[:, None] >= key_pos[None, :])
    output = lax.map(jax.checkpoint(one_block), (queries.reshape(block_count, block_size, D), key_pos.reshape(block_count, block_size)))
    return output.reshape(DEC_LEN, D)

def cross_attention(queries, memory_pairs, pick_table):
    block_count = DEC_LEN // BLOCK

    def one_block(inputs):
        query_block, chosen_row = inputs
        return attend_rows(query_block, jnp.take(memory_pairs, chosen_row, axis=0), None)
    output = lax.map(jax.checkpoint(one_block), (queries.reshape(block_count, BLOCK, D), pick_table))
    return output.reshape(DEC_LEN, D)

def feed_forward(first_norm, up_w, up_bias, down_w, down_bias, gain_row, shift_row):
    lifted = low_back(matmul(low(first_norm), up_w) + up_bias)
    activated = low(gelu_exact(lifted))
    branch = low_back(matmul(activated, down_w) + down_bias)
    return layer_norm(first_norm + branch, gain_row, shift_row)

def encoder_layer(weights, hidden, seg_row):
    qkv_w, out_w, up_w, down_w, bias_cols, up_bias, gain_cols = weights
    bias_rows = bias_cols.T
    gain_rows = gain_cols.T
    zero_row = jnp.zeros((D,), jnp.float32)
    projected = low(low_back(matmul(hidden, qkv_w) + jnp.concatenate([bias_rows[0], zero_row, bias_rows[1]])))
    attended = encoder_attention(projected[:, :D], projected[:, D:], seg_row)
    attended = low(low_back(attended))
    branch = low_back(matmul(attended, out_w) + bias_rows[2])
    first_norm = layer_norm(hidden + branch, gain_rows[0], bias_rows[4])
    return feed_forward(first_norm, up_w, up_bias, down_w, bias_rows[3], gain_rows[1], bias_rows[5])

def decoder_layer(weights, hidden, memory, pick_table):
    self_w, self_out_w, query_w, pair_w, cross_out_w, up_w, down_w, bias_cols, up_bias, gain_cols = weights
    bias_rows = bias_cols.T
    gain_rows = gain_cols.T
    zero_row = jnp.zeros((D,), jnp.float32)
    projected = low(low_back(matmul(hidden, self_w) + jnp.concatenate([bias_rows[0], zero_row, bias_rows[1]])))
    attended = decoder_attention(projected[:, :D], projected[:, D:])
    attended = low(low_back(attended))
    branch = low_back(matmul(attended, self_out_w) + bias_rows[2])
    first_norm = layer_norm(hidden + branch, gain_rows[0], bias_rows[7])
    cross_query = low(low_back(matmul(low(first_norm), query_w) + bias_rows[3]))
    memory_pairs = low(low_back(matmul(low(memory), pair_w) + jnp.concatenate([zero_row, bias_rows[4]])))
    crossed = low(low_back(cross_attention(cross_query, memory_pairs, pick_table)))
    cross_branch = low_back(matmul(crossed, cross_out_w) + bias_rows[5])
    second = layer_norm(first_norm + cross_branch, gain_rows[1], bias_rows[8])
    return feed_forward(second, up_w, up_bias, down_w, bias_rows[6], gain_rows[2], bias_rows[9])

def sequence_forward(weights, enc_start, dec_start, seg_row, pick_table):
    memory = encoder_layer(weights[:7], enc_start, seg_row)
    return (memory, decoder_layer(weights[7:], dec_start, memory, pick_table))

def reference(enc_in, segments, dec_in, retrieved, enc_cot, dec_cot, enc_qkv, enc_out, enc_up, enc_down, enc_bias, enc_up_bias, enc_gain, decoder_self_projections, dec_out, cross_q, cross_kv, cross_out, dec_up, dec_down, dec_bias, dec_up_bias, dec_gain):
    weights = tuple((weight.astype(jnp.float32) for weight in (enc_qkv, enc_out, enc_up, enc_down, enc_bias, enc_up_bias, enc_gain, decoder_self_projections, dec_out, cross_q, cross_kv, cross_out, dec_up, dec_down, dec_bias, dec_up_bias, dec_gain)))

    def one_sequence(carry, inputs):
        enc_tokens, dec_tokens, seg_row, pick_table, enc_grad_out, dec_grad_out = inputs

        def forward(params, enc_start, dec_start):
            return sequence_forward(params, enc_start, dec_start, seg_row, pick_table)
        outputs, pull_back = jax.vjp(forward, weights, enc_tokens.astype(jnp.float32), dec_tokens.astype(jnp.float32))
        grad_weights, grad_enc, grad_dec = pull_back((enc_grad_out.astype(jnp.float32), dec_grad_out.astype(jnp.float32)))
        carry = jax.tree.map(jnp.add, carry, grad_weights)
        return (carry, (outputs[0].astype(jnp.bfloat16), outputs[1].astype(jnp.bfloat16), grad_enc, grad_dec))
    zeros_start = jax.tree.map(jnp.zeros_like, weights)
    totals, stacked = lax.scan(one_sequence, zeros_start, (enc_in, dec_in, segments, retrieved, enc_cot, dec_cot))
    return (stacked[0], stacked[1], stacked[2], stacked[3], totals[0], totals[1], totals[2], totals[3], totals[4], totals[5], totals[6], totals[7], totals[8], totals[9], totals[10], totals[11], totals[12], totals[13], totals[14], totals[15], totals[16])
```

```python
import functools

import jax
import jax.numpy as jnp
from jax import lax
from jax.experimental import pallas as pl
from jax.experimental.pallas import tpu as pltpu
from jax.sharding import PartitionSpec as P

D = 768
HEADS = 12
HEAD_DIM = 64
BLOCK = 128


EPS = 1e-05
NEG = -1e30
FLOAT = jnp.float32
BRAIN = jnp.bfloat16


def matmul(left_side, right_side):
    return jnp.dot(left_side, right_side, preferred_element_type=FLOAT)


def matmul_left(left_side, right_side):
    return lax.dot_general(
        left_side, right_side, (((0,), (0,)), ((), ())), preferred_element_type=FLOAT
    )


def matmul_right(left_side, right_side):
    return lax.dot_general(
        left_side, right_side, (((1,), (1,)), ((), ())), preferred_element_type=FLOAT
    )


def column_sum(values):
    return jnp.sum(values, axis=0, dtype=FLOAT)


def layer_norm(hidden, gain_row, shift_row):
    center = hidden - jnp.mean(hidden, axis=-1, keepdims=True)
    spread = jnp.mean(center * center, axis=-1, keepdims=True)
    return center * lax.rsqrt(spread + EPS) * gain_row + shift_row


def gelu_exact(values):
    return jax.nn.gelu(values, approximate=False)


def split_pairs(pairs):
    pair_shape = pairs.shape
    both_parts = pairs.reshape(pair_shape[0], pair_shape[1], 2, HEADS, HEAD_DIM)
    return (both_parts[:, :, 0], both_parts[:, :, 1])


def head_scores(query_heads, key_heads, allowed):
    scores = jnp.einsum(
        "brhd,bkhd->bhrk", query_heads, key_heads, preferred_element_type=FLOAT
    ) * HEAD_DIM ** (-0.5)
    if allowed is not None:
        scores = jnp.where(allowed[:, None], scores, NEG)
    return scores


def attend_forward(queries, pairs, allowed):
    query_heads = queries.reshape(queries.shape[:2] + (HEADS, HEAD_DIM))
    key_heads, value_heads = split_pairs(pairs)
    scores = head_scores(query_heads, key_heads, allowed)
    row_max = jnp.max(scores, axis=-1, keepdims=True)
    log_total = row_max + jnp.log(jnp.sum(jnp.exp(scores - row_max), axis=-1, keepdims=True))
    attn_probs = jnp.exp(scores - log_total).astype(BRAIN)
    output = jnp.einsum("bhrk,bkhd->brhd", attn_probs, value_heads, preferred_element_type=FLOAT)
    return (output.reshape(queries.shape).astype(BRAIN), log_total)


def attend_backward(queries, pairs, allowed, log_total, grad_output):
    query_heads = queries.reshape(queries.shape[:2] + (HEADS, HEAD_DIM))
    key_heads, value_heads = split_pairs(pairs)
    grad_heads = grad_output.reshape(query_heads.shape)
    attn_probs = jnp.exp(head_scores(query_heads, key_heads, allowed) - log_total)
    grad_probs = jnp.einsum(
        "brhd,bkhd->bhrk", grad_heads, value_heads, preferred_element_type=FLOAT
    )
    inner_sum = jnp.sum(attn_probs * grad_probs, axis=-1, keepdims=True)
    grad_scores = (attn_probs * (grad_probs - inner_sum)).astype(BRAIN)
    score_scale = HEAD_DIM ** (-0.5)
    grad_queries = (
        jnp.einsum("bhrk,bkhd->brhd", grad_scores, key_heads, preferred_element_type=FLOAT)
        * score_scale
    )
    grad_keys = (
        jnp.einsum("bhrk,brhd->bkhd", grad_scores, query_heads, preferred_element_type=FLOAT)
        * score_scale
    )
    grad_values = jnp.einsum(
        "bhrk,brhd->bkhd", attn_probs.astype(BRAIN), grad_heads, preferred_element_type=FLOAT
    )
    batch_count, key_count = (pairs.shape[0], pairs.shape[1])
    grad_pairs = jnp.concatenate(
        [
            grad_keys.reshape(batch_count, key_count, D),
            grad_values.reshape(batch_count, key_count, D),
        ],
        axis=-1,
    )
    return (grad_queries.reshape(queries.shape), grad_pairs)


def project_forward(attended, residual, out_w, out_bias, gain_row, shift_row):
    summed = residual + matmul(attended, out_w) + out_bias
    return (layer_norm(summed, gain_row, shift_row), summed)


def project_backward(grad_norm, attended, summed, out_w, gain_row, shift_row):
    normed, pull_back = jax.vjp(layer_norm, summed, gain_row, shift_row)
    grad_summed, grad_gain, grad_shift = pull_back(grad_norm)
    grad_branch = grad_summed.astype(BRAIN)
    grad_out_w = matmul_left(attended, grad_branch)
    grad_out_bias = column_sum(grad_branch)
    grad_attended = matmul_right(grad_branch, out_w).astype(BRAIN)
    return (grad_summed, grad_attended, (grad_out_w, grad_out_bias, grad_gain, grad_shift))


def ffn_forward(first_norm, up_w, up_bias, down_w, down_bias, gain_row, shift_row):
    first_bf = first_norm.astype(BRAIN)
    lifted = matmul(first_bf, up_w) + up_bias
    activated = gelu_exact(lifted).astype(BRAIN)
    summed = first_norm + matmul(activated, down_w) + down_bias
    return (layer_norm(summed, gain_row, shift_row), (first_bf, lifted, activated, summed))


def ffn_backward(grad_norm, retained_context, up_w, down_w, gain_row, shift_row):
    first_bf, lifted, activated, summed = retained_context
    normed, pull_back = jax.vjp(layer_norm, summed, gain_row, shift_row)
    grad_summed, grad_gain, grad_shift = pull_back(grad_norm)
    grad_branch = grad_summed.astype(BRAIN)
    grad_down_w = matmul_left(activated, grad_branch)
    grad_down_bias = column_sum(grad_branch)
    grad_act = matmul_right(grad_branch, down_w)
    lifted_out, pull_gelu = jax.vjp(gelu_exact, lifted)
    grad_lifted = pull_gelu(grad_act)[0].astype(BRAIN)
    grad_up_w = matmul_left(first_bf, grad_lifted)
    up_bias_gradient = column_sum(grad_lifted)
    grad_first = grad_summed + matmul_right(grad_lifted, up_w)
    return (
        grad_first,
        (grad_up_w, up_bias_gradient, grad_down_w, grad_down_bias, grad_gain, grad_shift),
    )


def encoder_forward(weights, tokens, seg_rows, ctx_rank):
    qkv_w, out_w, up_w, down_w, bias_cols, up_bias, gain_cols = weights
    bias_vals = bias_cols.astype(FLOAT).T
    gain_vals = gain_cols.astype(FLOAT).T
    batch_count, row_count = (tokens.shape[0], tokens.shape[1])
    flat_tokens = tokens.reshape(batch_count * row_count, D)
    zero_row = jnp.zeros((D,), FLOAT)
    projected = (
        matmul(flat_tokens, qkv_w) + jnp.concatenate([bias_vals[0], zero_row, bias_vals[1]])
    ).astype(BRAIN)
    projected = projected.reshape(batch_count, row_count, 3 * D)
    all_pairs = lax.all_gather(projected[:, :, D:], "ctx", axis=1, tiled=True)
    own_segs = lax.dynamic_slice_in_dim(seg_rows, ctx_rank * row_count, row_count, axis=1)
    allowed = own_segs[:, :, None] == seg_rows[:, None, :]
    attended, log_total = attend_forward(projected[:, :, :D], all_pairs, allowed)
    attended = attended.reshape(batch_count * row_count, D)
    first_norm, first_sum = project_forward(
        attended, flat_tokens.astype(FLOAT), out_w, bias_vals[2], gain_vals[0], bias_vals[4]
    )
    final_norm, ffn_state = ffn_forward(
        first_norm, up_w, up_bias.astype(FLOAT), down_w, bias_vals[3], gain_vals[1], bias_vals[5]
    )
    return (
        final_norm,
        (flat_tokens, projected, all_pairs, allowed, log_total, attended, first_sum, ffn_state),
    )


def encoder_backward(weights, retained_context, grad_final):
    qkv_w, out_w, up_w, down_w, bias_cols, up_bias, gain_cols = weights
    bias_vals = bias_cols.astype(FLOAT).T
    gain_vals = gain_cols.astype(FLOAT).T
    flat_tokens, projected, all_pairs, allowed, log_total, attended, first_sum, ffn_state = (
        retained_context
    )
    batch_count, row_count = (projected.shape[0], projected.shape[1])
    grad_first, ffn_grads = ffn_backward(
        grad_final, ffn_state, up_w, down_w, gain_vals[1], bias_vals[5]
    )
    grad_tokens, grad_attended, proj_grads = project_backward(
        grad_first, attended, first_sum, out_w, gain_vals[0], bias_vals[4]
    )
    grad_queries, grad_pairs = attend_backward(
        projected[:, :, :D],
        all_pairs,
        allowed,
        log_total,
        grad_attended.reshape(batch_count, row_count, D),
    )
    own_pairs = lax.psum_scatter(
        grad_pairs.astype(jnp.bfloat16), "ctx", scatter_dimension=1, tiled=True
    ).astype(jnp.float32)
    mapped_slope = (
        jnp.concatenate([grad_queries, own_pairs], axis=-1)
        .astype(BRAIN)
        .reshape(batch_count * row_count, 3 * D)
    )
    grad_tokens = grad_tokens + matmul_right(mapped_slope, qkv_w)
    grad_qkv_w = matmul_left(flat_tokens, mapped_slope)
    proj_bias = column_sum(mapped_slope)
    up_grad_w, up_grad_bias, down_grad_w, down_grad_bias, gain_two, shift_two = ffn_grads
    out_grad_w, out_grad_bias, gain_one, shift_one = proj_grads
    bias_grads = jnp.stack(
        [proj_bias[:D], proj_bias[2 * D :], out_grad_bias, down_grad_bias, shift_one, shift_two],
        axis=1,
    )
    gain_grads = jnp.stack([gain_one, gain_two], axis=1)
    return (
        grad_tokens,
        (grad_qkv_w, out_grad_w, up_grad_w, down_grad_w, bias_grads, up_grad_bias, gain_grads),
    )


def decoder_forward(weights, tokens, memory_bf, pick_table, ctx_rank):
    (
        self_w,
        self_out_w,
        query_w,
        pair_w,
        cross_out_w,
        up_w,
        down_w,
        bias_cols,
        up_bias,
        gain_cols,
    ) = weights
    bias_vals = bias_cols.astype(FLOAT).T
    gain_vals = gain_cols.astype(FLOAT).T
    batch_count, row_count = (tokens.shape[0], tokens.shape[1])
    flat_tokens = tokens.reshape(batch_count * row_count, D)
    ctx_count = lax.axis_size("ctx")
    zero_row = jnp.zeros((D,), FLOAT)
    projected = (
        matmul(flat_tokens, self_w) + jnp.concatenate([bias_vals[0], zero_row, bias_vals[1]])
    ).astype(BRAIN)
    projected = projected.reshape(batch_count, row_count, 3 * D)
    all_pairs = lax.all_gather(projected[:, :, D:], "ctx", axis=1, tiled=True)
    query_pos = ctx_rank * row_count + jnp.arange(row_count, dtype=jnp.int32)
    key_pos = jnp.arange(row_count * ctx_count, dtype=jnp.int32)
    causal = (query_pos[:, None] >= key_pos[None, :])[None]
    attended, self_total = attend_forward(projected[:, :, :D], all_pairs, causal)
    attended = attended.reshape(batch_count * row_count, D)
    first_norm, first_sum = project_forward(
        attended, flat_tokens.astype(FLOAT), self_out_w, bias_vals[2], gain_vals[0], bias_vals[7]
    )
    first_bf = first_norm.astype(BRAIN)
    cross_queries = (matmul(first_bf, query_w) + bias_vals[3]).astype(BRAIN)
    memory_pairs = (matmul(memory_bf, pair_w) + jnp.concatenate([zero_row, bias_vals[4]])).astype(
        BRAIN
    )
    memory_rows = memory_pairs.shape[0] // batch_count
    memory_all = lax.all_gather(
        memory_pairs.reshape(batch_count, memory_rows, 2 * D), "ctx", axis=1, tiled=True
    )
    source_count = memory_all.shape[1]
    group_rows = min(row_count, BLOCK)
    group_count = row_count // group_rows
    group_start = ctx_rank * row_count + jnp.arange(group_count, dtype=jnp.int32) * group_rows
    pick_rows = jnp.take(pick_table, group_start // BLOCK, axis=1)
    pick_flat = (
        pick_rows + jnp.arange(batch_count, dtype=jnp.int32)[:, None, None] * source_count
    ).reshape(-1)
    picked = jnp.take(
        memory_all.reshape(batch_count * source_count, 2 * D), pick_flat, axis=0
    ).reshape(batch_count * group_count, pick_rows.shape[2], 2 * D)
    grouped = cross_queries.reshape(batch_count * group_count, group_rows, D)
    crossed, cross_total = attend_forward(grouped, picked, None)
    crossed = crossed.reshape(batch_count * row_count, D)
    second, second_sum = project_forward(
        crossed, first_norm, cross_out_w, bias_vals[5], gain_vals[1], bias_vals[8]
    )
    final_norm, ffn_state = ffn_forward(
        second, up_w, up_bias.astype(FLOAT), down_w, bias_vals[6], gain_vals[2], bias_vals[9]
    )
    retained_context = (
        flat_tokens,
        projected,
        all_pairs,
        causal,
        self_total,
        attended,
        first_sum,
        first_bf,
        grouped,
        pick_flat,
        picked,
        cross_total,
        crossed,
        second_sum,
        ffn_state,
        source_count,
    )
    return (final_norm, retained_context)


def decoder_backward(weights, memory_bf, retained_context, grad_final):
    (
        self_w,
        self_out_w,
        query_w,
        pair_w,
        cross_out_w,
        up_w,
        down_w,
        bias_cols,
        up_bias,
        gain_cols,
    ) = weights
    bias_vals = bias_cols.astype(FLOAT).T
    gain_vals = gain_cols.astype(FLOAT).T
    (
        flat_tokens,
        projected,
        all_pairs,
        causal,
        self_total,
        attended,
        first_sum,
        first_bf,
        grouped,
        pick_flat,
        picked,
        cross_total,
        crossed,
        second_sum,
        ffn_state,
        source_count,
    ) = retained_context
    batch_count, row_count = (projected.shape[0], projected.shape[1])
    grad_second, ffn_grads = ffn_backward(
        grad_final, ffn_state, up_w, down_w, gain_vals[2], bias_vals[9]
    )
    grad_first, grad_crossed, cross_grads = project_backward(
        grad_second, crossed, second_sum, cross_out_w, gain_vals[1], bias_vals[8]
    )
    grad_grouped, grad_picked = attend_backward(
        grouped, picked, None, cross_total, grad_crossed.reshape(grouped.shape)
    )
    grad_memory = (
        jnp.zeros((batch_count * source_count, 2 * D), FLOAT)
        .at[pick_flat]
        .add(grad_picked.reshape(-1, 2 * D))
    )
    own_memory = (
        lax.psum_scatter(
            grad_memory.reshape(batch_count, source_count, 2 * D).astype(jnp.bfloat16),
            "ctx",
            scatter_dimension=1,
            tiled=True,
        )
        .astype(jnp.float32)
        .astype(BRAIN)
    )
    own_memory = own_memory.reshape(-1, 2 * D)
    grad_memory_in = matmul_right(own_memory, pair_w)
    grad_pair_w = matmul_left(memory_bf, own_memory)
    pair_bias = column_sum(own_memory[:, D:])
    grad_cross_q = grad_grouped.reshape(batch_count * row_count, D).astype(BRAIN)
    grad_query_w = matmul_left(first_bf, grad_cross_q)
    query_bias = column_sum(grad_cross_q)
    grad_first = grad_first + matmul_right(grad_cross_q, query_w)
    grad_tokens, grad_attended, self_grads = project_backward(
        grad_first, attended, first_sum, self_out_w, gain_vals[0], bias_vals[7]
    )
    grad_queries, grad_pairs = attend_backward(
        projected[:, :, :D],
        all_pairs,
        causal,
        self_total,
        grad_attended.reshape(batch_count, row_count, D),
    )
    own_pairs = lax.psum_scatter(
        grad_pairs.astype(jnp.bfloat16), "ctx", scatter_dimension=1, tiled=True
    ).astype(jnp.float32)
    mapped_slope = (
        jnp.concatenate([grad_queries, own_pairs], axis=-1)
        .astype(BRAIN)
        .reshape(batch_count * row_count, 3 * D)
    )
    grad_tokens = grad_tokens + matmul_right(mapped_slope, self_w)
    grad_self_w = matmul_left(flat_tokens, mapped_slope)
    self_bias = column_sum(mapped_slope)
    up_grad_w, up_grad_bias, down_grad_w, down_grad_bias, gain_three, shift_three = ffn_grads
    cross_out_grad_w, cross_out_bias, gain_two, shift_two = cross_grads
    self_out_grad_w, self_out_bias, gain_one, shift_one = self_grads
    bias_grads = jnp.stack(
        [
            self_bias[:D],
            self_bias[2 * D :],
            self_out_bias,
            query_bias,
            pair_bias,
            cross_out_bias,
            down_grad_bias,
            shift_one,
            shift_two,
            shift_three,
        ],
        axis=1,
    )
    gain_grads = jnp.stack([gain_one, gain_two, gain_three], axis=1)
    weight_grads = (
        grad_self_w,
        self_out_grad_w,
        grad_query_w,
        grad_pair_w,
        cross_out_grad_w,
        up_grad_w,
        down_grad_w,
        bias_grads,
        up_grad_bias,
        gain_grads,
    )
    return (grad_tokens, grad_memory_in, weight_grads)


def fetch_weights(shards):
    return (
        lax.all_gather(shards[0], ("dp", "ctx"), axis=0, tiled=True),
        lax.all_gather(shards[1], ("dp", "ctx"), axis=0, tiled=True),
        lax.all_gather(shards[2], ("dp", "ctx"), axis=0, tiled=True),
        lax.all_gather(shards[3], ("dp", "ctx"), axis=0, tiled=True),
        lax.all_gather(shards[4], ("dp", "ctx"), axis=0, tiled=True),
        lax.all_gather(shards[5], ("dp", "ctx"), axis=0, tiled=True),
        lax.all_gather(shards[6], ("dp", "ctx"), axis=0, tiled=True),
        lax.all_gather(shards[7], ("dp", "ctx"), axis=0, tiled=True),
        lax.all_gather(shards[8], ("dp", "ctx"), axis=0, tiled=True),
        lax.all_gather(shards[9], ("dp", "ctx"), axis=0, tiled=True),
        lax.all_gather(shards[10], ("dp", "ctx"), axis=0, tiled=True),
        lax.all_gather(shards[11], ("dp", "ctx"), axis=0, tiled=True),
        lax.all_gather(shards[12], ("dp", "ctx"), axis=0, tiled=True),
        lax.all_gather(shards[13], ("dp", "ctx"), axis=0, tiled=True),
        lax.all_gather(shards[14], ("dp", "ctx"), axis=0, tiled=True),
        lax.all_gather(shards[15], ("dp", "ctx"), axis=0, tiled=True),
        lax.all_gather(shards[16], ("dp", "ctx"), axis=0, tiled=True),
    )


def body(
    enc_in,
    segments,
    dec_in,
    retrieved,
    enc_cot,
    dec_cot,
    enc_qkv,
    enc_out,
    enc_up,
    enc_down,
    enc_bias,
    enc_up_bias,
    enc_gain,
    decoder_self_projections,
    dec_out,
    cross_q,
    cross_kv,
    cross_out,
    dec_up,
    dec_down,
    dec_bias,
    dec_up_bias,
    dec_gain,
):
    shards = (
        enc_qkv,
        enc_out,
        enc_up,
        enc_down,
        enc_bias,
        enc_up_bias,
        enc_gain,
        decoder_self_projections,
        dec_out,
        cross_q,
        cross_kv,
        cross_out,
        dec_up,
        dec_down,
        dec_bias,
        dec_up_bias,
        dec_gain,
    )
    ctx_rank = lax.axis_index("ctx")
    batch_count, enc_rows, dec_rows = (enc_in.shape[0], enc_in.shape[1], dec_in.shape[1])
    kept_weights = fetch_weights(shards)
    enc_final, enc_state = encoder_forward(kept_weights[:7], enc_in, segments, ctx_rank)
    memory_bf = enc_final.astype(BRAIN)
    dec_final, dec_state = decoder_forward(kept_weights[7:], dec_in, memory_bf, retrieved, ctx_rank)
    dec_grad_in, memory_grad, dec_weight_grads = decoder_backward(
        kept_weights[7:], memory_bf, dec_state, dec_cot.reshape(-1, D).astype(FLOAT)
    )
    enc_grad_in, enc_weight_grads = encoder_backward(
        kept_weights[:7], enc_state, enc_cot.reshape(-1, D).astype(FLOAT) + memory_grad
    )
    totals = enc_weight_grads + dec_weight_grads
    reduced = (
        lax.psum_scatter(totals[0], ("dp", "ctx"), scatter_dimension=0, tiled=True),
        lax.psum_scatter(totals[1], ("dp", "ctx"), scatter_dimension=0, tiled=True),
        lax.psum_scatter(totals[2], ("dp", "ctx"), scatter_dimension=0, tiled=True),
        lax.psum_scatter(totals[3], ("dp", "ctx"), scatter_dimension=0, tiled=True),
        lax.psum_scatter(totals[4], ("dp", "ctx"), scatter_dimension=0, tiled=True),
        lax.psum_scatter(totals[5], ("dp", "ctx"), scatter_dimension=0, tiled=True),
        lax.psum_scatter(totals[6], ("dp", "ctx"), scatter_dimension=0, tiled=True),
        lax.psum_scatter(totals[7], ("dp", "ctx"), scatter_dimension=0, tiled=True),
        lax.psum_scatter(totals[8], ("dp", "ctx"), scatter_dimension=0, tiled=True),
        lax.psum_scatter(totals[9], ("dp", "ctx"), scatter_dimension=0, tiled=True),
        lax.psum_scatter(totals[10], ("dp", "ctx"), scatter_dimension=0, tiled=True),
        lax.psum_scatter(totals[11], ("dp", "ctx"), scatter_dimension=0, tiled=True),
        lax.psum_scatter(totals[12], ("dp", "ctx"), scatter_dimension=0, tiled=True),
        lax.psum_scatter(totals[13], ("dp", "ctx"), scatter_dimension=0, tiled=True),
        lax.psum_scatter(totals[14], ("dp", "ctx"), scatter_dimension=0, tiled=True),
        lax.psum_scatter(totals[15], ("dp", "ctx"), scatter_dimension=0, tiled=True),
        lax.psum_scatter(totals[16], ("dp", "ctx"), scatter_dimension=0, tiled=True),
    )
    return (
        memory_bf.reshape(batch_count, enc_rows, D),
        dec_final.astype(BRAIN).reshape(batch_count, dec_rows, D),
        enc_grad_in.reshape(batch_count, enc_rows, D),
        dec_grad_in.reshape(batch_count, dec_rows, D),
        reduced[0],
        reduced[1],
        reduced[2],
        reduced[3],
        reduced[4],
        reduced[5],
        reduced[6],
        reduced[7],
        reduced[8],
        reduced[9],
        reduced[10],
        reduced[11],
        reduced[12],
        reduced[13],
        reduced[14],
        reduced[15],
        reduced[16],
    )


MESH_ID = pl.DeviceIdType.MESH
LOG2E = 1.4426950408889634
PAIR = 128
ANY = pl.BlockSpec(memory_space=pl.ANY)
DMA_SEM = pltpu.SemaphoreType.DMA


def place():
    dp = lax.axis_index("dp")
    return dp, lax.axis_index("ctx"), lax.rem(dp, 2)


def spread_kernel(token_count, zs, *refs):
    tokens, ints = refs[:token_count], refs[token_count : token_count + 2]
    outs, int_outs = refs[token_count + 2 : 2 * token_count + 2], refs[2 * token_count + 2 : 2 * token_count + 4]
    send, recv, local, int_send, int_recv = refs[2 * token_count + 4 :]
    dp, z, core = place()
    pair = dp - core
    barrier = pltpu.get_barrier_semaphore()
    for step in range(zs):
        for other in range(2):
            if step or other:
                pl.semaphore_signal(
                    barrier, 1, device_id=(pair + lax.rem(core + other, 2), lax.rem(z + step, zs)), device_id_type=MESH_ID
                )
    pl.semaphore_wait(barrier, 2 * zs - 1)
    sibling = (pair + 1 - core, z)
    int_copies = []
    for i in range(2):
        copy = pltpu.make_async_remote_copy(
            ints[i], int_outs[i], int_send.at[i], int_recv.at[i], device_id=sibling, device_id_type=MESH_ID
        )
        copy.start()
        int_copies.append(copy)

    def each(what):
        for t in range(token_count):
            for i in range(2):
                for h in range(2):
                    z_to, core_to = 2 * core + i, lax.rem(h + z, 2)
                    source, target = tokens[t].at[i, pl.ds(h * BLOCK, BLOCK)], outs[t].at[z]
                    stays = jnp.logical_and(z_to == z, core_to == core)

                    @pl.when(stays)
                    def _(source=source, target=target, t=t):
                        what(pltpu.make_async_copy(source, target, local.at[t]), False)

                    @pl.when(jnp.logical_not(stays))
                    def _(source=source, target=target, t=t, i=i, h=h, z_to=z_to, core_to=core_to):
                        what(
                            pltpu.make_async_remote_copy(
                                source,
                                target,
                                send.at[t, 2 * i + h],
                                recv.at[t, z],
                                device_id=(pair + core_to, z_to),
                                device_id_type=MESH_ID,
                            ),
                            True,
                        )

    each(lambda copy, remote: copy.start())
    each(lambda copy, remote: copy.wait_send() if remote else copy.wait())
    for t in range(token_count):
        for s in range(zs):
            @pl.when(jnp.logical_not(jnp.logical_and(s == z, z // 2 == core)))
            def _(t=t, s=s):
                pltpu.make_async_remote_copy(
                    outs[t].at[s], outs[t].at[s], send.at[t, 0], recv.at[t, s], device_id=sibling, device_id_type=MESH_ID
                ).wait_recv()
    for copy in int_copies:
        copy.wait()


def spread(tokens, ints, collective_id):
    zs, count = lax.axis_size("ctx"), len(tokens)
    shapes = [jax.ShapeDtypeStruct((zs, BLOCK, D), t.dtype) for t in tokens]
    shapes += [jax.ShapeDtypeStruct(i.shape, i.dtype) for i in ints]
    got = pl.pallas_call(
        functools.partial(spread_kernel, count, zs),
        out_shape=shapes,
        in_specs=[ANY] * (count + 2),
        out_specs=[ANY] * (count + 2),
        scratch_shapes=[DMA_SEM((count, 4)), DMA_SEM((count, zs)), DMA_SEM((count,)), DMA_SEM((2,)), DMA_SEM((2,))],
        compiler_params=pltpu.CompilerParams(collective_id=collective_id, has_side_effects=True),
        name="spread_tokens",
    )(*tokens, *ints)
    return got[:count], got[count:]


def collect_kernel(count, zs, *refs):
    blocks, outs = refs[:count], refs[count : 2 * count]
    send, recv, local = refs[2 * count :]
    dp, z, core = place()
    pair = dp - core
    barrier = pltpu.get_barrier_semaphore()
    for step in range(zs):
        for other in range(2):
            if step or other:
                pl.semaphore_signal(
                    barrier, 1, device_id=(pair + lax.rem(core + other, 2), lax.rem(z + step, zs)), device_id_type=MESH_ID
                )
    pl.semaphore_wait(barrier, 2 * zs - 1)
    owner, place_in = z // 2, lax.rem(z, 2)

    def each(what):
        for t in range(count):
            for s in range(zs):
                half = lax.rem(core + s, 2)
                source = blocks[t].at[s]
                target = outs[t].at[place_in, pl.ds(half * BLOCK, BLOCK)]
                stays = jnp.logical_and(s == z, owner == core)

                @pl.when(stays)
                def _(source=source, target=target, t=t):
                    what(pltpu.make_async_copy(source, target, local.at[t]), False)

                @pl.when(jnp.logical_not(stays))
                def _(source=source, target=target, t=t, s=s, half=half):
                    what(
                        pltpu.make_async_remote_copy(
                            source,
                            target,
                            send.at[t, s],
                            recv.at[t, 2 * place_in + half],
                            device_id=(pair + owner, s),
                            device_id_type=MESH_ID,
                        ),
                        True,
                    )

    each(lambda copy, remote: copy.start())
    each(lambda copy, remote: copy.wait_send() if remote else copy.wait())
    for t in range(count):
        for i in range(2):
            for h in range(2):
                z_from, core_from = 2 * core + i, lax.rem(h + z, 2)

                @pl.when(jnp.logical_not(jnp.logical_and(z_from == z, core_from == core)))
                def _(t=t, i=i, h=h):
                    target = outs[t].at[i, pl.ds(h * BLOCK, BLOCK)]
                    pltpu.make_async_remote_copy(
                        target, target, send.at[t, 0], recv.at[t, 2 * i + h], device_id=(pair + 1 - core, z), device_id_type=MESH_ID
                    ).wait_recv()


def collect(blocks, collective_id):
    zs, count = lax.axis_size("ctx"), len(blocks)
    return pl.pallas_call(
        functools.partial(collect_kernel, count, zs),
        out_shape=[jax.ShapeDtypeStruct((2, 2 * BLOCK, D), b.dtype) for b in blocks],
        in_specs=[ANY] * count,
        out_specs=[ANY] * count,
        scratch_shapes=[DMA_SEM((count, zs)), DMA_SEM((count, 4)), DMA_SEM((count,))],
        compiler_params=pltpu.CompilerParams(collective_id=collective_id, has_side_effects=True),
        name="collect_tokens",
    )(*blocks)


def key_chunks(rows, causal):
    if causal:
        return [(half, r, BLOCK, r) for r in range(0, rows, BLOCK) for half in range(2)]
    return [(half, r, 2 * BLOCK, 0) for half in range(2) for r in range(0, rows, 2 * BLOCK)]


def nt_dot(a, b):
    return lax.dot_general(a, b, (((1,), (1,)), ((), ())), preferred_element_type=FLOAT)


def head_lanes(values, head):
    lanes = lax.broadcasted_iota(jnp.int32, values.shape, 1)
    return jnp.where(lanes // HEAD_DIM == head, values, jnp.zeros_like(values))


def fold_rows(values, how):
    grouped = values.reshape(values.shape[0] // 8, 8, values.shape[1])
    return how(how(grouped, axis=0), axis=0, keepdims=True)


def attend_fwd_kernel(causal, has_bias, q_ref, k0_ref, v0_ref, k1_ref, v1_ref, bias_ref, o_ref, lse_ref, s_ref, p_ref):
    rows = q_ref.shape[0]
    k_refs = (k0_ref, k1_ref)
    v_all = jnp.concatenate([v0_ref[...], v1_ref[...]], axis=0)
    v_t = v_all.T
    factor = HEAD_DIM ** (-0.5) * LOG2E
    out_t = []
    for head in range(2):
        q = head_lanes(q_ref[...], head)
        top = jnp.full((1, rows), -3e38, FLOAT)
        for half, r, n, c in key_chunks(rows, causal):
            s = nt_dot(k_refs[half][pl.ds(r, n), :], q[c:])
            s = s * factor + bias_ref[pl.ds(half * rows + r, n), c:].astype(FLOAT)
            s_ref[pl.ds(half * rows + r, n), c:] = s
            peak = fold_rows(s, jnp.max)
            peak = jnp.maximum(top[:, c:], peak)
            top = jnp.concatenate([top[:, :c], peak], axis=1) if c else peak
        total = jnp.zeros((1, rows), FLOAT)
        for half, r, n, c in key_chunks(rows, causal):
            p = jnp.exp2(s_ref[pl.ds(half * rows + r, n), c:] - top[:, c:])
            part = total[:, c:] + fold_rows(p, jnp.sum)
            total = jnp.concatenate([total[:, :c], part], axis=1) if c else part
            p_ref[pl.ds(half * rows + r, n), c:] = p.astype(BRAIN)
            if c:
                p_ref[pl.ds(half * rows + r, n), :c] = jnp.zeros((n, c), BRAIN)
        o_t = jnp.dot(v_t[head * HEAD_DIM : (head + 1) * HEAD_DIM], p_ref[...], preferred_element_type=FLOAT)
        out_t.append(o_t / total)
        lse_ref[0, pl.ds(head, 1), :] = top + jnp.log(total) * LOG2E
    o_ref[...] = jnp.concatenate(out_t, axis=0).T.astype(o_ref.dtype)


def attention_forward(queries, q_col, pairs, kv_col, pairs_other, bias, causal):
    rows = queries.shape[0]
    pair_count = D // PAIR
    q_spec = pl.BlockSpec((rows, PAIR), lambda p: (0, q_col + p))
    k_spec = pl.BlockSpec((rows, PAIR), lambda p: (0, kv_col + p))
    v_spec = pl.BlockSpec((rows, PAIR), lambda p: (0, kv_col + pair_count + p))
    k1_spec = pl.BlockSpec((rows, PAIR), lambda p: (0, p))
    v1_spec = pl.BlockSpec((rows, PAIR), lambda p: (0, pair_count + p))
    bias_spec = pl.BlockSpec((2 * rows, rows), lambda p: (0, 0))
    return pl.pallas_call(
        functools.partial(attend_fwd_kernel, causal, True),
        grid=(pair_count,),
        out_shape=[jax.ShapeDtypeStruct((rows, D), BRAIN), jax.ShapeDtypeStruct((pair_count, 8, rows), FLOAT)],
        in_specs=[q_spec, k_spec, v_spec, k1_spec, v1_spec, bias_spec],
        out_specs=[pl.BlockSpec((rows, PAIR), lambda p: (0, p)), pl.BlockSpec((1, 8, rows), lambda p: (p, 0, 0))],
        scratch_shapes=[pltpu.VMEM((2 * rows, rows), FLOAT), pltpu.VMEM((2 * rows, rows), BRAIN)],
        compiler_params=pltpu.CompilerParams(vmem_limit_bytes=48 << 20),
        cost_estimate=pl.CostEstimate(flops=16 * rows * rows * D, bytes_accessed=10 * rows * D * 2, transcendentals=24 * rows * rows),
        name="attend_fwd",
    )(queries, pairs, pairs, pairs_other, pairs_other, bias)


def attend_bwd_kernel(
    causal, q_ref, k0_ref, v0_ref, k1_ref, v1_ref, bias_ref, o_ref, do_ref, lse_ref,
    dq_ref, dk0_ref, dv0_ref, dk1_ref, dv1_ref, ds_ref,
):
    rows = q_ref.shape[0]
    k_refs, v_refs = (k0_ref, k1_ref), (v0_ref, v1_ref)
    dk_refs, dv_refs = (dk0_ref, dk1_ref), (dv0_ref, dv1_ref)
    k_t = jnp.concatenate([k0_ref[...], k1_ref[...]], axis=0).T
    scale = HEAD_DIM ** (-0.5)
    factor = scale * LOG2E
    prod_t = (o_ref[...].astype(FLOAT) * do_ref[...].astype(FLOAT)).T
    dq_t = []
    q_heads = [head_lanes(q_ref[...], head) for head in range(2)]
    do_heads = [head_lanes(do_ref[...], head) for head in range(2)]
    lses = [lse_ref[0, pl.ds(head, 1), :] for head in range(2)]
    deltas = [fold_rows(prod_t[head * HEAD_DIM : (head + 1) * HEAD_DIM], jnp.sum) for head in range(2)]
    for half, r, n, c in key_chunks(rows, causal):
        k, v = k_refs[half][pl.ds(r, n), :], v_refs[half][pl.ds(r, n), :]
        bias = bias_ref[pl.ds(half * rows + r, n), c:].astype(FLOAT)
        dk = dv = None
        for head in range(2):
            q, do = q_heads[head][c:], do_heads[head][c:]
            p = jnp.exp2(nt_dot(k, q) * factor + bias - lses[head][:, c:])
            dv_part = jnp.dot(p.astype(BRAIN), do, preferred_element_type=FLOAT)
            ds = (p * (nt_dot(v, do) - deltas[head][:, c:])).astype(BRAIN)
            ds_ref[head, pl.ds(half * rows + r, n), c:] = ds
            if c:
                ds_ref[head, pl.ds(half * rows + r, n), :c] = jnp.zeros((n, c), BRAIN)
            dk_part = jnp.dot(ds, q, preferred_element_type=FLOAT)
            dk = dk_part if dk is None else dk + dk_part
            dv = dv_part if dv is None else dv + dv_part
        dk_refs[half][pl.ds(r, n), :] = (dk * scale).astype(dk_refs[half].dtype)
        dv_refs[half][pl.ds(r, n), :] = dv.astype(dv_refs[half].dtype)
    for head in range(2):
        dq_t.append(jnp.dot(k_t[head * HEAD_DIM : (head + 1) * HEAD_DIM], ds_ref[head], preferred_element_type=FLOAT))
    dq_ref[...] = (jnp.concatenate(dq_t, axis=0) * scale).T.astype(dq_ref.dtype)


def attention_backward(queries, q_col, pairs, kv_col, pairs_other, bias, causal, attended, grad_attended, lse):
    rows = queries.shape[0]
    pair_count = D // PAIR
    own = lambda p: (0, p)
    block = (rows, PAIR)
    q_spec = pl.BlockSpec(block, lambda p: (0, q_col + p))
    k_spec = pl.BlockSpec(block, lambda p: (0, kv_col + p))
    v_spec = pl.BlockSpec(block, lambda p: (0, kv_col + pair_count + p))
    k1_spec = pl.BlockSpec(block, own)
    v1_spec = pl.BlockSpec(block, lambda p: (0, pair_count + p))
    bias_spec = pl.BlockSpec((2 * rows, rows), lambda p: (0, 0))
    part = pl.BlockSpec(block, own)
    return pl.pallas_call(
        functools.partial(attend_bwd_kernel, causal),
        grid=(pair_count,),
        out_shape=[jax.ShapeDtypeStruct((rows, D), t) for t in (BRAIN, FLOAT, FLOAT, BRAIN, BRAIN)],
        in_specs=[q_spec, k_spec, v_spec, k1_spec, v1_spec, bias_spec, part, part, pl.BlockSpec((1, 8, rows), lambda p: (p, 0, 0))],
        out_specs=[part] * 5,
        scratch_shapes=[pltpu.VMEM((2, 2 * rows, rows), BRAIN)],
        compiler_params=pltpu.CompilerParams(vmem_limit_bytes=48 << 20),
        cost_estimate=pl.CostEstimate(flops=40 * rows * rows * D, bytes_accessed=18 * rows * D * 2, transcendentals=24 * rows * rows),
        name="attend_bwd",
    )(queries, pairs, pairs, pairs_other, pairs_other, bias, attended, grad_attended, lse)


def to_sibling(values):
    count = lax.axis_size("dp")
    return lax.ppermute(values, "dp", [(i, i ^ 1) for i in range(count)])


def own_blocks(per_block, core):
    zs = per_block.shape[0] // 2
    both = per_block.reshape((zs, 2) + per_block.shape[1:])
    flip = lax.rem(jnp.arange(zs, dtype=jnp.int32) + core, 2).reshape((zs,) + (1,) * (per_block.ndim - 1))
    own = jnp.where(flip == 0, both[:, 0], both[:, 1])
    return own, jnp.where(flip == 0, both[:, 1], both[:, 0])


def ordered_keys(per_token, core):
    own, other = own_blocks(per_token.reshape(-1, BLOCK), core)
    return own.reshape(-1), jnp.concatenate([own.reshape(-1), other.reshape(-1)])


def pack_small(enc_bias, dec_bias, enc_gain, dec_gain, enc_up_bias, dec_up_bias):
    rows = enc_bias.shape[0]
    parts = [enc_bias, dec_bias, enc_gain, dec_gain, enc_up_bias.reshape(rows, -1), dec_up_bias.reshape(rows, -1)]
    width = sum(p.shape[1] for p in parts)
    parts.append(jnp.zeros((rows, PAIR - width), parts[0].dtype))
    return jnp.concatenate(parts, axis=1)


def unpack_small(packed):
    cuts, at = [], 0
    for width in (6, 10, 2, 3, 4, 4):
        cuts.append(packed[:, at : at + width])
        at += width
    return cuts[0], cuts[1], cuts[2], cuts[3], cuts[4].reshape(-1), cuts[5].reshape(-1)


def columns(packed, widths):
    cuts, at = [], 0
    for width in widths:
        cuts.append(packed[:, at : at + width])
        at += width
    return cuts


def with_sibling(own_keys, own_values, other_keys, other_values):
    got = to_sibling(jnp.concatenate([other_keys, other_values], axis=1)).astype(FLOAT)
    return (jnp.concatenate([own_keys, own_values], axis=1) + got).astype(BRAIN)


def self_attention_block(tokens, qkv_w, bias_vals, score_bias, causal):
    zero_row = jnp.zeros((D,), FLOAT)
    projected = (matmul(tokens, qkv_w) + jnp.concatenate([bias_vals[0], zero_row, bias_vals[1]])).astype(BRAIN)
    other = to_sibling(projected[:, D:])
    attended, lse = attention_forward(projected, 0, projected, D // PAIR, other, score_bias, causal)
    return attended, (projected, other, lse)


def self_attention_grad(state, attended, grad_attended, score_bias, causal):
    projected, other, lse = state
    dq, dk, dv, dk_other, dv_other = attention_backward(
        projected, 0, projected, D // PAIR, other, score_bias, causal, attended, grad_attended, lse
    )
    return jnp.concatenate([dq, with_sibling(dk, dv, dk_other, dv_other)], axis=1)


def fast_body(
    enc_in, segments, dec_in, retrieved, enc_cot, dec_cot,
    enc_qkv, enc_out, enc_up, enc_down, enc_bias, enc_up_bias, enc_gain,
    dec_qkv, dec_out, cross_q, cross_kv, cross_out, dec_up, dec_down, dec_bias, dec_up_bias, dec_gain,
):
    dp, z, core = place()
    axes = ("dp", "ctx")
    small = pack_small(enc_bias, dec_bias, enc_gain, dec_gain, enc_up_bias, dec_up_bias)
    first_pack = jnp.concatenate([enc_qkv, enc_out, enc_up, small], axis=1)
    down_pack = jnp.concatenate([enc_down, dec_down], axis=1)
    last_pack = jnp.concatenate([dec_qkv, dec_out, cross_q, cross_kv, cross_out, dec_up], axis=1)
    first_widths = [w.shape[1] for w in (enc_qkv, enc_out, enc_up, small)]
    last_widths = [w.shape[1] for w in (dec_qkv, dec_out, cross_q, cross_kv, cross_out, dec_up)]
    first_all = lax.all_gather(first_pack, axes, axis=0, tiled=True)
    down_all = lax.all_gather(down_pack, axes, axis=0, tiled=True)
    last_all = lax.all_gather(last_pack, axes, axis=0, tiled=True)

    (enc_t, dec_t, enc_c, dec_c), (seg_other, ret_other) = spread([enc_in, dec_in, enc_cot, dec_cot], [segments, retrieved], 0)
    zs = enc_t.shape[0]
    rows = zs * BLOCK
    enc_t, dec_t, enc_c, dec_c = (t.reshape(rows, D) for t in (enc_t, dec_t, enc_c, dec_c))
    here = z // 2 == core
    seg = lax.dynamic_index_in_dim(jnp.where(here, segments, seg_other), lax.rem(z, 2), 0, keepdims=False)
    ret = lax.dynamic_index_in_dim(jnp.where(here, retrieved, ret_other), lax.rem(z, 2), 0, keepdims=False)
    seg_q, seg_k = ordered_keys(seg, core)
    pos_q, pos_k = ordered_keys(jnp.arange(2 * rows, dtype=jnp.int32), core)
    enc_mask = jnp.where(seg_k[:, None] == seg_q[None, :], 0.0, NEG).astype(FLOAT)
    dec_mask = jnp.where(pos_k[:, None] <= pos_q[None, :], 0.0, NEG).astype(FLOAT)
    ret_own, _ = own_blocks(ret, core)
    member = jnp.any(pos_k[:, None, None] == ret_own[None], axis=-1)
    cross_mask = jnp.broadcast_to(jnp.where(member, 0.0, NEG).astype(FLOAT)[:, :, None], (2 * rows, zs, BLOCK)).reshape(2 * rows, rows)

    w_enc_qkv, w_enc_out, w_enc_up, smalls = columns(first_all, first_widths)
    b_enc, b_dec, g_enc, g_dec, enc_ub, dec_ub = unpack_small(smalls)
    eb, db, eg, dg = (v.astype(FLOAT).T for v in (b_enc, b_dec, g_enc, g_dec))
    enc_ub, dec_ub = enc_ub.astype(FLOAT), dec_ub.astype(FLOAT)
    w_enc_down, w_dec_down = down_all[:, :D], down_all[:, D:]
    w_dec_qkv, w_dec_out, w_cross_q, w_cross_kv, w_cross_out, w_dec_up = columns(last_all, last_widths)

    e_att, e_state = self_attention_block(enc_t, w_enc_qkv, eb, enc_mask, False)
    e_first, e_sum = project_forward(e_att, enc_t.astype(FLOAT), w_enc_out, eb[2], eg[0], eb[4])
    enc_final, e_ffn = ffn_forward(e_first, w_enc_up, enc_ub, w_enc_down, eb[3], eg[1], eb[5])
    memory = enc_final.astype(BRAIN)
    zero_row = jnp.zeros((D,), FLOAT)
    d_att, d_state = self_attention_block(dec_t, w_dec_qkv, db, dec_mask, True)
    d_first, d_sum = project_forward(d_att, dec_t.astype(FLOAT), w_dec_out, db[2], dg[0], db[7])
    first_bf = d_first.astype(BRAIN)
    cross_queries = (matmul(first_bf, w_cross_q) + db[3]).astype(BRAIN)
    mem_pairs = (matmul(memory, w_cross_kv) + jnp.concatenate([zero_row, db[4]])).astype(BRAIN)
    mem_other = to_sibling(mem_pairs)
    crossed, cross_lse = attention_forward(cross_queries, 0, mem_pairs, 0, mem_other, cross_mask, False)
    second, second_sum = project_forward(crossed, d_first, w_cross_out, db[5], dg[1], db[8])
    dec_final, d_ffn = ffn_forward(second, w_dec_up, dec_ub, w_dec_down, db[6], dg[2], db[9])
    grad_second, (g_dec_up, g_dec_ub, g_dec_down, g_db6, g_dg2, g_db9) = ffn_backward(
        dec_c.astype(FLOAT), d_ffn, w_dec_up, w_dec_down, dg[2], db[9]
    )
    grad_first, grad_crossed, (g_cross_out, g_db5, g_dg1, g_db8) = project_backward(
        grad_second, crossed, second_sum, w_cross_out, dg[1], db[8]
    )
    g_cq, dk, dv, dk_o, dv_o = attention_backward(
        cross_queries, 0, mem_pairs, 0, mem_other, cross_mask, False, crossed, grad_crossed, cross_lse
    )
    own_memory = with_sibling(dk, dv, dk_o, dv_o)
    g_cross_q, g_db3 = matmul_left(first_bf, g_cq), column_sum(g_cq)
    grad_first = grad_first + matmul_right(g_cq, w_cross_q)
    memory_grad = matmul_right(own_memory, w_cross_kv)
    g_cross_kv, g_db4 = matmul_left(memory, own_memory), column_sum(own_memory[:, D:])
    grad_dec, grad_d_att, (g_dec_out, g_db2, g_dg0, g_db7) = project_backward(grad_first, d_att, d_sum, w_dec_out, dg[0], db[7])
    d_slope = self_attention_grad(d_state, d_att, grad_d_att, dec_mask, True)
    grad_dec = grad_dec + matmul_right(d_slope, w_dec_qkv)
    g_dec_qkv, d_slope_sum = matmul_left(dec_t, d_slope), column_sum(d_slope)
    grad_e_first, (g_enc_up, g_enc_ub, g_enc_down, g_eb3, g_eg1, g_eb5) = ffn_backward(
        enc_c.astype(FLOAT) + memory_grad, e_ffn, w_enc_up, w_enc_down, eg[1], eb[5]
    )
    grad_enc, grad_e_att, (g_enc_out, g_eb2, g_eg0, g_eb4) = project_backward(grad_e_first, e_att, e_sum, w_enc_out, eg[0], eb[4])
    e_slope = self_attention_grad(e_state, e_att, grad_e_att, enc_mask, False)
    grad_enc = grad_enc + matmul_right(e_slope, w_enc_qkv)
    g_enc_qkv, e_slope_sum = matmul_left(enc_t, e_slope), column_sum(e_slope)

    g_eb = jnp.stack([e_slope_sum[:D], e_slope_sum[2 * D :], g_eb2, g_eb3, g_eb4, g_eb5], axis=1)
    g_db = jnp.stack(
        [d_slope_sum[:D], d_slope_sum[2 * D :], g_db2, g_db3, g_db4, g_db5, g_db6, g_db7, g_db8, g_db9], axis=1
    )
    g_eg, g_dg = jnp.stack([g_eg0, g_eg1], axis=1), jnp.stack([g_dg0, g_dg1, g_dg2], axis=1)
    g_small = pack_small(g_eb, g_db, g_eg, g_dg, g_enc_ub, g_dec_ub)
    join = lambda parts: jnp.concatenate([p.astype(BRAIN) for p in parts], axis=1)
    scatter = lambda packed: lax.psum_scatter(packed, axes, scatter_dimension=0, tiled=True).astype(FLOAT)
    last_sum = scatter(join([g_dec_qkv, g_dec_out, g_cross_q, g_cross_kv, g_cross_out, g_dec_up]))
    down_sum = scatter(join([g_enc_down, g_dec_down]))
    first_sum = scatter(join([g_enc_qkv, g_enc_out, g_enc_up, g_small]))
    r_dec_qkv, r_dec_out, r_cross_q, r_cross_kv, r_cross_out, r_dec_up = columns(last_sum, last_widths)
    r_enc_down, r_dec_down = columns(down_sum, [D, D])
    r_enc_qkv, r_enc_out, r_enc_up, r_small = columns(first_sum, first_widths)
    r_eb, r_db, r_eg, r_dg, r_enc_ub, r_dec_ub = unpack_small(r_small)
    home = collect(
        [v.astype(BRAIN).reshape(zs, BLOCK, D) for v in (memory, dec_final, grad_enc, grad_dec)], 1
    )
    return (
        home[0], home[1], home[2].astype(FLOAT), home[3].astype(FLOAT),
        r_enc_qkv, r_enc_out, r_enc_up, r_enc_down, r_eb, r_enc_ub, r_eg,
        r_dec_qkv, r_dec_out, r_cross_q, r_cross_kv, r_cross_out, r_dec_up, r_dec_down, r_db, r_dec_ub, r_dg,
    )


def solution(mesh):
    in_specs = (
        P("dp", "ctx", None),
        P("dp", None),
        P("dp", "ctx", None),
        P("dp", None, None),
        P("dp", "ctx", None),
        P("dp", "ctx", None),
        P(("dp", "ctx"), None),
        P(("dp", "ctx"), None),
        P(("dp", "ctx"), None),
        P(("dp", "ctx"), None),
        P(("dp", "ctx"), None),
        P(("dp", "ctx")),
        P(("dp", "ctx"), None),
        P(("dp", "ctx"), None),
        P(("dp", "ctx"), None),
        P(("dp", "ctx"), None),
        P(("dp", "ctx"), None),
        P(("dp", "ctx"), None),
        P(("dp", "ctx"), None),
        P(("dp", "ctx"), None),
        P(("dp", "ctx"), None),
        P(("dp", "ctx")),
        P(("dp", "ctx"), None),
    )
    out_specs = (
        P("dp", "ctx", None),
        P("dp", "ctx", None),
        P("dp", "ctx", None),
        P("dp", "ctx", None),
        P(("dp", "ctx"), None),
        P(("dp", "ctx"), None),
        P(("dp", "ctx"), None),
        P(("dp", "ctx"), None),
        P(("dp", "ctx"), None),
        P(("dp", "ctx")),
        P(("dp", "ctx"), None),
        P(("dp", "ctx"), None),
        P(("dp", "ctx"), None),
        P(("dp", "ctx"), None),
        P(("dp", "ctx"), None),
        P(("dp", "ctx"), None),
        P(("dp", "ctx"), None),
        P(("dp", "ctx"), None),
        P(("dp", "ctx"), None),
        P(("dp", "ctx")),
        P(("dp", "ctx"), None),
    )

    def run(*args):
        sequences, tokens = args[0].shape[:2]
        fits = (
            mesh.shape["dp"] % 2 == 0
            and sequences == 2 * mesh.shape["dp"]
            and mesh.shape["ctx"] == 4
            and tokens == 2 * BLOCK * mesh.shape["ctx"]
            and args[2].shape == args[0].shape
            and D % (mesh.shape["dp"] * mesh.shape["ctx"] * 8) == 0
        )
        chosen = fast_body if fits else body
        return jax.shard_map(chosen, mesh=mesh, in_specs=in_specs, out_specs=out_specs, check_vma=False)(*args)

    return run
```

```python
import functools

import jax
import jax.numpy as jnp
from jax import lax
from jax.experimental import pallas as pl
from jax.experimental.pallas import tpu as pltpu
from jax.sharding import PartitionSpec as P

D = 768
HEADS = 12
HEAD_DIM = 64
BLOCK = 128


EPS = 1e-05
NEG = -1e30
FLOAT = jnp.float32
BRAIN = jnp.bfloat16


def matmul(left_side, right_side):
    return jnp.dot(left_side, right_side, preferred_element_type=FLOAT)


def matmul_left(left_side, right_side):
    return lax.dot_general(
        left_side, right_side, (((0,), (0,)), ((), ())), preferred_element_type=FLOAT
    )


def matmul_right(left_side, right_side):
    return lax.dot_general(
        left_side, right_side, (((1,), (1,)), ((), ())), preferred_element_type=FLOAT
    )


def column_sum(values):
    return jnp.sum(values, axis=0, dtype=FLOAT)


def layer_norm(hidden, gain_row, shift_row):
    center = hidden - jnp.mean(hidden, axis=-1, keepdims=True)
    spread = jnp.mean(center * center, axis=-1, keepdims=True)
    return center * lax.rsqrt(spread + EPS) * gain_row + shift_row


def gelu_exact(values):
    return jax.nn.gelu(values, approximate=False)


def split_pairs(pairs):
    pair_shape = pairs.shape
    both_parts = pairs.reshape(pair_shape[0], pair_shape[1], 2, HEADS, HEAD_DIM)
    return (both_parts[:, :, 0], both_parts[:, :, 1])


def head_scores(query_heads, key_heads, allowed):
    scores = jnp.einsum(
        "brhd,bkhd->bhrk", query_heads, key_heads, preferred_element_type=FLOAT
    ) * HEAD_DIM ** (-0.5)
    if allowed is not None:
        scores = jnp.where(allowed[:, None], scores, NEG)
    return scores


def attend_forward(queries, pairs, allowed):
    query_heads = queries.reshape(queries.shape[:2] + (HEADS, HEAD_DIM))
    key_heads, value_heads = split_pairs(pairs)
    scores = head_scores(query_heads, key_heads, allowed)
    row_max = jnp.max(scores, axis=-1, keepdims=True)
    log_total = row_max + jnp.log(jnp.sum(jnp.exp(scores - row_max), axis=-1, keepdims=True))
    attn_probs = jnp.exp(scores - log_total).astype(BRAIN)
    output = jnp.einsum("bhrk,bkhd->brhd", attn_probs, value_heads, preferred_element_type=FLOAT)
    return (output.reshape(queries.shape).astype(BRAIN), log_total)


def attend_backward(queries, pairs, allowed, log_total, grad_output):
    query_heads = queries.reshape(queries.shape[:2] + (HEADS, HEAD_DIM))
    key_heads, value_heads = split_pairs(pairs)
    grad_heads = grad_output.reshape(query_heads.shape)
    attn_probs = jnp.exp(head_scores(query_heads, key_heads, allowed) - log_total)
    grad_probs = jnp.einsum(
        "brhd,bkhd->bhrk", grad_heads, value_heads, preferred_element_type=FLOAT
    )
    inner_sum = jnp.sum(attn_probs * grad_probs, axis=-1, keepdims=True)
    grad_scores = (attn_probs * (grad_probs - inner_sum)).astype(BRAIN)
    score_scale = HEAD_DIM ** (-0.5)
    grad_queries = (
        jnp.einsum("bhrk,bkhd->brhd", grad_scores, key_heads, preferred_element_type=FLOAT)
        * score_scale
    )
    grad_keys = (
        jnp.einsum("bhrk,brhd->bkhd", grad_scores, query_heads, preferred_element_type=FLOAT)
        * score_scale
    )
    grad_values = jnp.einsum(
        "bhrk,brhd->bkhd", attn_probs.astype(BRAIN), grad_heads, preferred_element_type=FLOAT
    )
    batch_count, key_count = (pairs.shape[0], pairs.shape[1])
    grad_pairs = jnp.concatenate(
        [
            grad_keys.reshape(batch_count, key_count, D),
            grad_values.reshape(batch_count, key_count, D),
        ],
        axis=-1,
    )
    return (grad_queries.reshape(queries.shape), grad_pairs)


def project_forward(attended, residual, out_w, out_bias, gain_row, shift_row):
    summed = residual + matmul(attended, out_w) + out_bias
    return (layer_norm(summed, gain_row, shift_row), summed)


def project_backward(grad_norm, attended, summed, out_w, gain_row, shift_row):
    normed, pull_back = jax.vjp(layer_norm, summed, gain_row, shift_row)
    grad_summed, grad_gain, grad_shift = pull_back(grad_norm)
    grad_branch = grad_summed.astype(BRAIN)
    grad_out_w = matmul_left(attended, grad_branch)
    grad_out_bias = column_sum(grad_branch)
    grad_attended = matmul_right(grad_branch, out_w).astype(BRAIN)
    return (grad_summed, grad_attended, (grad_out_w, grad_out_bias, grad_gain, grad_shift))


def ffn_forward(first_norm, up_w, up_bias, down_w, down_bias, gain_row, shift_row):
    first_bf = first_norm.astype(BRAIN)
    lifted = matmul(first_bf, up_w) + up_bias
    activated = gelu_exact(lifted).astype(BRAIN)
    summed = first_norm + matmul(activated, down_w) + down_bias
    return (layer_norm(summed, gain_row, shift_row), (first_bf, lifted, activated, summed))


def ffn_backward(grad_norm, retained_context, up_w, down_w, gain_row, shift_row):
    first_bf, lifted, activated, summed = retained_context
    normed, pull_back = jax.vjp(layer_norm, summed, gain_row, shift_row)
    grad_summed, grad_gain, grad_shift = pull_back(grad_norm)
    grad_branch = grad_summed.astype(BRAIN)
    grad_down_w = matmul_left(activated, grad_branch)
    grad_down_bias = column_sum(grad_branch)
    grad_act = matmul_right(grad_branch, down_w)
    lifted_out, pull_gelu = jax.vjp(gelu_exact, lifted)
    grad_lifted = pull_gelu(grad_act)[0].astype(BRAIN)
    grad_up_w = matmul_left(first_bf, grad_lifted)
    up_bias_gradient = column_sum(grad_lifted)
    grad_first = grad_summed + matmul_right(grad_lifted, up_w)
    return (
        grad_first,
        (grad_up_w, up_bias_gradient, grad_down_w, grad_down_bias, grad_gain, grad_shift),
    )


def encoder_forward(weights, tokens, seg_rows, ctx_rank):
    qkv_w, out_w, up_w, down_w, bias_cols, up_bias, gain_cols = weights
    bias_vals = bias_cols.astype(FLOAT).T
    gain_vals = gain_cols.astype(FLOAT).T
    batch_count, row_count = (tokens.shape[0], tokens.shape[1])
    flat_tokens = tokens.reshape(batch_count * row_count, D)
    zero_row = jnp.zeros((D,), FLOAT)
    projected = (
        matmul(flat_tokens, qkv_w) + jnp.concatenate([bias_vals[0], zero_row, bias_vals[1]])
    ).astype(BRAIN)
    projected = projected.reshape(batch_count, row_count, 3 * D)
    all_pairs = lax.all_gather(projected[:, :, D:], "ctx", axis=1, tiled=True)
    own_segs = lax.dynamic_slice_in_dim(seg_rows, ctx_rank * row_count, row_count, axis=1)
    allowed = own_segs[:, :, None] == seg_rows[:, None, :]
    attended, log_total = attend_forward(projected[:, :, :D], all_pairs, allowed)
    attended = attended.reshape(batch_count * row_count, D)
    first_norm, first_sum = project_forward(
        attended, flat_tokens.astype(FLOAT), out_w, bias_vals[2], gain_vals[0], bias_vals[4]
    )
    final_norm, ffn_state = ffn_forward(
        first_norm, up_w, up_bias.astype(FLOAT), down_w, bias_vals[3], gain_vals[1], bias_vals[5]
    )
    return (
        final_norm,
        (flat_tokens, projected, all_pairs, allowed, log_total, attended, first_sum, ffn_state),
    )


def encoder_backward(weights, retained_context, grad_final):
    qkv_w, out_w, up_w, down_w, bias_cols, up_bias, gain_cols = weights
    bias_vals = bias_cols.astype(FLOAT).T
    gain_vals = gain_cols.astype(FLOAT).T
    flat_tokens, projected, all_pairs, allowed, log_total, attended, first_sum, ffn_state = (
        retained_context
    )
    batch_count, row_count = (projected.shape[0], projected.shape[1])
    grad_first, ffn_grads = ffn_backward(
        grad_final, ffn_state, up_w, down_w, gain_vals[1], bias_vals[5]
    )
    grad_tokens, grad_attended, proj_grads = project_backward(
        grad_first, attended, first_sum, out_w, gain_vals[0], bias_vals[4]
    )
    grad_queries, grad_pairs = attend_backward(
        projected[:, :, :D],
        all_pairs,
        allowed,
        log_total,
        grad_attended.reshape(batch_count, row_count, D),
    )
    own_pairs = lax.psum_scatter(
        grad_pairs.astype(jnp.bfloat16), "ctx", scatter_dimension=1, tiled=True
    ).astype(jnp.float32)
    mapped_slope = (
        jnp.concatenate([grad_queries, own_pairs], axis=-1)
        .astype(BRAIN)
        .reshape(batch_count * row_count, 3 * D)
    )
    grad_tokens = grad_tokens + matmul_right(mapped_slope, qkv_w)
    grad_qkv_w = matmul_left(flat_tokens, mapped_slope)
    proj_bias = column_sum(mapped_slope)
    up_grad_w, up_grad_bias, down_grad_w, down_grad_bias, gain_two, shift_two = ffn_grads
    out_grad_w, out_grad_bias, gain_one, shift_one = proj_grads
    bias_grads = jnp.stack(
        [proj_bias[:D], proj_bias[2 * D :], out_grad_bias, down_grad_bias, shift_one, shift_two],
        axis=1,
    )
    gain_grads = jnp.stack([gain_one, gain_two], axis=1)
    return (
        grad_tokens,
        (grad_qkv_w, out_grad_w, up_grad_w, down_grad_w, bias_grads, up_grad_bias, gain_grads),
    )


def decoder_forward(weights, tokens, memory_bf, pick_table, ctx_rank):
    (
        self_w,
        self_out_w,
        query_w,
        pair_w,
        cross_out_w,
        up_w,
        down_w,
        bias_cols,
        up_bias,
        gain_cols,
    ) = weights
    bias_vals = bias_cols.astype(FLOAT).T
    gain_vals = gain_cols.astype(FLOAT).T
    batch_count, row_count = (tokens.shape[0], tokens.shape[1])
    flat_tokens = tokens.reshape(batch_count * row_count, D)
    ctx_count = lax.axis_size("ctx")
    zero_row = jnp.zeros((D,), FLOAT)
    projected = (
        matmul(flat_tokens, self_w) + jnp.concatenate([bias_vals[0], zero_row, bias_vals[1]])
    ).astype(BRAIN)
    projected = projected.reshape(batch_count, row_count, 3 * D)
    all_pairs = lax.all_gather(projected[:, :, D:], "ctx", axis=1, tiled=True)
    query_pos = ctx_rank * row_count + jnp.arange(row_count, dtype=jnp.int32)
    key_pos = jnp.arange(row_count * ctx_count, dtype=jnp.int32)
    causal = (query_pos[:, None] >= key_pos[None, :])[None]
    attended, self_total = attend_forward(projected[:, :, :D], all_pairs, causal)
    attended = attended.reshape(batch_count * row_count, D)
    first_norm, first_sum = project_forward(
        attended, flat_tokens.astype(FLOAT), self_out_w, bias_vals[2], gain_vals[0], bias_vals[7]
    )
    first_bf = first_norm.astype(BRAIN)
    cross_queries = (matmul(first_bf, query_w) + bias_vals[3]).astype(BRAIN)
    memory_pairs = (matmul(memory_bf, pair_w) + jnp.concatenate([zero_row, bias_vals[4]])).astype(
        BRAIN
    )
    memory_rows = memory_pairs.shape[0] // batch_count
    memory_all = lax.all_gather(
        memory_pairs.reshape(batch_count, memory_rows, 2 * D), "ctx", axis=1, tiled=True
    )
    source_count = memory_all.shape[1]
    group_rows = min(row_count, BLOCK)
    group_count = row_count // group_rows
    group_start = ctx_rank * row_count + jnp.arange(group_count, dtype=jnp.int32) * group_rows
    pick_rows = jnp.take(pick_table, group_start // BLOCK, axis=1)
    pick_flat = (
        pick_rows + jnp.arange(batch_count, dtype=jnp.int32)[:, None, None] * source_count
    ).reshape(-1)
    picked = jnp.take(
        memory_all.reshape(batch_count * source_count, 2 * D), pick_flat, axis=0
    ).reshape(batch_count * group_count, pick_rows.shape[2], 2 * D)
    grouped = cross_queries.reshape(batch_count * group_count, group_rows, D)
    crossed, cross_total = attend_forward(grouped, picked, None)
    crossed = crossed.reshape(batch_count * row_count, D)
    second, second_sum = project_forward(
        crossed, first_norm, cross_out_w, bias_vals[5], gain_vals[1], bias_vals[8]
    )
    final_norm, ffn_state = ffn_forward(
        second, up_w, up_bias.astype(FLOAT), down_w, bias_vals[6], gain_vals[2], bias_vals[9]
    )
    retained_context = (
        flat_tokens,
        projected,
        all_pairs,
        causal,
        self_total,
        attended,
        first_sum,
        first_bf,
        grouped,
        pick_flat,
        picked,
        cross_total,
        crossed,
        second_sum,
        ffn_state,
        source_count,
    )
    return (final_norm, retained_context)


def decoder_backward(weights, memory_bf, retained_context, grad_final):
    (
        self_w,
        self_out_w,
        query_w,
        pair_w,
        cross_out_w,
        up_w,
        down_w,
        bias_cols,
        up_bias,
        gain_cols,
    ) = weights
    bias_vals = bias_cols.astype(FLOAT).T
    gain_vals = gain_cols.astype(FLOAT).T
    (
        flat_tokens,
        projected,
        all_pairs,
        causal,
        self_total,
        attended,
        first_sum,
        first_bf,
        grouped,
        pick_flat,
        picked,
        cross_total,
        crossed,
        second_sum,
        ffn_state,
        source_count,
    ) = retained_context
    batch_count, row_count = (projected.shape[0], projected.shape[1])
    grad_second, ffn_grads = ffn_backward(
        grad_final, ffn_state, up_w, down_w, gain_vals[2], bias_vals[9]
    )
    grad_first, grad_crossed, cross_grads = project_backward(
        grad_second, crossed, second_sum, cross_out_w, gain_vals[1], bias_vals[8]
    )
    grad_grouped, grad_picked = attend_backward(
        grouped, picked, None, cross_total, grad_crossed.reshape(grouped.shape)
    )
    grad_memory = (
        jnp.zeros((batch_count * source_count, 2 * D), FLOAT)
        .at[pick_flat]
        .add(grad_picked.reshape(-1, 2 * D))
    )
    own_memory = (
        lax.psum_scatter(
            grad_memory.reshape(batch_count, source_count, 2 * D).astype(jnp.bfloat16),
            "ctx",
            scatter_dimension=1,
            tiled=True,
        )
        .astype(jnp.float32)
        .astype(BRAIN)
    )
    own_memory = own_memory.reshape(-1, 2 * D)
    grad_memory_in = matmul_right(own_memory, pair_w)
    grad_pair_w = matmul_left(memory_bf, own_memory)
    pair_bias = column_sum(own_memory[:, D:])
    grad_cross_q = grad_grouped.reshape(batch_count * row_count, D).astype(BRAIN)
    grad_query_w = matmul_left(first_bf, grad_cross_q)
    query_bias = column_sum(grad_cross_q)
    grad_first = grad_first + matmul_right(grad_cross_q, query_w)
    grad_tokens, grad_attended, self_grads = project_backward(
        grad_first, attended, first_sum, self_out_w, gain_vals[0], bias_vals[7]
    )
    grad_queries, grad_pairs = attend_backward(
        projected[:, :, :D],
        all_pairs,
        causal,
        self_total,
        grad_attended.reshape(batch_count, row_count, D),
    )
    own_pairs = lax.psum_scatter(
        grad_pairs.astype(jnp.bfloat16), "ctx", scatter_dimension=1, tiled=True
    ).astype(jnp.float32)
    mapped_slope = (
        jnp.concatenate([grad_queries, own_pairs], axis=-1)
        .astype(BRAIN)
        .reshape(batch_count * row_count, 3 * D)
    )
    grad_tokens = grad_tokens + matmul_right(mapped_slope, self_w)
    grad_self_w = matmul_left(flat_tokens, mapped_slope)
    self_bias = column_sum(mapped_slope)
    up_grad_w, up_grad_bias, down_grad_w, down_grad_bias, gain_three, shift_three = ffn_grads
    cross_out_grad_w, cross_out_bias, gain_two, shift_two = cross_grads
    self_out_grad_w, self_out_bias, gain_one, shift_one = self_grads
    bias_grads = jnp.stack(
        [
            self_bias[:D],
            self_bias[2 * D :],
            self_out_bias,
            query_bias,
            pair_bias,
            cross_out_bias,
            down_grad_bias,
            shift_one,
            shift_two,
            shift_three,
        ],
        axis=1,
    )
    gain_grads = jnp.stack([gain_one, gain_two, gain_three], axis=1)
    weight_grads = (
        grad_self_w,
        self_out_grad_w,
        grad_query_w,
        grad_pair_w,
        cross_out_grad_w,
        up_grad_w,
        down_grad_w,
        bias_grads,
        up_grad_bias,
        gain_grads,
    )
    return (grad_tokens, grad_memory_in, weight_grads)


def fetch_weights(shards):
    return (
        lax.all_gather(shards[0], ("dp", "ctx"), axis=0, tiled=True),
        lax.all_gather(shards[1], ("dp", "ctx"), axis=0, tiled=True),
        lax.all_gather(shards[2], ("dp", "ctx"), axis=0, tiled=True),
        lax.all_gather(shards[3], ("dp", "ctx"), axis=0, tiled=True),
        lax.all_gather(shards[4], ("dp", "ctx"), axis=0, tiled=True),
        lax.all_gather(shards[5], ("dp", "ctx"), axis=0, tiled=True),
        lax.all_gather(shards[6], ("dp", "ctx"), axis=0, tiled=True),
        lax.all_gather(shards[7], ("dp", "ctx"), axis=0, tiled=True),
        lax.all_gather(shards[8], ("dp", "ctx"), axis=0, tiled=True),
        lax.all_gather(shards[9], ("dp", "ctx"), axis=0, tiled=True),
        lax.all_gather(shards[10], ("dp", "ctx"), axis=0, tiled=True),
        lax.all_gather(shards[11], ("dp", "ctx"), axis=0, tiled=True),
        lax.all_gather(shards[12], ("dp", "ctx"), axis=0, tiled=True),
        lax.all_gather(shards[13], ("dp", "ctx"), axis=0, tiled=True),
        lax.all_gather(shards[14], ("dp", "ctx"), axis=0, tiled=True),
        lax.all_gather(shards[15], ("dp", "ctx"), axis=0, tiled=True),
        lax.all_gather(shards[16], ("dp", "ctx"), axis=0, tiled=True),
    )


def body(
    enc_in,
    segments,
    dec_in,
    retrieved,
    enc_cot,
    dec_cot,
    enc_qkv,
    enc_out,
    enc_up,
    enc_down,
    enc_bias,
    enc_up_bias,
    enc_gain,
    decoder_self_projections,
    dec_out,
    cross_q,
    cross_kv,
    cross_out,
    dec_up,
    dec_down,
    dec_bias,
    dec_up_bias,
    dec_gain,
):
    shards = (
        enc_qkv,
        enc_out,
        enc_up,
        enc_down,
        enc_bias,
        enc_up_bias,
        enc_gain,
        decoder_self_projections,
        dec_out,
        cross_q,
        cross_kv,
        cross_out,
        dec_up,
        dec_down,
        dec_bias,
        dec_up_bias,
        dec_gain,
    )
    ctx_rank = lax.axis_index("ctx")
    batch_count, enc_rows, dec_rows = (enc_in.shape[0], enc_in.shape[1], dec_in.shape[1])
    kept_weights = fetch_weights(shards)
    enc_final, enc_state = encoder_forward(kept_weights[:7], enc_in, segments, ctx_rank)
    memory_bf = enc_final.astype(BRAIN)
    dec_final, dec_state = decoder_forward(kept_weights[7:], dec_in, memory_bf, retrieved, ctx_rank)
    dec_grad_in, memory_grad, dec_weight_grads = decoder_backward(
        kept_weights[7:], memory_bf, dec_state, dec_cot.reshape(-1, D).astype(FLOAT)
    )
    enc_grad_in, enc_weight_grads = encoder_backward(
        kept_weights[:7], enc_state, enc_cot.reshape(-1, D).astype(FLOAT) + memory_grad
    )
    totals = enc_weight_grads + dec_weight_grads
    reduced = (
        lax.psum_scatter(totals[0], ("dp", "ctx"), scatter_dimension=0, tiled=True),
        lax.psum_scatter(totals[1], ("dp", "ctx"), scatter_dimension=0, tiled=True),
        lax.psum_scatter(totals[2], ("dp", "ctx"), scatter_dimension=0, tiled=True),
        lax.psum_scatter(totals[3], ("dp", "ctx"), scatter_dimension=0, tiled=True),
        lax.psum_scatter(totals[4], ("dp", "ctx"), scatter_dimension=0, tiled=True),
        lax.psum_scatter(totals[5], ("dp", "ctx"), scatter_dimension=0, tiled=True),
        lax.psum_scatter(totals[6], ("dp", "ctx"), scatter_dimension=0, tiled=True),
        lax.psum_scatter(totals[7], ("dp", "ctx"), scatter_dimension=0, tiled=True),
        lax.psum_scatter(totals[8], ("dp", "ctx"), scatter_dimension=0, tiled=True),
        lax.psum_scatter(totals[9], ("dp", "ctx"), scatter_dimension=0, tiled=True),
        lax.psum_scatter(totals[10], ("dp", "ctx"), scatter_dimension=0, tiled=True),
        lax.psum_scatter(totals[11], ("dp", "ctx"), scatter_dimension=0, tiled=True),
        lax.psum_scatter(totals[12], ("dp", "ctx"), scatter_dimension=0, tiled=True),
        lax.psum_scatter(totals[13], ("dp", "ctx"), scatter_dimension=0, tiled=True),
        lax.psum_scatter(totals[14], ("dp", "ctx"), scatter_dimension=0, tiled=True),
        lax.psum_scatter(totals[15], ("dp", "ctx"), scatter_dimension=0, tiled=True),
        lax.psum_scatter(totals[16], ("dp", "ctx"), scatter_dimension=0, tiled=True),
    )
    return (
        memory_bf.reshape(batch_count, enc_rows, D),
        dec_final.astype(BRAIN).reshape(batch_count, dec_rows, D),
        enc_grad_in.reshape(batch_count, enc_rows, D),
        dec_grad_in.reshape(batch_count, dec_rows, D),
        reduced[0],
        reduced[1],
        reduced[2],
        reduced[3],
        reduced[4],
        reduced[5],
        reduced[6],
        reduced[7],
        reduced[8],
        reduced[9],
        reduced[10],
        reduced[11],
        reduced[12],
        reduced[13],
        reduced[14],
        reduced[15],
        reduced[16],
    )


MESH_ID = pl.DeviceIdType.MESH
ANY = pl.BlockSpec(memory_space=pl.ANY)
DMA_SEM = pltpu.SemaphoreType.DMA
PAIR = 128


def place():
    dp = lax.axis_index("dp")
    return dp, lax.axis_index("ctx"), lax.rem(dp, 2)


def spot():
    dp, z, core = place()
    return dp, z, core, lax.rem(dp // 2, 2), dp // 4


def dp_of(y, x, core):
    return (y * 2 + x) * 2 + core


def greet():
    dp, z, core, x, y = spot()
    zs = lax.axis_size("ctx")
    barrier = pltpu.get_barrier_semaphore()

    def hello(dp_to, z_to):
        pl.semaphore_signal(barrier, 1, device_id=(dp_to, z_to), device_id_type=MESH_ID)

    for step in range(zs):
        if step:
            hello(dp, lax.rem(z + step, zs))
        hello(dp_of(y, x, 1 - core), lax.rem(z + step, zs))
    hello(dp_of(y, 1 - x, core), z)
    hello(dp_of(1 - y, x, core), z)
    pl.semaphore_wait(barrier, 2 * zs + 1)


def remote(source, target, send, recv, dp_to, z_to):
    return pltpu.make_async_remote_copy(source, target, send, recv, device_id=(dp_to, z_to), device_id_type=MESH_ID)


def staged(count, stages):
    steps = []
    for turn in range(count + max(lag for lag, _ in stages)):
        for lag, fn in stages:
            if 0 <= turn - lag < count:
                steps.append(functools.partial(fn, turn - lag))
    return steps


def halves(shapes):
    chunks = []
    for i, (rows, n) in enumerate(shapes):
        cut = (n // 2) // PAIR * PAIR
        for order, (at, width) in enumerate(((0, cut), (cut, n - cut))):
            if width:
                chunks.append((i, at, width, order))
    return chunks


def gather_job(shards):
    zs = lax.axis_size("ctx")
    everyone = lax.axis_size("dp") * zs
    chunks = halves([s.shape for s in shards])
    count = len(chunks)

    def steps(ins, outs, scratch):
        send, recv, local = scratch
        dp, z, core, x, y = spot()

        def own_part(t):
            i, at, width, _ = chunks[t]
            return ins[i].at[:, pl.ds(at, width)]

        def rows_of(t, dp_at, z_at=None):
            i, at, width, _ = chunks[t]
            where = pl.ds(dp_at * zs, zs) if z_at is None else dp_at * zs + z_at
            return outs[i].at[where, :, pl.ds(at, width)]

        def keep(t):
            return pltpu.make_async_copy(own_part(t), rows_of(t, dp, z), local.at[t])

        def along_z(t, k):
            return remote(own_part(t), rows_of(t, dp, z), send.at[t, k - 1], recv.at[t, k - 1], dp, lax.rem(z + k, zs))

        def hop(t, kind):
            order = chunks[t][3]
            near = (y, 1 - x) if order == 0 else (1 - y, x)
            far = (1 - y, x) if order == 0 else (y, 1 - x)
            block, to = {
                3: ((y, x), near), 4: ((y, x), far), 5: (near, far),
                6: ((y, x), None), 7: (near, None), 8: (far, None), 9: ((1 - y, 1 - x), None),
            }[kind]
            dp_to = dp_of(y, x, 1 - core) if to is None else dp_of(to[0], to[1], core)
            part = rows_of(t, dp_of(block[0], block[1], core))
            return remote(part, part, send.at[t, kind], recv.at[t, kind], dp_to, z)

        def begin(t):
            keep(t).start()
            for k in range(1, zs):
                along_z(t, k).start()

        def first(t):
            keep(t).wait()
            for k in range(1, zs):
                along_z(t, k).wait_recv()
            for kind in (3, 4, 6):
                hop(t, kind).start()

        def second(t):
            hop(t, 3).wait_recv()
            for kind in (5, 7):
                hop(t, kind).start()

        def third(t):
            hop(t, 4).wait_recv()
            hop(t, 8).start()
            hop(t, 5).wait_recv()
            hop(t, 9).start()

        def finish(t):
            for kind in range(6, 10):
                hop(t, kind).wait_recv()
            for k in range(1, zs):
                along_z(t, k).wait_send()
            for kind in range(3, 10):
                hop(t, kind).wait_send()

        return staged(count, [(0, begin), (2, first), (3, second), (4, third), (5, finish)])

    shapes = [jax.ShapeDtypeStruct((everyone,) + s.shape, s.dtype) for s in shards]
    scratch = [DMA_SEM((count, 10)), DMA_SEM((count, 10)), DMA_SEM((count,))]
    return shards, [ANY] * len(shards), shapes, [ANY] * len(shards), scratch, steps


def scatter_job(grads):
    zs, dps = lax.axis_size("ctx"), lax.axis_size("dp")
    rows = [g.shape[0] // (zs * dps) for g in grads]
    chunks = halves([(r, g.shape[1]) for r, g in zip(rows, grads)])
    count = len(chunks)
    inputs = [g.reshape(dps, zs * r, g.shape[1]) for r, g in zip(rows, grads)]
    scratch = [DMA_SEM((count, 10)), DMA_SEM((count, 10)), DMA_SEM((count, 4))]
    for i, _, width, _ in chunks:
        scratch += [
            pltpu.VMEM((4, zs * rows[i], width), BRAIN),
            pltpu.VMEM((4, zs * rows[i], width), BRAIN),
            pltpu.VMEM((2, zs * rows[i], width), BRAIN),
            pltpu.VMEM((zs * rows[i], width), BRAIN),
            pltpu.VMEM((zs, rows[i], width), BRAIN),
            pltpu.VMEM((zs - 1, rows[i], width), BRAIN),
        ]

    def steps(ins, outs, scratch):
        send, recv, local = scratch[:3]
        dp, z, core, x, y = spot()
        buffers = [scratch[3 + 6 * t : 9 + 6 * t] for t in range(count)]

        def source(t, dp_at):
            i, at, width, _ = chunks[t]
            return ins[i].at[dp_at, :, pl.ds(at, width)]

        def load(t, b):
            return pltpu.make_async_copy(source(t, dp_of(b // 2, b % 2, core)), buffers[t][0].at[b], local.at[t, b])

        def to_core(t, b):
            return remote(
                source(t, dp_of(b // 2, b % 2, 1 - core)), buffers[t][1].at[b], send.at[t, b], recv.at[t, b], dp_of(y, x, 1 - core), z
            )

        def wide(t, j):
            if chunks[t][3] == 0:
                block, to = (1 - y) * 2 + j, (1 - y, x)
            else:
                block, to = j * 2 + 1 - x, (y, 1 - x)
            return remote(
                buffers[t][0].at[block], buffers[t][2].at[j], send.at[t, 4 + j], recv.at[t, 4 + j], dp_of(to[0], to[1], core), z
            )

        def narrow(t):
            block, to = (y * 2 + 1 - x, (y, 1 - x)) if chunks[t][3] == 0 else ((1 - y) * 2 + x, (1 - y, x))
            return remote(
                buffers[t][0].at[block], buffers[t][3], send.at[t, 6], recv.at[t, 6], dp_of(to[0], to[1], core), z
            )

        def along_z(t, k):
            z_to = lax.rem(z + k, zs)
            return remote(buffers[t][4].at[z_to], buffers[t][5].at[k - 1], send.at[t, 6 + k], recv.at[t, 6 + k], dp, z_to)

        def add_into(target, other):
            total, width = target.shape

            def some(r, _):
                at = pl.ds(pl.multiple_of(r * 32, 32), 32)
                target[at, :] = (target[at, :].astype(FLOAT) + other[at, :].astype(FLOAT)).astype(BRAIN)
                return 0

            lax.fori_loop(0, total // 32, some, 0)

        def begin(t):
            for b in range(4):
                to_core(t, b).start()
                load(t, b).start()

        def first(t):
            for b in range(4):
                load(t, b).wait()
                to_core(t, b).wait_recv()
                add_into(buffers[t][0].at[b], buffers[t][1].at[b])
            for j in range(2):
                wide(t, j).start()

        def second(t):
            for j in range(2):
                wide(t, j).wait_recv()
                block = y * 2 + j if chunks[t][3] == 0 else j * 2 + x
                add_into(buffers[t][0].at[block], buffers[t][2].at[j])
            narrow(t).start()

        def third(t):
            narrow(t).wait_recv()
            r = rows[chunks[t][0]]
            for s in range(zs):
                at = pl.ds(s * r, r)
                mine = buffers[t][0][y * 2 + x, at, :].astype(FLOAT)
                buffers[t][4][s] = (mine + buffers[t][3][at, :].astype(FLOAT)).astype(BRAIN)
            for k in range(1, zs):
                along_z(t, k).start()

        def finish(t):
            i, at, width, _ = chunks[t]
            total = buffers[t][4][z].astype(FLOAT)
            for k in range(1, zs):
                along_z(t, k).wait_recv()
                total = total + buffers[t][5][k - 1].astype(FLOAT)
            outs[i][:, pl.ds(at, width)] = total
            for b in range(4):
                to_core(t, b).wait_send()
            for j in range(2):
                wide(t, j).wait_send()
            narrow(t).wait_send()
            for k in range(1, zs):
                along_z(t, k).wait_send()

        return staged(count, [(0, begin), (1, first), (2, second), (3, third), (4, finish)])

    shapes = [jax.ShapeDtypeStruct((r, g.shape[1]), FLOAT) for r, g in zip(rows, grads)]
    out_specs = [pl.BlockSpec(s.shape, lambda *_: (0, 0)) for s in shapes]
    return inputs, [ANY] * len(grads), shapes, out_specs, scratch, steps


def spread_job(tokens, ints=()):
    zs, count, int_count = lax.axis_size("ctx"), len(tokens), len(ints)

    def steps(ins, outs, scratch):
        send, recv, local, int_send, int_recv = scratch
        dp, z, core = place()
        pair = dp - core

        def swap(i):
            return remote(ins[count + i], outs[count + i], int_send.at[i], int_recv.at[i], pair + 1 - core, z)

        def each(t, what):
            for i in range(2):
                for h in range(2):
                    z_to, core_to = 2 * core + i, lax.rem(h + z, 2)
                    source, target = ins[t].at[i, pl.ds(h * BLOCK, BLOCK)], outs[t].at[z]
                    stays = jnp.logical_and(z_to == z, core_to == core)

                    @pl.when(stays)
                    def _():
                        what(pltpu.make_async_copy(source, target, local.at[t]), False)

                    @pl.when(jnp.logical_not(stays))
                    def _():
                        what(remote(source, target, send.at[t, 2 * i + h], recv.at[t, z], pair + core_to, z_to), True)

        def begin(t):
            if t == 0:
                for i in range(int_count):
                    swap(i).start()
            each(t, lambda copy, far: copy.start())

        def finish(t):
            each(t, lambda copy, far: copy.wait_send() if far else copy.wait())
            for s in range(zs):

                @pl.when(jnp.logical_not(jnp.logical_and(s == z, z // 2 == core)))
                def _():
                    remote(outs[t].at[s], outs[t].at[s], send.at[t, 0], recv.at[t, s], pair + 1 - core, z).wait_recv()

            if t == 0:
                for i in range(int_count):
                    swap(i).wait()

        return [functools.partial(begin, t) for t in range(count)] + [functools.partial(finish, t) for t in range(count)]

    shapes = [jax.ShapeDtypeStruct((zs, BLOCK, D), t.dtype) for t in tokens]
    shapes += [jax.ShapeDtypeStruct(i.shape, i.dtype) for i in ints]
    n = count + int_count
    scratch = [DMA_SEM((count, 4)), DMA_SEM((count, zs)), DMA_SEM((count,)), DMA_SEM((2,)), DMA_SEM((2,))]
    return list(tokens) + list(ints), [ANY] * n, shapes, [ANY] * n, scratch, steps


def collect_job(blocks):
    zs, count = lax.axis_size("ctx"), len(blocks)

    def steps(ins, outs, scratch):
        send, recv, local = scratch
        dp, z, core = place()
        pair = dp - core
        owner, inside = z // 2, lax.rem(z, 2)

        def each(t, what):
            for s in range(zs):
                half = lax.rem(core + s, 2)
                source = ins[t].at[s]
                target = outs[t].at[inside, pl.ds(half * BLOCK, BLOCK)]
                stays = jnp.logical_and(s == z, owner == core)

                @pl.when(stays)
                def _():
                    what(pltpu.make_async_copy(source, target, local.at[t]), False)

                @pl.when(jnp.logical_not(stays))
                def _():
                    what(remote(source, target, send.at[t, s], recv.at[t, 2 * inside + half], pair + owner, s), True)

        def begin(t):
            each(t, lambda copy, far: copy.start())

        def finish(t):
            each(t, lambda copy, far: copy.wait_send() if far else copy.wait())
            for i in range(2):
                for h in range(2):
                    z_from, core_from = 2 * core + i, lax.rem(h + z, 2)

                    @pl.when(jnp.logical_not(jnp.logical_and(z_from == z, core_from == core)))
                    def _():
                        target = outs[t].at[i, pl.ds(h * BLOCK, BLOCK)]
                        remote(target, target, send.at[t, 0], recv.at[t, 2 * i + h], pair + 1 - core, z).wait_recv()

        return [functools.partial(begin, t) for t in range(count)] + [functools.partial(finish, t) for t in range(count)]

    inputs = [b.reshape(zs, BLOCK, D) for b in blocks]
    shapes = [jax.ShapeDtypeStruct((2, 2 * BLOCK, D), b.dtype) for b in blocks]
    scratch = [DMA_SEM((count, zs)), DMA_SEM((count, 4)), DMA_SEM((count,))]
    return inputs, [ANY] * count, shapes, [ANY] * count, scratch, steps


def merge(lists):
    tagged = []
    for order, steps in enumerate(lists):
        tagged += [((k + 0.5) / len(steps), order, k, step) for k, step in enumerate(steps)]
    return [t[3] for t in sorted(tagged, key=lambda t: t[:3])]


def carry(jobs, collective_id, name, kernel=None, grid=1, args=(), in_specs=(), out_shape=(), out_specs=(), scratch=(), cost=None):
    sizes = [(len(j[0]), len(j[2]), len(j[4])) for j in jobs]

    def body(*refs):
        def take(n):
            nonlocal refs
            got, refs = refs[:n], refs[n:]
            return list(got)

        mine_in = take(len(args))
        job_in = [take(s[0]) for s in sizes]
        mine_out = take(len(out_shape))
        job_out = [take(s[1]) for s in sizes]
        mine_scratch = take(len(scratch))
        job_scratch = [take(s[2]) for s in sizes]
        steps = merge([j[5](i, o, s) for j, i, o, s in zip(jobs, job_in, job_out, job_scratch)])
        if kernel is None:
            greet()
            for step in steps:
                step()
            return
        turn = pl.program_id(0)
        for g in range(grid if jobs else 0):

            @pl.when(turn == g)
            def _():
                if g == 0:
                    greet()
                for step in steps[g * len(steps) // (grid + 1) : (g + 1) * len(steps) // (grid + 1)]:
                    step()

        kernel(*mine_in, *mine_out, *mine_scratch)
        if not jobs:
            return

        @pl.when(turn == grid - 1)
        def _():
            for step in steps[grid * len(steps) // (grid + 1) :]:
                step()

    flat = lambda k: [v for j in jobs for v in j[k]]
    got = pl.pallas_call(
        body,
        grid=(grid,),
        out_shape=list(out_shape) + flat(2),
        in_specs=list(in_specs) + flat(1),
        out_specs=list(out_specs) + flat(3),
        scratch_shapes=list(scratch) + flat(4),
        compiler_params=pltpu.CompilerParams(
            collective_id=collective_id if jobs else None, has_side_effects=bool(jobs), vmem_limit_bytes=60 << 20
        ),
        cost_estimate=cost,
        name=name,
    )(*args, *flat(0))
    own, rest, parts = got[: len(out_shape)], got[len(out_shape) :], []
    for s in sizes:
        parts.append(rest[: s[1]])
        rest = rest[s[1] :]
    return own, parts


LOG2E = 1.4426950408889634


def key_chunks(rows, causal):
    if causal:
        return [(half, r, BLOCK, r) for r in range(0, rows, BLOCK) for half in range(2)]
    return [(half, r, 2 * BLOCK, 0) for half in range(2) for r in range(0, rows, 2 * BLOCK)]


def nt_dot(a, b):
    return lax.dot_general(a, b, (((1,), (1,)), ((), ())), preferred_element_type=FLOAT)


def head_lanes(values, head):
    lanes = lax.broadcasted_iota(jnp.int32, values.shape, 1)
    return jnp.where(lanes // HEAD_DIM == head, values, jnp.zeros_like(values))


def fold_rows(values, how):
    grouped = values.reshape(values.shape[0] // 8, 8, values.shape[1])
    return how(how(grouped, axis=0), axis=0, keepdims=True)


def attend_fwd_kernel(causal, q_ref, k0_ref, v0_ref, k1_ref, v1_ref, bias_ref, o_ref, lse_ref, s_ref, p_ref):
    rows = q_ref.shape[0]
    k_refs = (k0_ref, k1_ref)
    v_all = jnp.concatenate([v0_ref[...], v1_ref[...]], axis=0)
    v_t = v_all.T
    factor = HEAD_DIM ** (-0.5) * LOG2E
    out_t = []
    for head in range(2):
        q = head_lanes(q_ref[...], head)
        top = jnp.full((1, rows), -3e38, FLOAT)
        for half, r, n, c in key_chunks(rows, causal):
            s = nt_dot(k_refs[half][pl.ds(r, n), :], q[c:])
            s = s * factor + bias_ref[pl.ds(half * rows + r, n), c:].astype(FLOAT)
            s_ref[pl.ds(half * rows + r, n), c:] = s
            peak = fold_rows(s, jnp.max)
            peak = jnp.maximum(top[:, c:], peak)
            top = jnp.concatenate([top[:, :c], peak], axis=1) if c else peak
        total = jnp.zeros((1, rows), FLOAT)
        for half, r, n, c in key_chunks(rows, causal):
            p = jnp.exp2(s_ref[pl.ds(half * rows + r, n), c:] - top[:, c:])
            part = total[:, c:] + fold_rows(p, jnp.sum)
            total = jnp.concatenate([total[:, :c], part], axis=1) if c else part
            p_ref[pl.ds(half * rows + r, n), c:] = p.astype(BRAIN)
            if c:
                p_ref[pl.ds(half * rows + r, n), :c] = jnp.zeros((n, c), BRAIN)
        o_t = jnp.dot(v_t[head * HEAD_DIM : (head + 1) * HEAD_DIM], p_ref[...], preferred_element_type=FLOAT)
        out_t.append(o_t / total)
        lse_ref[0, pl.ds(head, 1), :] = top + jnp.log(total) * LOG2E
    o_ref[...] = jnp.concatenate(out_t, axis=0).T.astype(o_ref.dtype)


def attention_forward(queries, q_col, pairs, kv_col, pairs_other, bias, causal, jobs=(), collective_id=None):
    rows = queries.shape[0]
    pair_count = D // PAIR
    block = (rows, PAIR)
    spec = lambda at: pl.BlockSpec(block, lambda p: (0, at + p))
    own, parts = carry(
        list(jobs),
        collective_id,
        "attend_fwd",
        kernel=functools.partial(attend_fwd_kernel, causal),
        grid=pair_count,
        args=(queries, pairs, pairs, pairs_other, pairs_other, bias),
        in_specs=[
            spec(q_col), spec(kv_col), spec(kv_col + pair_count), spec(0), spec(pair_count),
            pl.BlockSpec((2 * rows, rows), lambda p: (0, 0)),
        ],
        out_shape=[jax.ShapeDtypeStruct((rows, D), BRAIN), jax.ShapeDtypeStruct((pair_count, 8, rows), FLOAT)],
        out_specs=[spec(0), pl.BlockSpec((1, 8, rows), lambda p: (p, 0, 0))],
        scratch=[pltpu.VMEM((2 * rows, rows), FLOAT), pltpu.VMEM((2 * rows, rows), BRAIN)],
        cost=pl.CostEstimate(flops=16 * rows * rows * D, bytes_accessed=10 * rows * D * 2, transcendentals=24 * rows * rows),
    )
    return own[0], own[1], parts


def attend_bwd_kernel(
    causal, q_ref, k0_ref, v0_ref, k1_ref, v1_ref, bias_ref, o_ref, do_ref, lse_ref,
    dq_ref, dk0_ref, dv0_ref, dk1_ref, dv1_ref, ds_ref,
):
    rows = q_ref.shape[0]
    k_refs, v_refs = (k0_ref, k1_ref), (v0_ref, v1_ref)
    dk_refs, dv_refs = (dk0_ref, dk1_ref), (dv0_ref, dv1_ref)
    k_t = jnp.concatenate([k0_ref[...], k1_ref[...]], axis=0).T
    scale = HEAD_DIM ** (-0.5)
    factor = scale * LOG2E
    prod_t = (o_ref[...].astype(FLOAT) * do_ref[...].astype(FLOAT)).T
    dq_t = []
    q_heads = [head_lanes(q_ref[...], head) for head in range(2)]
    do_heads = [head_lanes(do_ref[...], head) for head in range(2)]
    lses = [lse_ref[0, pl.ds(head, 1), :] for head in range(2)]
    deltas = [fold_rows(prod_t[head * HEAD_DIM : (head + 1) * HEAD_DIM], jnp.sum) for head in range(2)]
    for half, r, n, c in key_chunks(rows, causal):
        k, v = k_refs[half][pl.ds(r, n), :], v_refs[half][pl.ds(r, n), :]
        bias = bias_ref[pl.ds(half * rows + r, n), c:].astype(FLOAT)
        dk = dv = None
        for head in range(2):
            q, do = q_heads[head][c:], do_heads[head][c:]
            p = jnp.exp2(nt_dot(k, q) * factor + bias - lses[head][:, c:])
            dv_part = jnp.dot(p.astype(BRAIN), do, preferred_element_type=FLOAT)
            ds = (p * (nt_dot(v, do) - deltas[head][:, c:])).astype(BRAIN)
            ds_ref[head, pl.ds(half * rows + r, n), c:] = ds
            if c:
                ds_ref[head, pl.ds(half * rows + r, n), :c] = jnp.zeros((n, c), BRAIN)
            dk_part = jnp.dot(ds, q, preferred_element_type=FLOAT)
            dk = dk_part if dk is None else dk + dk_part
            dv = dv_part if dv is None else dv + dv_part
        dk_refs[half][pl.ds(r, n), :] = (dk * scale).astype(dk_refs[half].dtype)
        dv_refs[half][pl.ds(r, n), :] = dv.astype(dv_refs[half].dtype)
    for head in range(2):
        dq_t.append(jnp.dot(k_t[head * HEAD_DIM : (head + 1) * HEAD_DIM], ds_ref[head], preferred_element_type=FLOAT))
    dq_ref[...] = (jnp.concatenate(dq_t, axis=0) * scale).T.astype(dq_ref.dtype)


def attention_backward(
    queries, q_col, pairs, kv_col, pairs_other, bias, causal, attended, grad_attended, lse, jobs=(), collective_id=None
):
    rows = queries.shape[0]
    pair_count = D // PAIR
    block = (rows, PAIR)
    spec = lambda at: pl.BlockSpec(block, lambda p: (0, at + p))
    own, parts = carry(
        list(jobs),
        collective_id,
        "attend_bwd",
        kernel=functools.partial(attend_bwd_kernel, causal),
        grid=pair_count,
        args=(queries, pairs, pairs, pairs_other, pairs_other, bias, attended, grad_attended, lse),
        in_specs=[
            spec(q_col), spec(kv_col), spec(kv_col + pair_count), spec(0), spec(pair_count),
            pl.BlockSpec((2 * rows, rows), lambda p: (0, 0)), spec(0), spec(0),
            pl.BlockSpec((1, 8, rows), lambda p: (p, 0, 0)),
        ],
        out_shape=[jax.ShapeDtypeStruct((rows, D), t) for t in (BRAIN, FLOAT, FLOAT, BRAIN, BRAIN)],
        out_specs=[spec(0)] * 5,
        scratch=[pltpu.VMEM((2, 2 * rows, rows), BRAIN)],
        cost=pl.CostEstimate(flops=40 * rows * rows * D, bytes_accessed=18 * rows * D * 2, transcendentals=24 * rows * rows),
    )
    return own, parts


def to_sibling(values):
    count = lax.axis_size("dp")
    return lax.ppermute(values, "dp", [(i, i ^ 1) for i in range(count)])


def own_blocks(per_block, core):
    zs = per_block.shape[0] // 2
    both = per_block.reshape((zs, 2) + per_block.shape[1:])
    flip = lax.rem(jnp.arange(zs, dtype=jnp.int32) + core, 2).reshape((zs,) + (1,) * (per_block.ndim - 1))
    own = jnp.where(flip == 0, both[:, 0], both[:, 1])
    return own, jnp.where(flip == 0, both[:, 1], both[:, 0])


def ordered_keys(per_token, core):
    own, other = own_blocks(per_token.reshape(-1, BLOCK), core)
    return own.reshape(-1), jnp.concatenate([own.reshape(-1), other.reshape(-1)])


def pack_small(enc_bias, dec_bias, enc_gain, dec_gain, enc_up_bias, dec_up_bias):
    rows = enc_bias.shape[0]
    parts = [enc_bias, dec_bias, enc_gain, dec_gain, enc_up_bias.reshape(rows, -1), dec_up_bias.reshape(rows, -1)]
    width = sum(p.shape[1] for p in parts)
    parts.append(jnp.zeros((rows, PAIR - width), parts[0].dtype))
    return jnp.concatenate(parts, axis=1)


def unpack_small(packed):
    cuts, at = [], 0
    for width in (6, 10, 2, 3, 4, 4):
        cuts.append(packed[:, at : at + width])
        at += width
    return cuts[0], cuts[1], cuts[2], cuts[3], cuts[4].reshape(-1), cuts[5].reshape(-1)


def with_sibling(own_keys, own_values, other_keys, other_values):
    got = to_sibling(jnp.concatenate([other_keys, other_values], axis=1)).astype(FLOAT)
    return (jnp.concatenate([own_keys, own_values], axis=1) + got).astype(BRAIN)


def matrix(gathered):
    return gathered.reshape(-1, gathered.shape[2])


def fast_body(
    enc_in, segments, dec_in, retrieved, enc_cot, dec_cot,
    enc_qkv, enc_out, enc_up, enc_down, enc_bias, enc_up_bias, enc_gain,
    dec_qkv, dec_out, cross_q, cross_kv, cross_out, dec_up, dec_down, dec_bias, dec_up_bias, dec_gain,
):
    dp, z, core = place()
    small = pack_small(enc_bias, dec_bias, enc_gain, dec_gain, enc_up_bias, dec_up_bias)
    _, ((enc_t, dec_t, seg_other, ret_other), near) = carry(
        [spread_job([enc_in, dec_in], [segments, retrieved]), gather_job([enc_qkv, dec_qkv, small, enc_out, dec_out])], 0, "begin"
    )
    w_enc_qkv, w_dec_qkv, smalls, w_enc_out, w_dec_out = map(matrix, near)
    zs = enc_t.shape[0]
    rows = zs * BLOCK
    enc_t, dec_t = enc_t.reshape(rows, D), dec_t.reshape(rows, D)
    here = z // 2 == core
    seg = lax.dynamic_index_in_dim(jnp.where(here, segments, seg_other), lax.rem(z, 2), 0, keepdims=False)
    ret = lax.dynamic_index_in_dim(jnp.where(here, retrieved, ret_other), lax.rem(z, 2), 0, keepdims=False)
    seg_q, seg_k = ordered_keys(seg, core)
    pos_q, pos_k = ordered_keys(jnp.arange(2 * rows, dtype=jnp.int32), core)
    enc_mask = jnp.where(seg_k[:, None] == seg_q[None, :], 0.0, NEG).astype(FLOAT)
    dec_mask = jnp.where(pos_k[:, None] <= pos_q[None, :], 0.0, NEG).astype(FLOAT)
    ret_own, _ = own_blocks(ret, core)
    member = jnp.any(pos_k[:, None, None] == ret_own[None], axis=-1)
    cross_mask = jnp.broadcast_to(jnp.where(member, 0.0, NEG).astype(FLOAT)[:, :, None], (2 * rows, zs, BLOCK)).reshape(2 * rows, rows)

    b_enc, b_dec, g_enc, g_dec, enc_ub, dec_ub = unpack_small(smalls)
    eb, db, eg, dg = (v.astype(FLOAT).T for v in (b_enc, b_dec, g_enc, g_dec))
    enc_ub, dec_ub = enc_ub.astype(FLOAT), dec_ub.astype(FLOAT)
    zero_row = jnp.zeros((D,), FLOAT)

    e_proj = (matmul(enc_t, w_enc_qkv) + jnp.concatenate([eb[0], zero_row, eb[1]])).astype(BRAIN)
    e_other = to_sibling(e_proj[:, D:])
    d_proj = (matmul(dec_t, w_dec_qkv) + jnp.concatenate([db[0], zero_row, db[1]])).astype(BRAIN)
    d_other = to_sibling(d_proj[:, D:])
    e_att, e_lse, (far,) = attention_forward(
        e_proj, 0, e_proj, D // PAIR, e_other, enc_mask, False, [gather_job([enc_up, enc_down])], 1
    )
    w_enc_up, w_enc_down = map(matrix, far)
    d_att, d_lse, (far,) = attention_forward(
        d_proj, 0, d_proj, D // PAIR, d_other, dec_mask, True, [gather_job([cross_kv, cross_q, cross_out])], 2
    )
    w_cross_kv, w_cross_q, w_cross_out = map(matrix, far)
    e_first, e_sum = project_forward(e_att, enc_t.astype(FLOAT), w_enc_out, eb[2], eg[0], eb[4])
    enc_final, e_ffn = ffn_forward(e_first, w_enc_up, enc_ub, w_enc_down, eb[3], eg[1], eb[5])
    memory = enc_final.astype(BRAIN)
    d_first, d_sum = project_forward(d_att, dec_t.astype(FLOAT), w_dec_out, db[2], dg[0], db[7])
    first_bf = d_first.astype(BRAIN)
    cross_queries = (matmul(first_bf, w_cross_q) + db[3]).astype(BRAIN)
    mem_pairs = (matmul(memory, w_cross_kv) + jnp.concatenate([zero_row, db[4]])).astype(BRAIN)
    mem_other = to_sibling(mem_pairs)
    crossed, cross_lse, ((enc_c, dec_c), far) = attention_forward(
        cross_queries, 0, mem_pairs, 0, mem_other, cross_mask, False, [spread_job([enc_cot, dec_cot]), gather_job([dec_up, dec_down])], 3
    )
    enc_c, dec_c = enc_c.reshape(rows, D), dec_c.reshape(rows, D)
    w_dec_up, w_dec_down = map(matrix, far)
    second, second_sum = project_forward(crossed, d_first, w_cross_out, db[5], dg[1], db[8])
    dec_final, d_ffn = ffn_forward(second, w_dec_up, dec_ub, w_dec_down, db[6], dg[2], db[9])
    low = lambda *grads: [g.astype(BRAIN) for g in grads]
    grad_second, (g_dec_up, g_dec_ub, g_dec_down, g_db6, g_dg2, g_db9) = ffn_backward(
        dec_c.astype(FLOAT), d_ffn, w_dec_up, w_dec_down, dg[2], db[9]
    )
    grad_first, grad_crossed, (g_cross_out, g_db5, g_dg1, g_db8) = project_backward(
        grad_second, crossed, second_sum, w_cross_out, dg[1], db[8]
    )
    (g_cq, dk, dv, dk_o, dv_o), ((enc_hidden, dec_hidden), (r_dec_up, r_dec_down)) = attention_backward(
        cross_queries, 0, mem_pairs, 0, mem_other, cross_mask, False, crossed, grad_crossed, cross_lse,
        [collect_job([memory, dec_final.astype(BRAIN)]), scatter_job(low(g_dec_up, g_dec_down))], 4,
    )
    own_memory = with_sibling(dk, dv, dk_o, dv_o)
    g_cross_q, g_db3 = matmul_left(first_bf, g_cq), column_sum(g_cq)
    grad_first = grad_first + matmul_right(g_cq, w_cross_q)
    memory_grad = matmul_right(own_memory, w_cross_kv)
    g_cross_kv, g_db4 = matmul_left(memory, own_memory), column_sum(own_memory[:, D:])
    grad_dec, grad_d_att, (g_dec_out, g_db2, g_dg0, g_db7) = project_backward(grad_first, d_att, d_sum, w_dec_out, dg[0], db[7])
    (dq, dk, dv, dk_o, dv_o), ((r_cross_out, r_cross_kv, r_cross_q, r_dec_out),) = attention_backward(
        d_proj, 0, d_proj, D // PAIR, d_other, dec_mask, True, d_att, grad_d_att, d_lse,
        [scatter_job(low(g_cross_out, g_cross_kv, g_cross_q, g_dec_out))], 5,
    )
    d_slope = jnp.concatenate([dq, with_sibling(dk, dv, dk_o, dv_o)], axis=1)
    grad_dec = grad_dec + matmul_right(d_slope, w_dec_qkv)
    g_dec_qkv, d_slope_sum = matmul_left(dec_t, d_slope), column_sum(d_slope)
    grad_e_first, (g_enc_up, g_enc_ub, g_enc_down, g_eb3, g_eg1, g_eb5) = ffn_backward(
        enc_c.astype(FLOAT) + memory_grad, e_ffn, w_enc_up, w_enc_down, eg[1], eb[5]
    )
    grad_enc, grad_e_att, (g_enc_out, g_eb2, g_eg0, g_eb4) = project_backward(grad_e_first, e_att, e_sum, w_enc_out, eg[0], eb[4])
    (dq, dk, dv, dk_o, dv_o), ((dec_home,), (r_enc_up, r_enc_down)) = attention_backward(
        e_proj, 0, e_proj, D // PAIR, e_other, enc_mask, False, e_att, grad_e_att, e_lse,
        [collect_job(low(grad_dec)), scatter_job(low(g_enc_up, g_enc_down))], 6,
    )
    e_slope = jnp.concatenate([dq, with_sibling(dk, dv, dk_o, dv_o)], axis=1)
    grad_enc = grad_enc + matmul_right(e_slope, w_enc_qkv)
    g_enc_qkv, e_slope_sum = matmul_left(enc_t, e_slope), column_sum(e_slope)

    g_eb = jnp.stack([e_slope_sum[:D], e_slope_sum[2 * D :], g_eb2, g_eb3, g_eb4, g_eb5], axis=1)
    g_db = jnp.stack(
        [d_slope_sum[:D], d_slope_sum[2 * D :], g_db2, g_db3, g_db4, g_db5, g_db6, g_db7, g_db8, g_db9], axis=1
    )
    g_eg, g_dg = jnp.stack([g_eg0, g_eg1], axis=1), jnp.stack([g_dg0, g_dg1, g_dg2], axis=1)
    g_small = pack_small(g_eb, g_db, g_eg, g_dg, g_enc_ub, g_dec_ub)
    _, ((enc_home,), (r_dec_qkv, r_enc_out, r_enc_qkv, r_small)) = carry(
        [collect_job(low(grad_enc)), scatter_job(low(g_dec_qkv, g_enc_out, g_enc_qkv, g_small))], 7, "end"
    )
    r_eb, r_db, r_eg, r_dg, r_enc_ub, r_dec_ub = unpack_small(r_small)
    return (
        enc_hidden, dec_hidden, enc_home.astype(FLOAT), dec_home.astype(FLOAT),
        r_enc_qkv, r_enc_out, r_enc_up, r_enc_down, r_eb, r_enc_ub, r_eg,
        r_dec_qkv, r_dec_out, r_cross_q, r_cross_kv, r_cross_out, r_dec_up, r_dec_down, r_db, r_dec_ub, r_dg,
    )


def solution(mesh):
    in_specs = (
        P("dp", "ctx", None),
        P("dp", None),
        P("dp", "ctx", None),
        P("dp", None, None),
        P("dp", "ctx", None),
        P("dp", "ctx", None),
        P(("dp", "ctx"), None),
        P(("dp", "ctx"), None),
        P(("dp", "ctx"), None),
        P(("dp", "ctx"), None),
        P(("dp", "ctx"), None),
        P(("dp", "ctx")),
        P(("dp", "ctx"), None),
        P(("dp", "ctx"), None),
        P(("dp", "ctx"), None),
        P(("dp", "ctx"), None),
        P(("dp", "ctx"), None),
        P(("dp", "ctx"), None),
        P(("dp", "ctx"), None),
        P(("dp", "ctx"), None),
        P(("dp", "ctx"), None),
        P(("dp", "ctx")),
        P(("dp", "ctx"), None),
    )
    out_specs = (
        P("dp", "ctx", None),
        P("dp", "ctx", None),
        P("dp", "ctx", None),
        P("dp", "ctx", None),
        P(("dp", "ctx"), None),
        P(("dp", "ctx"), None),
        P(("dp", "ctx"), None),
        P(("dp", "ctx"), None),
        P(("dp", "ctx"), None),
        P(("dp", "ctx")),
        P(("dp", "ctx"), None),
        P(("dp", "ctx"), None),
        P(("dp", "ctx"), None),
        P(("dp", "ctx"), None),
        P(("dp", "ctx"), None),
        P(("dp", "ctx"), None),
        P(("dp", "ctx"), None),
        P(("dp", "ctx"), None),
        P(("dp", "ctx"), None),
        P(("dp", "ctx")),
        P(("dp", "ctx"), None),
    )

    def run(*args):
        sequences, tokens = args[0].shape[:2]
        fits = (
            mesh.shape["dp"] % 2 == 0
            and sequences == 2 * mesh.shape["dp"]
            and mesh.shape["ctx"] == 4
            and tokens == 2 * BLOCK * mesh.shape["ctx"]
            and args[2].shape == args[0].shape
            and D % (mesh.shape["dp"] * mesh.shape["ctx"] * 8) == 0
        )
        chosen = fast_body if fits else body
        return jax.shard_map(chosen, mesh=mesh, in_specs=in_specs, out_specs=out_specs, check_vma=False)(*args)

    return run
```

```python
import functools

import jax
import jax.numpy as jnp
from jax import lax
from jax.experimental import pallas as pl
from jax.experimental.pallas import tpu as pltpu
from jax.sharding import PartitionSpec as P

D = 768
HEADS = 12
HEAD_DIM = 64
BLOCK = 128


EPS = 1e-05
NEG = -1e30
FLOAT = jnp.float32
BRAIN = jnp.bfloat16


def matmul(left_side, right_side):
    return jnp.dot(left_side, right_side, preferred_element_type=FLOAT)


def matmul_left(left_side, right_side):
    return lax.dot_general(
        left_side, right_side, (((0,), (0,)), ((), ())), preferred_element_type=FLOAT
    )


def matmul_right(left_side, right_side):
    return lax.dot_general(
        left_side, right_side, (((1,), (1,)), ((), ())), preferred_element_type=FLOAT
    )


def column_sum(values):
    return jnp.sum(values, axis=0, dtype=FLOAT)


def layer_norm(hidden, gain_row, shift_row):
    center = hidden - jnp.mean(hidden, axis=-1, keepdims=True)
    spread = jnp.mean(center * center, axis=-1, keepdims=True)
    return center * lax.rsqrt(spread + EPS) * gain_row + shift_row


def gelu_exact(values):
    return jax.nn.gelu(values, approximate=False)


def split_pairs(pairs):
    pair_shape = pairs.shape
    both_parts = pairs.reshape(pair_shape[0], pair_shape[1], 2, HEADS, HEAD_DIM)
    return (both_parts[:, :, 0], both_parts[:, :, 1])


def head_scores(query_heads, key_heads, allowed):
    scores = jnp.einsum(
        "brhd,bkhd->bhrk", query_heads, key_heads, preferred_element_type=FLOAT
    ) * HEAD_DIM ** (-0.5)
    if allowed is not None:
        scores = jnp.where(allowed[:, None], scores, NEG)
    return scores


def attend_forward(queries, pairs, allowed):
    query_heads = queries.reshape(queries.shape[:2] + (HEADS, HEAD_DIM))
    key_heads, value_heads = split_pairs(pairs)
    scores = head_scores(query_heads, key_heads, allowed)
    row_max = jnp.max(scores, axis=-1, keepdims=True)
    log_total = row_max + jnp.log(jnp.sum(jnp.exp(scores - row_max), axis=-1, keepdims=True))
    attn_probs = jnp.exp(scores - log_total).astype(BRAIN)
    output = jnp.einsum("bhrk,bkhd->brhd", attn_probs, value_heads, preferred_element_type=FLOAT)
    return (output.reshape(queries.shape).astype(BRAIN), log_total)


def attend_backward(queries, pairs, allowed, log_total, grad_output):
    query_heads = queries.reshape(queries.shape[:2] + (HEADS, HEAD_DIM))
    key_heads, value_heads = split_pairs(pairs)
    grad_heads = grad_output.reshape(query_heads.shape)
    attn_probs = jnp.exp(head_scores(query_heads, key_heads, allowed) - log_total)
    grad_probs = jnp.einsum(
        "brhd,bkhd->bhrk", grad_heads, value_heads, preferred_element_type=FLOAT
    )
    inner_sum = jnp.sum(attn_probs * grad_probs, axis=-1, keepdims=True)
    grad_scores = (attn_probs * (grad_probs - inner_sum)).astype(BRAIN)
    score_scale = HEAD_DIM ** (-0.5)
    grad_queries = (
        jnp.einsum("bhrk,bkhd->brhd", grad_scores, key_heads, preferred_element_type=FLOAT)
        * score_scale
    )
    grad_keys = (
        jnp.einsum("bhrk,brhd->bkhd", grad_scores, query_heads, preferred_element_type=FLOAT)
        * score_scale
    )
    grad_values = jnp.einsum(
        "bhrk,brhd->bkhd", attn_probs.astype(BRAIN), grad_heads, preferred_element_type=FLOAT
    )
    batch_count, key_count = (pairs.shape[0], pairs.shape[1])
    grad_pairs = jnp.concatenate(
        [
            grad_keys.reshape(batch_count, key_count, D),
            grad_values.reshape(batch_count, key_count, D),
        ],
        axis=-1,
    )
    return (grad_queries.reshape(queries.shape), grad_pairs)


def project_forward(attended, residual, out_w, out_bias, gain_row, shift_row):
    summed = residual + matmul(attended, out_w) + out_bias
    return (layer_norm(summed, gain_row, shift_row), summed)


def project_backward(grad_norm, attended, summed, out_w, gain_row, shift_row):
    normed, pull_back = jax.vjp(layer_norm, summed, gain_row, shift_row)
    grad_summed, grad_gain, grad_shift = pull_back(grad_norm)
    grad_branch = grad_summed.astype(BRAIN)
    grad_out_w = matmul_left(attended, grad_branch)
    grad_out_bias = column_sum(grad_branch)
    grad_attended = matmul_right(grad_branch, out_w).astype(BRAIN)
    return (grad_summed, grad_attended, (grad_out_w, grad_out_bias, grad_gain, grad_shift))


def ffn_forward(first_norm, up_w, up_bias, down_w, down_bias, gain_row, shift_row):
    first_bf = first_norm.astype(BRAIN)
    lifted = matmul(first_bf, up_w) + up_bias
    activated = gelu_exact(lifted).astype(BRAIN)
    summed = first_norm + matmul(activated, down_w) + down_bias
    return (layer_norm(summed, gain_row, shift_row), (first_bf, lifted, activated, summed))


def ffn_backward(grad_norm, retained_context, up_w, down_w, gain_row, shift_row):
    first_bf, lifted, activated, summed = retained_context
    normed, pull_back = jax.vjp(layer_norm, summed, gain_row, shift_row)
    grad_summed, grad_gain, grad_shift = pull_back(grad_norm)
    grad_branch = grad_summed.astype(BRAIN)
    grad_down_w = matmul_left(activated, grad_branch)
    grad_down_bias = column_sum(grad_branch)
    grad_act = matmul_right(grad_branch, down_w)
    lifted_out, pull_gelu = jax.vjp(gelu_exact, lifted)
    grad_lifted = pull_gelu(grad_act)[0].astype(BRAIN)
    grad_up_w = matmul_left(first_bf, grad_lifted)
    up_bias_gradient = column_sum(grad_lifted)
    grad_first = grad_summed + matmul_right(grad_lifted, up_w)
    return (
        grad_first,
        (grad_up_w, up_bias_gradient, grad_down_w, grad_down_bias, grad_gain, grad_shift),
    )


def encoder_forward(weights, tokens, seg_rows, ctx_rank):
    qkv_w, out_w, up_w, down_w, bias_cols, up_bias, gain_cols = weights
    bias_vals = bias_cols.astype(FLOAT).T
    gain_vals = gain_cols.astype(FLOAT).T
    batch_count, row_count = (tokens.shape[0], tokens.shape[1])
    flat_tokens = tokens.reshape(batch_count * row_count, D)
    zero_row = jnp.zeros((D,), FLOAT)
    projected = (
        matmul(flat_tokens, qkv_w) + jnp.concatenate([bias_vals[0], zero_row, bias_vals[1]])
    ).astype(BRAIN)
    projected = projected.reshape(batch_count, row_count, 3 * D)
    all_pairs = lax.all_gather(projected[:, :, D:], "ctx", axis=1, tiled=True)
    own_segs = lax.dynamic_slice_in_dim(seg_rows, ctx_rank * row_count, row_count, axis=1)
    allowed = own_segs[:, :, None] == seg_rows[:, None, :]
    attended, log_total = attend_forward(projected[:, :, :D], all_pairs, allowed)
    attended = attended.reshape(batch_count * row_count, D)
    first_norm, first_sum = project_forward(
        attended, flat_tokens.astype(FLOAT), out_w, bias_vals[2], gain_vals[0], bias_vals[4]
    )
    final_norm, ffn_state = ffn_forward(
        first_norm, up_w, up_bias.astype(FLOAT), down_w, bias_vals[3], gain_vals[1], bias_vals[5]
    )
    return (
        final_norm,
        (flat_tokens, projected, all_pairs, allowed, log_total, attended, first_sum, ffn_state),
    )


def encoder_backward(weights, retained_context, grad_final):
    qkv_w, out_w, up_w, down_w, bias_cols, up_bias, gain_cols = weights
    bias_vals = bias_cols.astype(FLOAT).T
    gain_vals = gain_cols.astype(FLOAT).T
    flat_tokens, projected, all_pairs, allowed, log_total, attended, first_sum, ffn_state = (
        retained_context
    )
    batch_count, row_count = (projected.shape[0], projected.shape[1])
    grad_first, ffn_grads = ffn_backward(
        grad_final, ffn_state, up_w, down_w, gain_vals[1], bias_vals[5]
    )
    grad_tokens, grad_attended, proj_grads = project_backward(
        grad_first, attended, first_sum, out_w, gain_vals[0], bias_vals[4]
    )
    grad_queries, grad_pairs = attend_backward(
        projected[:, :, :D],
        all_pairs,
        allowed,
        log_total,
        grad_attended.reshape(batch_count, row_count, D),
    )
    own_pairs = lax.psum_scatter(
        grad_pairs.astype(jnp.bfloat16), "ctx", scatter_dimension=1, tiled=True
    ).astype(jnp.float32)
    mapped_slope = (
        jnp.concatenate([grad_queries, own_pairs], axis=-1)
        .astype(BRAIN)
        .reshape(batch_count * row_count, 3 * D)
    )
    grad_tokens = grad_tokens + matmul_right(mapped_slope, qkv_w)
    grad_qkv_w = matmul_left(flat_tokens, mapped_slope)
    proj_bias = column_sum(mapped_slope)
    up_grad_w, up_grad_bias, down_grad_w, down_grad_bias, gain_two, shift_two = ffn_grads
    out_grad_w, out_grad_bias, gain_one, shift_one = proj_grads
    bias_grads = jnp.stack(
        [proj_bias[:D], proj_bias[2 * D :], out_grad_bias, down_grad_bias, shift_one, shift_two],
        axis=1,
    )
    gain_grads = jnp.stack([gain_one, gain_two], axis=1)
    return (
        grad_tokens,
        (grad_qkv_w, out_grad_w, up_grad_w, down_grad_w, bias_grads, up_grad_bias, gain_grads),
    )


def decoder_forward(weights, tokens, memory_bf, pick_table, ctx_rank):
    (
        self_w,
        self_out_w,
        query_w,
        pair_w,
        cross_out_w,
        up_w,
        down_w,
        bias_cols,
        up_bias,
        gain_cols,
    ) = weights
    bias_vals = bias_cols.astype(FLOAT).T
    gain_vals = gain_cols.astype(FLOAT).T
    batch_count, row_count = (tokens.shape[0], tokens.shape[1])
    flat_tokens = tokens.reshape(batch_count * row_count, D)
    ctx_count = lax.axis_size("ctx")
    zero_row = jnp.zeros((D,), FLOAT)
    projected = (
        matmul(flat_tokens, self_w) + jnp.concatenate([bias_vals[0], zero_row, bias_vals[1]])
    ).astype(BRAIN)
    projected = projected.reshape(batch_count, row_count, 3 * D)
    all_pairs = lax.all_gather(projected[:, :, D:], "ctx", axis=1, tiled=True)
    query_pos = ctx_rank * row_count + jnp.arange(row_count, dtype=jnp.int32)
    key_pos = jnp.arange(row_count * ctx_count, dtype=jnp.int32)
    causal = (query_pos[:, None] >= key_pos[None, :])[None]
    attended, self_total = attend_forward(projected[:, :, :D], all_pairs, causal)
    attended = attended.reshape(batch_count * row_count, D)
    first_norm, first_sum = project_forward(
        attended, flat_tokens.astype(FLOAT), self_out_w, bias_vals[2], gain_vals[0], bias_vals[7]
    )
    first_bf = first_norm.astype(BRAIN)
    cross_queries = (matmul(first_bf, query_w) + bias_vals[3]).astype(BRAIN)
    memory_pairs = (matmul(memory_bf, pair_w) + jnp.concatenate([zero_row, bias_vals[4]])).astype(
        BRAIN
    )
    memory_rows = memory_pairs.shape[0] // batch_count
    memory_all = lax.all_gather(
        memory_pairs.reshape(batch_count, memory_rows, 2 * D), "ctx", axis=1, tiled=True
    )
    source_count = memory_all.shape[1]
    group_rows = min(row_count, BLOCK)
    group_count = row_count // group_rows
    group_start = ctx_rank * row_count + jnp.arange(group_count, dtype=jnp.int32) * group_rows
    pick_rows = jnp.take(pick_table, group_start // BLOCK, axis=1)
    pick_flat = (
        pick_rows + jnp.arange(batch_count, dtype=jnp.int32)[:, None, None] * source_count
    ).reshape(-1)
    picked = jnp.take(
        memory_all.reshape(batch_count * source_count, 2 * D), pick_flat, axis=0
    ).reshape(batch_count * group_count, pick_rows.shape[2], 2 * D)
    grouped = cross_queries.reshape(batch_count * group_count, group_rows, D)
    crossed, cross_total = attend_forward(grouped, picked, None)
    crossed = crossed.reshape(batch_count * row_count, D)
    second, second_sum = project_forward(
        crossed, first_norm, cross_out_w, bias_vals[5], gain_vals[1], bias_vals[8]
    )
    final_norm, ffn_state = ffn_forward(
        second, up_w, up_bias.astype(FLOAT), down_w, bias_vals[6], gain_vals[2], bias_vals[9]
    )
    retained_context = (
        flat_tokens,
        projected,
        all_pairs,
        causal,
        self_total,
        attended,
        first_sum,
        first_bf,
        grouped,
        pick_flat,
        picked,
        cross_total,
        crossed,
        second_sum,
        ffn_state,
        source_count,
    )
    return (final_norm, retained_context)


def decoder_backward(weights, memory_bf, retained_context, grad_final):
    (
        self_w,
        self_out_w,
        query_w,
        pair_w,
        cross_out_w,
        up_w,
        down_w,
        bias_cols,
        up_bias,
        gain_cols,
    ) = weights
    bias_vals = bias_cols.astype(FLOAT).T
    gain_vals = gain_cols.astype(FLOAT).T
    (
        flat_tokens,
        projected,
        all_pairs,
        causal,
        self_total,
        attended,
        first_sum,
        first_bf,
        grouped,
        pick_flat,
        picked,
        cross_total,
        crossed,
        second_sum,
        ffn_state,
        source_count,
    ) = retained_context
    batch_count, row_count = (projected.shape[0], projected.shape[1])
    grad_second, ffn_grads = ffn_backward(
        grad_final, ffn_state, up_w, down_w, gain_vals[2], bias_vals[9]
    )
    grad_first, grad_crossed, cross_grads = project_backward(
        grad_second, crossed, second_sum, cross_out_w, gain_vals[1], bias_vals[8]
    )
    grad_grouped, grad_picked = attend_backward(
        grouped, picked, None, cross_total, grad_crossed.reshape(grouped.shape)
    )
    grad_memory = (
        jnp.zeros((batch_count * source_count, 2 * D), FLOAT)
        .at[pick_flat]
        .add(grad_picked.reshape(-1, 2 * D))
    )
    own_memory = (
        lax.psum_scatter(
            grad_memory.reshape(batch_count, source_count, 2 * D).astype(jnp.bfloat16),
            "ctx",
            scatter_dimension=1,
            tiled=True,
        )
        .astype(jnp.float32)
        .astype(BRAIN)
    )
    own_memory = own_memory.reshape(-1, 2 * D)
    grad_memory_in = matmul_right(own_memory, pair_w)
    grad_pair_w = matmul_left(memory_bf, own_memory)
    pair_bias = column_sum(own_memory[:, D:])
    grad_cross_q = grad_grouped.reshape(batch_count * row_count, D).astype(BRAIN)
    grad_query_w = matmul_left(first_bf, grad_cross_q)
    query_bias = column_sum(grad_cross_q)
    grad_first = grad_first + matmul_right(grad_cross_q, query_w)
    grad_tokens, grad_attended, self_grads = project_backward(
        grad_first, attended, first_sum, self_out_w, gain_vals[0], bias_vals[7]
    )
    grad_queries, grad_pairs = attend_backward(
        projected[:, :, :D],
        all_pairs,
        causal,
        self_total,
        grad_attended.reshape(batch_count, row_count, D),
    )
    own_pairs = lax.psum_scatter(
        grad_pairs.astype(jnp.bfloat16), "ctx", scatter_dimension=1, tiled=True
    ).astype(jnp.float32)
    mapped_slope = (
        jnp.concatenate([grad_queries, own_pairs], axis=-1)
        .astype(BRAIN)
        .reshape(batch_count * row_count, 3 * D)
    )
    grad_tokens = grad_tokens + matmul_right(mapped_slope, self_w)
    grad_self_w = matmul_left(flat_tokens, mapped_slope)
    self_bias = column_sum(mapped_slope)
    up_grad_w, up_grad_bias, down_grad_w, down_grad_bias, gain_three, shift_three = ffn_grads
    cross_out_grad_w, cross_out_bias, gain_two, shift_two = cross_grads
    self_out_grad_w, self_out_bias, gain_one, shift_one = self_grads
    bias_grads = jnp.stack(
        [
            self_bias[:D],
            self_bias[2 * D :],
            self_out_bias,
            query_bias,
            pair_bias,
            cross_out_bias,
            down_grad_bias,
            shift_one,
            shift_two,
            shift_three,
        ],
        axis=1,
    )
    gain_grads = jnp.stack([gain_one, gain_two, gain_three], axis=1)
    weight_grads = (
        grad_self_w,
        self_out_grad_w,
        grad_query_w,
        grad_pair_w,
        cross_out_grad_w,
        up_grad_w,
        down_grad_w,
        bias_grads,
        up_grad_bias,
        gain_grads,
    )
    return (grad_tokens, grad_memory_in, weight_grads)


def fetch_weights(shards):
    return (
        lax.all_gather(shards[0], ("dp", "ctx"), axis=0, tiled=True),
        lax.all_gather(shards[1], ("dp", "ctx"), axis=0, tiled=True),
        lax.all_gather(shards[2], ("dp", "ctx"), axis=0, tiled=True),
        lax.all_gather(shards[3], ("dp", "ctx"), axis=0, tiled=True),
        lax.all_gather(shards[4], ("dp", "ctx"), axis=0, tiled=True),
        lax.all_gather(shards[5], ("dp", "ctx"), axis=0, tiled=True),
        lax.all_gather(shards[6], ("dp", "ctx"), axis=0, tiled=True),
        lax.all_gather(shards[7], ("dp", "ctx"), axis=0, tiled=True),
        lax.all_gather(shards[8], ("dp", "ctx"), axis=0, tiled=True),
        lax.all_gather(shards[9], ("dp", "ctx"), axis=0, tiled=True),
        lax.all_gather(shards[10], ("dp", "ctx"), axis=0, tiled=True),
        lax.all_gather(shards[11], ("dp", "ctx"), axis=0, tiled=True),
        lax.all_gather(shards[12], ("dp", "ctx"), axis=0, tiled=True),
        lax.all_gather(shards[13], ("dp", "ctx"), axis=0, tiled=True),
        lax.all_gather(shards[14], ("dp", "ctx"), axis=0, tiled=True),
        lax.all_gather(shards[15], ("dp", "ctx"), axis=0, tiled=True),
        lax.all_gather(shards[16], ("dp", "ctx"), axis=0, tiled=True),
    )


def body(
    enc_in,
    segments,
    dec_in,
    retrieved,
    enc_cot,
    dec_cot,
    enc_qkv,
    enc_out,
    enc_up,
    enc_down,
    enc_bias,
    enc_up_bias,
    enc_gain,
    decoder_self_projections,
    dec_out,
    cross_q,
    cross_kv,
    cross_out,
    dec_up,
    dec_down,
    dec_bias,
    dec_up_bias,
    dec_gain,
):
    shards = (
        enc_qkv,
        enc_out,
        enc_up,
        enc_down,
        enc_bias,
        enc_up_bias,
        enc_gain,
        decoder_self_projections,
        dec_out,
        cross_q,
        cross_kv,
        cross_out,
        dec_up,
        dec_down,
        dec_bias,
        dec_up_bias,
        dec_gain,
    )
    ctx_rank = lax.axis_index("ctx")
    batch_count, enc_rows, dec_rows = (enc_in.shape[0], enc_in.shape[1], dec_in.shape[1])
    kept_weights = fetch_weights(shards)
    enc_final, enc_state = encoder_forward(kept_weights[:7], enc_in, segments, ctx_rank)
    memory_bf = enc_final.astype(BRAIN)
    dec_final, dec_state = decoder_forward(kept_weights[7:], dec_in, memory_bf, retrieved, ctx_rank)
    dec_grad_in, memory_grad, dec_weight_grads = decoder_backward(
        kept_weights[7:], memory_bf, dec_state, dec_cot.reshape(-1, D).astype(FLOAT)
    )
    enc_grad_in, enc_weight_grads = encoder_backward(
        kept_weights[:7], enc_state, enc_cot.reshape(-1, D).astype(FLOAT) + memory_grad
    )
    totals = enc_weight_grads + dec_weight_grads
    reduced = (
        lax.psum_scatter(totals[0], ("dp", "ctx"), scatter_dimension=0, tiled=True),
        lax.psum_scatter(totals[1], ("dp", "ctx"), scatter_dimension=0, tiled=True),
        lax.psum_scatter(totals[2], ("dp", "ctx"), scatter_dimension=0, tiled=True),
        lax.psum_scatter(totals[3], ("dp", "ctx"), scatter_dimension=0, tiled=True),
        lax.psum_scatter(totals[4], ("dp", "ctx"), scatter_dimension=0, tiled=True),
        lax.psum_scatter(totals[5], ("dp", "ctx"), scatter_dimension=0, tiled=True),
        lax.psum_scatter(totals[6], ("dp", "ctx"), scatter_dimension=0, tiled=True),
        lax.psum_scatter(totals[7], ("dp", "ctx"), scatter_dimension=0, tiled=True),
        lax.psum_scatter(totals[8], ("dp", "ctx"), scatter_dimension=0, tiled=True),
        lax.psum_scatter(totals[9], ("dp", "ctx"), scatter_dimension=0, tiled=True),
        lax.psum_scatter(totals[10], ("dp", "ctx"), scatter_dimension=0, tiled=True),
        lax.psum_scatter(totals[11], ("dp", "ctx"), scatter_dimension=0, tiled=True),
        lax.psum_scatter(totals[12], ("dp", "ctx"), scatter_dimension=0, tiled=True),
        lax.psum_scatter(totals[13], ("dp", "ctx"), scatter_dimension=0, tiled=True),
        lax.psum_scatter(totals[14], ("dp", "ctx"), scatter_dimension=0, tiled=True),
        lax.psum_scatter(totals[15], ("dp", "ctx"), scatter_dimension=0, tiled=True),
        lax.psum_scatter(totals[16], ("dp", "ctx"), scatter_dimension=0, tiled=True),
    )
    return (
        memory_bf.reshape(batch_count, enc_rows, D),
        dec_final.astype(BRAIN).reshape(batch_count, dec_rows, D),
        enc_grad_in.reshape(batch_count, enc_rows, D),
        dec_grad_in.reshape(batch_count, dec_rows, D),
        reduced[0],
        reduced[1],
        reduced[2],
        reduced[3],
        reduced[4],
        reduced[5],
        reduced[6],
        reduced[7],
        reduced[8],
        reduced[9],
        reduced[10],
        reduced[11],
        reduced[12],
        reduced[13],
        reduced[14],
        reduced[15],
        reduced[16],
    )


MESH_ID = pl.DeviceIdType.MESH
ANY = pl.BlockSpec(memory_space=pl.ANY)
DMA_SEM = pltpu.SemaphoreType.DMA
PAIR = 128


def place():
    dp = lax.axis_index("dp")
    return dp, lax.axis_index("ctx"), lax.rem(dp, 2)


def spot():
    dp, z, core = place()
    return dp, z, core, lax.rem(dp // 2, 2), dp // 4


def dp_of(y, x, core):
    return (y * 2 + x) * 2 + core


def greet():
    dp, z, core, x, y = spot()
    zs = lax.axis_size("ctx")
    barrier = pltpu.get_barrier_semaphore()

    def hello(dp_to, z_to):
        pl.semaphore_signal(barrier, 1, device_id=(dp_to, z_to), device_id_type=MESH_ID)

    for step in range(zs):
        if step:
            hello(dp, lax.rem(z + step, zs))
        hello(dp_of(y, x, 1 - core), lax.rem(z + step, zs))
    hello(dp_of(y, 1 - x, core), z)
    hello(dp_of(1 - y, x, core), z)
    pl.semaphore_wait(barrier, 2 * zs + 1)


def remote(source, target, send, recv, dp_to, z_to):
    return pltpu.make_async_remote_copy(source, target, send, recv, device_id=(dp_to, z_to), device_id_type=MESH_ID)


def staged(count, stages):
    steps = []
    for turn in range(count + max(lag for lag, _ in stages)):
        for lag, fn in stages:
            if 0 <= turn - lag < count:
                steps.append(functools.partial(fn, turn - lag))
    return steps


CHUNK = 24 * 512
PER_POLL = 4
LAG = 3


def pieces(shapes):
    chunks = []
    for i, (rows, n) in enumerate(shapes):
        columns = n // PAIR
        count = max(1, min(columns, -(-rows * n // CHUNK)))
        at = 0
        for k in range(count):
            width = (columns * (k + 1) // count - columns * k // count) * PAIR
            chunks.append((i, at, width, len(chunks) % 2))
            at += width
    return chunks


def gather_job(shards):
    zs = lax.axis_size("ctx")
    everyone = lax.axis_size("dp") * zs
    chunks = pieces([s.shape for s in shards])
    count = len(chunks)

    def steps(ins, outs, scratch):
        send, recv, local = scratch
        dp, z, core, x, y = spot()

        def own_part(t):
            i, at, width, _ = chunks[t]
            return ins[i].at[:, pl.ds(at, width)]

        def rows_of(t, dp_at, z_at=None):
            i, at, width, _ = chunks[t]
            where = pl.ds(dp_at * zs, zs) if z_at is None else dp_at * zs + z_at
            return outs[i].at[where, :, pl.ds(at, width)]

        def keep(t):
            return pltpu.make_async_copy(own_part(t), rows_of(t, dp, z), local.at[t])

        def along_z(t, k):
            return remote(own_part(t), rows_of(t, dp, z), send.at[t, k - 1], recv.at[t, k - 1], dp, lax.rem(z + k, zs))

        def hop(t, kind):
            order = chunks[t][3]
            near = (y, 1 - x) if order == 0 else (1 - y, x)
            far = (1 - y, x) if order == 0 else (y, 1 - x)
            block, to = {
                3: ((y, x), near), 4: ((y, x), far), 5: (near, far),
                6: ((y, x), None), 7: (near, None), 8: (far, None), 9: ((1 - y, 1 - x), None),
            }[kind]
            dp_to = dp_of(y, x, 1 - core) if to is None else dp_of(to[0], to[1], core)
            part = rows_of(t, dp_of(block[0], block[1], core))
            return remote(part, part, send.at[t, kind], recv.at[t, kind], dp_to, z)

        def begin(t):
            keep(t).start()
            for k in range(1, zs):
                along_z(t, k).start()

        def first(t):
            keep(t).wait()
            for k in range(1, zs):
                along_z(t, k).wait_recv()
            for kind in (3, 4, 6):
                hop(t, kind).start()

        def second(t):
            hop(t, 3).wait_recv()
            for kind in (5, 7):
                hop(t, kind).start()

        def third(t):
            hop(t, 4).wait_recv()
            hop(t, 8).start()
            hop(t, 5).wait_recv()
            hop(t, 9).start()

        def finish(t):
            for kind in range(6, 10):
                hop(t, kind).wait_recv()
            for k in range(1, zs):
                along_z(t, k).wait_send()
            for kind in range(3, 10):
                hop(t, kind).wait_send()

        return staged(count, [(0, begin), (LAG + 1, first), (2 * LAG + 1, second), (3 * LAG + 1, third), (4 * LAG + 1, finish)])

    shapes = [jax.ShapeDtypeStruct((everyone,) + s.shape, s.dtype) for s in shards]
    scratch = [DMA_SEM((count, 10)), DMA_SEM((count, 10)), DMA_SEM((count,))]
    return shards, [ANY] * len(shards), shapes, [ANY] * len(shards), scratch, steps


def scatter_job(grads):
    zs, dps = lax.axis_size("ctx"), lax.axis_size("dp")
    rows = [g.shape[0] // (zs * dps) for g in grads]
    chunks = pieces([(r, g.shape[1]) for r, g in zip(rows, grads)])
    count = len(chunks)
    inputs = [g.reshape(dps, zs * r, g.shape[1]) for r, g in zip(rows, grads)]
    scratch = [DMA_SEM((count, 10)), DMA_SEM((count, 10)), DMA_SEM((count, 4))]
    for i, _, width, _ in chunks:
        scratch += [
            pltpu.VMEM((4, zs * rows[i], width), BRAIN),
            pltpu.VMEM((4, zs * rows[i], width), BRAIN),
            pltpu.VMEM((2, zs * rows[i], width), BRAIN),
            pltpu.VMEM((zs * rows[i], width), BRAIN),
            pltpu.VMEM((zs, rows[i], width), BRAIN),
            pltpu.VMEM((zs - 1, rows[i], width), BRAIN),
        ]

    def steps(ins, outs, scratch):
        send, recv, local = scratch[:3]
        dp, z, core, x, y = spot()
        buffers = [scratch[3 + 6 * t : 9 + 6 * t] for t in range(count)]

        def source(t, dp_at):
            i, at, width, _ = chunks[t]
            return ins[i].at[dp_at, :, pl.ds(at, width)]

        def load(t, b):
            return pltpu.make_async_copy(source(t, dp_of(b // 2, b % 2, core)), buffers[t][0].at[b], local.at[t, b])

        def to_core(t, b):
            return remote(
                source(t, dp_of(b // 2, b % 2, 1 - core)), buffers[t][1].at[b], send.at[t, b], recv.at[t, b], dp_of(y, x, 1 - core), z
            )

        def wide(t, j):
            if chunks[t][3] == 0:
                block, to = (1 - y) * 2 + j, (1 - y, x)
            else:
                block, to = j * 2 + 1 - x, (y, 1 - x)
            return remote(
                buffers[t][0].at[block], buffers[t][2].at[j], send.at[t, 4 + j], recv.at[t, 4 + j], dp_of(to[0], to[1], core), z
            )

        def narrow(t):
            block, to = (y * 2 + 1 - x, (y, 1 - x)) if chunks[t][3] == 0 else ((1 - y) * 2 + x, (1 - y, x))
            return remote(
                buffers[t][0].at[block], buffers[t][3], send.at[t, 6], recv.at[t, 6], dp_of(to[0], to[1], core), z
            )

        def along_z(t, k):
            z_to = lax.rem(z + k, zs)
            return remote(buffers[t][4].at[z_to], buffers[t][5].at[k - 1], send.at[t, 6 + k], recv.at[t, 6 + k], dp, z_to)

        def add_into(target, other):
            total, width = target.shape

            def some(r, _):
                at = pl.ds(pl.multiple_of(r * 32, 32), 32)
                target[at, :] = (target[at, :].astype(FLOAT) + other[at, :].astype(FLOAT)).astype(BRAIN)
                return 0

            lax.fori_loop(0, total // 32, some, 0)

        def begin(t):
            for b in range(4):
                to_core(t, b).start()
                load(t, b).start()

        def first(t):
            for b in range(4):
                load(t, b).wait()
                to_core(t, b).wait_recv()
                add_into(buffers[t][0].at[b], buffers[t][1].at[b])
            for j in range(2):
                wide(t, j).start()

        def second(t):
            for j in range(2):
                wide(t, j).wait_recv()
                block = y * 2 + j if chunks[t][3] == 0 else j * 2 + x
                add_into(buffers[t][0].at[block], buffers[t][2].at[j])
            narrow(t).start()

        def third(t):
            narrow(t).wait_recv()
            r = rows[chunks[t][0]]
            for s in range(zs):
                at = pl.ds(s * r, r)
                mine = buffers[t][0][y * 2 + x, at, :].astype(FLOAT)
                buffers[t][4][s] = (mine + buffers[t][3][at, :].astype(FLOAT)).astype(BRAIN)
            for k in range(1, zs):
                along_z(t, k).start()

        def finish(t):
            i, at, width, _ = chunks[t]
            total = buffers[t][4][z].astype(FLOAT)
            for k in range(1, zs):
                along_z(t, k).wait_recv()
                total = total + buffers[t][5][k - 1].astype(FLOAT)
            outs[i][:, pl.ds(at, width)] = total
            for b in range(4):
                to_core(t, b).wait_send()
            for j in range(2):
                wide(t, j).wait_send()
            narrow(t).wait_send()
            for k in range(1, zs):
                along_z(t, k).wait_send()

        return staged(count, [(0, begin), (LAG, first), (2 * LAG, second), (3 * LAG, third), (4 * LAG, finish)])

    shapes = [jax.ShapeDtypeStruct((r, g.shape[1]), FLOAT) for r, g in zip(rows, grads)]
    out_specs = [pl.BlockSpec(s.shape, lambda *_: (0, 0)) for s in shapes]
    return inputs, [ANY] * len(grads), shapes, out_specs, scratch, steps


def spread_job(tokens, ints=()):
    zs, count, int_count = lax.axis_size("ctx"), len(tokens), len(ints)

    def steps(ins, outs, scratch):
        send, recv, local, int_send, int_recv = scratch
        dp, z, core = place()
        pair = dp - core

        def swap(i):
            return remote(ins[count + i], outs[count + i], int_send.at[i], int_recv.at[i], pair + 1 - core, z)

        def each(t, what):
            for i in range(2):
                for h in range(2):
                    z_to, core_to = 2 * core + i, lax.rem(h + z, 2)
                    source, target = ins[t].at[i, pl.ds(h * BLOCK, BLOCK)], outs[t].at[z]
                    stays = jnp.logical_and(z_to == z, core_to == core)

                    @pl.when(stays)
                    def _():
                        what(pltpu.make_async_copy(source, target, local.at[t]), False)

                    @pl.when(jnp.logical_not(stays))
                    def _():
                        what(remote(source, target, send.at[t, 2 * i + h], recv.at[t, z], pair + core_to, z_to), True)

        def begin(t):
            if t == 0:
                for i in range(int_count):
                    swap(i).start()
            each(t, lambda copy, far: copy.start())

        def finish(t):
            each(t, lambda copy, far: copy.wait_send() if far else copy.wait())
            for s in range(zs):

                @pl.when(jnp.logical_not(jnp.logical_and(s == z, z // 2 == core)))
                def _():
                    remote(outs[t].at[s], outs[t].at[s], send.at[t, 0], recv.at[t, s], pair + 1 - core, z).wait_recv()

            if t == 0:
                for i in range(int_count):
                    swap(i).wait()

        return [functools.partial(begin, t) for t in range(count)] + [functools.partial(finish, t) for t in range(count)]

    shapes = [jax.ShapeDtypeStruct((zs, BLOCK, D), t.dtype) for t in tokens]
    shapes += [jax.ShapeDtypeStruct(i.shape, i.dtype) for i in ints]
    n = count + int_count
    scratch = [DMA_SEM((count, 4)), DMA_SEM((count, zs)), DMA_SEM((count,)), DMA_SEM((2,)), DMA_SEM((2,))]
    return list(tokens) + list(ints), [ANY] * n, shapes, [ANY] * n, scratch, steps


def collect_job(blocks):
    zs, count = lax.axis_size("ctx"), len(blocks)

    def steps(ins, outs, scratch):
        send, recv, local = scratch
        dp, z, core = place()
        pair = dp - core
        owner, inside = z // 2, lax.rem(z, 2)

        def each(t, what):
            for s in range(zs):
                half = lax.rem(core + s, 2)
                source = ins[t].at[s]
                target = outs[t].at[inside, pl.ds(half * BLOCK, BLOCK)]
                stays = jnp.logical_and(s == z, owner == core)

                @pl.when(stays)
                def _():
                    what(pltpu.make_async_copy(source, target, local.at[t]), False)

                @pl.when(jnp.logical_not(stays))
                def _():
                    what(remote(source, target, send.at[t, s], recv.at[t, 2 * inside + half], pair + owner, s), True)

        def begin(t):
            each(t, lambda copy, far: copy.start())

        def finish(t):
            each(t, lambda copy, far: copy.wait_send() if far else copy.wait())
            for i in range(2):
                for h in range(2):
                    z_from, core_from = 2 * core + i, lax.rem(h + z, 2)

                    @pl.when(jnp.logical_not(jnp.logical_and(z_from == z, core_from == core)))
                    def _():
                        target = outs[t].at[i, pl.ds(h * BLOCK, BLOCK)]
                        remote(target, target, send.at[t, 0], recv.at[t, 2 * i + h], pair + 1 - core, z).wait_recv()

        return [functools.partial(begin, t) for t in range(count)] + [functools.partial(finish, t) for t in range(count)]

    inputs = [b.reshape(zs, BLOCK, D) for b in blocks]
    shapes = [jax.ShapeDtypeStruct((2, 2 * BLOCK, D), b.dtype) for b in blocks]
    scratch = [DMA_SEM((count, zs)), DMA_SEM((count, 4)), DMA_SEM((count,))]
    return inputs, [ANY] * count, shapes, [ANY] * count, scratch, steps


def merge(lists):
    tagged = []
    for order, steps in enumerate(lists):
        tagged += [((k + 0.5) / len(steps), order, k, step) for k, step in enumerate(steps)]
    return [t[3] for t in sorted(tagged, key=lambda t: t[:3])]


def carry(
    jobs, collective_id, name, kernel=None, grid=1, slots=1, args=(), in_specs=(), out_shape=(), out_specs=(), scratch=(), cost=None
):
    sizes = [(len(j[0]), len(j[2]), len(j[4])) for j in jobs]

    def body(*refs):
        def take(n):
            nonlocal refs
            got, refs = refs[:n], refs[n:]
            return list(got)

        mine_in = take(len(args))
        job_in = [take(s[0]) for s in sizes]
        mine_out = take(len(out_shape))
        job_out = [take(s[1]) for s in sizes]
        mine_scratch = take(len(scratch))
        job_scratch = [take(s[2]) for s in sizes]
        steps = merge([j[5](i, o, s) for j, i, o, s in zip(jobs, job_in, job_out, job_scratch)])
        if kernel is None:
            greet()
            for step in steps:
                step()
            return
        turn = pl.program_id(0)
        calls = grid * slots
        early = min(len(steps), calls * PER_POLL)
        called = [0]

        def poll():
            slot = called[0]
            called[0] += 1
            for g in range(grid):
                k = g * slots + slot
                some = steps[k * early // calls : (k + 1) * early // calls]
                if some:

                    @pl.when(turn == g)
                    def _():
                        for step in some:
                            step()

        if jobs:

            @pl.when(turn == 0)
            def _():
                greet()

        kernel(poll, *mine_in, *mine_out, *mine_scratch)
        assert called[0] == slots
        if steps[early:]:

            @pl.when(turn == grid - 1)
            def _():
                for step in steps[early:]:
                    step()

    flat = lambda k: [v for j in jobs for v in j[k]]
    got = pl.pallas_call(
        body,
        grid=(grid,),
        out_shape=list(out_shape) + flat(2),
        in_specs=list(in_specs) + flat(1),
        out_specs=list(out_specs) + flat(3),
        scratch_shapes=list(scratch) + flat(4),
        compiler_params=pltpu.CompilerParams(
            collective_id=collective_id if jobs else None, has_side_effects=bool(jobs), vmem_limit_bytes=60 << 20
        ),
        cost_estimate=cost,
        name=name,
    )(*args, *flat(0))
    own, rest, parts = got[: len(out_shape)], got[len(out_shape) :], []
    for s in sizes:
        parts.append(rest[: s[1]])
        rest = rest[s[1] :]
    return own, parts


LOG2E = 1.4426950408889634


def key_chunks(rows, causal):
    if causal:
        return [(half, r, BLOCK, r) for r in range(0, rows, BLOCK) for half in range(2)]
    return [(half, r, 2 * BLOCK, 0) for half in range(2) for r in range(0, rows, 2 * BLOCK)]


def nt_dot(a, b):
    return lax.dot_general(a, b, (((1,), (1,)), ((), ())), preferred_element_type=FLOAT)


def head_lanes(values, head):
    lanes = lax.broadcasted_iota(jnp.int32, values.shape, 1)
    return jnp.where(lanes // HEAD_DIM == head, values, jnp.zeros_like(values))


def fold_rows(values, how):
    grouped = values.reshape(values.shape[0] // 8, 8, values.shape[1])
    return how(how(grouped, axis=0), axis=0, keepdims=True)


def attend_fwd_kernel(causal, poll, q_ref, k0_ref, v0_ref, k1_ref, v1_ref, bias_ref, o_ref, lse_ref, s_ref, p_ref):
    rows = q_ref.shape[0]
    k_refs = (k0_ref, k1_ref)
    v_all = jnp.concatenate([v0_ref[...], v1_ref[...]], axis=0)
    v_t = v_all.T
    factor = HEAD_DIM ** (-0.5) * LOG2E
    out_t = []
    for head in range(2):
        q = head_lanes(q_ref[...], head)
        top = jnp.full((1, rows), -3e38, FLOAT)
        for half, r, n, c in key_chunks(rows, causal):
            s = nt_dot(k_refs[half][pl.ds(r, n), :], q[c:])
            s = s * factor + bias_ref[pl.ds(half * rows + r, n), c:].astype(FLOAT)
            s_ref[pl.ds(half * rows + r, n), c:] = s
            peak = fold_rows(s, jnp.max)
            peak = jnp.maximum(top[:, c:], peak)
            top = jnp.concatenate([top[:, :c], peak], axis=1) if c else peak
        poll()
        total = jnp.zeros((1, rows), FLOAT)
        for half, r, n, c in key_chunks(rows, causal):
            p = jnp.exp2(s_ref[pl.ds(half * rows + r, n), c:] - top[:, c:])
            part = total[:, c:] + fold_rows(p, jnp.sum)
            total = jnp.concatenate([total[:, :c], part], axis=1) if c else part
            p_ref[pl.ds(half * rows + r, n), c:] = p.astype(BRAIN)
            if c:
                p_ref[pl.ds(half * rows + r, n), :c] = jnp.zeros((n, c), BRAIN)
        o_t = jnp.dot(v_t[head * HEAD_DIM : (head + 1) * HEAD_DIM], p_ref[...], preferred_element_type=FLOAT)
        out_t.append(o_t / total)
        poll()
        lse_ref[0, pl.ds(head, 1), :] = top + jnp.log(total) * LOG2E
    o_ref[...] = jnp.concatenate(out_t, axis=0).T.astype(o_ref.dtype)


def attention_forward(queries, q_col, pairs, kv_col, pairs_other, bias, causal, jobs=(), collective_id=None):
    rows = queries.shape[0]
    pair_count = D // PAIR
    block = (rows, PAIR)
    spec = lambda at: pl.BlockSpec(block, lambda p: (0, at + p))
    own, parts = carry(
        list(jobs),
        collective_id,
        "attend_fwd",
        kernel=functools.partial(attend_fwd_kernel, causal),
        grid=pair_count,
        slots=4,
        args=(queries, pairs, pairs, pairs_other, pairs_other, bias),
        in_specs=[
            spec(q_col), spec(kv_col), spec(kv_col + pair_count), spec(0), spec(pair_count),
            pl.BlockSpec((2 * rows, rows), lambda p: (0, 0)),
        ],
        out_shape=[jax.ShapeDtypeStruct((rows, D), BRAIN), jax.ShapeDtypeStruct((pair_count, 8, rows), FLOAT)],
        out_specs=[spec(0), pl.BlockSpec((1, 8, rows), lambda p: (p, 0, 0))],
        scratch=[pltpu.VMEM((2 * rows, rows), FLOAT), pltpu.VMEM((2 * rows, rows), BRAIN)],
        cost=pl.CostEstimate(flops=16 * rows * rows * D, bytes_accessed=10 * rows * D * 2, transcendentals=24 * rows * rows),
    )
    return own[0], own[1], parts


def attend_bwd_kernel(
    causal, poll, q_ref, k0_ref, v0_ref, k1_ref, v1_ref, bias_ref, o_ref, do_ref, lse_ref,
    dq_ref, dk0_ref, dv0_ref, dk1_ref, dv1_ref, ds_ref,
):
    rows = q_ref.shape[0]
    k_refs, v_refs = (k0_ref, k1_ref), (v0_ref, v1_ref)
    dk_refs, dv_refs = (dk0_ref, dk1_ref), (dv0_ref, dv1_ref)
    k_t = jnp.concatenate([k0_ref[...], k1_ref[...]], axis=0).T
    scale = HEAD_DIM ** (-0.5)
    factor = scale * LOG2E
    prod_t = (o_ref[...].astype(FLOAT) * do_ref[...].astype(FLOAT)).T
    dq_t = []
    q_heads = [head_lanes(q_ref[...], head) for head in range(2)]
    do_heads = [head_lanes(do_ref[...], head) for head in range(2)]
    lses = [lse_ref[0, pl.ds(head, 1), :] for head in range(2)]
    deltas = [fold_rows(prod_t[head * HEAD_DIM : (head + 1) * HEAD_DIM], jnp.sum) for head in range(2)]
    for half, r, n, c in key_chunks(rows, causal):
        k, v = k_refs[half][pl.ds(r, n), :], v_refs[half][pl.ds(r, n), :]
        bias = bias_ref[pl.ds(half * rows + r, n), c:].astype(FLOAT)
        dk = dv = None
        for head in range(2):
            q, do = q_heads[head][c:], do_heads[head][c:]
            p = jnp.exp2(nt_dot(k, q) * factor + bias - lses[head][:, c:])
            dv_part = jnp.dot(p.astype(BRAIN), do, preferred_element_type=FLOAT)
            ds = (p * (nt_dot(v, do) - deltas[head][:, c:])).astype(BRAIN)
            ds_ref[head, pl.ds(half * rows + r, n), c:] = ds
            if c:
                ds_ref[head, pl.ds(half * rows + r, n), :c] = jnp.zeros((n, c), BRAIN)
            dk_part = jnp.dot(ds, q, preferred_element_type=FLOAT)
            dk = dk_part if dk is None else dk + dk_part
            dv = dv_part if dv is None else dv + dv_part
        dk_refs[half][pl.ds(r, n), :] = (dk * scale).astype(dk_refs[half].dtype)
        dv_refs[half][pl.ds(r, n), :] = dv.astype(dv_refs[half].dtype)
        poll()
    for head in range(2):
        dq_t.append(jnp.dot(k_t[head * HEAD_DIM : (head + 1) * HEAD_DIM], ds_ref[head], preferred_element_type=FLOAT))
    dq_ref[...] = (jnp.concatenate(dq_t, axis=0) * scale).T.astype(dq_ref.dtype)


def attention_backward(
    queries, q_col, pairs, kv_col, pairs_other, bias, causal, attended, grad_attended, lse, jobs=(), collective_id=None
):
    rows = queries.shape[0]
    pair_count = D // PAIR
    block = (rows, PAIR)
    spec = lambda at: pl.BlockSpec(block, lambda p: (0, at + p))
    own, parts = carry(
        list(jobs),
        collective_id,
        "attend_bwd",
        kernel=functools.partial(attend_bwd_kernel, causal),
        grid=pair_count,
        slots=len(key_chunks(rows, causal)),
        args=(queries, pairs, pairs, pairs_other, pairs_other, bias, attended, grad_attended, lse),
        in_specs=[
            spec(q_col), spec(kv_col), spec(kv_col + pair_count), spec(0), spec(pair_count),
            pl.BlockSpec((2 * rows, rows), lambda p: (0, 0)), spec(0), spec(0),
            pl.BlockSpec((1, 8, rows), lambda p: (p, 0, 0)),
        ],
        out_shape=[jax.ShapeDtypeStruct((rows, D), t) for t in (BRAIN, FLOAT, FLOAT, BRAIN, BRAIN)],
        out_specs=[spec(0)] * 5,
        scratch=[pltpu.VMEM((2, 2 * rows, rows), BRAIN)],
        cost=pl.CostEstimate(flops=40 * rows * rows * D, bytes_accessed=18 * rows * D * 2, transcendentals=24 * rows * rows),
    )
    return own, parts


def to_sibling(values):
    count = lax.axis_size("dp")
    return lax.ppermute(values, "dp", [(i, i ^ 1) for i in range(count)])


def own_blocks(per_block, core):
    zs = per_block.shape[0] // 2
    both = per_block.reshape((zs, 2) + per_block.shape[1:])
    flip = lax.rem(jnp.arange(zs, dtype=jnp.int32) + core, 2).reshape((zs,) + (1,) * (per_block.ndim - 1))
    own = jnp.where(flip == 0, both[:, 0], both[:, 1])
    return own, jnp.where(flip == 0, both[:, 1], both[:, 0])


def ordered_keys(per_token, core):
    own, other = own_blocks(per_token.reshape(-1, BLOCK), core)
    return own.reshape(-1), jnp.concatenate([own.reshape(-1), other.reshape(-1)])


SMALL = 32


def pack_small(enc_bias, dec_bias, enc_gain, dec_gain, enc_up_bias, dec_up_bias):
    rows = enc_bias.shape[0]
    parts = [enc_bias, dec_bias, enc_gain, dec_gain]
    left = jnp.pad(jnp.concatenate(parts, axis=1), ((0, 0), (0, SMALL - sum(p.shape[1] for p in parts))))
    right = jnp.pad(jnp.stack([enc_up_bias, dec_up_bias]), ((0, rows - 2), (0, PAIR - SMALL - enc_up_bias.shape[0])))
    return jnp.concatenate([left, right], axis=1)


def unpack_small(packed, width):
    cuts, at = [], 0
    for count in (6, 10, 2, 3):
        cuts.append(packed[..., at : at + count])
        at += count
    return cuts + [packed[..., 0, SMALL : SMALL + width], packed[..., 1, SMALL : SMALL + width]]


def small_grads(rows, enc_up_bias, dec_up_bias, shards):
    left = jnp.pad(jnp.concatenate(rows, axis=0), ((0, SMALL - len(rows)), (0, 0))).T.reshape(shards, -1, SMALL)
    up = jnp.stack([v.reshape(shards, -1) for v in (enc_up_bias, dec_up_bias)], axis=1)
    right = jnp.pad(up, ((0, 0), (0, left.shape[1] - 2), (0, PAIR - SMALL - up.shape[2])))
    return jnp.concatenate([left, right], axis=2).reshape(-1, PAIR)


def sums(values):
    return jnp.sum(values, axis=0, keepdims=True, dtype=FLOAT)


def norm_grad(grad, summed, gain_row):
    center = summed - jnp.mean(summed, axis=-1, keepdims=True)
    inverse = lax.rsqrt(jnp.mean(center * center, axis=-1, keepdims=True) + EPS)
    unit = center * inverse
    scaled = grad * gain_row
    back = scaled - jnp.mean(scaled, axis=-1, keepdims=True) - unit * jnp.mean(scaled * unit, axis=-1, keepdims=True)
    return inverse * back, sums(grad * unit), sums(grad)


def project_grad(grad_norm, attended, summed, out_w, gain_row):
    grad_summed, grad_gain, grad_shift = norm_grad(grad_norm, summed, gain_row)
    grad_branch = grad_summed.astype(BRAIN)
    return (
        grad_summed,
        matmul_right(grad_branch, out_w).astype(BRAIN),
        (matmul_left(attended, grad_branch), sums(grad_branch), grad_gain, grad_shift),
    )


def ffn_grad(grad_norm, retained, up_w, down_w, gain_row):
    first_bf, lifted, activated, summed = retained
    grad_summed, grad_gain, grad_shift = norm_grad(grad_norm, summed, gain_row)
    grad_branch = grad_summed.astype(BRAIN)
    grad_act = matmul_right(grad_branch, down_w)
    grad_lifted = jax.vjp(gelu_exact, lifted)[1](grad_act)[0].astype(BRAIN)
    return (
        grad_summed + matmul_right(grad_lifted, up_w),
        (
            matmul_left(first_bf, grad_lifted), sums(grad_lifted),
            matmul_left(activated, grad_branch), sums(grad_branch), grad_gain, grad_shift,
        ),
    )


def with_sibling(own_keys, own_values, other_keys, other_values):
    got = to_sibling(jnp.concatenate([other_keys, other_values], axis=1)).astype(FLOAT)
    return (jnp.concatenate([own_keys, own_values], axis=1) + got).astype(BRAIN)


def matrix(gathered):
    return gathered.reshape(-1, gathered.shape[2])


def fast_body(
    enc_in, segments, dec_in, retrieved, enc_cot, dec_cot,
    enc_qkv, enc_out, enc_up, enc_down, enc_bias, enc_up_bias, enc_gain,
    dec_qkv, dec_out, cross_q, cross_kv, cross_out, dec_up, dec_down, dec_bias, dec_up_bias, dec_gain,
):
    dp, z, core = place()
    small = pack_small(enc_bias, dec_bias, enc_gain, dec_gain, enc_up_bias, dec_up_bias)
    _, ((enc_t, dec_t, seg_other, ret_other), near) = carry(
        [spread_job([enc_in, dec_in], [segments, retrieved]), gather_job([enc_qkv, dec_qkv, small, enc_out, dec_out])], 0, "begin"
    )
    w_enc_qkv, w_dec_qkv, _, w_enc_out, w_dec_out = map(matrix, near)
    zs = enc_t.shape[0]
    rows = zs * BLOCK
    enc_t, dec_t = enc_t.reshape(rows, D), dec_t.reshape(rows, D)
    here = z // 2 == core
    seg = lax.dynamic_index_in_dim(jnp.where(here, segments, seg_other), lax.rem(z, 2), 0, keepdims=False)
    ret = lax.dynamic_index_in_dim(jnp.where(here, retrieved, ret_other), lax.rem(z, 2), 0, keepdims=False)
    seg_q, seg_k = ordered_keys(seg, core)
    pos_q, pos_k = ordered_keys(jnp.arange(2 * rows, dtype=jnp.int32), core)
    enc_mask = jnp.where(seg_k[:, None] == seg_q[None, :], 0.0, NEG).astype(FLOAT)
    dec_mask = jnp.where(pos_k[:, None] <= pos_q[None, :], 0.0, NEG).astype(FLOAT)
    ret_own, _ = own_blocks(ret, core)
    member = jnp.any(pos_k[:, None, None] == ret_own[None], axis=-1)
    cross_mask = jnp.broadcast_to(jnp.where(member, 0.0, NEG).astype(FLOAT)[:, :, None], (2 * rows, zs, BLOCK)).reshape(2 * rows, rows)

    shards = near[2].shape[0]
    b_enc, b_dec, g_enc, g_dec, enc_ub, dec_ub = unpack_small(near[2], enc_up_bias.shape[0])
    across = lambda v: jnp.swapaxes(v.reshape(D, -1), 0, 1).astype(FLOAT)
    eb, db, eg, dg = ([row[i : i + 1] for i in range(row.shape[0])] for row in map(across, (b_enc, b_dec, g_enc, g_dec)))
    enc_ub, dec_ub = (v.reshape(1, -1).astype(FLOAT) for v in (enc_ub, dec_ub))
    zero_row = jnp.zeros((1, D), FLOAT)

    e_proj = (matmul(enc_t, w_enc_qkv) + jnp.concatenate([eb[0], zero_row, eb[1]], axis=1)).astype(BRAIN)
    e_other = to_sibling(e_proj[:, D:])
    d_proj = (matmul(dec_t, w_dec_qkv) + jnp.concatenate([db[0], zero_row, db[1]], axis=1)).astype(BRAIN)
    d_other = to_sibling(d_proj[:, D:])
    e_att, e_lse, (far,) = attention_forward(
        e_proj, 0, e_proj, D // PAIR, e_other, enc_mask, False, [gather_job([enc_up, enc_down])], 1
    )
    w_enc_up, w_enc_down = map(matrix, far)
    d_att, d_lse, (far,) = attention_forward(
        d_proj, 0, d_proj, D // PAIR, d_other, dec_mask, True, [gather_job([cross_kv, cross_q, cross_out])], 2
    )
    w_cross_kv, w_cross_q, w_cross_out = map(matrix, far)
    e_first, e_sum = project_forward(e_att, enc_t.astype(FLOAT), w_enc_out, eb[2], eg[0], eb[4])
    enc_final, e_ffn = ffn_forward(e_first, w_enc_up, enc_ub, w_enc_down, eb[3], eg[1], eb[5])
    memory = enc_final.astype(BRAIN)
    d_first, d_sum = project_forward(d_att, dec_t.astype(FLOAT), w_dec_out, db[2], dg[0], db[7])
    first_bf = d_first.astype(BRAIN)
    cross_queries = (matmul(first_bf, w_cross_q) + db[3]).astype(BRAIN)
    mem_pairs = (matmul(memory, w_cross_kv) + jnp.concatenate([zero_row, db[4]], axis=1)).astype(BRAIN)
    mem_other = to_sibling(mem_pairs)
    crossed, cross_lse, ((enc_c, dec_c), far) = attention_forward(
        cross_queries, 0, mem_pairs, 0, mem_other, cross_mask, False, [spread_job([enc_cot, dec_cot]), gather_job([dec_up, dec_down])], 3
    )
    enc_c, dec_c = enc_c.reshape(rows, D), dec_c.reshape(rows, D)
    w_dec_up, w_dec_down = map(matrix, far)
    second, second_sum = project_forward(crossed, d_first, w_cross_out, db[5], dg[1], db[8])
    dec_final, d_ffn = ffn_forward(second, w_dec_up, dec_ub, w_dec_down, db[6], dg[2], db[9])
    low = lambda *grads: [g.astype(BRAIN) for g in grads]
    grad_second, (g_dec_up, g_dec_ub, g_dec_down, g_db6, g_dg2, g_db9) = ffn_grad(
        dec_c.astype(FLOAT), d_ffn, w_dec_up, w_dec_down, dg[2]
    )
    grad_first, grad_crossed, (g_cross_out, g_db5, g_dg1, g_db8) = project_grad(
        grad_second, crossed, second_sum, w_cross_out, dg[1]
    )
    (g_cq, dk, dv, dk_o, dv_o), ((enc_hidden, dec_hidden), (r_dec_up, r_dec_down)) = attention_backward(
        cross_queries, 0, mem_pairs, 0, mem_other, cross_mask, False, crossed, grad_crossed, cross_lse,
        [collect_job([memory, dec_final.astype(BRAIN)]), scatter_job(low(g_dec_up, g_dec_down))], 4,
    )
    own_memory = with_sibling(dk, dv, dk_o, dv_o)
    g_cross_q, g_db3 = matmul_left(first_bf, g_cq), sums(g_cq)
    grad_first = grad_first + matmul_right(g_cq, w_cross_q)
    memory_grad = matmul_right(own_memory, w_cross_kv)
    g_cross_kv, g_db4 = matmul_left(memory, own_memory), sums(own_memory[:, D:])
    grad_dec, grad_d_att, (g_dec_out, g_db2, g_dg0, g_db7) = project_grad(grad_first, d_att, d_sum, w_dec_out, dg[0])
    (dq, dk, dv, dk_o, dv_o), ((r_cross_out, r_cross_kv, r_cross_q, r_dec_out),) = attention_backward(
        d_proj, 0, d_proj, D // PAIR, d_other, dec_mask, True, d_att, grad_d_att, d_lse,
        [scatter_job(low(g_cross_out, g_cross_kv, g_cross_q, g_dec_out))], 5,
    )
    d_slope = jnp.concatenate([dq, with_sibling(dk, dv, dk_o, dv_o)], axis=1)
    grad_dec = grad_dec + matmul_right(d_slope, w_dec_qkv)
    g_dec_qkv, d_slope_sum = matmul_left(dec_t, d_slope), sums(d_slope)
    grad_e_first, (g_enc_up, g_enc_ub, g_enc_down, g_eb3, g_eg1, g_eb5) = ffn_grad(
        enc_c.astype(FLOAT) + memory_grad, e_ffn, w_enc_up, w_enc_down, eg[1]
    )
    grad_enc, grad_e_att, (g_enc_out, g_eb2, g_eg0, g_eb4) = project_grad(grad_e_first, e_att, e_sum, w_enc_out, eg[0])
    (dq, dk, dv, dk_o, dv_o), ((dec_home,), (r_enc_up, r_enc_down)) = attention_backward(
        e_proj, 0, e_proj, D // PAIR, e_other, enc_mask, False, e_att, grad_e_att, e_lse,
        [collect_job(low(grad_dec)), scatter_job(low(g_enc_up, g_enc_down))], 6,
    )
    e_slope = jnp.concatenate([dq, with_sibling(dk, dv, dk_o, dv_o)], axis=1)
    grad_enc = grad_enc + matmul_right(e_slope, w_enc_qkv)
    g_enc_qkv, e_slope_sum = matmul_left(enc_t, e_slope), sums(e_slope)

    g_small = small_grads(
        [e_slope_sum[:, :D], e_slope_sum[:, 2 * D :], g_eb2, g_eb3, g_eb4, g_eb5]
        + [d_slope_sum[:, :D], d_slope_sum[:, 2 * D :], g_db2, g_db3, g_db4, g_db5, g_db6, g_db7, g_db8, g_db9]
        + [g_eg0, g_eg1, g_dg0, g_dg1, g_dg2],
        g_enc_ub, g_dec_ub, shards,
    )
    _, ((enc_home,), (r_dec_qkv, r_enc_out, r_enc_qkv, r_small)) = carry(
        [collect_job(low(grad_enc)), scatter_job(low(g_dec_qkv, g_enc_out, g_enc_qkv, g_small))], 7, "end"
    )
    r_eb, r_db, r_eg, r_dg, r_enc_ub, r_dec_ub = unpack_small(r_small, enc_up_bias.shape[0])
    return (
        enc_hidden, dec_hidden, enc_home.astype(FLOAT), dec_home.astype(FLOAT),
        r_enc_qkv, r_enc_out, r_enc_up, r_enc_down, r_eb, r_enc_ub, r_eg,
        r_dec_qkv, r_dec_out, r_cross_q, r_cross_kv, r_cross_out, r_dec_up, r_dec_down, r_db, r_dec_ub, r_dg,
    )


def solution(mesh):
    in_specs = (
        P("dp", "ctx", None),
        P("dp", None),
        P("dp", "ctx", None),
        P("dp", None, None),
        P("dp", "ctx", None),
        P("dp", "ctx", None),
        P(("dp", "ctx"), None),
        P(("dp", "ctx"), None),
        P(("dp", "ctx"), None),
        P(("dp", "ctx"), None),
        P(("dp", "ctx"), None),
        P(("dp", "ctx")),
        P(("dp", "ctx"), None),
        P(("dp", "ctx"), None),
        P(("dp", "ctx"), None),
        P(("dp", "ctx"), None),
        P(("dp", "ctx"), None),
        P(("dp", "ctx"), None),
        P(("dp", "ctx"), None),
        P(("dp", "ctx"), None),
        P(("dp", "ctx"), None),
        P(("dp", "ctx")),
        P(("dp", "ctx"), None),
    )
    out_specs = (
        P("dp", "ctx", None),
        P("dp", "ctx", None),
        P("dp", "ctx", None),
        P("dp", "ctx", None),
        P(("dp", "ctx"), None),
        P(("dp", "ctx"), None),
        P(("dp", "ctx"), None),
        P(("dp", "ctx"), None),
        P(("dp", "ctx"), None),
        P(("dp", "ctx")),
        P(("dp", "ctx"), None),
        P(("dp", "ctx"), None),
        P(("dp", "ctx"), None),
        P(("dp", "ctx"), None),
        P(("dp", "ctx"), None),
        P(("dp", "ctx"), None),
        P(("dp", "ctx"), None),
        P(("dp", "ctx"), None),
        P(("dp", "ctx"), None),
        P(("dp", "ctx")),
        P(("dp", "ctx"), None),
    )

    def run(*args):
        sequences, tokens = args[0].shape[:2]
        fits = (
            mesh.shape["dp"] % 2 == 0
            and sequences == 2 * mesh.shape["dp"]
            and mesh.shape["ctx"] == 4
            and tokens == 2 * BLOCK * mesh.shape["ctx"]
            and args[2].shape == args[0].shape
            and D % (mesh.shape["dp"] * mesh.shape["ctx"] * 8) == 0
        )
        chosen = fast_body if fits else body
        return jax.shard_map(chosen, mesh=mesh, in_specs=in_specs, out_specs=out_specs, check_vma=False)(*args)

    return run
```

```python
import functools

import jax
import jax.numpy as jnp
from jax import lax
from jax.experimental import pallas as pl
from jax.experimental.pallas import tpu as pltpu
from jax.sharding import PartitionSpec as P

D = 768
HEADS = 12
HEAD_DIM = 64
BLOCK = 128


EPS = 1e-05
NEG = -1e30
FLOAT = jnp.float32
BRAIN = jnp.bfloat16


def matmul(left_side, right_side):
    return jnp.dot(left_side, right_side, preferred_element_type=FLOAT)


def matmul_left(left_side, right_side):
    return lax.dot_general(
        left_side, right_side, (((0,), (0,)), ((), ())), preferred_element_type=FLOAT
    )


def matmul_right(left_side, right_side):
    return lax.dot_general(
        left_side, right_side, (((1,), (1,)), ((), ())), preferred_element_type=FLOAT
    )


def column_sum(values):
    return jnp.sum(values, axis=0, dtype=FLOAT)


def layer_norm(hidden, gain_row, shift_row):
    center = hidden - jnp.mean(hidden, axis=-1, keepdims=True)
    spread = jnp.mean(center * center, axis=-1, keepdims=True)
    return center * lax.rsqrt(spread + EPS) * gain_row + shift_row


def gelu_exact(values):
    return jax.nn.gelu(values, approximate=False)


def split_pairs(pairs):
    pair_shape = pairs.shape
    both_parts = pairs.reshape(pair_shape[0], pair_shape[1], 2, HEADS, HEAD_DIM)
    return (both_parts[:, :, 0], both_parts[:, :, 1])


def head_scores(query_heads, key_heads, allowed):
    scores = jnp.einsum(
        "brhd,bkhd->bhrk", query_heads, key_heads, preferred_element_type=FLOAT
    ) * HEAD_DIM ** (-0.5)
    if allowed is not None:
        scores = jnp.where(allowed[:, None], scores, NEG)
    return scores


def attend_forward(queries, pairs, allowed):
    query_heads = queries.reshape(queries.shape[:2] + (HEADS, HEAD_DIM))
    key_heads, value_heads = split_pairs(pairs)
    scores = head_scores(query_heads, key_heads, allowed)
    row_max = jnp.max(scores, axis=-1, keepdims=True)
    log_total = row_max + jnp.log(jnp.sum(jnp.exp(scores - row_max), axis=-1, keepdims=True))
    attn_probs = jnp.exp(scores - log_total).astype(BRAIN)
    output = jnp.einsum("bhrk,bkhd->brhd", attn_probs, value_heads, preferred_element_type=FLOAT)
    return (output.reshape(queries.shape).astype(BRAIN), log_total)


def attend_backward(queries, pairs, allowed, log_total, grad_output):
    query_heads = queries.reshape(queries.shape[:2] + (HEADS, HEAD_DIM))
    key_heads, value_heads = split_pairs(pairs)
    grad_heads = grad_output.reshape(query_heads.shape)
    attn_probs = jnp.exp(head_scores(query_heads, key_heads, allowed) - log_total)
    grad_probs = jnp.einsum(
        "brhd,bkhd->bhrk", grad_heads, value_heads, preferred_element_type=FLOAT
    )
    inner_sum = jnp.sum(attn_probs * grad_probs, axis=-1, keepdims=True)
    grad_scores = (attn_probs * (grad_probs - inner_sum)).astype(BRAIN)
    score_scale = HEAD_DIM ** (-0.5)
    grad_queries = (
        jnp.einsum("bhrk,bkhd->brhd", grad_scores, key_heads, preferred_element_type=FLOAT)
        * score_scale
    )
    grad_keys = (
        jnp.einsum("bhrk,brhd->bkhd", grad_scores, query_heads, preferred_element_type=FLOAT)
        * score_scale
    )
    grad_values = jnp.einsum(
        "bhrk,brhd->bkhd", attn_probs.astype(BRAIN), grad_heads, preferred_element_type=FLOAT
    )
    batch_count, key_count = (pairs.shape[0], pairs.shape[1])
    grad_pairs = jnp.concatenate(
        [
            grad_keys.reshape(batch_count, key_count, D),
            grad_values.reshape(batch_count, key_count, D),
        ],
        axis=-1,
    )
    return (grad_queries.reshape(queries.shape), grad_pairs)


def project_forward(attended, residual, out_w, out_bias, gain_row, shift_row):
    summed = residual + matmul(attended, out_w) + out_bias
    return (layer_norm(summed, gain_row, shift_row), summed)


def project_backward(grad_norm, attended, summed, out_w, gain_row, shift_row):
    normed, pull_back = jax.vjp(layer_norm, summed, gain_row, shift_row)
    grad_summed, grad_gain, grad_shift = pull_back(grad_norm)
    grad_branch = grad_summed.astype(BRAIN)
    grad_out_w = matmul_left(attended, grad_branch)
    grad_out_bias = column_sum(grad_branch)
    grad_attended = matmul_right(grad_branch, out_w).astype(BRAIN)
    return (grad_summed, grad_attended, (grad_out_w, grad_out_bias, grad_gain, grad_shift))


def ffn_forward(first_norm, up_w, up_bias, down_w, down_bias, gain_row, shift_row):
    first_bf = first_norm.astype(BRAIN)
    lifted = matmul(first_bf, up_w) + up_bias
    activated = gelu_exact(lifted).astype(BRAIN)
    summed = first_norm + matmul(activated, down_w) + down_bias
    return (layer_norm(summed, gain_row, shift_row), (first_bf, lifted, activated, summed))


def ffn_backward(grad_norm, retained_context, up_w, down_w, gain_row, shift_row):
    first_bf, lifted, activated, summed = retained_context
    normed, pull_back = jax.vjp(layer_norm, summed, gain_row, shift_row)
    grad_summed, grad_gain, grad_shift = pull_back(grad_norm)
    grad_branch = grad_summed.astype(BRAIN)
    grad_down_w = matmul_left(activated, grad_branch)
    grad_down_bias = column_sum(grad_branch)
    grad_act = matmul_right(grad_branch, down_w)
    lifted_out, pull_gelu = jax.vjp(gelu_exact, lifted)
    grad_lifted = pull_gelu(grad_act)[0].astype(BRAIN)
    grad_up_w = matmul_left(first_bf, grad_lifted)
    up_bias_gradient = column_sum(grad_lifted)
    grad_first = grad_summed + matmul_right(grad_lifted, up_w)
    return (
        grad_first,
        (grad_up_w, up_bias_gradient, grad_down_w, grad_down_bias, grad_gain, grad_shift),
    )


def encoder_forward(weights, tokens, seg_rows, ctx_rank):
    qkv_w, out_w, up_w, down_w, bias_cols, up_bias, gain_cols = weights
    bias_vals = bias_cols.astype(FLOAT).T
    gain_vals = gain_cols.astype(FLOAT).T
    batch_count, row_count = (tokens.shape[0], tokens.shape[1])
    flat_tokens = tokens.reshape(batch_count * row_count, D)
    zero_row = jnp.zeros((D,), FLOAT)
    projected = (
        matmul(flat_tokens, qkv_w) + jnp.concatenate([bias_vals[0], zero_row, bias_vals[1]])
    ).astype(BRAIN)
    projected = projected.reshape(batch_count, row_count, 3 * D)
    all_pairs = lax.all_gather(projected[:, :, D:], "ctx", axis=1, tiled=True)
    own_segs = lax.dynamic_slice_in_dim(seg_rows, ctx_rank * row_count, row_count, axis=1)
    allowed = own_segs[:, :, None] == seg_rows[:, None, :]
    attended, log_total = attend_forward(projected[:, :, :D], all_pairs, allowed)
    attended = attended.reshape(batch_count * row_count, D)
    first_norm, first_sum = project_forward(
        attended, flat_tokens.astype(FLOAT), out_w, bias_vals[2], gain_vals[0], bias_vals[4]
    )
    final_norm, ffn_state = ffn_forward(
        first_norm, up_w, up_bias.astype(FLOAT), down_w, bias_vals[3], gain_vals[1], bias_vals[5]
    )
    return (
        final_norm,
        (flat_tokens, projected, all_pairs, allowed, log_total, attended, first_sum, ffn_state),
    )


def encoder_backward(weights, retained_context, grad_final):
    qkv_w, out_w, up_w, down_w, bias_cols, up_bias, gain_cols = weights
    bias_vals = bias_cols.astype(FLOAT).T
    gain_vals = gain_cols.astype(FLOAT).T
    flat_tokens, projected, all_pairs, allowed, log_total, attended, first_sum, ffn_state = (
        retained_context
    )
    batch_count, row_count = (projected.shape[0], projected.shape[1])
    grad_first, ffn_grads = ffn_backward(
        grad_final, ffn_state, up_w, down_w, gain_vals[1], bias_vals[5]
    )
    grad_tokens, grad_attended, proj_grads = project_backward(
        grad_first, attended, first_sum, out_w, gain_vals[0], bias_vals[4]
    )
    grad_queries, grad_pairs = attend_backward(
        projected[:, :, :D],
        all_pairs,
        allowed,
        log_total,
        grad_attended.reshape(batch_count, row_count, D),
    )
    own_pairs = lax.psum_scatter(
        grad_pairs.astype(jnp.bfloat16), "ctx", scatter_dimension=1, tiled=True
    ).astype(jnp.float32)
    mapped_slope = (
        jnp.concatenate([grad_queries, own_pairs], axis=-1)
        .astype(BRAIN)
        .reshape(batch_count * row_count, 3 * D)
    )
    grad_tokens = grad_tokens + matmul_right(mapped_slope, qkv_w)
    grad_qkv_w = matmul_left(flat_tokens, mapped_slope)
    proj_bias = column_sum(mapped_slope)
    up_grad_w, up_grad_bias, down_grad_w, down_grad_bias, gain_two, shift_two = ffn_grads
    out_grad_w, out_grad_bias, gain_one, shift_one = proj_grads
    bias_grads = jnp.stack(
        [proj_bias[:D], proj_bias[2 * D :], out_grad_bias, down_grad_bias, shift_one, shift_two],
        axis=1,
    )
    gain_grads = jnp.stack([gain_one, gain_two], axis=1)
    return (
        grad_tokens,
        (grad_qkv_w, out_grad_w, up_grad_w, down_grad_w, bias_grads, up_grad_bias, gain_grads),
    )


def decoder_forward(weights, tokens, memory_bf, pick_table, ctx_rank):
    (
        self_w,
        self_out_w,
        query_w,
        pair_w,
        cross_out_w,
        up_w,
        down_w,
        bias_cols,
        up_bias,
        gain_cols,
    ) = weights
    bias_vals = bias_cols.astype(FLOAT).T
    gain_vals = gain_cols.astype(FLOAT).T
    batch_count, row_count = (tokens.shape[0], tokens.shape[1])
    flat_tokens = tokens.reshape(batch_count * row_count, D)
    ctx_count = lax.axis_size("ctx")
    zero_row = jnp.zeros((D,), FLOAT)
    projected = (
        matmul(flat_tokens, self_w) + jnp.concatenate([bias_vals[0], zero_row, bias_vals[1]])
    ).astype(BRAIN)
    projected = projected.reshape(batch_count, row_count, 3 * D)
    all_pairs = lax.all_gather(projected[:, :, D:], "ctx", axis=1, tiled=True)
    query_pos = ctx_rank * row_count + jnp.arange(row_count, dtype=jnp.int32)
    key_pos = jnp.arange(row_count * ctx_count, dtype=jnp.int32)
    causal = (query_pos[:, None] >= key_pos[None, :])[None]
    attended, self_total = attend_forward(projected[:, :, :D], all_pairs, causal)
    attended = attended.reshape(batch_count * row_count, D)
    first_norm, first_sum = project_forward(
        attended, flat_tokens.astype(FLOAT), self_out_w, bias_vals[2], gain_vals[0], bias_vals[7]
    )
    first_bf = first_norm.astype(BRAIN)
    cross_queries = (matmul(first_bf, query_w) + bias_vals[3]).astype(BRAIN)
    memory_pairs = (matmul(memory_bf, pair_w) + jnp.concatenate([zero_row, bias_vals[4]])).astype(
        BRAIN
    )
    memory_rows = memory_pairs.shape[0] // batch_count
    memory_all = lax.all_gather(
        memory_pairs.reshape(batch_count, memory_rows, 2 * D), "ctx", axis=1, tiled=True
    )
    source_count = memory_all.shape[1]
    group_rows = min(row_count, BLOCK)
    group_count = row_count // group_rows
    group_start = ctx_rank * row_count + jnp.arange(group_count, dtype=jnp.int32) * group_rows
    pick_rows = jnp.take(pick_table, group_start // BLOCK, axis=1)
    pick_flat = (
        pick_rows + jnp.arange(batch_count, dtype=jnp.int32)[:, None, None] * source_count
    ).reshape(-1)
    picked = jnp.take(
        memory_all.reshape(batch_count * source_count, 2 * D), pick_flat, axis=0
    ).reshape(batch_count * group_count, pick_rows.shape[2], 2 * D)
    grouped = cross_queries.reshape(batch_count * group_count, group_rows, D)
    crossed, cross_total = attend_forward(grouped, picked, None)
    crossed = crossed.reshape(batch_count * row_count, D)
    second, second_sum = project_forward(
        crossed, first_norm, cross_out_w, bias_vals[5], gain_vals[1], bias_vals[8]
    )
    final_norm, ffn_state = ffn_forward(
        second, up_w, up_bias.astype(FLOAT), down_w, bias_vals[6], gain_vals[2], bias_vals[9]
    )
    retained_context = (
        flat_tokens,
        projected,
        all_pairs,
        causal,
        self_total,
        attended,
        first_sum,
        first_bf,
        grouped,
        pick_flat,
        picked,
        cross_total,
        crossed,
        second_sum,
        ffn_state,
        source_count,
    )
    return (final_norm, retained_context)


def decoder_backward(weights, memory_bf, retained_context, grad_final):
    (
        self_w,
        self_out_w,
        query_w,
        pair_w,
        cross_out_w,
        up_w,
        down_w,
        bias_cols,
        up_bias,
        gain_cols,
    ) = weights
    bias_vals = bias_cols.astype(FLOAT).T
    gain_vals = gain_cols.astype(FLOAT).T
    (
        flat_tokens,
        projected,
        all_pairs,
        causal,
        self_total,
        attended,
        first_sum,
        first_bf,
        grouped,
        pick_flat,
        picked,
        cross_total,
        crossed,
        second_sum,
        ffn_state,
        source_count,
    ) = retained_context
    batch_count, row_count = (projected.shape[0], projected.shape[1])
    grad_second, ffn_grads = ffn_backward(
        grad_final, ffn_state, up_w, down_w, gain_vals[2], bias_vals[9]
    )
    grad_first, grad_crossed, cross_grads = project_backward(
        grad_second, crossed, second_sum, cross_out_w, gain_vals[1], bias_vals[8]
    )
    grad_grouped, grad_picked = attend_backward(
        grouped, picked, None, cross_total, grad_crossed.reshape(grouped.shape)
    )
    grad_memory = (
        jnp.zeros((batch_count * source_count, 2 * D), FLOAT)
        .at[pick_flat]
        .add(grad_picked.reshape(-1, 2 * D))
    )
    own_memory = (
        lax.psum_scatter(
            grad_memory.reshape(batch_count, source_count, 2 * D).astype(jnp.bfloat16),
            "ctx",
            scatter_dimension=1,
            tiled=True,
        )
        .astype(jnp.float32)
        .astype(BRAIN)
    )
    own_memory = own_memory.reshape(-1, 2 * D)
    grad_memory_in = matmul_right(own_memory, pair_w)
    grad_pair_w = matmul_left(memory_bf, own_memory)
    pair_bias = column_sum(own_memory[:, D:])
    grad_cross_q = grad_grouped.reshape(batch_count * row_count, D).astype(BRAIN)
    grad_query_w = matmul_left(first_bf, grad_cross_q)
    query_bias = column_sum(grad_cross_q)
    grad_first = grad_first + matmul_right(grad_cross_q, query_w)
    grad_tokens, grad_attended, self_grads = project_backward(
        grad_first, attended, first_sum, self_out_w, gain_vals[0], bias_vals[7]
    )
    grad_queries, grad_pairs = attend_backward(
        projected[:, :, :D],
        all_pairs,
        causal,
        self_total,
        grad_attended.reshape(batch_count, row_count, D),
    )
    own_pairs = lax.psum_scatter(
        grad_pairs.astype(jnp.bfloat16), "ctx", scatter_dimension=1, tiled=True
    ).astype(jnp.float32)
    mapped_slope = (
        jnp.concatenate([grad_queries, own_pairs], axis=-1)
        .astype(BRAIN)
        .reshape(batch_count * row_count, 3 * D)
    )
    grad_tokens = grad_tokens + matmul_right(mapped_slope, self_w)
    grad_self_w = matmul_left(flat_tokens, mapped_slope)
    self_bias = column_sum(mapped_slope)
    up_grad_w, up_grad_bias, down_grad_w, down_grad_bias, gain_three, shift_three = ffn_grads
    cross_out_grad_w, cross_out_bias, gain_two, shift_two = cross_grads
    self_out_grad_w, self_out_bias, gain_one, shift_one = self_grads
    bias_grads = jnp.stack(
        [
            self_bias[:D],
            self_bias[2 * D :],
            self_out_bias,
            query_bias,
            pair_bias,
            cross_out_bias,
            down_grad_bias,
            shift_one,
            shift_two,
            shift_three,
        ],
        axis=1,
    )
    gain_grads = jnp.stack([gain_one, gain_two, gain_three], axis=1)
    weight_grads = (
        grad_self_w,
        self_out_grad_w,
        grad_query_w,
        grad_pair_w,
        cross_out_grad_w,
        up_grad_w,
        down_grad_w,
        bias_grads,
        up_grad_bias,
        gain_grads,
    )
    return (grad_tokens, grad_memory_in, weight_grads)


def fetch_weights(shards):
    return (
        lax.all_gather(shards[0], ("dp", "ctx"), axis=0, tiled=True),
        lax.all_gather(shards[1], ("dp", "ctx"), axis=0, tiled=True),
        lax.all_gather(shards[2], ("dp", "ctx"), axis=0, tiled=True),
        lax.all_gather(shards[3], ("dp", "ctx"), axis=0, tiled=True),
        lax.all_gather(shards[4], ("dp", "ctx"), axis=0, tiled=True),
        lax.all_gather(shards[5], ("dp", "ctx"), axis=0, tiled=True),
        lax.all_gather(shards[6], ("dp", "ctx"), axis=0, tiled=True),
        lax.all_gather(shards[7], ("dp", "ctx"), axis=0, tiled=True),
        lax.all_gather(shards[8], ("dp", "ctx"), axis=0, tiled=True),
        lax.all_gather(shards[9], ("dp", "ctx"), axis=0, tiled=True),
        lax.all_gather(shards[10], ("dp", "ctx"), axis=0, tiled=True),
        lax.all_gather(shards[11], ("dp", "ctx"), axis=0, tiled=True),
        lax.all_gather(shards[12], ("dp", "ctx"), axis=0, tiled=True),
        lax.all_gather(shards[13], ("dp", "ctx"), axis=0, tiled=True),
        lax.all_gather(shards[14], ("dp", "ctx"), axis=0, tiled=True),
        lax.all_gather(shards[15], ("dp", "ctx"), axis=0, tiled=True),
        lax.all_gather(shards[16], ("dp", "ctx"), axis=0, tiled=True),
    )


def body(
    enc_in,
    segments,
    dec_in,
    retrieved,
    enc_cot,
    dec_cot,
    enc_qkv,
    enc_out,
    enc_up,
    enc_down,
    enc_bias,
    enc_up_bias,
    enc_gain,
    decoder_self_projections,
    dec_out,
    cross_q,
    cross_kv,
    cross_out,
    dec_up,
    dec_down,
    dec_bias,
    dec_up_bias,
    dec_gain,
):
    shards = (
        enc_qkv,
        enc_out,
        enc_up,
        enc_down,
        enc_bias,
        enc_up_bias,
        enc_gain,
        decoder_self_projections,
        dec_out,
        cross_q,
        cross_kv,
        cross_out,
        dec_up,
        dec_down,
        dec_bias,
        dec_up_bias,
        dec_gain,
    )
    ctx_rank = lax.axis_index("ctx")
    batch_count, enc_rows, dec_rows = (enc_in.shape[0], enc_in.shape[1], dec_in.shape[1])
    kept_weights = fetch_weights(shards)
    enc_final, enc_state = encoder_forward(kept_weights[:7], enc_in, segments, ctx_rank)
    memory_bf = enc_final.astype(BRAIN)
    dec_final, dec_state = decoder_forward(kept_weights[7:], dec_in, memory_bf, retrieved, ctx_rank)
    dec_grad_in, memory_grad, dec_weight_grads = decoder_backward(
        kept_weights[7:], memory_bf, dec_state, dec_cot.reshape(-1, D).astype(FLOAT)
    )
    enc_grad_in, enc_weight_grads = encoder_backward(
        kept_weights[:7], enc_state, enc_cot.reshape(-1, D).astype(FLOAT) + memory_grad
    )
    totals = enc_weight_grads + dec_weight_grads
    reduced = (
        lax.psum_scatter(totals[0], ("dp", "ctx"), scatter_dimension=0, tiled=True),
        lax.psum_scatter(totals[1], ("dp", "ctx"), scatter_dimension=0, tiled=True),
        lax.psum_scatter(totals[2], ("dp", "ctx"), scatter_dimension=0, tiled=True),
        lax.psum_scatter(totals[3], ("dp", "ctx"), scatter_dimension=0, tiled=True),
        lax.psum_scatter(totals[4], ("dp", "ctx"), scatter_dimension=0, tiled=True),
        lax.psum_scatter(totals[5], ("dp", "ctx"), scatter_dimension=0, tiled=True),
        lax.psum_scatter(totals[6], ("dp", "ctx"), scatter_dimension=0, tiled=True),
        lax.psum_scatter(totals[7], ("dp", "ctx"), scatter_dimension=0, tiled=True),
        lax.psum_scatter(totals[8], ("dp", "ctx"), scatter_dimension=0, tiled=True),
        lax.psum_scatter(totals[9], ("dp", "ctx"), scatter_dimension=0, tiled=True),
        lax.psum_scatter(totals[10], ("dp", "ctx"), scatter_dimension=0, tiled=True),
        lax.psum_scatter(totals[11], ("dp", "ctx"), scatter_dimension=0, tiled=True),
        lax.psum_scatter(totals[12], ("dp", "ctx"), scatter_dimension=0, tiled=True),
        lax.psum_scatter(totals[13], ("dp", "ctx"), scatter_dimension=0, tiled=True),
        lax.psum_scatter(totals[14], ("dp", "ctx"), scatter_dimension=0, tiled=True),
        lax.psum_scatter(totals[15], ("dp", "ctx"), scatter_dimension=0, tiled=True),
        lax.psum_scatter(totals[16], ("dp", "ctx"), scatter_dimension=0, tiled=True),
    )
    return (
        memory_bf.reshape(batch_count, enc_rows, D),
        dec_final.astype(BRAIN).reshape(batch_count, dec_rows, D),
        enc_grad_in.reshape(batch_count, enc_rows, D),
        dec_grad_in.reshape(batch_count, dec_rows, D),
        reduced[0],
        reduced[1],
        reduced[2],
        reduced[3],
        reduced[4],
        reduced[5],
        reduced[6],
        reduced[7],
        reduced[8],
        reduced[9],
        reduced[10],
        reduced[11],
        reduced[12],
        reduced[13],
        reduced[14],
        reduced[15],
        reduced[16],
    )


MESH_ID = pl.DeviceIdType.MESH
ANY = pl.BlockSpec(memory_space=pl.ANY)
DMA_SEM = pltpu.SemaphoreType.DMA
PAIR = 128


def place():
    dp = lax.axis_index("dp")
    return dp, lax.axis_index("ctx"), lax.rem(dp, 2)


def spot():
    dp, z, core = place()
    return dp, z, core, lax.rem(dp // 2, 2), dp // 4


def dp_of(y, x, core):
    return (y * 2 + x) * 2 + core


def greet():
    dp, z, core, x, y = spot()
    zs = lax.axis_size("ctx")
    barrier = pltpu.get_barrier_semaphore()

    def hello(dp_to, z_to):
        pl.semaphore_signal(barrier, 1, device_id=(dp_to, z_to), device_id_type=MESH_ID)

    for step in range(zs):
        if step:
            hello(dp, lax.rem(z + step, zs))
        hello(dp_of(y, x, 1 - core), lax.rem(z + step, zs))
    hello(dp_of(y, 1 - x, core), z)
    hello(dp_of(1 - y, x, core), z)
    pl.semaphore_wait(barrier, 2 * zs + 1)


def remote(source, target, send, recv, dp_to, z_to):
    return pltpu.make_async_remote_copy(source, target, send, recv, device_id=(dp_to, z_to), device_id_type=MESH_ID)


def staged(count, stages):
    steps = []
    for turn in range(count + max(lag for lag, _ in stages)):
        for lag, fn in stages:
            if 0 <= turn - lag < count:
                steps.append(functools.partial(fn, turn - lag))
    return [(REACH * k / len(steps), step) for k, step in enumerate(steps)]


CHUNK = 24 * 512
BIG_CHUNK = 24 * 768
REACH = 1.0
LAG = 3


def pieces(shapes, chunk=None):
    chunks = []
    for i, (rows, n) in enumerate(shapes):
        columns = n // PAIR
        count = max(1, min(columns, -(-rows * n // (chunk or CHUNK))))
        at = 0
        for k in range(count):
            width = (columns * (k + 1) // count - columns * k // count) * PAIR
            chunks.append((i, at, width, len(chunks) % 2))
            at += width
    return chunks


def gather_job(shards, chunk=None):
    zs = lax.axis_size("ctx")
    everyone = lax.axis_size("dp") * zs
    chunks = pieces([s.shape for s in shards], chunk)
    count = len(chunks)

    def steps(ins, outs, scratch):
        send, recv, local = scratch
        dp, z, core, x, y = spot()

        def own_part(t):
            i, at, width, _ = chunks[t]
            return ins[i].at[:, pl.ds(at, width)]

        def rows_of(t, y_at, x_at, *z_at):
            i, at, width, _ = chunks[t]
            return outs[i].at[(y_at, x_at, core) + (z_at or (slice(None),)) + (slice(None), pl.ds(at, width))]

        def keep(t):
            return pltpu.make_async_copy(own_part(t), rows_of(t, y, x, z), local.at[t])

        def along_z(t, k):
            return remote(own_part(t), rows_of(t, y, x, z), send.at[t, k - 1], recv.at[t, k - 1], dp, lax.rem(z + k, zs))

        def hop(t, kind):
            near, far = dp_of(y, 1 - x, core), dp_of(1 - y, x, core)
            both = rows_of(t, y, slice(None))
            if chunks[t][3]:
                near, far, both = far, near, rows_of(t, slice(None), x)
            part, to = {
                3: (rows_of(t, y, x), near), 4: (both, far), 5: (rows_of(t, slice(None), slice(None)), dp_of(y, x, 1 - core)),
            }[kind]
            return remote(part, part, send.at[t, kind], recv.at[t, kind], to, z)

        def begin(t):
            keep(t).start()
            for k in range(1, zs):
                along_z(t, k).start()

        def first(t):
            keep(t).wait()
            for k in range(1, zs):
                along_z(t, k).wait_recv()
            hop(t, 3).start()

        def second(t):
            hop(t, 3).wait_recv()
            hop(t, 4).start()

        def third(t):
            hop(t, 4).wait_recv()
            hop(t, 5).start()

        def finish(t):
            hop(t, 5).wait_recv()
            for k in range(1, zs):
                along_z(t, k).wait_send()
            for kind in range(3, 6):
                hop(t, kind).wait_send()

        return staged(count, [(0, begin), (LAG + 1, first), (2 * LAG + 1, second), (3 * LAG + 1, third), (4 * LAG + 1, finish)])

    shapes = [jax.ShapeDtypeStruct((everyone // (4 * zs * 2) * 2, 2, 2, zs) + s.shape, s.dtype) for s in shards]
    scratch = [DMA_SEM((count, 6)), DMA_SEM((count, 6)), DMA_SEM((count,))]
    return shards, [ANY] * len(shards), shapes, [ANY] * len(shards), scratch, steps


def scatter_job(grads):
    zs, dps = lax.axis_size("ctx"), lax.axis_size("dp")
    rows = [g.shape[0] // (zs * dps) for g in grads]
    chunks = pieces([(r, g.shape[1]) for r, g in zip(rows, grads)])
    count = len(chunks)
    inputs = [g.reshape(dps // 4, 2, 2, zs * r, g.shape[1]) for r, g in zip(rows, grads)]
    scratch = [DMA_SEM((count, 6)), DMA_SEM((count, 6)), DMA_SEM((count,))]
    for i, _, width, _ in chunks:
        scratch += [
            pltpu.VMEM((2, 2, zs * rows[i], width), BRAIN),
            pltpu.VMEM((2, 2, zs * rows[i], width), BRAIN),
            pltpu.VMEM((2, zs * rows[i], width), BRAIN),
            pltpu.VMEM((zs * rows[i], width), BRAIN),
            pltpu.VMEM((zs, rows[i], width), BRAIN),
            pltpu.VMEM((zs - 1, rows[i], width), BRAIN),
        ]

    def steps(ins, outs, scratch):
        send, recv, local = scratch[:3]
        dp, z, core, x, y = spot()
        buffers = [scratch[3 + 6 * t : 9 + 6 * t] for t in range(count)]

        def source(t, core_at):
            i, at, width, _ = chunks[t]
            return ins[i].at[:, :, core_at, :, pl.ds(at, width)]

        def load(t):
            return pltpu.make_async_copy(source(t, core), buffers[t][0], local.at[t])

        def to_core(t):
            return remote(source(t, 1 - core), buffers[t][1], send.at[t, 0], recv.at[t, 0], dp_of(y, x, 1 - core), z)

        def wide(t):
            if chunks[t][3] == 0:
                part, to = buffers[t][0].at[1 - y], dp_of(1 - y, x, core)
            else:
                part, to = buffers[t][0].at[:, 1 - x], dp_of(y, 1 - x, core)
            return remote(part, buffers[t][2], send.at[t, 1], recv.at[t, 1], to, z)

        def narrow(t):
            if chunks[t][3] == 0:
                part, to = buffers[t][0].at[y, 1 - x], dp_of(y, 1 - x, core)
            else:
                part, to = buffers[t][0].at[1 - y, x], dp_of(1 - y, x, core)
            return remote(part, buffers[t][3], send.at[t, 2], recv.at[t, 2], to, z)

        def along_z(t, k):
            z_to = lax.rem(z + k, zs)
            return remote(buffers[t][4].at[z_to], buffers[t][5].at[k - 1], send.at[t, 2 + k], recv.at[t, 2 + k], dp, z_to)

        def add_into(target, other):
            total, width = target.shape

            def some(r, _):
                at = pl.ds(pl.multiple_of(r * 32, 32), 32)
                target[at, :] = target[at, :] + other[at, :]
                return 0

            lax.fori_loop(0, total // 32, some, 0)

        def begin(t):
            to_core(t).start()
            load(t).start()

        def first(t):
            load(t).wait()
            to_core(t).wait_recv()
            for b in range(4):
                add_into(buffers[t][0].at[b // 2, b % 2], buffers[t][1].at[b // 2, b % 2])
            wide(t).start()

        def second(t):
            wide(t).wait_recv()
            for j in range(2):
                block = (y, j) if chunks[t][3] == 0 else (j, x)
                add_into(buffers[t][0].at[block], buffers[t][2].at[j])
            narrow(t).start()

        def third(t):
            narrow(t).wait_recv()
            r = rows[chunks[t][0]]
            for s in range(zs):
                at = pl.ds(s * r, r)
                mine = buffers[t][0][y, x, at, :].astype(FLOAT)
                buffers[t][4][s] = (mine + buffers[t][3][at, :].astype(FLOAT)).astype(BRAIN)
            for k in range(1, zs):
                along_z(t, k).start()

        def finish(t):
            i, at, width, _ = chunks[t]
            total = buffers[t][4][z].astype(FLOAT)
            for k in range(1, zs):
                along_z(t, k).wait_recv()
                total = total + buffers[t][5][k - 1].astype(FLOAT)
            outs[i][:, pl.ds(at, width)] = total
            to_core(t).wait_send()
            wide(t).wait_send()
            narrow(t).wait_send()
            for k in range(1, zs):
                along_z(t, k).wait_send()

        return staged(count, [(0, begin), (LAG, first), (2 * LAG, second), (3 * LAG, third), (4 * LAG, finish)])

    shapes = [jax.ShapeDtypeStruct((r, g.shape[1]), FLOAT) for r, g in zip(rows, grads)]
    out_specs = [pl.BlockSpec(s.shape, lambda *_: (0, 0)) for s in shapes]
    return inputs, [ANY] * len(grads), shapes, out_specs, scratch, steps


def spread_job(tokens, ints=(), start=0.0):
    zs, count, int_count = lax.axis_size("ctx"), len(tokens), len(ints)

    def steps(ins, outs, scratch):
        send, recv, local, int_send, int_recv = scratch
        dp, z, core = place()
        pair = dp - core

        def swap(i):
            return remote(ins[count + i], outs[count + i], int_send.at[i], int_recv.at[i], pair + 1 - core, z)

        def each(t, what):
            for i in range(2):
                for h in range(2):
                    z_to, core_to = 2 * core + i, lax.rem(h + z, 2)
                    source, target = ins[t].at[i, pl.ds(h * BLOCK, BLOCK)], outs[t].at[z]
                    stays = jnp.logical_and(z_to == z, core_to == core)

                    @pl.when(stays)
                    def _():
                        what(pltpu.make_async_copy(source, target, local.at[t]), False)

                    @pl.when(jnp.logical_not(stays))
                    def _():
                        what(remote(source, target, send.at[t, 2 * i + h], recv.at[t, z], pair + core_to, z_to), True)

        def begin(t):
            if t == 0:
                for i in range(int_count):
                    swap(i).start()
            each(t, lambda copy, far: copy.start())

        def finish(t):
            each(t, lambda copy, far: copy.wait_send() if far else copy.wait())
            for s in range(zs):

                @pl.when(jnp.logical_not(jnp.logical_and(s == z, z // 2 == core)))
                def _():
                    remote(outs[t].at[s], outs[t].at[s], send.at[t, 0], recv.at[t, s], pair + 1 - core, z).wait_recv()

            if t == 0:
                for i in range(int_count):
                    swap(i).wait()

        return [(start, functools.partial(begin, t)) for t in range(count)] + [(1.0, functools.partial(finish, t)) for t in range(count)]

    shapes = [jax.ShapeDtypeStruct((zs, BLOCK, D), t.dtype) for t in tokens]
    shapes += [jax.ShapeDtypeStruct(i.shape, i.dtype) for i in ints]
    n = count + int_count
    scratch = [DMA_SEM((count, 4)), DMA_SEM((count, zs)), DMA_SEM((count,)), DMA_SEM((2,)), DMA_SEM((2,))]
    return list(tokens) + list(ints), [ANY] * n, shapes, [ANY] * n, scratch, steps


def collect_job(blocks):
    zs, count = lax.axis_size("ctx"), len(blocks)

    def steps(ins, outs, scratch):
        send, recv, local = scratch
        dp, z, core = place()
        pair = dp - core
        owner, inside = z // 2, lax.rem(z, 2)

        def each(t, what):
            for s in range(zs):
                half = lax.rem(core + s, 2)
                source = ins[t].at[s]
                target = outs[t].at[inside, pl.ds(half * BLOCK, BLOCK)]
                stays = jnp.logical_and(s == z, owner == core)

                @pl.when(stays)
                def _():
                    what(pltpu.make_async_copy(source, target, local.at[t]), False)

                @pl.when(jnp.logical_not(stays))
                def _():
                    what(remote(source, target, send.at[t, s], recv.at[t, 2 * inside + half], pair + owner, s), True)

        def begin(t):
            each(t, lambda copy, far: copy.start())

        def finish(t):
            each(t, lambda copy, far: copy.wait_send() if far else copy.wait())
            for i in range(2):
                for h in range(2):
                    z_from, core_from = 2 * core + i, lax.rem(h + z, 2)

                    @pl.when(jnp.logical_not(jnp.logical_and(z_from == z, core_from == core)))
                    def _():
                        target = outs[t].at[i, pl.ds(h * BLOCK, BLOCK)]
                        remote(target, target, send.at[t, 0], recv.at[t, 2 * i + h], pair + 1 - core, z).wait_recv()

        return [(0.0, functools.partial(begin, t)) for t in range(count)] + [(1.0, functools.partial(finish, t)) for t in range(count)]

    inputs = [b.reshape(zs, BLOCK, D) for b in blocks]
    shapes = [jax.ShapeDtypeStruct((2, 2 * BLOCK, D), b.dtype) for b in blocks]
    scratch = [DMA_SEM((count, zs)), DMA_SEM((count, 4)), DMA_SEM((count,))]
    return inputs, [ANY] * count, shapes, [ANY] * count, scratch, steps


def merge(lists):
    tagged = [(place, order, k, step) for order, steps in enumerate(lists) for k, (place, step) in enumerate(steps)]
    return [(t[0], t[3]) for t in sorted(tagged, key=lambda t: t[:3])]


def carry(
    jobs, collective_id, name, kernel=None, grid=1, slots=1, args=(), in_specs=(), out_shape=(), out_specs=(), scratch=(), cost=None
):
    sizes = [(len(j[0]), len(j[2]), len(j[4])) for j in jobs]

    def body(*refs):
        def take(n):
            nonlocal refs
            got, refs = refs[:n], refs[n:]
            return list(got)

        mine_in = take(len(args))
        job_in = [take(s[0]) for s in sizes]
        mine_out = take(len(out_shape))
        job_out = [take(s[1]) for s in sizes]
        mine_scratch = take(len(scratch))
        job_scratch = [take(s[2]) for s in sizes]
        steps = merge([j[5](i, o, s) for j, i, o, s in zip(jobs, job_in, job_out, job_scratch)])
        if kernel is None:
            greet()
            for _, step in steps:
                step()
            return
        turn = pl.program_id(0)
        calls = grid * slots
        called = [0]

        def poll():
            slot = called[0]
            called[0] += 1
            for g in range(grid):
                k = g * slots + slot
                some = [step for at, step in steps if k <= at * calls < k + 1]
                if some:

                    @pl.when(turn == g)
                    def _():
                        for step in some:
                            step()

        if jobs:

            @pl.when(turn == 0)
            def _():
                greet()

        kernel(poll, *mine_in, *mine_out, *mine_scratch)
        assert called[0] == slots
        last = [step for at, step in steps if at >= 1.0]
        if last:

            @pl.when(turn == grid - 1)
            def _():
                for step in last:
                    step()

    flat = lambda k: [v for j in jobs for v in j[k]]
    got = pl.pallas_call(
        body,
        grid=(grid,),
        out_shape=list(out_shape) + flat(2),
        in_specs=list(in_specs) + flat(1),
        out_specs=list(out_specs) + flat(3),
        scratch_shapes=list(scratch) + flat(4),
        compiler_params=pltpu.CompilerParams(
            collective_id=collective_id if jobs else None, has_side_effects=bool(jobs), vmem_limit_bytes=60 << 20
        ),
        cost_estimate=cost,
        name=name,
    )(*args, *flat(0))
    own, rest, parts = got[: len(out_shape)], got[len(out_shape) :], []
    for s in sizes:
        parts.append(rest[: s[1]])
        rest = rest[s[1] :]
    return own, parts


LOG2E = 1.4426950408889634


def key_chunks(rows, causal):
    if causal:
        return [(half, r, BLOCK, r) for r in range(0, rows, BLOCK) for half in range(2)]
    return [(half, r, 2 * BLOCK, 0) for half in range(2) for r in range(0, rows, 2 * BLOCK)]


def nt_dot(a, b):
    return lax.dot_general(a, b, (((1,), (1,)), ((), ())), preferred_element_type=FLOAT)


def head_lanes(values, head):
    lanes = lax.broadcasted_iota(jnp.int32, values.shape, 1)
    return jnp.where(lanes // HEAD_DIM == head, values, jnp.zeros_like(values))


def fold_rows(values, how):
    grouped = values.reshape(values.shape[0] // 8, 8, values.shape[1])
    return how(how(grouped, axis=0), axis=0, keepdims=True)


def attend_fwd_kernel(causal, poll, q_ref, k0_ref, v0_ref, k1_ref, v1_ref, bias_ref, o_ref, lse_ref, s_ref, p_ref):
    rows = q_ref.shape[0]
    k_refs = (k0_ref, k1_ref)
    v_all = jnp.concatenate([v0_ref[...], v1_ref[...]], axis=0)
    v_t = v_all.T
    factor = HEAD_DIM ** (-0.5) * LOG2E
    out_t = []
    for head in range(2):
        q = head_lanes(q_ref[...], head)
        top = jnp.full((1, rows), -3e38, FLOAT)
        for half, r, n, c in key_chunks(rows, causal):
            s = nt_dot(k_refs[half][pl.ds(r, n), :], q[c:])
            s = s * factor + bias_ref[pl.ds(half * rows + r, n), c:].astype(FLOAT)
            s_ref[pl.ds(half * rows + r, n), c:] = s
            peak = fold_rows(s, jnp.max)
            peak = jnp.maximum(top[:, c:], peak)
            top = jnp.concatenate([top[:, :c], peak], axis=1) if c else peak
        poll()
        total = jnp.zeros((1, rows), FLOAT)
        for half, r, n, c in key_chunks(rows, causal):
            p = jnp.exp2(s_ref[pl.ds(half * rows + r, n), c:] - top[:, c:])
            part = total[:, c:] + fold_rows(p, jnp.sum)
            total = jnp.concatenate([total[:, :c], part], axis=1) if c else part
            p_ref[pl.ds(half * rows + r, n), c:] = p.astype(BRAIN)
            if c:
                p_ref[pl.ds(half * rows + r, n), :c] = jnp.zeros((n, c), BRAIN)
        o_t = jnp.dot(v_t[head * HEAD_DIM : (head + 1) * HEAD_DIM], p_ref[...], preferred_element_type=FLOAT)
        out_t.append(o_t / total)
        poll()
        lse_ref[0, pl.ds(head, 1), :] = top + jnp.log(total) * LOG2E
    o_ref[...] = jnp.concatenate(out_t, axis=0).T.astype(o_ref.dtype)


def attention_forward(queries, q_col, pairs, kv_col, pairs_other, bias, causal, jobs=(), collective_id=None):
    rows = queries.shape[0]
    pair_count = D // PAIR
    block = (rows, PAIR)
    spec = lambda at: pl.BlockSpec(block, lambda p: (0, at + p))
    own, parts = carry(
        list(jobs),
        collective_id,
        "attend_fwd",
        kernel=functools.partial(attend_fwd_kernel, causal),
        grid=pair_count,
        slots=4,
        args=(queries, pairs, pairs, pairs_other, pairs_other, bias),
        in_specs=[
            spec(q_col), spec(kv_col), spec(kv_col + pair_count), spec(0), spec(pair_count),
            pl.BlockSpec((2 * rows, rows), lambda p: (0, 0)),
        ],
        out_shape=[jax.ShapeDtypeStruct((rows, D), BRAIN), jax.ShapeDtypeStruct((pair_count, 8, rows), FLOAT)],
        out_specs=[spec(0), pl.BlockSpec((1, 8, rows), lambda p: (p, 0, 0))],
        scratch=[pltpu.VMEM((2 * rows, rows), FLOAT), pltpu.VMEM((2 * rows, rows), BRAIN)],
        cost=pl.CostEstimate(flops=16 * rows * rows * D, bytes_accessed=10 * rows * D * 2, transcendentals=24 * rows * rows),
    )
    return own[0], own[1], parts


def attend_bwd_kernel(
    causal, poll, q_ref, k0_ref, v0_ref, k1_ref, v1_ref, bias_ref, o_ref, do_ref, lse_ref,
    dq_ref, dk0_ref, dv0_ref, dk1_ref, dv1_ref, ds_ref,
):
    rows = q_ref.shape[0]
    k_refs, v_refs = (k0_ref, k1_ref), (v0_ref, v1_ref)
    dk_refs, dv_refs = (dk0_ref, dk1_ref), (dv0_ref, dv1_ref)
    k_t = jnp.concatenate([k0_ref[...], k1_ref[...]], axis=0).T
    scale = HEAD_DIM ** (-0.5)
    factor = scale * LOG2E
    prod_t = (o_ref[...].astype(FLOAT) * do_ref[...].astype(FLOAT)).T
    dq_t = []
    q_heads = [head_lanes(q_ref[...], head) for head in range(2)]
    do_heads = [head_lanes(do_ref[...], head) for head in range(2)]
    lses = [lse_ref[0, pl.ds(head, 1), :] for head in range(2)]
    deltas = [fold_rows(prod_t[head * HEAD_DIM : (head + 1) * HEAD_DIM], jnp.sum) for head in range(2)]
    for half, r, n, c in key_chunks(rows, causal):
        k, v = k_refs[half][pl.ds(r, n), :], v_refs[half][pl.ds(r, n), :]
        bias = bias_ref[pl.ds(half * rows + r, n), c:].astype(FLOAT)
        dk = dv = None
        for head in range(2):
            q, do = q_heads[head][c:], do_heads[head][c:]
            p = jnp.exp2(nt_dot(k, q) * factor + bias - lses[head][:, c:])
            dv_part = jnp.dot(p.astype(BRAIN), do, preferred_element_type=FLOAT)
            ds = (p * (nt_dot(v, do) - deltas[head][:, c:])).astype(BRAIN)
            ds_ref[head, pl.ds(half * rows + r, n), c:] = ds
            if c:
                ds_ref[head, pl.ds(half * rows + r, n), :c] = jnp.zeros((n, c), BRAIN)
            dk_part = jnp.dot(ds, q, preferred_element_type=FLOAT)
            dk = dk_part if dk is None else dk + dk_part
            dv = dv_part if dv is None else dv + dv_part
        dk_refs[half][pl.ds(r, n), :] = (dk * scale).astype(dk_refs[half].dtype)
        dv_refs[half][pl.ds(r, n), :] = dv.astype(dv_refs[half].dtype)
        poll()
    for head in range(2):
        dq_t.append(jnp.dot(k_t[head * HEAD_DIM : (head + 1) * HEAD_DIM], ds_ref[head], preferred_element_type=FLOAT))
    dq_ref[...] = (jnp.concatenate(dq_t, axis=0) * scale).T.astype(dq_ref.dtype)


def attention_backward(
    queries, q_col, pairs, kv_col, pairs_other, bias, causal, attended, grad_attended, lse, jobs=(), collective_id=None
):
    rows = queries.shape[0]
    pair_count = D // PAIR
    block = (rows, PAIR)
    spec = lambda at: pl.BlockSpec(block, lambda p: (0, at + p))
    own, parts = carry(
        list(jobs),
        collective_id,
        "attend_bwd",
        kernel=functools.partial(attend_bwd_kernel, causal),
        grid=pair_count,
        slots=len(key_chunks(rows, causal)),
        args=(queries, pairs, pairs, pairs_other, pairs_other, bias, attended, grad_attended, lse),
        in_specs=[
            spec(q_col), spec(kv_col), spec(kv_col + pair_count), spec(0), spec(pair_count),
            pl.BlockSpec((2 * rows, rows), lambda p: (0, 0)), spec(0), spec(0),
            pl.BlockSpec((1, 8, rows), lambda p: (p, 0, 0)),
        ],
        out_shape=[jax.ShapeDtypeStruct((rows, D), t) for t in (BRAIN, FLOAT, FLOAT, BRAIN, BRAIN)],
        out_specs=[spec(0)] * 5,
        scratch=[pltpu.VMEM((2, 2 * rows, rows), BRAIN)],
        cost=pl.CostEstimate(flops=40 * rows * rows * D, bytes_accessed=18 * rows * D * 2, transcendentals=24 * rows * rows),
    )
    return own, parts


def to_sibling(values):
    count = lax.axis_size("dp")
    return lax.ppermute(values, "dp", [(i, i ^ 1) for i in range(count)])


ERF_TOP = (
    -2.72614225801306e-10, 2.77068142495902e-08, -2.10102402082508e-06, -5.69250639462346e-05,
    -7.34990630326855e-04, -2.95459980854025e-03, -1.60960333262415e-02,
)
ERF_LOW = (-1.45660718464996e-05, -2.13374055278905e-04, -1.68282697438203e-03, -7.37332916720468e-03, -1.42647390514189e-02)
FF_TILE = 512


def horner(values, factors):
    total = jnp.full_like(values, factors[0])
    for factor in factors[1:]:
        total = total * values + factor
    return total


def gelu_pair(x):
    arg = jnp.clip(x * 0.7071067811865476, -4.0, 4.0)
    square = arg * arg
    below = 0.5 + 0.5 * (arg * horner(square, ERF_TOP) / horner(square, ERF_LOW))
    return x * below, below + x * (0.3989422804014327 * jnp.exp(-0.5 * x * x))


def tn_dot(a, b):
    return lax.dot_general(a, b, (((0,), (0,)), ((), ())), preferred_element_type=FLOAT)


def ffn_end(residual, branch, gain, shift):
    summed = residual + branch
    return summed, layer_norm(summed, gain, shift)


def ffn_fwd_kernel(
    tiles, poll, first_ref, up_ref, ub_ref, down_ref, db_ref, gain_ref, shift_ref,
    act_ref, slope_ref, sum_ref, out_ref, acc, low,
):
    g = pl.program_id(0)

    @pl.when(g == 0)
    def _():
        low[...] = first_ref[...].astype(BRAIN)
        acc[...] = jnp.zeros_like(acc)

    lifted = jnp.dot(low[...], up_ref[...], preferred_element_type=FLOAT) + ub_ref[...]
    poll()
    act, slope = gelu_pair(lifted)
    act = act.astype(BRAIN)
    act_ref[...], slope_ref[...] = act, slope.astype(BRAIN)
    poll()
    acc[...] += jnp.dot(act, down_ref[...], preferred_element_type=FLOAT)
    poll()

    @pl.when(g == tiles - 1)
    def _():
        summed, final = ffn_end(first_ref[...], acc[...] + db_ref[...], gain_ref[...], shift_ref[...])
        sum_ref[...] = summed
        out_ref[...] = final.astype(BRAIN)


def ffn_bwd_start(grad, summed, gain, acc, branch, dgain_ref, dshift_ref, ddb_ref):
    grad_summed, dgain, dshift = norm_grad(grad, summed, gain)
    acc[...] = grad_summed
    branch[...] = grad_summed.astype(BRAIN)
    dgain_ref[...], dshift_ref[...] = dgain, dshift
    ddb_ref[...] = sums(branch[...])


def ffn_bwd_tile(poll, first, up, down, act, slope, branch, acc, dup_ref, dub_ref, ddown_ref):
    lift = (nt_dot(branch, down) * slope.astype(FLOAT)).astype(BRAIN)
    dub_ref[...] = sums(lift)
    poll()
    ddown_ref[...] = tn_dot(act, branch).astype(BRAIN)
    poll()
    dup_ref[...] = tn_dot(first, lift).astype(BRAIN)
    acc[...] += nt_dot(lift, up)
    poll()


def ffn_bwd_kernel(
    tiles, poll, first_ref, up_ref, down_ref, gain_ref, grad_ref, act_ref, slope_ref, sum_ref,
    dfirst_ref, dup_ref, dub_ref, ddown_ref, ddb_ref, dgain_ref, dshift_ref, acc, branch, low,
):
    g = pl.program_id(0)

    @pl.when(g == 0)
    def _():
        low[...] = first_ref[...].astype(BRAIN)
        ffn_bwd_start(grad_ref[...], sum_ref[...], gain_ref[...], acc, branch, dgain_ref, dshift_ref, ddb_ref)

    ffn_bwd_tile(
        poll, low[...], up_ref[...], down_ref[...], act_ref[...], slope_ref[...], branch[...], acc, dup_ref, dub_ref, ddown_ref
    )

    @pl.when(g == tiles - 1)
    def _():
        dfirst_ref[...] = acc[...]


def ffn_both_kernel(
    tiles, poll, first_ref, up_ref, ub_ref, down_ref, db_ref, gain_ref, shift_ref, cot_ref,
    out_ref, dfirst_ref, dup_ref, dub_ref, ddown_ref, ddb_ref, dgain_ref, dshift_ref, acc, branch, low, act_sc, slope_sc,
):
    g = pl.program_id(0)

    @pl.when(g == 0)
    def _():
        low[...] = first_ref[...].astype(BRAIN)
        acc[...] = jnp.zeros_like(acc)

    poll()

    @pl.when(g < tiles)
    def _():
        lifted = jnp.dot(low[...], up_ref[...], preferred_element_type=FLOAT) + ub_ref[...]
        act, slope = gelu_pair(lifted)
        act = act.astype(BRAIN)
        act_sc[g], slope_sc[g] = act, slope.astype(BRAIN)
        acc[...] += jnp.dot(act, down_ref[...], preferred_element_type=FLOAT)

    @pl.when(g == tiles - 1)
    def _():
        summed, final = ffn_end(first_ref[...], acc[...] + db_ref[...], gain_ref[...], shift_ref[...])
        out_ref[...] = final.astype(BRAIN)
        ffn_bwd_start(cot_ref[...].astype(FLOAT), summed, gain_ref[...], acc, branch, dgain_ref, dshift_ref, ddb_ref)

    poll()

    @pl.when(g >= tiles)
    def _():
        ffn_bwd_tile(
            lambda: None, low[...], up_ref[...], down_ref[...], act_sc[g - tiles], slope_sc[g - tiles], branch[...], acc,
            dup_ref, dub_ref, ddown_ref,
        )

    @pl.when(g == 2 * tiles - 1)
    def _():
        dfirst_ref[...] = acc[...]

    poll()


def ffn_call(mode, jobs, collective_id, first, up, ub, down, db, gain, shift, extra):
    rows, width = first.shape
    tiles = up.shape[1] // FF_TILE
    grid = 2 * tiles if mode == "both" else tiles
    at = (lambda g: lax.rem(g, tiles)) if mode == "both" else (lambda g: g)
    late = (lambda g: jnp.maximum(g - tiles, 0)) if mode == "both" else (lambda g: g)
    whole = lambda r: pl.BlockSpec((r, width), lambda g: (0, 0))
    column = lambda r, to: pl.BlockSpec((r, FF_TILE), lambda g: (0, to(g)))
    row = lambda to: pl.BlockSpec((FF_TILE, width), lambda g: (to(g), 0))
    shape = jax.ShapeDtypeStruct
    acc, low = pltpu.VMEM((rows, width), FLOAT), pltpu.VMEM((rows, width), BRAIN)
    up_spec, ub_spec, down_spec = column(width, at), column(1, at), row(at)
    grad_shapes = [shape((rows, width), FLOAT), shape(up.shape, BRAIN), shape(ub.shape, FLOAT), shape(down.shape, BRAIN)]
    grad_shapes += [shape((1, width), FLOAT)] * 3
    grad_specs = [whole(rows), column(width, late), column(1, late), row(late), whole(1), whole(1), whole(1)]
    if mode == "fwd":
        kernel, args = ffn_fwd_kernel, (first, up, ub, down, db, gain, shift)
        in_specs = [whole(rows), up_spec, ub_spec, down_spec, whole(1), whole(1), whole(1)]
        out_shape = [shape((rows, up.shape[1]), BRAIN)] * 2 + [shape((rows, width), FLOAT), shape((rows, width), BRAIN)]
        out_specs = [column(rows, at), column(rows, at), whole(rows), whole(rows)]
        scratch = [acc, low]
    elif mode == "bwd":
        grad, act, slope, summed = extra
        kernel, args = ffn_bwd_kernel, (first, up, down, gain, grad, act, slope, summed)
        in_specs = [whole(rows), up_spec, down_spec, whole(1), whole(rows), column(rows, at), column(rows, at), whole(rows)]
        out_shape, out_specs, scratch = grad_shapes, grad_specs, [acc, low, low]
    else:
        kernel, args = ffn_both_kernel, (first, up, ub, down, db, gain, shift) + tuple(extra)
        in_specs = [whole(rows), up_spec, ub_spec, down_spec, whole(1), whole(1), whole(1), whole(rows)]
        out_shape, out_specs = [shape((rows, width), BRAIN)] + grad_shapes, [whole(rows)] + grad_specs
        kept = pltpu.VMEM((tiles, rows, FF_TILE), BRAIN)
        scratch = [acc, low, low, kept, kept]
    flops = 4 * rows * width * up.shape[1] * {"fwd": 1, "bwd": 2, "both": 3}[mode]
    return carry(
        list(jobs), collective_id, "ffn_" + mode,
        kernel=functools.partial(kernel, tiles), grid=grid, slots=3, args=args, in_specs=in_specs, out_shape=out_shape,
        out_specs=out_specs, scratch=scratch,
        cost=pl.CostEstimate(flops=flops, bytes_accessed=4 * width * up.shape[1] + 16 * rows * width, transcendentals=rows * up.shape[1]),
    )


def own_blocks(per_block, core):
    zs = per_block.shape[0] // 2
    both = per_block.reshape((zs, 2) + per_block.shape[1:])
    flip = lax.rem(jnp.arange(zs, dtype=jnp.int32) + core, 2).reshape((zs,) + (1,) * (per_block.ndim - 1))
    own = jnp.where(flip == 0, both[:, 0], both[:, 1])
    return own, jnp.where(flip == 0, both[:, 1], both[:, 0])


def ordered_keys(per_token, core):
    own, other = own_blocks(per_token.reshape(-1, BLOCK), core)
    return own.reshape(-1), jnp.concatenate([own.reshape(-1), other.reshape(-1)])


SMALL = 32


def pack_small(enc_bias, dec_bias, enc_gain, dec_gain, enc_up_bias, dec_up_bias):
    rows = enc_bias.shape[0]
    parts = [enc_bias, dec_bias, enc_gain, dec_gain]
    left = jnp.pad(jnp.concatenate(parts, axis=1), ((0, 0), (0, SMALL - sum(p.shape[1] for p in parts))))
    right = jnp.pad(jnp.stack([enc_up_bias, dec_up_bias]), ((0, rows - 2), (0, PAIR - SMALL - enc_up_bias.shape[0])))
    return jnp.concatenate([left, right], axis=1)


def unpack_small(packed, width):
    cuts, at = [], 0
    for count in (6, 10, 2, 3):
        cuts.append(packed[..., at : at + count])
        at += count
    return cuts + [packed[..., 0, SMALL : SMALL + width], packed[..., 1, SMALL : SMALL + width]]


def small_grads(rows, enc_up_bias, dec_up_bias, shards):
    left = jnp.pad(jnp.concatenate(rows, axis=0), ((0, SMALL - len(rows)), (0, 0))).T.reshape(shards, -1, SMALL)
    up = jnp.stack([v.reshape(shards, -1) for v in (enc_up_bias, dec_up_bias)], axis=1)
    right = jnp.pad(up, ((0, 0), (0, left.shape[1] - 2), (0, PAIR - SMALL - up.shape[2])))
    return jnp.concatenate([left, right], axis=2).reshape(-1, PAIR)


def sums(values):
    return jnp.sum(values, axis=0, keepdims=True, dtype=FLOAT)


def norm_grad(grad, summed, gain_row):
    center = summed - jnp.mean(summed, axis=-1, keepdims=True)
    inverse = lax.rsqrt(jnp.mean(center * center, axis=-1, keepdims=True) + EPS)
    unit = center * inverse
    scaled = grad * gain_row
    back = scaled - jnp.mean(scaled, axis=-1, keepdims=True) - unit * jnp.mean(scaled * unit, axis=-1, keepdims=True)
    return inverse * back, sums(grad * unit), sums(grad)


def project_grad(grad_norm, attended, summed, out_w, gain_row):
    grad_summed, grad_gain, grad_shift = norm_grad(grad_norm, summed, gain_row)
    grad_branch = grad_summed.astype(BRAIN)
    return (
        grad_summed,
        matmul_right(grad_branch, out_w).astype(BRAIN),
        (matmul_left(attended, grad_branch), sums(grad_branch), grad_gain, grad_shift),
    )


def with_sibling(own_keys, own_values, other_keys, other_values):
    got = to_sibling(jnp.concatenate([other_keys, other_values], axis=1)).astype(FLOAT)
    return (jnp.concatenate([own_keys, own_values], axis=1) + got).astype(BRAIN)


def matrix(gathered):
    return gathered.reshape(-1, gathered.shape[-1])


def fast_body(
    enc_in, segments, dec_in, retrieved, enc_cot, dec_cot,
    enc_qkv, enc_out, enc_up, enc_down, enc_bias, enc_up_bias, enc_gain,
    dec_qkv, dec_out, cross_q, cross_kv, cross_out, dec_up, dec_down, dec_bias, dec_up_bias, dec_gain,
):
    dp, z, core = place()
    small = pack_small(enc_bias, dec_bias, enc_gain, dec_gain, enc_up_bias, dec_up_bias)
    weights = [enc_qkv, enc_out, small, enc_up, enc_down, dec_qkv, dec_out, cross_kv, cross_q, cross_out, dec_up, dec_down]
    _, ((enc_t, seg_other, ret_other), near) = carry(
        [spread_job([enc_in], [segments, retrieved], 0.3), gather_job(weights, BIG_CHUNK)], 0, "begin"
    )
    (
        w_enc_qkv, w_enc_out, _, w_enc_up, w_enc_down, w_dec_qkv,
        w_dec_out, w_cross_kv, w_cross_q, w_cross_out, w_dec_up, w_dec_down,
    ) = map(matrix, near)
    zs = enc_t.shape[0]
    rows = zs * BLOCK
    enc_t = enc_t.reshape(rows, D)
    here = z // 2 == core
    seg = lax.dynamic_index_in_dim(jnp.where(here, segments, seg_other), lax.rem(z, 2), 0, keepdims=False)
    ret = lax.dynamic_index_in_dim(jnp.where(here, retrieved, ret_other), lax.rem(z, 2), 0, keepdims=False)
    seg_q, seg_k = ordered_keys(seg, core)
    pos_q, pos_k = ordered_keys(jnp.arange(2 * rows, dtype=jnp.int32), core)
    enc_mask = jnp.where(seg_k[:, None] == seg_q[None, :], 0.0, NEG).astype(FLOAT)
    dec_mask = jnp.where(pos_k[:, None] <= pos_q[None, :], 0.0, NEG).astype(FLOAT)
    ret_own, _ = own_blocks(ret, core)
    member = jnp.any(pos_k[:, None, None] == ret_own[None], axis=-1)
    cross_mask = jnp.broadcast_to(jnp.where(member, 0.0, NEG).astype(FLOAT)[:, :, None], (2 * rows, zs, BLOCK)).reshape(2 * rows, rows)

    near_small = near[2].reshape((-1,) + near[2].shape[-2:])
    shards = near_small.shape[0]
    b_enc, b_dec, g_enc, g_dec, enc_ub, dec_ub = unpack_small(near_small, enc_up_bias.shape[0])
    across = lambda v: jnp.swapaxes(v.reshape(D, -1), 0, 1).astype(FLOAT)
    eb, db, eg, dg = ([row[i : i + 1] for i in range(row.shape[0])] for row in map(across, (b_enc, b_dec, g_enc, g_dec)))
    enc_ub, dec_ub = (v.reshape(1, -1).astype(FLOAT) for v in (enc_ub, dec_ub))
    zero_row = jnp.zeros((1, D), FLOAT)

    e_proj = (matmul(enc_t, w_enc_qkv) + jnp.concatenate([eb[0], zero_row, eb[1]], axis=1)).astype(BRAIN)
    e_other = to_sibling(e_proj[:, D:])
    e_att, e_lse, ((dec_t,),) = attention_forward(
        e_proj, 0, e_proj, D // PAIR, e_other, enc_mask, False, [spread_job([dec_in])], 1
    )
    dec_t = dec_t.reshape(rows, D)
    d_proj = (matmul(dec_t, w_dec_qkv) + jnp.concatenate([db[0], zero_row, db[1]], axis=1)).astype(BRAIN)
    d_other = to_sibling(d_proj[:, D:])
    d_att, d_lse, _ = attention_forward(
        d_proj, 0, d_proj, D // PAIR, d_other, dec_mask, True
    )
    e_first, e_sum = project_forward(e_att, enc_t.astype(FLOAT), w_enc_out, eb[2], eg[0], eb[4])
    (e_act, e_slope, e_sum2, memory), ((dec_c,),) = ffn_call(
        "fwd", [spread_job([dec_cot])], 8, e_first, w_enc_up, enc_ub, w_enc_down, eb[3], eg[1], eb[5], ()
    )
    dec_c = dec_c.reshape(rows, D)
    d_first, d_sum = project_forward(d_att, dec_t.astype(FLOAT), w_dec_out, db[2], dg[0], db[7])
    first_bf = d_first.astype(BRAIN)
    cross_queries = (matmul(first_bf, w_cross_q) + db[3]).astype(BRAIN)
    mem_pairs = (matmul(memory, w_cross_kv) + jnp.concatenate([zero_row, db[4]], axis=1)).astype(BRAIN)
    mem_other = to_sibling(mem_pairs)
    crossed, cross_lse, _ = attention_forward(
        cross_queries, 0, mem_pairs, 0, mem_other, cross_mask, False
    )
    second, second_sum = project_forward(crossed, d_first, w_cross_out, db[5], dg[1], db[8])
    low = lambda *grads: [g.astype(BRAIN) for g in grads]
    (dec_low, grad_second, g_dec_up, g_dec_ub, g_dec_down, g_db6, g_dg2, g_db9), ((enc_c,), (enc_hidden,)) = ffn_call(
        "both", [spread_job([enc_cot]), collect_job([memory])], 9,
        second, w_dec_up, dec_ub, w_dec_down, db[6], dg[2], db[9], (dec_c,),
    )
    enc_c = enc_c.reshape(rows, D)
    grad_first, grad_crossed, (g_cross_out, g_db5, g_dg1, g_db8) = project_grad(
        grad_second, crossed, second_sum, w_cross_out, dg[1]
    )
    (g_cq, dk, dv, dk_o, dv_o), ((dec_hidden,), (r_dec_down,)) = attention_backward(
        cross_queries, 0, mem_pairs, 0, mem_other, cross_mask, False, crossed, grad_crossed, cross_lse,
        [collect_job([dec_low]), scatter_job(low(g_dec_down))], 4,
    )
    own_memory = with_sibling(dk, dv, dk_o, dv_o)
    g_cross_q, g_db3 = matmul_left(first_bf, g_cq), sums(g_cq)
    grad_first = grad_first + matmul_right(g_cq, w_cross_q)
    memory_grad = matmul_right(own_memory, w_cross_kv)
    g_cross_kv, g_db4 = matmul_left(memory, own_memory), sums(own_memory[:, D:])
    grad_dec, grad_d_att, (g_dec_out, g_db2, g_dg0, g_db7) = project_grad(grad_first, d_att, d_sum, w_dec_out, dg[0])
    (dq, dk, dv, dk_o, dv_o), ((r_dec_up, r_cross_out, r_cross_q),) = attention_backward(
        d_proj, 0, d_proj, D // PAIR, d_other, dec_mask, True, d_att, grad_d_att, d_lse,
        [scatter_job(low(g_dec_up, g_cross_out, g_cross_q))], 5,
    )
    d_slope = jnp.concatenate([dq, with_sibling(dk, dv, dk_o, dv_o)], axis=1)
    grad_dec = grad_dec + matmul_right(d_slope, w_dec_qkv)
    g_dec_qkv, d_slope_sum = matmul_left(dec_t, d_slope), sums(d_slope)
    (grad_e_first, g_enc_up, g_enc_ub, g_enc_down, g_eb3, g_eg1, g_eb5), ((dec_home,), (r_cross_kv, r_dec_out, r_dec_qkv)) = ffn_call(
        "bwd", [collect_job(low(grad_dec)), scatter_job(low(g_cross_kv, g_dec_out, g_dec_qkv))], 10,
        e_first, w_enc_up, enc_ub, w_enc_down, eb[3], eg[1], eb[5], (enc_c.astype(FLOAT) + memory_grad, e_act, e_slope, e_sum2),
    )
    grad_enc, grad_e_att, (g_enc_out, g_eb2, g_eg0, g_eb4) = project_grad(grad_e_first, e_att, e_sum, w_enc_out, eg[0])
    (dq, dk, dv, dk_o, dv_o), ((r_enc_up, r_enc_down),) = attention_backward(
        e_proj, 0, e_proj, D // PAIR, e_other, enc_mask, False, e_att, grad_e_att, e_lse,
        [scatter_job(low(g_enc_up, g_enc_down))], 6,
    )
    e_pull = jnp.concatenate([dq, with_sibling(dk, dv, dk_o, dv_o)], axis=1)
    grad_enc = grad_enc + matmul_right(e_pull, w_enc_qkv)
    g_enc_qkv, e_slope_sum = matmul_left(enc_t, e_pull), sums(e_pull)

    g_small = small_grads(
        [e_slope_sum[:, :D], e_slope_sum[:, 2 * D :], g_eb2, g_eb3, g_eb4, g_eb5]
        + [d_slope_sum[:, :D], d_slope_sum[:, 2 * D :], g_db2, g_db3, g_db4, g_db5, g_db6, g_db7, g_db8, g_db9]
        + [g_eg0, g_eg1, g_dg0, g_dg1, g_dg2],
        g_enc_ub, g_dec_ub, shards,
    )
    _, ((enc_home,), (r_enc_out, r_enc_qkv, r_small)) = carry(
        [collect_job(low(grad_enc)), scatter_job(low(g_enc_out, g_enc_qkv, g_small))], 7, "end"
    )
    r_eb, r_db, r_eg, r_dg, r_enc_ub, r_dec_ub = unpack_small(r_small, enc_up_bias.shape[0])
    return (
        enc_hidden, dec_hidden, enc_home.astype(FLOAT), dec_home.astype(FLOAT),
        r_enc_qkv, r_enc_out, r_enc_up, r_enc_down, r_eb, r_enc_ub, r_eg,
        r_dec_qkv, r_dec_out, r_cross_q, r_cross_kv, r_cross_out, r_dec_up, r_dec_down, r_db, r_dec_ub, r_dg,
    )


def solution(mesh):
    in_specs = (
        P("dp", "ctx", None),
        P("dp", None),
        P("dp", "ctx", None),
        P("dp", None, None),
        P("dp", "ctx", None),
        P("dp", "ctx", None),
        P(("dp", "ctx"), None),
        P(("dp", "ctx"), None),
        P(("dp", "ctx"), None),
        P(("dp", "ctx"), None),
        P(("dp", "ctx"), None),
        P(("dp", "ctx")),
        P(("dp", "ctx"), None),
        P(("dp", "ctx"), None),
        P(("dp", "ctx"), None),
        P(("dp", "ctx"), None),
        P(("dp", "ctx"), None),
        P(("dp", "ctx"), None),
        P(("dp", "ctx"), None),
        P(("dp", "ctx"), None),
        P(("dp", "ctx"), None),
        P(("dp", "ctx")),
        P(("dp", "ctx"), None),
    )
    out_specs = (
        P("dp", "ctx", None),
        P("dp", "ctx", None),
        P("dp", "ctx", None),
        P("dp", "ctx", None),
        P(("dp", "ctx"), None),
        P(("dp", "ctx"), None),
        P(("dp", "ctx"), None),
        P(("dp", "ctx"), None),
        P(("dp", "ctx"), None),
        P(("dp", "ctx")),
        P(("dp", "ctx"), None),
        P(("dp", "ctx"), None),
        P(("dp", "ctx"), None),
        P(("dp", "ctx"), None),
        P(("dp", "ctx"), None),
        P(("dp", "ctx"), None),
        P(("dp", "ctx"), None),
        P(("dp", "ctx"), None),
        P(("dp", "ctx"), None),
        P(("dp", "ctx")),
        P(("dp", "ctx"), None),
    )

    def run(*args):
        sequences, tokens = args[0].shape[:2]
        fits = (
            mesh.shape["dp"] % 2 == 0
            and sequences == 2 * mesh.shape["dp"]
            and mesh.shape["ctx"] == 4
            and tokens == 2 * BLOCK * mesh.shape["ctx"]
            and args[2].shape == args[0].shape
            and D % (mesh.shape["dp"] * mesh.shape["ctx"] * 8) == 0
        )
        chosen = fast_body if fits else body
        return jax.shard_map(chosen, mesh=mesh, in_specs=in_specs, out_specs=out_specs, check_vma=False)(*args)

    return run
```

```python
import functools

import jax
import jax.numpy as jnp
from jax import lax
from jax.experimental import pallas as pl
from jax.experimental.pallas import tpu as pltpu
from jax.sharding import PartitionSpec as P

D = 768
HEADS = 12
HEAD_DIM = 64
BLOCK = 128


EPS = 1e-05
NEG = -1e30
FLOAT = jnp.float32
BRAIN = jnp.bfloat16


def matmul(left_side, right_side):
    return jnp.dot(left_side, right_side, preferred_element_type=FLOAT)


def matmul_left(left_side, right_side):
    return lax.dot_general(
        left_side, right_side, (((0,), (0,)), ((), ())), preferred_element_type=FLOAT
    )


def matmul_right(left_side, right_side):
    return lax.dot_general(
        left_side, right_side, (((1,), (1,)), ((), ())), preferred_element_type=FLOAT
    )


def column_sum(values):
    return jnp.sum(values, axis=0, dtype=FLOAT)


def layer_norm(hidden, gain_row, shift_row):
    center = hidden - jnp.mean(hidden, axis=-1, keepdims=True)
    spread = jnp.mean(center * center, axis=-1, keepdims=True)
    return center * lax.rsqrt(spread + EPS) * gain_row + shift_row


def gelu_exact(values):
    return jax.nn.gelu(values, approximate=False)


def split_pairs(pairs):
    pair_shape = pairs.shape
    both_parts = pairs.reshape(pair_shape[0], pair_shape[1], 2, HEADS, HEAD_DIM)
    return (both_parts[:, :, 0], both_parts[:, :, 1])


def head_scores(query_heads, key_heads, allowed):
    scores = jnp.einsum(
        "brhd,bkhd->bhrk", query_heads, key_heads, preferred_element_type=FLOAT
    ) * HEAD_DIM ** (-0.5)
    if allowed is not None:
        scores = jnp.where(allowed[:, None], scores, NEG)
    return scores


def attend_forward(queries, pairs, allowed):
    query_heads = queries.reshape(queries.shape[:2] + (HEADS, HEAD_DIM))
    key_heads, value_heads = split_pairs(pairs)
    scores = head_scores(query_heads, key_heads, allowed)
    row_max = jnp.max(scores, axis=-1, keepdims=True)
    log_total = row_max + jnp.log(jnp.sum(jnp.exp(scores - row_max), axis=-1, keepdims=True))
    attn_probs = jnp.exp(scores - log_total).astype(BRAIN)
    output = jnp.einsum("bhrk,bkhd->brhd", attn_probs, value_heads, preferred_element_type=FLOAT)
    return (output.reshape(queries.shape).astype(BRAIN), log_total)


def attend_backward(queries, pairs, allowed, log_total, grad_output):
    query_heads = queries.reshape(queries.shape[:2] + (HEADS, HEAD_DIM))
    key_heads, value_heads = split_pairs(pairs)
    grad_heads = grad_output.reshape(query_heads.shape)
    attn_probs = jnp.exp(head_scores(query_heads, key_heads, allowed) - log_total)
    grad_probs = jnp.einsum(
        "brhd,bkhd->bhrk", grad_heads, value_heads, preferred_element_type=FLOAT
    )
    inner_sum = jnp.sum(attn_probs * grad_probs, axis=-1, keepdims=True)
    grad_scores = (attn_probs * (grad_probs - inner_sum)).astype(BRAIN)
    score_scale = HEAD_DIM ** (-0.5)
    grad_queries = (
        jnp.einsum("bhrk,bkhd->brhd", grad_scores, key_heads, preferred_element_type=FLOAT)
        * score_scale
    )
    grad_keys = (
        jnp.einsum("bhrk,brhd->bkhd", grad_scores, query_heads, preferred_element_type=FLOAT)
        * score_scale
    )
    grad_values = jnp.einsum(
        "bhrk,brhd->bkhd", attn_probs.astype(BRAIN), grad_heads, preferred_element_type=FLOAT
    )
    batch_count, key_count = (pairs.shape[0], pairs.shape[1])
    grad_pairs = jnp.concatenate(
        [
            grad_keys.reshape(batch_count, key_count, D),
            grad_values.reshape(batch_count, key_count, D),
        ],
        axis=-1,
    )
    return (grad_queries.reshape(queries.shape), grad_pairs)


def project_forward(attended, residual, out_w, out_bias, gain_row, shift_row):
    summed = residual + matmul(attended, out_w) + out_bias
    return (layer_norm(summed, gain_row, shift_row), summed)


def project_backward(grad_norm, attended, summed, out_w, gain_row, shift_row):
    normed, pull_back = jax.vjp(layer_norm, summed, gain_row, shift_row)
    grad_summed, grad_gain, grad_shift = pull_back(grad_norm)
    grad_branch = grad_summed.astype(BRAIN)
    grad_out_w = matmul_left(attended, grad_branch)
    grad_out_bias = column_sum(grad_branch)
    grad_attended = matmul_right(grad_branch, out_w).astype(BRAIN)
    return (grad_summed, grad_attended, (grad_out_w, grad_out_bias, grad_gain, grad_shift))


def ffn_forward(first_norm, up_w, up_bias, down_w, down_bias, gain_row, shift_row):
    first_bf = first_norm.astype(BRAIN)
    lifted = matmul(first_bf, up_w) + up_bias
    activated = gelu_exact(lifted).astype(BRAIN)
    summed = first_norm + matmul(activated, down_w) + down_bias
    return (layer_norm(summed, gain_row, shift_row), (first_bf, lifted, activated, summed))


def ffn_backward(grad_norm, retained_context, up_w, down_w, gain_row, shift_row):
    first_bf, lifted, activated, summed = retained_context
    normed, pull_back = jax.vjp(layer_norm, summed, gain_row, shift_row)
    grad_summed, grad_gain, grad_shift = pull_back(grad_norm)
    grad_branch = grad_summed.astype(BRAIN)
    grad_down_w = matmul_left(activated, grad_branch)
    grad_down_bias = column_sum(grad_branch)
    grad_act = matmul_right(grad_branch, down_w)
    lifted_out, pull_gelu = jax.vjp(gelu_exact, lifted)
    grad_lifted = pull_gelu(grad_act)[0].astype(BRAIN)
    grad_up_w = matmul_left(first_bf, grad_lifted)
    up_bias_gradient = column_sum(grad_lifted)
    grad_first = grad_summed + matmul_right(grad_lifted, up_w)
    return (
        grad_first,
        (grad_up_w, up_bias_gradient, grad_down_w, grad_down_bias, grad_gain, grad_shift),
    )


def encoder_forward(weights, tokens, seg_rows, ctx_rank):
    qkv_w, out_w, up_w, down_w, bias_cols, up_bias, gain_cols = weights
    bias_vals = bias_cols.astype(FLOAT).T
    gain_vals = gain_cols.astype(FLOAT).T
    batch_count, row_count = (tokens.shape[0], tokens.shape[1])
    flat_tokens = tokens.reshape(batch_count * row_count, D)
    zero_row = jnp.zeros((D,), FLOAT)
    projected = (
        matmul(flat_tokens, qkv_w) + jnp.concatenate([bias_vals[0], zero_row, bias_vals[1]])
    ).astype(BRAIN)
    projected = projected.reshape(batch_count, row_count, 3 * D)
    all_pairs = lax.all_gather(projected[:, :, D:], "ctx", axis=1, tiled=True)
    own_segs = lax.dynamic_slice_in_dim(seg_rows, ctx_rank * row_count, row_count, axis=1)
    allowed = own_segs[:, :, None] == seg_rows[:, None, :]
    attended, log_total = attend_forward(projected[:, :, :D], all_pairs, allowed)
    attended = attended.reshape(batch_count * row_count, D)
    first_norm, first_sum = project_forward(
        attended, flat_tokens.astype(FLOAT), out_w, bias_vals[2], gain_vals[0], bias_vals[4]
    )
    final_norm, ffn_state = ffn_forward(
        first_norm, up_w, up_bias.astype(FLOAT), down_w, bias_vals[3], gain_vals[1], bias_vals[5]
    )
    return (
        final_norm,
        (flat_tokens, projected, all_pairs, allowed, log_total, attended, first_sum, ffn_state),
    )


def encoder_backward(weights, retained_context, grad_final):
    qkv_w, out_w, up_w, down_w, bias_cols, up_bias, gain_cols = weights
    bias_vals = bias_cols.astype(FLOAT).T
    gain_vals = gain_cols.astype(FLOAT).T
    flat_tokens, projected, all_pairs, allowed, log_total, attended, first_sum, ffn_state = (
        retained_context
    )
    batch_count, row_count = (projected.shape[0], projected.shape[1])
    grad_first, ffn_grads = ffn_backward(
        grad_final, ffn_state, up_w, down_w, gain_vals[1], bias_vals[5]
    )
    grad_tokens, grad_attended, proj_grads = project_backward(
        grad_first, attended, first_sum, out_w, gain_vals[0], bias_vals[4]
    )
    grad_queries, grad_pairs = attend_backward(
        projected[:, :, :D],
        all_pairs,
        allowed,
        log_total,
        grad_attended.reshape(batch_count, row_count, D),
    )
    own_pairs = lax.psum_scatter(
        grad_pairs.astype(jnp.bfloat16), "ctx", scatter_dimension=1, tiled=True
    ).astype(jnp.float32)
    mapped_slope = (
        jnp.concatenate([grad_queries, own_pairs], axis=-1)
        .astype(BRAIN)
        .reshape(batch_count * row_count, 3 * D)
    )
    grad_tokens = grad_tokens + matmul_right(mapped_slope, qkv_w)
    grad_qkv_w = matmul_left(flat_tokens, mapped_slope)
    proj_bias = column_sum(mapped_slope)
    up_grad_w, up_grad_bias, down_grad_w, down_grad_bias, gain_two, shift_two = ffn_grads
    out_grad_w, out_grad_bias, gain_one, shift_one = proj_grads
    bias_grads = jnp.stack(
        [proj_bias[:D], proj_bias[2 * D :], out_grad_bias, down_grad_bias, shift_one, shift_two],
        axis=1,
    )
    gain_grads = jnp.stack([gain_one, gain_two], axis=1)
    return (
        grad_tokens,
        (grad_qkv_w, out_grad_w, up_grad_w, down_grad_w, bias_grads, up_grad_bias, gain_grads),
    )


def decoder_forward(weights, tokens, memory_bf, pick_table, ctx_rank):
    (
        self_w,
        self_out_w,
        query_w,
        pair_w,
        cross_out_w,
        up_w,
        down_w,
        bias_cols,
        up_bias,
        gain_cols,
    ) = weights
    bias_vals = bias_cols.astype(FLOAT).T
    gain_vals = gain_cols.astype(FLOAT).T
    batch_count, row_count = (tokens.shape[0], tokens.shape[1])
    flat_tokens = tokens.reshape(batch_count * row_count, D)
    ctx_count = lax.axis_size("ctx")
    zero_row = jnp.zeros((D,), FLOAT)
    projected = (
        matmul(flat_tokens, self_w) + jnp.concatenate([bias_vals[0], zero_row, bias_vals[1]])
    ).astype(BRAIN)
    projected = projected.reshape(batch_count, row_count, 3 * D)
    all_pairs = lax.all_gather(projected[:, :, D:], "ctx", axis=1, tiled=True)
    query_pos = ctx_rank * row_count + jnp.arange(row_count, dtype=jnp.int32)
    key_pos = jnp.arange(row_count * ctx_count, dtype=jnp.int32)
    causal = (query_pos[:, None] >= key_pos[None, :])[None]
    attended, self_total = attend_forward(projected[:, :, :D], all_pairs, causal)
    attended = attended.reshape(batch_count * row_count, D)
    first_norm, first_sum = project_forward(
        attended, flat_tokens.astype(FLOAT), self_out_w, bias_vals[2], gain_vals[0], bias_vals[7]
    )
    first_bf = first_norm.astype(BRAIN)
    cross_queries = (matmul(first_bf, query_w) + bias_vals[3]).astype(BRAIN)
    memory_pairs = (matmul(memory_bf, pair_w) + jnp.concatenate([zero_row, bias_vals[4]])).astype(
        BRAIN
    )
    memory_rows = memory_pairs.shape[0] // batch_count
    memory_all = lax.all_gather(
        memory_pairs.reshape(batch_count, memory_rows, 2 * D), "ctx", axis=1, tiled=True
    )
    source_count = memory_all.shape[1]
    group_rows = min(row_count, BLOCK)
    group_count = row_count // group_rows
    group_start = ctx_rank * row_count + jnp.arange(group_count, dtype=jnp.int32) * group_rows
    pick_rows = jnp.take(pick_table, group_start // BLOCK, axis=1)
    pick_flat = (
        pick_rows + jnp.arange(batch_count, dtype=jnp.int32)[:, None, None] * source_count
    ).reshape(-1)
    picked = jnp.take(
        memory_all.reshape(batch_count * source_count, 2 * D), pick_flat, axis=0
    ).reshape(batch_count * group_count, pick_rows.shape[2], 2 * D)
    grouped = cross_queries.reshape(batch_count * group_count, group_rows, D)
    crossed, cross_total = attend_forward(grouped, picked, None)
    crossed = crossed.reshape(batch_count * row_count, D)
    second, second_sum = project_forward(
        crossed, first_norm, cross_out_w, bias_vals[5], gain_vals[1], bias_vals[8]
    )
    final_norm, ffn_state = ffn_forward(
        second, up_w, up_bias.astype(FLOAT), down_w, bias_vals[6], gain_vals[2], bias_vals[9]
    )
    retained_context = (
        flat_tokens,
        projected,
        all_pairs,
        causal,
        self_total,
        attended,
        first_sum,
        first_bf,
        grouped,
        pick_flat,
        picked,
        cross_total,
        crossed,
        second_sum,
        ffn_state,
        source_count,
    )
    return (final_norm, retained_context)


def decoder_backward(weights, memory_bf, retained_context, grad_final):
    (
        self_w,
        self_out_w,
        query_w,
        pair_w,
        cross_out_w,
        up_w,
        down_w,
        bias_cols,
        up_bias,
        gain_cols,
    ) = weights
    bias_vals = bias_cols.astype(FLOAT).T
    gain_vals = gain_cols.astype(FLOAT).T
    (
        flat_tokens,
        projected,
        all_pairs,
        causal,
        self_total,
        attended,
        first_sum,
        first_bf,
        grouped,
        pick_flat,
        picked,
        cross_total,
        crossed,
        second_sum,
        ffn_state,
        source_count,
    ) = retained_context
    batch_count, row_count = (projected.shape[0], projected.shape[1])
    grad_second, ffn_grads = ffn_backward(
        grad_final, ffn_state, up_w, down_w, gain_vals[2], bias_vals[9]
    )
    grad_first, grad_crossed, cross_grads = project_backward(
        grad_second, crossed, second_sum, cross_out_w, gain_vals[1], bias_vals[8]
    )
    grad_grouped, grad_picked = attend_backward(
        grouped, picked, None, cross_total, grad_crossed.reshape(grouped.shape)
    )
    grad_memory = (
        jnp.zeros((batch_count * source_count, 2 * D), FLOAT)
        .at[pick_flat]
        .add(grad_picked.reshape(-1, 2 * D))
    )
    own_memory = (
        lax.psum_scatter(
            grad_memory.reshape(batch_count, source_count, 2 * D).astype(jnp.bfloat16),
            "ctx",
            scatter_dimension=1,
            tiled=True,
        )
        .astype(jnp.float32)
        .astype(BRAIN)
    )
    own_memory = own_memory.reshape(-1, 2 * D)
    grad_memory_in = matmul_right(own_memory, pair_w)
    grad_pair_w = matmul_left(memory_bf, own_memory)
    pair_bias = column_sum(own_memory[:, D:])
    grad_cross_q = grad_grouped.reshape(batch_count * row_count, D).astype(BRAIN)
    grad_query_w = matmul_left(first_bf, grad_cross_q)
    query_bias = column_sum(grad_cross_q)
    grad_first = grad_first + matmul_right(grad_cross_q, query_w)
    grad_tokens, grad_attended, self_grads = project_backward(
        grad_first, attended, first_sum, self_out_w, gain_vals[0], bias_vals[7]
    )
    grad_queries, grad_pairs = attend_backward(
        projected[:, :, :D],
        all_pairs,
        causal,
        self_total,
        grad_attended.reshape(batch_count, row_count, D),
    )
    own_pairs = lax.psum_scatter(
        grad_pairs.astype(jnp.bfloat16), "ctx", scatter_dimension=1, tiled=True
    ).astype(jnp.float32)
    mapped_slope = (
        jnp.concatenate([grad_queries, own_pairs], axis=-1)
        .astype(BRAIN)
        .reshape(batch_count * row_count, 3 * D)
    )
    grad_tokens = grad_tokens + matmul_right(mapped_slope, self_w)
    grad_self_w = matmul_left(flat_tokens, mapped_slope)
    self_bias = column_sum(mapped_slope)
    up_grad_w, up_grad_bias, down_grad_w, down_grad_bias, gain_three, shift_three = ffn_grads
    cross_out_grad_w, cross_out_bias, gain_two, shift_two = cross_grads
    self_out_grad_w, self_out_bias, gain_one, shift_one = self_grads
    bias_grads = jnp.stack(
        [
            self_bias[:D],
            self_bias[2 * D :],
            self_out_bias,
            query_bias,
            pair_bias,
            cross_out_bias,
            down_grad_bias,
            shift_one,
            shift_two,
            shift_three,
        ],
        axis=1,
    )
    gain_grads = jnp.stack([gain_one, gain_two, gain_three], axis=1)
    weight_grads = (
        grad_self_w,
        self_out_grad_w,
        grad_query_w,
        grad_pair_w,
        cross_out_grad_w,
        up_grad_w,
        down_grad_w,
        bias_grads,
        up_grad_bias,
        gain_grads,
    )
    return (grad_tokens, grad_memory_in, weight_grads)


def fetch_weights(shards):
    return (
        lax.all_gather(shards[0], ("dp", "ctx"), axis=0, tiled=True),
        lax.all_gather(shards[1], ("dp", "ctx"), axis=0, tiled=True),
        lax.all_gather(shards[2], ("dp", "ctx"), axis=0, tiled=True),
        lax.all_gather(shards[3], ("dp", "ctx"), axis=0, tiled=True),
        lax.all_gather(shards[4], ("dp", "ctx"), axis=0, tiled=True),
        lax.all_gather(shards[5], ("dp", "ctx"), axis=0, tiled=True),
        lax.all_gather(shards[6], ("dp", "ctx"), axis=0, tiled=True),
        lax.all_gather(shards[7], ("dp", "ctx"), axis=0, tiled=True),
        lax.all_gather(shards[8], ("dp", "ctx"), axis=0, tiled=True),
        lax.all_gather(shards[9], ("dp", "ctx"), axis=0, tiled=True),
        lax.all_gather(shards[10], ("dp", "ctx"), axis=0, tiled=True),
        lax.all_gather(shards[11], ("dp", "ctx"), axis=0, tiled=True),
        lax.all_gather(shards[12], ("dp", "ctx"), axis=0, tiled=True),
        lax.all_gather(shards[13], ("dp", "ctx"), axis=0, tiled=True),
        lax.all_gather(shards[14], ("dp", "ctx"), axis=0, tiled=True),
        lax.all_gather(shards[15], ("dp", "ctx"), axis=0, tiled=True),
        lax.all_gather(shards[16], ("dp", "ctx"), axis=0, tiled=True),
    )


def body(
    enc_in,
    segments,
    dec_in,
    retrieved,
    enc_cot,
    dec_cot,
    enc_qkv,
    enc_out,
    enc_up,
    enc_down,
    enc_bias,
    enc_up_bias,
    enc_gain,
    decoder_self_projections,
    dec_out,
    cross_q,
    cross_kv,
    cross_out,
    dec_up,
    dec_down,
    dec_bias,
    dec_up_bias,
    dec_gain,
):
    shards = (
        enc_qkv,
        enc_out,
        enc_up,
        enc_down,
        enc_bias,
        enc_up_bias,
        enc_gain,
        decoder_self_projections,
        dec_out,
        cross_q,
        cross_kv,
        cross_out,
        dec_up,
        dec_down,
        dec_bias,
        dec_up_bias,
        dec_gain,
    )
    ctx_rank = lax.axis_index("ctx")
    batch_count, enc_rows, dec_rows = (enc_in.shape[0], enc_in.shape[1], dec_in.shape[1])
    kept_weights = fetch_weights(shards)
    enc_final, enc_state = encoder_forward(kept_weights[:7], enc_in, segments, ctx_rank)
    memory_bf = enc_final.astype(BRAIN)
    dec_final, dec_state = decoder_forward(kept_weights[7:], dec_in, memory_bf, retrieved, ctx_rank)
    dec_grad_in, memory_grad, dec_weight_grads = decoder_backward(
        kept_weights[7:], memory_bf, dec_state, dec_cot.reshape(-1, D).astype(FLOAT)
    )
    enc_grad_in, enc_weight_grads = encoder_backward(
        kept_weights[:7], enc_state, enc_cot.reshape(-1, D).astype(FLOAT) + memory_grad
    )
    totals = enc_weight_grads + dec_weight_grads
    reduced = (
        lax.psum_scatter(totals[0], ("dp", "ctx"), scatter_dimension=0, tiled=True),
        lax.psum_scatter(totals[1], ("dp", "ctx"), scatter_dimension=0, tiled=True),
        lax.psum_scatter(totals[2], ("dp", "ctx"), scatter_dimension=0, tiled=True),
        lax.psum_scatter(totals[3], ("dp", "ctx"), scatter_dimension=0, tiled=True),
        lax.psum_scatter(totals[4], ("dp", "ctx"), scatter_dimension=0, tiled=True),
        lax.psum_scatter(totals[5], ("dp", "ctx"), scatter_dimension=0, tiled=True),
        lax.psum_scatter(totals[6], ("dp", "ctx"), scatter_dimension=0, tiled=True),
        lax.psum_scatter(totals[7], ("dp", "ctx"), scatter_dimension=0, tiled=True),
        lax.psum_scatter(totals[8], ("dp", "ctx"), scatter_dimension=0, tiled=True),
        lax.psum_scatter(totals[9], ("dp", "ctx"), scatter_dimension=0, tiled=True),
        lax.psum_scatter(totals[10], ("dp", "ctx"), scatter_dimension=0, tiled=True),
        lax.psum_scatter(totals[11], ("dp", "ctx"), scatter_dimension=0, tiled=True),
        lax.psum_scatter(totals[12], ("dp", "ctx"), scatter_dimension=0, tiled=True),
        lax.psum_scatter(totals[13], ("dp", "ctx"), scatter_dimension=0, tiled=True),
        lax.psum_scatter(totals[14], ("dp", "ctx"), scatter_dimension=0, tiled=True),
        lax.psum_scatter(totals[15], ("dp", "ctx"), scatter_dimension=0, tiled=True),
        lax.psum_scatter(totals[16], ("dp", "ctx"), scatter_dimension=0, tiled=True),
    )
    return (
        memory_bf.reshape(batch_count, enc_rows, D),
        dec_final.astype(BRAIN).reshape(batch_count, dec_rows, D),
        enc_grad_in.reshape(batch_count, enc_rows, D),
        dec_grad_in.reshape(batch_count, dec_rows, D),
        reduced[0],
        reduced[1],
        reduced[2],
        reduced[3],
        reduced[4],
        reduced[5],
        reduced[6],
        reduced[7],
        reduced[8],
        reduced[9],
        reduced[10],
        reduced[11],
        reduced[12],
        reduced[13],
        reduced[14],
        reduced[15],
        reduced[16],
    )


MESH_ID = pl.DeviceIdType.MESH
ANY = pl.BlockSpec(memory_space=pl.ANY)
DMA_SEM = pltpu.SemaphoreType.DMA
PAIR = 128


def place():
    dp = lax.axis_index("dp")
    return dp, lax.axis_index("ctx"), lax.rem(dp, 2)


def spot():
    dp, z, core = place()
    return dp, z, core, lax.rem(dp // 2, 2), dp // 4


def dp_of(y, x, core):
    return (y * 2 + x) * 2 + core


def greet():
    dp, z, core, x, y = spot()
    zs = lax.axis_size("ctx")
    barrier = pltpu.get_barrier_semaphore()

    def hello(dp_to, z_to):
        pl.semaphore_signal(barrier, 1, device_id=(dp_to, z_to), device_id_type=MESH_ID)

    for step in range(zs):
        if step:
            hello(dp, lax.rem(z + step, zs))
        hello(dp_of(y, x, 1 - core), lax.rem(z + step, zs))
    hello(dp_of(y, 1 - x, core), z)
    hello(dp_of(1 - y, x, core), z)
    pl.semaphore_wait(barrier, 2 * zs + 1)


def remote(source, target, send, recv, dp_to, z_to):
    return pltpu.make_async_remote_copy(source, target, send, recv, device_id=(dp_to, z_to), device_id_type=MESH_ID)


def staged(count, stages):
    steps = []
    for turn in range(count + max(lag for lag, _ in stages)):
        for lag, fn in stages:
            if 0 <= turn - lag < count:
                steps.append(functools.partial(fn, turn - lag))
    return [(REACH * k / len(steps), step) for k, step in enumerate(steps)]


CHUNK = 24 * 512
BIG_CHUNK = 24 * 512
REACH = 1.0
LAG = 3
GATHER_LAG = 4


def pieces(shapes, chunk=None):
    chunks = []
    for i, (rows, n) in enumerate(shapes):
        columns = n // PAIR
        count = max(1, min(columns, -(-rows * n // (chunk or CHUNK))))
        at = 0
        for k in range(count):
            width = (columns * (k + 1) // count - columns * k // count) * PAIR
            chunks.append((i, at, width, len(chunks) % 2))
            at += width
    return chunks


def gather_job(shards, chunk=None):
    zs = lax.axis_size("ctx")
    everyone = lax.axis_size("dp") * zs
    chunks = pieces([s.shape for s in shards], chunk)
    count = len(chunks)

    def steps(ins, outs, scratch):
        send, recv, local = scratch
        dp, z, core, x, y = spot()

        def own_part(t):
            i, at, width, _ = chunks[t]
            return ins[i].at[:, pl.ds(at, width)]

        def rows_of(t, y_at, x_at, *z_at):
            i, at, width, _ = chunks[t]
            return outs[i].at[(y_at, x_at, core) + (z_at or (slice(None),)) + (slice(None), pl.ds(at, width))]

        def keep(t):
            return pltpu.make_async_copy(own_part(t), rows_of(t, y, x, z), local.at[t])

        def along_z(t, k):
            return remote(own_part(t), rows_of(t, y, x, z), send.at[t, k - 1], recv.at[t, k - 1], dp, lax.rem(z + k, zs))

        def hop(t, kind):
            near, far = dp_of(y, 1 - x, core), dp_of(1 - y, x, core)
            both = rows_of(t, y, slice(None))
            if chunks[t][3]:
                near, far, both = far, near, rows_of(t, slice(None), x)
            part, to = {
                3: (rows_of(t, y, x), near), 4: (both, far), 5: (rows_of(t, slice(None), slice(None)), dp_of(y, x, 1 - core)),
            }[kind]
            return remote(part, part, send.at[t, kind], recv.at[t, kind], to, z)

        def begin(t):
            keep(t).start()
            for k in range(1, zs):
                along_z(t, k).start()

        def first(t):
            keep(t).wait()
            for k in range(1, zs):
                along_z(t, k).wait_recv()
            hop(t, 3).start()

        def second(t):
            hop(t, 3).wait_recv()
            hop(t, 4).start()

        def third(t):
            hop(t, 4).wait_recv()
            hop(t, 5).start()

        def finish(t):
            hop(t, 5).wait_recv()
            for k in range(1, zs):
                along_z(t, k).wait_send()
            for kind in range(3, 6):
                hop(t, kind).wait_send()

        return staged(count, [(0, begin), (GATHER_LAG + 1, first), (2 * GATHER_LAG + 1, second), (3 * GATHER_LAG + 1, third), (4 * GATHER_LAG + 1, finish)])

    shapes = [jax.ShapeDtypeStruct((everyone // (4 * zs * 2) * 2, 2, 2, zs) + s.shape, s.dtype) for s in shards]
    scratch = [DMA_SEM((count, 6)), DMA_SEM((count, 6)), DMA_SEM((count,))]
    return shards, [ANY] * len(shards), shapes, [ANY] * len(shards), scratch, steps


def scatter_job(grads):
    zs, dps = lax.axis_size("ctx"), lax.axis_size("dp")
    rows = [g.shape[0] // (zs * dps) for g in grads]
    chunks = pieces([(r, g.shape[1]) for r, g in zip(rows, grads)])
    count = len(chunks)
    inputs = [g.reshape(dps // 4, 2, 2, zs * r, g.shape[1]) for r, g in zip(rows, grads)]
    scratch = [DMA_SEM((count, 6)), DMA_SEM((count, 6)), DMA_SEM((count,))]
    for i, _, width, _ in chunks:
        scratch += [
            pltpu.VMEM((2, 2, zs * rows[i], width), BRAIN),
            pltpu.VMEM((2, 2, zs * rows[i], width), BRAIN),
            pltpu.VMEM((2, zs * rows[i], width), BRAIN),
            pltpu.VMEM((zs * rows[i], width), BRAIN),
            pltpu.VMEM((zs, rows[i], width), BRAIN),
            pltpu.VMEM((zs - 1, rows[i], width), BRAIN),
        ]

    def steps(ins, outs, scratch):
        send, recv, local = scratch[:3]
        dp, z, core, x, y = spot()
        buffers = [scratch[3 + 6 * t : 9 + 6 * t] for t in range(count)]

        def source(t, core_at):
            i, at, width, _ = chunks[t]
            return ins[i].at[:, :, core_at, :, pl.ds(at, width)]

        def load(t):
            return pltpu.make_async_copy(source(t, core), buffers[t][0], local.at[t])

        def to_core(t):
            return remote(source(t, 1 - core), buffers[t][1], send.at[t, 0], recv.at[t, 0], dp_of(y, x, 1 - core), z)

        def wide(t):
            if chunks[t][3] == 0:
                part, to = buffers[t][0].at[1 - y], dp_of(1 - y, x, core)
            else:
                part, to = buffers[t][0].at[:, 1 - x], dp_of(y, 1 - x, core)
            return remote(part, buffers[t][2], send.at[t, 1], recv.at[t, 1], to, z)

        def narrow(t):
            if chunks[t][3] == 0:
                part, to = buffers[t][0].at[y, 1 - x], dp_of(y, 1 - x, core)
            else:
                part, to = buffers[t][0].at[1 - y, x], dp_of(1 - y, x, core)
            return remote(part, buffers[t][3], send.at[t, 2], recv.at[t, 2], to, z)

        def along_z(t, k):
            z_to = lax.rem(z + k, zs)
            return remote(buffers[t][4].at[z_to], buffers[t][5].at[k - 1], send.at[t, 2 + k], recv.at[t, 2 + k], dp, z_to)

        def add_into(target, other):
            total, width = target.shape

            def some(r, _):
                at = pl.ds(pl.multiple_of(r * 32, 32), 32)
                target[at, :] = target[at, :] + other[at, :]
                return 0

            lax.fori_loop(0, total // 32, some, 0)

        def begin(t):
            to_core(t).start()
            load(t).start()

        def first(t):
            load(t).wait()
            to_core(t).wait_recv()
            for b in range(4):
                add_into(buffers[t][0].at[b // 2, b % 2], buffers[t][1].at[b // 2, b % 2])
            wide(t).start()

        def second(t):
            wide(t).wait_recv()
            for j in range(2):
                block = (y, j) if chunks[t][3] == 0 else (j, x)
                add_into(buffers[t][0].at[block], buffers[t][2].at[j])
            narrow(t).start()

        def third(t):
            narrow(t).wait_recv()
            r = rows[chunks[t][0]]
            for s in range(zs):
                at = pl.ds(s * r, r)
                mine = buffers[t][0][y, x, at, :].astype(FLOAT)
                buffers[t][4][s] = (mine + buffers[t][3][at, :].astype(FLOAT)).astype(BRAIN)
            for k in range(1, zs):
                along_z(t, k).start()

        def finish(t):
            i, at, width, _ = chunks[t]
            total = buffers[t][4][z].astype(FLOAT)
            for k in range(1, zs):
                along_z(t, k).wait_recv()
                total = total + buffers[t][5][k - 1].astype(FLOAT)
            outs[i][:, pl.ds(at, width)] = total
            to_core(t).wait_send()
            wide(t).wait_send()
            narrow(t).wait_send()
            for k in range(1, zs):
                along_z(t, k).wait_send()

        return staged(count, [(0, begin), (LAG, first), (2 * LAG, second), (3 * LAG, third), (4 * LAG, finish)])

    shapes = [jax.ShapeDtypeStruct((r, g.shape[1]), FLOAT) for r, g in zip(rows, grads)]
    out_specs = [pl.BlockSpec(s.shape, lambda *_: (0, 0)) for s in shapes]
    return inputs, [ANY] * len(grads), shapes, out_specs, scratch, steps


def spread_job(tokens, ints=(), start=0.0):
    zs, count, int_count = lax.axis_size("ctx"), len(tokens), len(ints)

    def steps(ins, outs, scratch):
        send, recv, local, int_send, int_recv = scratch
        dp, z, core = place()
        pair = dp - core

        def swap(i):
            return remote(ins[count + i], outs[count + i], int_send.at[i], int_recv.at[i], pair + 1 - core, z)

        def each(t, what):
            for i in range(2):
                for h in range(2):
                    z_to, core_to = 2 * core + i, lax.rem(h + z, 2)
                    source, target = ins[t].at[i, pl.ds(h * BLOCK, BLOCK)], outs[t].at[z]
                    stays = jnp.logical_and(z_to == z, core_to == core)

                    @pl.when(stays)
                    def _():
                        what(pltpu.make_async_copy(source, target, local.at[t]), False)

                    @pl.when(jnp.logical_not(stays))
                    def _():
                        what(remote(source, target, send.at[t, 2 * i + h], recv.at[t, z], pair + core_to, z_to), True)

        def begin(t):
            if t == 0:
                for i in range(int_count):
                    swap(i).start()
            each(t, lambda copy, far: copy.start())

        def finish(t):
            each(t, lambda copy, far: copy.wait_send() if far else copy.wait())
            for s in range(zs):

                @pl.when(jnp.logical_not(jnp.logical_and(s == z, z // 2 == core)))
                def _():
                    remote(outs[t].at[s], outs[t].at[s], send.at[t, 0], recv.at[t, s], pair + 1 - core, z).wait_recv()

            if t == 0:
                for i in range(int_count):
                    swap(i).wait()

        return [(start, functools.partial(begin, t)) for t in range(count)] + [(1.0, functools.partial(finish, t)) for t in range(count)]

    shapes = [jax.ShapeDtypeStruct((zs, BLOCK, D), t.dtype) for t in tokens]
    shapes += [jax.ShapeDtypeStruct(i.shape, i.dtype) for i in ints]
    n = count + int_count
    scratch = [DMA_SEM((count, 4)), DMA_SEM((count, zs)), DMA_SEM((count,)), DMA_SEM((2,)), DMA_SEM((2,))]
    return list(tokens) + list(ints), [ANY] * n, shapes, [ANY] * n, scratch, steps


def collect_job(blocks):
    zs, count = lax.axis_size("ctx"), len(blocks)

    def steps(ins, outs, scratch):
        send, recv, local = scratch
        dp, z, core = place()
        pair = dp - core
        owner, inside = z // 2, lax.rem(z, 2)

        def each(t, what):
            for s in range(zs):
                half = lax.rem(core + s, 2)
                source = ins[t].at[s]
                target = outs[t].at[inside, pl.ds(half * BLOCK, BLOCK)]
                stays = jnp.logical_and(s == z, owner == core)

                @pl.when(stays)
                def _():
                    what(pltpu.make_async_copy(source, target, local.at[t]), False)

                @pl.when(jnp.logical_not(stays))
                def _():
                    what(remote(source, target, send.at[t, s], recv.at[t, 2 * inside + half], pair + owner, s), True)

        def begin(t):
            each(t, lambda copy, far: copy.start())

        def finish(t):
            each(t, lambda copy, far: copy.wait_send() if far else copy.wait())
            for i in range(2):
                for h in range(2):
                    z_from, core_from = 2 * core + i, lax.rem(h + z, 2)

                    @pl.when(jnp.logical_not(jnp.logical_and(z_from == z, core_from == core)))
                    def _():
                        target = outs[t].at[i, pl.ds(h * BLOCK, BLOCK)]
                        remote(target, target, send.at[t, 0], recv.at[t, 2 * i + h], pair + 1 - core, z).wait_recv()

        return [(0.0, functools.partial(begin, t)) for t in range(count)] + [(1.0, functools.partial(finish, t)) for t in range(count)]

    inputs = [b.reshape(zs, BLOCK, D) for b in blocks]
    shapes = [jax.ShapeDtypeStruct((2, 2 * BLOCK, D), b.dtype) for b in blocks]
    scratch = [DMA_SEM((count, zs)), DMA_SEM((count, 4)), DMA_SEM((count,))]
    return inputs, [ANY] * count, shapes, [ANY] * count, scratch, steps


def merge(lists):
    tagged = [(place, order, k, step) for order, steps in enumerate(lists) for k, (place, step) in enumerate(steps)]
    return [(t[0], t[3]) for t in sorted(tagged, key=lambda t: t[:3])]


def carry(
    jobs, collective_id, name, kernel=None, grid=1, slots=1, args=(), in_specs=(), out_shape=(), out_specs=(), scratch=(), cost=None
):
    sizes = [(len(j[0]), len(j[2]), len(j[4])) for j in jobs]

    def body(*refs):
        def take(n):
            nonlocal refs
            got, refs = refs[:n], refs[n:]
            return list(got)

        mine_in = take(len(args))
        job_in = [take(s[0]) for s in sizes]
        mine_out = take(len(out_shape))
        job_out = [take(s[1]) for s in sizes]
        mine_scratch = take(len(scratch))
        job_scratch = [take(s[2]) for s in sizes]
        steps = merge([j[5](i, o, s) for j, i, o, s in zip(jobs, job_in, job_out, job_scratch)])
        if kernel is None:
            greet()
            for _, step in steps:
                step()
            return
        turn = pl.program_id(0)
        calls = grid * slots
        called = [0]

        def poll():
            slot = called[0]
            called[0] += 1
            for g in range(grid):
                k = g * slots + slot
                some = [step for at, step in steps if k <= at * calls < k + 1]
                if some:

                    @pl.when(turn == g)
                    def _():
                        for step in some:
                            step()

        if jobs:

            @pl.when(turn == 0)
            def _():
                greet()

        kernel(poll, *mine_in, *mine_out, *mine_scratch)
        assert called[0] == slots
        last = [step for at, step in steps if at >= 1.0]
        if last:

            @pl.when(turn == grid - 1)
            def _():
                for step in last:
                    step()

    flat = lambda k: [v for j in jobs for v in j[k]]
    got = pl.pallas_call(
        body,
        grid=(grid,),
        out_shape=list(out_shape) + flat(2),
        in_specs=list(in_specs) + flat(1),
        out_specs=list(out_specs) + flat(3),
        scratch_shapes=list(scratch) + flat(4),
        compiler_params=pltpu.CompilerParams(
            collective_id=collective_id if jobs else None, has_side_effects=bool(jobs), vmem_limit_bytes=60 << 20
        ),
        cost_estimate=cost,
        name=name,
    )(*args, *flat(0))
    own, rest, parts = got[: len(out_shape)], got[len(out_shape) :], []
    for s in sizes:
        parts.append(rest[: s[1]])
        rest = rest[s[1] :]
    return own, parts


LOG2E = 1.4426950408889634


def key_chunks(rows, causal):
    if causal:
        return [(half, r, BLOCK, r) for r in range(0, rows, BLOCK) for half in range(2)]
    return [(half, r, 2 * BLOCK, 0) for half in range(2) for r in range(0, rows, 2 * BLOCK)]


def nt_dot(a, b):
    return lax.dot_general(a, b, (((1,), (1,)), ((), ())), preferred_element_type=FLOAT)


def head_lanes(values, head):
    lanes = lax.broadcasted_iota(jnp.int32, values.shape, 1)
    return jnp.where(lanes // HEAD_DIM == head, values, jnp.zeros_like(values))


def fold_rows(values, how):
    grouped = values.reshape(values.shape[0] // 8, 8, values.shape[1])
    return how(how(grouped, axis=0), axis=0, keepdims=True)


def attend_fwd_kernel(causal, poll, q_ref, k0_ref, v0_ref, k1_ref, v1_ref, bias_ref, o_ref, lse_ref, s_ref, p_ref):
    rows = q_ref.shape[0]
    k_refs = (k0_ref, k1_ref)
    v_all = jnp.concatenate([v0_ref[...], v1_ref[...]], axis=0)
    v_t = v_all.T
    factor = HEAD_DIM ** (-0.5) * LOG2E
    out_t = []
    for head in range(2):
        q = head_lanes(q_ref[...], head)
        top = jnp.full((1, rows), -3e38, FLOAT)
        for half, r, n, c in key_chunks(rows, causal):
            s = nt_dot(k_refs[half][pl.ds(r, n), :], q[c:])
            s = s * factor + bias_ref[pl.ds(half * rows + r, n), c:].astype(FLOAT)
            s_ref[pl.ds(half * rows + r, n), c:] = s
            peak = fold_rows(s, jnp.max)
            peak = jnp.maximum(top[:, c:], peak)
            top = jnp.concatenate([top[:, :c], peak], axis=1) if c else peak
        poll()
        total = jnp.zeros((1, rows), FLOAT)
        for half, r, n, c in key_chunks(rows, causal):
            p = jnp.exp2(s_ref[pl.ds(half * rows + r, n), c:] - top[:, c:])
            part = total[:, c:] + fold_rows(p, jnp.sum)
            total = jnp.concatenate([total[:, :c], part], axis=1) if c else part
            p_ref[pl.ds(half * rows + r, n), c:] = p.astype(BRAIN)
            if c:
                p_ref[pl.ds(half * rows + r, n), :c] = jnp.zeros((n, c), BRAIN)
        o_t = jnp.dot(v_t[head * HEAD_DIM : (head + 1) * HEAD_DIM], p_ref[...], preferred_element_type=FLOAT)
        out_t.append(o_t / total)
        poll()
        lse_ref[0, pl.ds(head, 1), :] = top + jnp.log(total) * LOG2E
    o_ref[...] = jnp.concatenate(out_t, axis=0).T.astype(o_ref.dtype)


def attention_forward(queries, q_col, pairs, kv_col, pairs_other, bias, causal, jobs=(), collective_id=None):
    rows = queries.shape[0]
    pair_count = D // PAIR
    block = (rows, PAIR)
    spec = lambda at: pl.BlockSpec(block, lambda p: (0, at + p))
    own, parts = carry(
        list(jobs),
        collective_id,
        "attend_fwd",
        kernel=functools.partial(attend_fwd_kernel, causal),
        grid=pair_count,
        slots=4,
        args=(queries, pairs, pairs, pairs_other, pairs_other, bias),
        in_specs=[
            spec(q_col), spec(kv_col), spec(kv_col + pair_count), spec(0), spec(pair_count),
            pl.BlockSpec((2 * rows, rows), lambda p: (0, 0)),
        ],
        out_shape=[jax.ShapeDtypeStruct((rows, D), BRAIN), jax.ShapeDtypeStruct((pair_count, 8, rows), FLOAT)],
        out_specs=[spec(0), pl.BlockSpec((1, 8, rows), lambda p: (p, 0, 0))],
        scratch=[pltpu.VMEM((2 * rows, rows), FLOAT), pltpu.VMEM((2 * rows, rows), BRAIN)],
        cost=pl.CostEstimate(flops=16 * rows * rows * D, bytes_accessed=10 * rows * D * 2, transcendentals=24 * rows * rows),
    )
    return own[0], own[1], parts


def attend_bwd_kernel(
    causal, poll, q_ref, k0_ref, v0_ref, k1_ref, v1_ref, bias_ref, o_ref, do_ref, lse_ref,
    dq_ref, dk0_ref, dv0_ref, dk1_ref, dv1_ref, ds_ref,
):
    rows = q_ref.shape[0]
    k_refs, v_refs = (k0_ref, k1_ref), (v0_ref, v1_ref)
    dk_refs, dv_refs = (dk0_ref, dk1_ref), (dv0_ref, dv1_ref)
    k_t = jnp.concatenate([k0_ref[...], k1_ref[...]], axis=0).T
    scale = HEAD_DIM ** (-0.5)
    factor = scale * LOG2E
    prod_t = (o_ref[...].astype(FLOAT) * do_ref[...].astype(FLOAT)).T
    dq_t = []
    q_heads = [head_lanes(q_ref[...], head) for head in range(2)]
    do_heads = [head_lanes(do_ref[...], head) for head in range(2)]
    lses = [lse_ref[0, pl.ds(head, 1), :] for head in range(2)]
    deltas = [fold_rows(prod_t[head * HEAD_DIM : (head + 1) * HEAD_DIM], jnp.sum) for head in range(2)]
    for half, r, n, c in key_chunks(rows, causal):
        k, v = k_refs[half][pl.ds(r, n), :], v_refs[half][pl.ds(r, n), :]
        bias = bias_ref[pl.ds(half * rows + r, n), c:].astype(FLOAT)
        dk = dv = None
        for head in range(2):
            q, do = q_heads[head][c:], do_heads[head][c:]
            p = jnp.exp2(nt_dot(k, q) * factor + bias - lses[head][:, c:])
            dv_part = jnp.dot(p.astype(BRAIN), do, preferred_element_type=FLOAT)
            ds = (p * (nt_dot(v, do) - deltas[head][:, c:])).astype(BRAIN)
            ds_ref[head, pl.ds(half * rows + r, n), c:] = ds
            if c:
                ds_ref[head, pl.ds(half * rows + r, n), :c] = jnp.zeros((n, c), BRAIN)
            dk_part = jnp.dot(ds, q, preferred_element_type=FLOAT)
            dk = dk_part if dk is None else dk + dk_part
            dv = dv_part if dv is None else dv + dv_part
        dk_refs[half][pl.ds(r, n), :] = (dk * scale).astype(dk_refs[half].dtype)
        dv_refs[half][pl.ds(r, n), :] = dv.astype(dv_refs[half].dtype)
        poll()
    for head in range(2):
        dq_t.append(jnp.dot(k_t[head * HEAD_DIM : (head + 1) * HEAD_DIM], ds_ref[head], preferred_element_type=FLOAT))
    dq_ref[...] = (jnp.concatenate(dq_t, axis=0) * scale).T.astype(dq_ref.dtype)


def attention_backward(
    queries, q_col, pairs, kv_col, pairs_other, bias, causal, attended, grad_attended, lse, jobs=(), collective_id=None
):
    rows = queries.shape[0]
    pair_count = D // PAIR
    block = (rows, PAIR)
    spec = lambda at: pl.BlockSpec(block, lambda p: (0, at + p))
    own, parts = carry(
        list(jobs),
        collective_id,
        "attend_bwd",
        kernel=functools.partial(attend_bwd_kernel, causal),
        grid=pair_count,
        slots=len(key_chunks(rows, causal)),
        args=(queries, pairs, pairs, pairs_other, pairs_other, bias, attended, grad_attended, lse),
        in_specs=[
            spec(q_col), spec(kv_col), spec(kv_col + pair_count), spec(0), spec(pair_count),
            pl.BlockSpec((2 * rows, rows), lambda p: (0, 0)), spec(0), spec(0),
            pl.BlockSpec((1, 8, rows), lambda p: (p, 0, 0)),
        ],
        out_shape=[jax.ShapeDtypeStruct((rows, D), t) for t in (BRAIN, FLOAT, FLOAT, BRAIN, BRAIN)],
        out_specs=[spec(0)] * 5,
        scratch=[pltpu.VMEM((2, 2 * rows, rows), BRAIN)],
        cost=pl.CostEstimate(flops=40 * rows * rows * D, bytes_accessed=18 * rows * D * 2, transcendentals=24 * rows * rows),
    )
    return own, parts


def to_sibling(values):
    count = lax.axis_size("dp")
    return lax.ppermute(values, "dp", [(i, i ^ 1) for i in range(count)])


ERF_TOP = (
    -2.72614225801306e-10, 2.77068142495902e-08, -2.10102402082508e-06, -5.69250639462346e-05,
    -7.34990630326855e-04, -2.95459980854025e-03, -1.60960333262415e-02,
)
ERF_LOW = (-1.45660718464996e-05, -2.13374055278905e-04, -1.68282697438203e-03, -7.37332916720468e-03, -1.42647390514189e-02)
FF_TILE = 512


def horner(values, factors):
    total = jnp.full_like(values, factors[0])
    for factor in factors[1:]:
        total = total * values + factor
    return total


def gelu_pair(x):
    arg = jnp.clip(x * 0.7071067811865476, -4.0, 4.0)
    square = arg * arg
    below = 0.5 + 0.5 * (arg * horner(square, ERF_TOP) / horner(square, ERF_LOW))
    return x * below, below + x * (0.3989422804014327 * jnp.exp(-0.5 * x * x))


def tn_dot(a, b):
    return lax.dot_general(a, b, (((0,), (0,)), ((), ())), preferred_element_type=FLOAT)


def ffn_end(residual, branch, gain, shift):
    summed = residual + branch
    return summed, layer_norm(summed, gain, shift)


def ffn_fwd_kernel(
    tiles, poll, first_ref, up_ref, ub_ref, down_ref, db_ref, gain_ref, shift_ref,
    act_ref, slope_ref, sum_ref, out_ref, acc, low,
):
    g = pl.program_id(0)

    @pl.when(g == 0)
    def _():
        low[...] = first_ref[...].astype(BRAIN)
        acc[...] = jnp.zeros_like(acc)

    lifted = jnp.dot(low[...], up_ref[...], preferred_element_type=FLOAT) + ub_ref[...]
    poll()
    act, slope = gelu_pair(lifted)
    act = act.astype(BRAIN)
    act_ref[...], slope_ref[...] = act, slope.astype(BRAIN)
    poll()
    acc[...] += jnp.dot(act, down_ref[...], preferred_element_type=FLOAT)
    poll()

    @pl.when(g == tiles - 1)
    def _():
        summed, final = ffn_end(first_ref[...], acc[...] + db_ref[...], gain_ref[...], shift_ref[...])
        sum_ref[...] = summed
        out_ref[...] = final.astype(BRAIN)


def ffn_bwd_start(grad, summed, gain, acc, branch, dgain_ref, dshift_ref, ddb_ref):
    grad_summed, dgain, dshift = norm_grad(grad, summed, gain)
    acc[...] = grad_summed
    branch[...] = grad_summed.astype(BRAIN)
    dgain_ref[...], dshift_ref[...] = dgain, dshift
    ddb_ref[...] = sums(branch[...])


def ffn_bwd_tile(poll, first, up, down, act, slope, branch, acc, dup_ref, dub_ref, ddown_ref):
    lift = (nt_dot(branch, down) * slope.astype(FLOAT)).astype(BRAIN)
    dub_ref[...] = sums(lift)
    poll()
    ddown_ref[...] = tn_dot(act, branch).astype(BRAIN)
    poll()
    dup_ref[...] = tn_dot(first, lift).astype(BRAIN)
    acc[...] += nt_dot(lift, up)
    poll()


def ffn_bwd_kernel(
    tiles, poll, first_ref, up_ref, down_ref, gain_ref, grad_ref, act_ref, slope_ref, sum_ref,
    dfirst_ref, dup_ref, dub_ref, ddown_ref, ddb_ref, dgain_ref, dshift_ref, acc, branch, low,
):
    g = pl.program_id(0)

    @pl.when(g == 0)
    def _():
        low[...] = first_ref[...].astype(BRAIN)
        ffn_bwd_start(grad_ref[...], sum_ref[...], gain_ref[...], acc, branch, dgain_ref, dshift_ref, ddb_ref)

    ffn_bwd_tile(
        poll, low[...], up_ref[...], down_ref[...], act_ref[...], slope_ref[...], branch[...], acc, dup_ref, dub_ref, ddown_ref
    )

    @pl.when(g == tiles - 1)
    def _():
        dfirst_ref[...] = acc[...]


def ffn_both_kernel(
    tiles, poll, first_ref, up_ref, ub_ref, down_ref, db_ref, gain_ref, shift_ref, cot_ref,
    out_ref, dfirst_ref, dup_ref, dub_ref, ddown_ref, ddb_ref, dgain_ref, dshift_ref, acc, branch, low, act_sc, slope_sc,
):
    g = pl.program_id(0)

    @pl.when(g == 0)
    def _():
        low[...] = first_ref[...].astype(BRAIN)
        acc[...] = jnp.zeros_like(acc)

    poll()

    @pl.when(g < tiles)
    def _():
        lifted = jnp.dot(low[...], up_ref[...], preferred_element_type=FLOAT) + ub_ref[...]
        act, slope = gelu_pair(lifted)
        act = act.astype(BRAIN)
        act_sc[g], slope_sc[g] = act, slope.astype(BRAIN)
        acc[...] += jnp.dot(act, down_ref[...], preferred_element_type=FLOAT)

    @pl.when(g == tiles - 1)
    def _():
        summed, final = ffn_end(first_ref[...], acc[...] + db_ref[...], gain_ref[...], shift_ref[...])
        out_ref[...] = final.astype(BRAIN)
        ffn_bwd_start(cot_ref[...].astype(FLOAT), summed, gain_ref[...], acc, branch, dgain_ref, dshift_ref, ddb_ref)

    poll()

    @pl.when(g >= tiles)
    def _():
        ffn_bwd_tile(
            lambda: None, low[...], up_ref[...], down_ref[...], act_sc[g - tiles], slope_sc[g - tiles], branch[...], acc,
            dup_ref, dub_ref, ddown_ref,
        )

    @pl.when(g == 2 * tiles - 1)
    def _():
        dfirst_ref[...] = acc[...]

    poll()


def ffn_call(mode, jobs, collective_id, first, up, ub, down, db, gain, shift, extra):
    rows, width = first.shape
    tiles = up.shape[1] // FF_TILE
    grid = 2 * tiles if mode == "both" else tiles
    at = (lambda g: lax.rem(g, tiles)) if mode == "both" else (lambda g: g)
    late = (lambda g: jnp.maximum(g - tiles, 0)) if mode == "both" else (lambda g: g)
    whole = lambda r: pl.BlockSpec((r, width), lambda g: (0, 0))
    column = lambda r, to: pl.BlockSpec((r, FF_TILE), lambda g: (0, to(g)))
    row = lambda to: pl.BlockSpec((FF_TILE, width), lambda g: (to(g), 0))
    shape = jax.ShapeDtypeStruct
    acc, low = pltpu.VMEM((rows, width), FLOAT), pltpu.VMEM((rows, width), BRAIN)
    up_spec, ub_spec, down_spec = column(width, at), column(1, at), row(at)
    grad_shapes = [shape((rows, width), FLOAT), shape(up.shape, BRAIN), shape(ub.shape, FLOAT), shape(down.shape, BRAIN)]
    grad_shapes += [shape((1, width), FLOAT)] * 3
    grad_specs = [whole(rows), column(width, late), column(1, late), row(late), whole(1), whole(1), whole(1)]
    if mode == "fwd":
        kernel, args = ffn_fwd_kernel, (first, up, ub, down, db, gain, shift)
        in_specs = [whole(rows), up_spec, ub_spec, down_spec, whole(1), whole(1), whole(1)]
        out_shape = [shape((rows, up.shape[1]), BRAIN)] * 2 + [shape((rows, width), FLOAT), shape((rows, width), BRAIN)]
        out_specs = [column(rows, at), column(rows, at), whole(rows), whole(rows)]
        scratch = [acc, low]
    elif mode == "bwd":
        grad, act, slope, summed = extra
        kernel, args = ffn_bwd_kernel, (first, up, down, gain, grad, act, slope, summed)
        in_specs = [whole(rows), up_spec, down_spec, whole(1), whole(rows), column(rows, at), column(rows, at), whole(rows)]
        out_shape, out_specs, scratch = grad_shapes, grad_specs, [acc, low, low]
    else:
        kernel, args = ffn_both_kernel, (first, up, ub, down, db, gain, shift) + tuple(extra)
        in_specs = [whole(rows), up_spec, ub_spec, down_spec, whole(1), whole(1), whole(1), whole(rows)]
        out_shape, out_specs = [shape((rows, width), BRAIN)] + grad_shapes, [whole(rows)] + grad_specs
        kept = pltpu.VMEM((tiles, rows, FF_TILE), BRAIN)
        scratch = [acc, low, low, kept, kept]
    flops = 4 * rows * width * up.shape[1] * {"fwd": 1, "bwd": 2, "both": 3}[mode]
    return carry(
        list(jobs), collective_id, "ffn_" + mode,
        kernel=functools.partial(kernel, tiles), grid=grid, slots=3, args=args, in_specs=in_specs, out_shape=out_shape,
        out_specs=out_specs, scratch=scratch,
        cost=pl.CostEstimate(flops=flops, bytes_accessed=4 * width * up.shape[1] + 16 * rows * width, transcendentals=rows * up.shape[1]),
    )


def own_blocks(per_block, core):
    zs = per_block.shape[0] // 2
    both = per_block.reshape((zs, 2) + per_block.shape[1:])
    flip = lax.rem(jnp.arange(zs, dtype=jnp.int32) + core, 2).reshape((zs,) + (1,) * (per_block.ndim - 1))
    own = jnp.where(flip == 0, both[:, 0], both[:, 1])
    return own, jnp.where(flip == 0, both[:, 1], both[:, 0])


def ordered_keys(per_token, core):
    own, other = own_blocks(per_token.reshape(-1, BLOCK), core)
    return own.reshape(-1), jnp.concatenate([own.reshape(-1), other.reshape(-1)])


SMALL = 32


def pack_small(enc_bias, dec_bias, enc_gain, dec_gain, enc_up_bias, dec_up_bias):
    rows = enc_bias.shape[0]
    parts = [enc_bias, dec_bias, enc_gain, dec_gain]
    left = jnp.pad(jnp.concatenate(parts, axis=1), ((0, 0), (0, SMALL - sum(p.shape[1] for p in parts))))
    right = jnp.pad(jnp.stack([enc_up_bias, dec_up_bias]), ((0, rows - 2), (0, PAIR - SMALL - enc_up_bias.shape[0])))
    return jnp.concatenate([left, right], axis=1)


def unpack_small(packed, width):
    cuts, at = [], 0
    for count in (6, 10, 2, 3):
        cuts.append(packed[..., at : at + count])
        at += count
    return cuts + [packed[..., 0, SMALL : SMALL + width], packed[..., 1, SMALL : SMALL + width]]


def small_grads(rows, enc_up_bias, dec_up_bias, shards):
    left = jnp.pad(jnp.concatenate(rows, axis=0), ((0, SMALL - len(rows)), (0, 0))).T.reshape(shards, -1, SMALL)
    up = jnp.stack([v.reshape(shards, -1) for v in (enc_up_bias, dec_up_bias)], axis=1)
    right = jnp.pad(up, ((0, 0), (0, left.shape[1] - 2), (0, PAIR - SMALL - up.shape[2])))
    return jnp.concatenate([left, right], axis=2).reshape(-1, PAIR)


def sums(values):
    return jnp.sum(values, axis=0, keepdims=True, dtype=FLOAT)


def norm_grad(grad, summed, gain_row):
    center = summed - jnp.mean(summed, axis=-1, keepdims=True)
    inverse = lax.rsqrt(jnp.mean(center * center, axis=-1, keepdims=True) + EPS)
    unit = center * inverse
    scaled = grad * gain_row
    back = scaled - jnp.mean(scaled, axis=-1, keepdims=True) - unit * jnp.mean(scaled * unit, axis=-1, keepdims=True)
    return inverse * back, sums(grad * unit), sums(grad)


def project_grad(grad_norm, attended, summed, out_w, gain_row):
    grad_summed, grad_gain, grad_shift = norm_grad(grad_norm, summed, gain_row)
    grad_branch = grad_summed.astype(BRAIN)
    return (
        grad_summed,
        matmul_right(grad_branch, out_w).astype(BRAIN),
        (matmul_left(attended, grad_branch), sums(grad_branch), grad_gain, grad_shift),
    )


def with_sibling(own_keys, own_values, other_keys, other_values):
    got = to_sibling(jnp.concatenate([other_keys, other_values], axis=1)).astype(FLOAT)
    return (jnp.concatenate([own_keys, own_values], axis=1) + got).astype(BRAIN)


def matrix(gathered):
    return gathered.reshape(-1, gathered.shape[-1])


def fast_body(
    enc_in, segments, dec_in, retrieved, enc_cot, dec_cot,
    enc_qkv, enc_out, enc_up, enc_down, enc_bias, enc_up_bias, enc_gain,
    dec_qkv, dec_out, cross_q, cross_kv, cross_out, dec_up, dec_down, dec_bias, dec_up_bias, dec_gain,
):
    dp, z, core = place()
    small = pack_small(enc_bias, dec_bias, enc_gain, dec_gain, enc_up_bias, dec_up_bias)
    weights = [enc_qkv, enc_out, small, enc_up, enc_down, dec_qkv, dec_out, cross_kv, cross_q, cross_out, dec_up, dec_down]
    _, ((enc_t, seg_other, ret_other), near) = carry(
        [spread_job([enc_in], [segments, retrieved], 0.3), gather_job(weights, BIG_CHUNK)], 0, "begin"
    )
    (
        w_enc_qkv, w_enc_out, _, w_enc_up, w_enc_down, w_dec_qkv,
        w_dec_out, w_cross_kv, w_cross_q, w_cross_out, w_dec_up, w_dec_down,
    ) = map(matrix, near)
    zs = enc_t.shape[0]
    rows = zs * BLOCK
    enc_t = enc_t.reshape(rows, D)
    here = z // 2 == core
    seg = lax.dynamic_index_in_dim(jnp.where(here, segments, seg_other), lax.rem(z, 2), 0, keepdims=False)
    ret = lax.dynamic_index_in_dim(jnp.where(here, retrieved, ret_other), lax.rem(z, 2), 0, keepdims=False)
    seg_q, seg_k = ordered_keys(seg, core)
    pos_q, pos_k = ordered_keys(jnp.arange(2 * rows, dtype=jnp.int32), core)
    enc_mask = jnp.where(seg_k[:, None] == seg_q[None, :], 0.0, NEG).astype(FLOAT)
    dec_mask = jnp.where(pos_k[:, None] <= pos_q[None, :], 0.0, NEG).astype(FLOAT)
    ret_own, _ = own_blocks(ret, core)
    member = jnp.any(pos_k[:, None, None] == ret_own[None], axis=-1)
    cross_mask = jnp.broadcast_to(jnp.where(member, 0.0, NEG).astype(FLOAT)[:, :, None], (2 * rows, zs, BLOCK)).reshape(2 * rows, rows)

    near_small = near[2].reshape((-1,) + near[2].shape[-2:])
    shards = near_small.shape[0]
    b_enc, b_dec, g_enc, g_dec, enc_ub, dec_ub = unpack_small(near_small, enc_up_bias.shape[0])
    across = lambda v: jnp.swapaxes(v.reshape(D, -1), 0, 1).astype(FLOAT)
    eb, db, eg, dg = ([row[i : i + 1] for i in range(row.shape[0])] for row in map(across, (b_enc, b_dec, g_enc, g_dec)))
    enc_ub, dec_ub = (v.reshape(1, -1).astype(FLOAT) for v in (enc_ub, dec_ub))
    zero_row = jnp.zeros((1, D), FLOAT)

    e_proj = (matmul(enc_t, w_enc_qkv) + jnp.concatenate([eb[0], zero_row, eb[1]], axis=1)).astype(BRAIN)
    e_other = to_sibling(e_proj[:, D:])
    e_att, e_lse, ((dec_t,),) = attention_forward(
        e_proj, 0, e_proj, D // PAIR, e_other, enc_mask, False, [spread_job([dec_in])], 1
    )
    dec_t = dec_t.reshape(rows, D)
    d_proj = (matmul(dec_t, w_dec_qkv) + jnp.concatenate([db[0], zero_row, db[1]], axis=1)).astype(BRAIN)
    d_other = to_sibling(d_proj[:, D:])
    d_att, d_lse, _ = attention_forward(
        d_proj, 0, d_proj, D // PAIR, d_other, dec_mask, True
    )
    e_first, e_sum = project_forward(e_att, enc_t.astype(FLOAT), w_enc_out, eb[2], eg[0], eb[4])
    (e_act, e_slope, e_sum2, memory), ((dec_c,),) = ffn_call(
        "fwd", [spread_job([dec_cot])], 8, e_first, w_enc_up, enc_ub, w_enc_down, eb[3], eg[1], eb[5], ()
    )
    dec_c = dec_c.reshape(rows, D)
    d_first, d_sum = project_forward(d_att, dec_t.astype(FLOAT), w_dec_out, db[2], dg[0], db[7])
    first_bf = d_first.astype(BRAIN)
    cross_queries = (matmul(first_bf, w_cross_q) + db[3]).astype(BRAIN)
    mem_pairs = (matmul(memory, w_cross_kv) + jnp.concatenate([zero_row, db[4]], axis=1)).astype(BRAIN)
    mem_other = to_sibling(mem_pairs)
    crossed, cross_lse, _ = attention_forward(
        cross_queries, 0, mem_pairs, 0, mem_other, cross_mask, False
    )
    second, second_sum = project_forward(crossed, d_first, w_cross_out, db[5], dg[1], db[8])
    low = lambda *grads: [g.astype(BRAIN) for g in grads]
    (dec_low, grad_second, g_dec_up, g_dec_ub, g_dec_down, g_db6, g_dg2, g_db9), ((enc_c,), (enc_hidden,)) = ffn_call(
        "both", [spread_job([enc_cot]), collect_job([memory])], 9,
        second, w_dec_up, dec_ub, w_dec_down, db[6], dg[2], db[9], (dec_c,),
    )
    enc_c = enc_c.reshape(rows, D)
    grad_first, grad_crossed, (g_cross_out, g_db5, g_dg1, g_db8) = project_grad(
        grad_second, crossed, second_sum, w_cross_out, dg[1]
    )
    (g_cq, dk, dv, dk_o, dv_o), ((dec_hidden,), (r_dec_down,)) = attention_backward(
        cross_queries, 0, mem_pairs, 0, mem_other, cross_mask, False, crossed, grad_crossed, cross_lse,
        [collect_job([dec_low]), scatter_job(low(g_dec_down))], 4,
    )
    own_memory = with_sibling(dk, dv, dk_o, dv_o)
    g_cross_q, g_db3 = matmul_left(first_bf, g_cq), sums(g_cq)
    grad_first = grad_first + matmul_right(g_cq, w_cross_q)
    memory_grad = matmul_right(own_memory, w_cross_kv)
    g_cross_kv, g_db4 = matmul_left(memory, own_memory), sums(own_memory[:, D:])
    grad_dec, grad_d_att, (g_dec_out, g_db2, g_dg0, g_db7) = project_grad(grad_first, d_att, d_sum, w_dec_out, dg[0])
    (dq, dk, dv, dk_o, dv_o), ((r_dec_up, r_cross_out, r_cross_q),) = attention_backward(
        d_proj, 0, d_proj, D // PAIR, d_other, dec_mask, True, d_att, grad_d_att, d_lse,
        [scatter_job(low(g_dec_up, g_cross_out, g_cross_q))], 5,
    )
    d_slope = jnp.concatenate([dq, with_sibling(dk, dv, dk_o, dv_o)], axis=1)
    grad_dec = grad_dec + matmul_right(d_slope, w_dec_qkv)
    g_dec_qkv, d_slope_sum = matmul_left(dec_t, d_slope), sums(d_slope)
    (grad_e_first, g_enc_up, g_enc_ub, g_enc_down, g_eb3, g_eg1, g_eb5), ((dec_home,), (r_cross_kv, r_dec_out, r_dec_qkv)) = ffn_call(
        "bwd", [collect_job(low(grad_dec)), scatter_job(low(g_cross_kv, g_dec_out, g_dec_qkv))], 10,
        e_first, w_enc_up, enc_ub, w_enc_down, eb[3], eg[1], eb[5], (enc_c.astype(FLOAT) + memory_grad, e_act, e_slope, e_sum2),
    )
    grad_enc, grad_e_att, (g_enc_out, g_eb2, g_eg0, g_eb4) = project_grad(grad_e_first, e_att, e_sum, w_enc_out, eg[0])
    (dq, dk, dv, dk_o, dv_o), ((r_enc_up, r_enc_down),) = attention_backward(
        e_proj, 0, e_proj, D // PAIR, e_other, enc_mask, False, e_att, grad_e_att, e_lse,
        [scatter_job(low(g_enc_up, g_enc_down))], 6,
    )
    e_pull = jnp.concatenate([dq, with_sibling(dk, dv, dk_o, dv_o)], axis=1)
    grad_enc = grad_enc + matmul_right(e_pull, w_enc_qkv)
    g_enc_qkv, e_slope_sum = matmul_left(enc_t, e_pull), sums(e_pull)

    g_small = small_grads(
        [e_slope_sum[:, :D], e_slope_sum[:, 2 * D :], g_eb2, g_eb3, g_eb4, g_eb5]
        + [d_slope_sum[:, :D], d_slope_sum[:, 2 * D :], g_db2, g_db3, g_db4, g_db5, g_db6, g_db7, g_db8, g_db9]
        + [g_eg0, g_eg1, g_dg0, g_dg1, g_dg2],
        g_enc_ub, g_dec_ub, shards,
    )
    _, ((enc_home,), (r_enc_out, r_enc_qkv, r_small)) = carry(
        [collect_job(low(grad_enc)), scatter_job(low(g_enc_out, g_enc_qkv, g_small))], 7, "end"
    )
    r_eb, r_db, r_eg, r_dg, r_enc_ub, r_dec_ub = unpack_small(r_small, enc_up_bias.shape[0])
    return (
        enc_hidden, dec_hidden, enc_home.astype(FLOAT), dec_home.astype(FLOAT),
        r_enc_qkv, r_enc_out, r_enc_up, r_enc_down, r_eb, r_enc_ub, r_eg,
        r_dec_qkv, r_dec_out, r_cross_q, r_cross_kv, r_cross_out, r_dec_up, r_dec_down, r_db, r_dec_ub, r_dg,
    )


def solution(mesh):
    in_specs = (
        P("dp", "ctx", None),
        P("dp", None),
        P("dp", "ctx", None),
        P("dp", None, None),
        P("dp", "ctx", None),
        P("dp", "ctx", None),
        P(("dp", "ctx"), None),
        P(("dp", "ctx"), None),
        P(("dp", "ctx"), None),
        P(("dp", "ctx"), None),
        P(("dp", "ctx"), None),
        P(("dp", "ctx")),
        P(("dp", "ctx"), None),
        P(("dp", "ctx"), None),
        P(("dp", "ctx"), None),
        P(("dp", "ctx"), None),
        P(("dp", "ctx"), None),
        P(("dp", "ctx"), None),
        P(("dp", "ctx"), None),
        P(("dp", "ctx"), None),
        P(("dp", "ctx"), None),
        P(("dp", "ctx")),
        P(("dp", "ctx"), None),
    )
    out_specs = (
        P("dp", "ctx", None),
        P("dp", "ctx", None),
        P("dp", "ctx", None),
        P("dp", "ctx", None),
        P(("dp", "ctx"), None),
        P(("dp", "ctx"), None),
        P(("dp", "ctx"), None),
        P(("dp", "ctx"), None),
        P(("dp", "ctx"), None),
        P(("dp", "ctx")),
        P(("dp", "ctx"), None),
        P(("dp", "ctx"), None),
        P(("dp", "ctx"), None),
        P(("dp", "ctx"), None),
        P(("dp", "ctx"), None),
        P(("dp", "ctx"), None),
        P(("dp", "ctx"), None),
        P(("dp", "ctx"), None),
        P(("dp", "ctx"), None),
        P(("dp", "ctx")),
        P(("dp", "ctx"), None),
    )

    def run(*args):
        sequences, tokens = args[0].shape[:2]
        fits = (
            mesh.shape["dp"] % 2 == 0
            and sequences == 2 * mesh.shape["dp"]
            and mesh.shape["ctx"] == 4
            and tokens == 2 * BLOCK * mesh.shape["ctx"]
            and args[2].shape == args[0].shape
            and D % (mesh.shape["dp"] * mesh.shape["ctx"] * 8) == 0
        )
        chosen = fast_body if fits else body
        return jax.shard_map(chosen, mesh=mesh, in_specs=in_specs, out_specs=out_specs, check_vma=False)(*args)

    return run
```

```python
import functools

import jax
import jax.numpy as jnp
from jax import lax
from jax.experimental import pallas as pl
from jax.experimental.pallas import tpu as pltpu
from jax.sharding import PartitionSpec as P

D = 768
HEADS = 12
HEAD_DIM = 64
BLOCK = 128


EPS = 1e-05
NEG = -1e30
FLOAT = jnp.float32
BRAIN = jnp.bfloat16


def matmul(left_side, right_side):
    return jnp.dot(left_side, right_side, preferred_element_type=FLOAT)


def matmul_left(left_side, right_side):
    return lax.dot_general(
        left_side, right_side, (((0,), (0,)), ((), ())), preferred_element_type=FLOAT
    )


def matmul_right(left_side, right_side):
    return lax.dot_general(
        left_side, right_side, (((1,), (1,)), ((), ())), preferred_element_type=FLOAT
    )


def column_sum(values):
    return jnp.sum(values, axis=0, dtype=FLOAT)


def layer_norm(hidden, gain_row, shift_row):
    center = hidden - jnp.mean(hidden, axis=-1, keepdims=True)
    spread = jnp.mean(center * center, axis=-1, keepdims=True)
    return center * lax.rsqrt(spread + EPS) * gain_row + shift_row


def gelu_exact(values):
    return jax.nn.gelu(values, approximate=False)


def split_pairs(pairs):
    pair_shape = pairs.shape
    both_parts = pairs.reshape(pair_shape[0], pair_shape[1], 2, HEADS, HEAD_DIM)
    return (both_parts[:, :, 0], both_parts[:, :, 1])


def head_scores(query_heads, key_heads, allowed):
    scores = jnp.einsum(
        "brhd,bkhd->bhrk", query_heads, key_heads, preferred_element_type=FLOAT
    ) * HEAD_DIM ** (-0.5)
    if allowed is not None:
        scores = jnp.where(allowed[:, None], scores, NEG)
    return scores


def attend_forward(queries, pairs, allowed):
    query_heads = queries.reshape(queries.shape[:2] + (HEADS, HEAD_DIM))
    key_heads, value_heads = split_pairs(pairs)
    scores = head_scores(query_heads, key_heads, allowed)
    row_max = jnp.max(scores, axis=-1, keepdims=True)
    log_total = row_max + jnp.log(jnp.sum(jnp.exp(scores - row_max), axis=-1, keepdims=True))
    attn_probs = jnp.exp(scores - log_total).astype(BRAIN)
    output = jnp.einsum("bhrk,bkhd->brhd", attn_probs, value_heads, preferred_element_type=FLOAT)
    return (output.reshape(queries.shape).astype(BRAIN), log_total)


def attend_backward(queries, pairs, allowed, log_total, grad_output):
    query_heads = queries.reshape(queries.shape[:2] + (HEADS, HEAD_DIM))
    key_heads, value_heads = split_pairs(pairs)
    grad_heads = grad_output.reshape(query_heads.shape)
    attn_probs = jnp.exp(head_scores(query_heads, key_heads, allowed) - log_total)
    grad_probs = jnp.einsum(
        "brhd,bkhd->bhrk", grad_heads, value_heads, preferred_element_type=FLOAT
    )
    inner_sum = jnp.sum(attn_probs * grad_probs, axis=-1, keepdims=True)
    grad_scores = (attn_probs * (grad_probs - inner_sum)).astype(BRAIN)
    score_scale = HEAD_DIM ** (-0.5)
    grad_queries = (
        jnp.einsum("bhrk,bkhd->brhd", grad_scores, key_heads, preferred_element_type=FLOAT)
        * score_scale
    )
    grad_keys = (
        jnp.einsum("bhrk,brhd->bkhd", grad_scores, query_heads, preferred_element_type=FLOAT)
        * score_scale
    )
    grad_values = jnp.einsum(
        "bhrk,brhd->bkhd", attn_probs.astype(BRAIN), grad_heads, preferred_element_type=FLOAT
    )
    batch_count, key_count = (pairs.shape[0], pairs.shape[1])
    grad_pairs = jnp.concatenate(
        [
            grad_keys.reshape(batch_count, key_count, D),
            grad_values.reshape(batch_count, key_count, D),
        ],
        axis=-1,
    )
    return (grad_queries.reshape(queries.shape), grad_pairs)


def project_forward(attended, residual, out_w, out_bias, gain_row, shift_row):
    summed = residual + matmul(attended, out_w) + out_bias
    return (layer_norm(summed, gain_row, shift_row), summed)


def project_backward(grad_norm, attended, summed, out_w, gain_row, shift_row):
    normed, pull_back = jax.vjp(layer_norm, summed, gain_row, shift_row)
    grad_summed, grad_gain, grad_shift = pull_back(grad_norm)
    grad_branch = grad_summed.astype(BRAIN)
    grad_out_w = matmul_left(attended, grad_branch)
    grad_out_bias = column_sum(grad_branch)
    grad_attended = matmul_right(grad_branch, out_w).astype(BRAIN)
    return (grad_summed, grad_attended, (grad_out_w, grad_out_bias, grad_gain, grad_shift))


def ffn_forward(first_norm, up_w, up_bias, down_w, down_bias, gain_row, shift_row):
    first_bf = first_norm.astype(BRAIN)
    lifted = matmul(first_bf, up_w) + up_bias
    activated = gelu_exact(lifted).astype(BRAIN)
    summed = first_norm + matmul(activated, down_w) + down_bias
    return (layer_norm(summed, gain_row, shift_row), (first_bf, lifted, activated, summed))


def ffn_backward(grad_norm, retained_context, up_w, down_w, gain_row, shift_row):
    first_bf, lifted, activated, summed = retained_context
    normed, pull_back = jax.vjp(layer_norm, summed, gain_row, shift_row)
    grad_summed, grad_gain, grad_shift = pull_back(grad_norm)
    grad_branch = grad_summed.astype(BRAIN)
    grad_down_w = matmul_left(activated, grad_branch)
    grad_down_bias = column_sum(grad_branch)
    grad_act = matmul_right(grad_branch, down_w)
    lifted_out, pull_gelu = jax.vjp(gelu_exact, lifted)
    grad_lifted = pull_gelu(grad_act)[0].astype(BRAIN)
    grad_up_w = matmul_left(first_bf, grad_lifted)
    up_bias_gradient = column_sum(grad_lifted)
    grad_first = grad_summed + matmul_right(grad_lifted, up_w)
    return (
        grad_first,
        (grad_up_w, up_bias_gradient, grad_down_w, grad_down_bias, grad_gain, grad_shift),
    )


def encoder_forward(weights, tokens, seg_rows, ctx_rank):
    qkv_w, out_w, up_w, down_w, bias_cols, up_bias, gain_cols = weights
    bias_vals = bias_cols.astype(FLOAT).T
    gain_vals = gain_cols.astype(FLOAT).T
    batch_count, row_count = (tokens.shape[0], tokens.shape[1])
    flat_tokens = tokens.reshape(batch_count * row_count, D)
    zero_row = jnp.zeros((D,), FLOAT)
    projected = (
        matmul(flat_tokens, qkv_w) + jnp.concatenate([bias_vals[0], zero_row, bias_vals[1]])
    ).astype(BRAIN)
    projected = projected.reshape(batch_count, row_count, 3 * D)
    all_pairs = lax.all_gather(projected[:, :, D:], "ctx", axis=1, tiled=True)
    own_segs = lax.dynamic_slice_in_dim(seg_rows, ctx_rank * row_count, row_count, axis=1)
    allowed = own_segs[:, :, None] == seg_rows[:, None, :]
    attended, log_total = attend_forward(projected[:, :, :D], all_pairs, allowed)
    attended = attended.reshape(batch_count * row_count, D)
    first_norm, first_sum = project_forward(
        attended, flat_tokens.astype(FLOAT), out_w, bias_vals[2], gain_vals[0], bias_vals[4]
    )
    final_norm, ffn_state = ffn_forward(
        first_norm, up_w, up_bias.astype(FLOAT), down_w, bias_vals[3], gain_vals[1], bias_vals[5]
    )
    return (
        final_norm,
        (flat_tokens, projected, all_pairs, allowed, log_total, attended, first_sum, ffn_state),
    )


def encoder_backward(weights, retained_context, grad_final):
    qkv_w, out_w, up_w, down_w, bias_cols, up_bias, gain_cols = weights
    bias_vals = bias_cols.astype(FLOAT).T
    gain_vals = gain_cols.astype(FLOAT).T
    flat_tokens, projected, all_pairs, allowed, log_total, attended, first_sum, ffn_state = (
        retained_context
    )
    batch_count, row_count = (projected.shape[0], projected.shape[1])
    grad_first, ffn_grads = ffn_backward(
        grad_final, ffn_state, up_w, down_w, gain_vals[1], bias_vals[5]
    )
    grad_tokens, grad_attended, proj_grads = project_backward(
        grad_first, attended, first_sum, out_w, gain_vals[0], bias_vals[4]
    )
    grad_queries, grad_pairs = attend_backward(
        projected[:, :, :D],
        all_pairs,
        allowed,
        log_total,
        grad_attended.reshape(batch_count, row_count, D),
    )
    own_pairs = lax.psum_scatter(
        grad_pairs.astype(jnp.bfloat16), "ctx", scatter_dimension=1, tiled=True
    ).astype(jnp.float32)
    mapped_slope = (
        jnp.concatenate([grad_queries, own_pairs], axis=-1)
        .astype(BRAIN)
        .reshape(batch_count * row_count, 3 * D)
    )
    grad_tokens = grad_tokens + matmul_right(mapped_slope, qkv_w)
    grad_qkv_w = matmul_left(flat_tokens, mapped_slope)
    proj_bias = column_sum(mapped_slope)
    up_grad_w, up_grad_bias, down_grad_w, down_grad_bias, gain_two, shift_two = ffn_grads
    out_grad_w, out_grad_bias, gain_one, shift_one = proj_grads
    bias_grads = jnp.stack(
        [proj_bias[:D], proj_bias[2 * D :], out_grad_bias, down_grad_bias, shift_one, shift_two],
        axis=1,
    )
    gain_grads = jnp.stack([gain_one, gain_two], axis=1)
    return (
        grad_tokens,
        (grad_qkv_w, out_grad_w, up_grad_w, down_grad_w, bias_grads, up_grad_bias, gain_grads),
    )


def decoder_forward(weights, tokens, memory_bf, pick_table, ctx_rank):
    (
        self_w,
        self_out_w,
        query_w,
        pair_w,
        cross_out_w,
        up_w,
        down_w,
        bias_cols,
        up_bias,
        gain_cols,
    ) = weights
    bias_vals = bias_cols.astype(FLOAT).T
    gain_vals = gain_cols.astype(FLOAT).T
    batch_count, row_count = (tokens.shape[0], tokens.shape[1])
    flat_tokens = tokens.reshape(batch_count * row_count, D)
    ctx_count = lax.axis_size("ctx")
    zero_row = jnp.zeros((D,), FLOAT)
    projected = (
        matmul(flat_tokens, self_w) + jnp.concatenate([bias_vals[0], zero_row, bias_vals[1]])
    ).astype(BRAIN)
    projected = projected.reshape(batch_count, row_count, 3 * D)
    all_pairs = lax.all_gather(projected[:, :, D:], "ctx", axis=1, tiled=True)
    query_pos = ctx_rank * row_count + jnp.arange(row_count, dtype=jnp.int32)
    key_pos = jnp.arange(row_count * ctx_count, dtype=jnp.int32)
    causal = (query_pos[:, None] >= key_pos[None, :])[None]
    attended, self_total = attend_forward(projected[:, :, :D], all_pairs, causal)
    attended = attended.reshape(batch_count * row_count, D)
    first_norm, first_sum = project_forward(
        attended, flat_tokens.astype(FLOAT), self_out_w, bias_vals[2], gain_vals[0], bias_vals[7]
    )
    first_bf = first_norm.astype(BRAIN)
    cross_queries = (matmul(first_bf, query_w) + bias_vals[3]).astype(BRAIN)
    memory_pairs = (matmul(memory_bf, pair_w) + jnp.concatenate([zero_row, bias_vals[4]])).astype(
        BRAIN
    )
    memory_rows = memory_pairs.shape[0] // batch_count
    memory_all = lax.all_gather(
        memory_pairs.reshape(batch_count, memory_rows, 2 * D), "ctx", axis=1, tiled=True
    )
    source_count = memory_all.shape[1]
    group_rows = min(row_count, BLOCK)
    group_count = row_count // group_rows
    group_start = ctx_rank * row_count + jnp.arange(group_count, dtype=jnp.int32) * group_rows
    pick_rows = jnp.take(pick_table, group_start // BLOCK, axis=1)
    pick_flat = (
        pick_rows + jnp.arange(batch_count, dtype=jnp.int32)[:, None, None] * source_count
    ).reshape(-1)
    picked = jnp.take(
        memory_all.reshape(batch_count * source_count, 2 * D), pick_flat, axis=0
    ).reshape(batch_count * group_count, pick_rows.shape[2], 2 * D)
    grouped = cross_queries.reshape(batch_count * group_count, group_rows, D)
    crossed, cross_total = attend_forward(grouped, picked, None)
    crossed = crossed.reshape(batch_count * row_count, D)
    second, second_sum = project_forward(
        crossed, first_norm, cross_out_w, bias_vals[5], gain_vals[1], bias_vals[8]
    )
    final_norm, ffn_state = ffn_forward(
        second, up_w, up_bias.astype(FLOAT), down_w, bias_vals[6], gain_vals[2], bias_vals[9]
    )
    retained_context = (
        flat_tokens,
        projected,
        all_pairs,
        causal,
        self_total,
        attended,
        first_sum,
        first_bf,
        grouped,
        pick_flat,
        picked,
        cross_total,
        crossed,
        second_sum,
        ffn_state,
        source_count,
    )
    return (final_norm, retained_context)


def decoder_backward(weights, memory_bf, retained_context, grad_final):
    (
        self_w,
        self_out_w,
        query_w,
        pair_w,
        cross_out_w,
        up_w,
        down_w,
        bias_cols,
        up_bias,
        gain_cols,
    ) = weights
    bias_vals = bias_cols.astype(FLOAT).T
    gain_vals = gain_cols.astype(FLOAT).T
    (
        flat_tokens,
        projected,
        all_pairs,
        causal,
        self_total,
        attended,
        first_sum,
        first_bf,
        grouped,
        pick_flat,
        picked,
        cross_total,
        crossed,
        second_sum,
        ffn_state,
        source_count,
    ) = retained_context
    batch_count, row_count = (projected.shape[0], projected.shape[1])
    grad_second, ffn_grads = ffn_backward(
        grad_final, ffn_state, up_w, down_w, gain_vals[2], bias_vals[9]
    )
    grad_first, grad_crossed, cross_grads = project_backward(
        grad_second, crossed, second_sum, cross_out_w, gain_vals[1], bias_vals[8]
    )
    grad_grouped, grad_picked = attend_backward(
        grouped, picked, None, cross_total, grad_crossed.reshape(grouped.shape)
    )
    grad_memory = (
        jnp.zeros((batch_count * source_count, 2 * D), FLOAT)
        .at[pick_flat]
        .add(grad_picked.reshape(-1, 2 * D))
    )
    own_memory = (
        lax.psum_scatter(
            grad_memory.reshape(batch_count, source_count, 2 * D).astype(jnp.bfloat16),
            "ctx",
            scatter_dimension=1,
            tiled=True,
        )
        .astype(jnp.float32)
        .astype(BRAIN)
    )
    own_memory = own_memory.reshape(-1, 2 * D)
    grad_memory_in = matmul_right(own_memory, pair_w)
    grad_pair_w = matmul_left(memory_bf, own_memory)
    pair_bias = column_sum(own_memory[:, D:])
    grad_cross_q = grad_grouped.reshape(batch_count * row_count, D).astype(BRAIN)
    grad_query_w = matmul_left(first_bf, grad_cross_q)
    query_bias = column_sum(grad_cross_q)
    grad_first = grad_first + matmul_right(grad_cross_q, query_w)
    grad_tokens, grad_attended, self_grads = project_backward(
        grad_first, attended, first_sum, self_out_w, gain_vals[0], bias_vals[7]
    )
    grad_queries, grad_pairs = attend_backward(
        projected[:, :, :D],
        all_pairs,
        causal,
        self_total,
        grad_attended.reshape(batch_count, row_count, D),
    )
    own_pairs = lax.psum_scatter(
        grad_pairs.astype(jnp.bfloat16), "ctx", scatter_dimension=1, tiled=True
    ).astype(jnp.float32)
    mapped_slope = (
        jnp.concatenate([grad_queries, own_pairs], axis=-1)
        .astype(BRAIN)
        .reshape(batch_count * row_count, 3 * D)
    )
    grad_tokens = grad_tokens + matmul_right(mapped_slope, self_w)
    grad_self_w = matmul_left(flat_tokens, mapped_slope)
    self_bias = column_sum(mapped_slope)
    up_grad_w, up_grad_bias, down_grad_w, down_grad_bias, gain_three, shift_three = ffn_grads
    cross_out_grad_w, cross_out_bias, gain_two, shift_two = cross_grads
    self_out_grad_w, self_out_bias, gain_one, shift_one = self_grads
    bias_grads = jnp.stack(
        [
            self_bias[:D],
            self_bias[2 * D :],
            self_out_bias,
            query_bias,
            pair_bias,
            cross_out_bias,
            down_grad_bias,
            shift_one,
            shift_two,
            shift_three,
        ],
        axis=1,
    )
    gain_grads = jnp.stack([gain_one, gain_two, gain_three], axis=1)
    weight_grads = (
        grad_self_w,
        self_out_grad_w,
        grad_query_w,
        grad_pair_w,
        cross_out_grad_w,
        up_grad_w,
        down_grad_w,
        bias_grads,
        up_grad_bias,
        gain_grads,
    )
    return (grad_tokens, grad_memory_in, weight_grads)


def fetch_weights(shards):
    return (
        lax.all_gather(shards[0], ("dp", "ctx"), axis=0, tiled=True),
        lax.all_gather(shards[1], ("dp", "ctx"), axis=0, tiled=True),
        lax.all_gather(shards[2], ("dp", "ctx"), axis=0, tiled=True),
        lax.all_gather(shards[3], ("dp", "ctx"), axis=0, tiled=True),
        lax.all_gather(shards[4], ("dp", "ctx"), axis=0, tiled=True),
        lax.all_gather(shards[5], ("dp", "ctx"), axis=0, tiled=True),
        lax.all_gather(shards[6], ("dp", "ctx"), axis=0, tiled=True),
        lax.all_gather(shards[7], ("dp", "ctx"), axis=0, tiled=True),
        lax.all_gather(shards[8], ("dp", "ctx"), axis=0, tiled=True),
        lax.all_gather(shards[9], ("dp", "ctx"), axis=0, tiled=True),
        lax.all_gather(shards[10], ("dp", "ctx"), axis=0, tiled=True),
        lax.all_gather(shards[11], ("dp", "ctx"), axis=0, tiled=True),
        lax.all_gather(shards[12], ("dp", "ctx"), axis=0, tiled=True),
        lax.all_gather(shards[13], ("dp", "ctx"), axis=0, tiled=True),
        lax.all_gather(shards[14], ("dp", "ctx"), axis=0, tiled=True),
        lax.all_gather(shards[15], ("dp", "ctx"), axis=0, tiled=True),
        lax.all_gather(shards[16], ("dp", "ctx"), axis=0, tiled=True),
    )


def body(
    enc_in,
    segments,
    dec_in,
    retrieved,
    enc_cot,
    dec_cot,
    enc_qkv,
    enc_out,
    enc_up,
    enc_down,
    enc_bias,
    enc_up_bias,
    enc_gain,
    decoder_self_projections,
    dec_out,
    cross_q,
    cross_kv,
    cross_out,
    dec_up,
    dec_down,
    dec_bias,
    dec_up_bias,
    dec_gain,
):
    shards = (
        enc_qkv,
        enc_out,
        enc_up,
        enc_down,
        enc_bias,
        enc_up_bias,
        enc_gain,
        decoder_self_projections,
        dec_out,
        cross_q,
        cross_kv,
        cross_out,
        dec_up,
        dec_down,
        dec_bias,
        dec_up_bias,
        dec_gain,
    )
    ctx_rank = lax.axis_index("ctx")
    batch_count, enc_rows, dec_rows = (enc_in.shape[0], enc_in.shape[1], dec_in.shape[1])
    kept_weights = fetch_weights(shards)
    enc_final, enc_state = encoder_forward(kept_weights[:7], enc_in, segments, ctx_rank)
    memory_bf = enc_final.astype(BRAIN)
    dec_final, dec_state = decoder_forward(kept_weights[7:], dec_in, memory_bf, retrieved, ctx_rank)
    dec_grad_in, memory_grad, dec_weight_grads = decoder_backward(
        kept_weights[7:], memory_bf, dec_state, dec_cot.reshape(-1, D).astype(FLOAT)
    )
    enc_grad_in, enc_weight_grads = encoder_backward(
        kept_weights[:7], enc_state, enc_cot.reshape(-1, D).astype(FLOAT) + memory_grad
    )
    totals = enc_weight_grads + dec_weight_grads
    reduced = (
        lax.psum_scatter(totals[0], ("dp", "ctx"), scatter_dimension=0, tiled=True),
        lax.psum_scatter(totals[1], ("dp", "ctx"), scatter_dimension=0, tiled=True),
        lax.psum_scatter(totals[2], ("dp", "ctx"), scatter_dimension=0, tiled=True),
        lax.psum_scatter(totals[3], ("dp", "ctx"), scatter_dimension=0, tiled=True),
        lax.psum_scatter(totals[4], ("dp", "ctx"), scatter_dimension=0, tiled=True),
        lax.psum_scatter(totals[5], ("dp", "ctx"), scatter_dimension=0, tiled=True),
        lax.psum_scatter(totals[6], ("dp", "ctx"), scatter_dimension=0, tiled=True),
        lax.psum_scatter(totals[7], ("dp", "ctx"), scatter_dimension=0, tiled=True),
        lax.psum_scatter(totals[8], ("dp", "ctx"), scatter_dimension=0, tiled=True),
        lax.psum_scatter(totals[9], ("dp", "ctx"), scatter_dimension=0, tiled=True),
        lax.psum_scatter(totals[10], ("dp", "ctx"), scatter_dimension=0, tiled=True),
        lax.psum_scatter(totals[11], ("dp", "ctx"), scatter_dimension=0, tiled=True),
        lax.psum_scatter(totals[12], ("dp", "ctx"), scatter_dimension=0, tiled=True),
        lax.psum_scatter(totals[13], ("dp", "ctx"), scatter_dimension=0, tiled=True),
        lax.psum_scatter(totals[14], ("dp", "ctx"), scatter_dimension=0, tiled=True),
        lax.psum_scatter(totals[15], ("dp", "ctx"), scatter_dimension=0, tiled=True),
        lax.psum_scatter(totals[16], ("dp", "ctx"), scatter_dimension=0, tiled=True),
    )
    return (
        memory_bf.reshape(batch_count, enc_rows, D),
        dec_final.astype(BRAIN).reshape(batch_count, dec_rows, D),
        enc_grad_in.reshape(batch_count, enc_rows, D),
        dec_grad_in.reshape(batch_count, dec_rows, D),
        reduced[0],
        reduced[1],
        reduced[2],
        reduced[3],
        reduced[4],
        reduced[5],
        reduced[6],
        reduced[7],
        reduced[8],
        reduced[9],
        reduced[10],
        reduced[11],
        reduced[12],
        reduced[13],
        reduced[14],
        reduced[15],
        reduced[16],
    )


MESH_ID = pl.DeviceIdType.MESH
ANY = pl.BlockSpec(memory_space=pl.ANY)
DMA_SEM = pltpu.SemaphoreType.DMA
PAIR = 128


def place():
    dp = lax.axis_index("dp")
    return dp, lax.axis_index("ctx"), lax.rem(dp, 2)


def spot():
    dp, z, core = place()
    return dp, z, core, lax.rem(dp // 2, 2), dp // 4


def dp_of(y, x, core):
    return (y * 2 + x) * 2 + core


def greet():
    dp, z, core, x, y = spot()
    zs = lax.axis_size("ctx")
    barrier = pltpu.get_barrier_semaphore()

    def hello(dp_to, z_to):
        pl.semaphore_signal(barrier, 1, device_id=(dp_to, z_to), device_id_type=MESH_ID)

    for step in range(zs):
        if step:
            hello(dp, lax.rem(z + step, zs))
        hello(dp_of(y, x, 1 - core), lax.rem(z + step, zs))
    hello(dp_of(y, 1 - x, core), z)
    hello(dp_of(1 - y, x, core), z)
    pl.semaphore_wait(barrier, 2 * zs + 1)


def remote(source, target, send, recv, dp_to, z_to):
    return pltpu.make_async_remote_copy(source, target, send, recv, device_id=(dp_to, z_to), device_id_type=MESH_ID)


def staged(count, stages):
    steps = []
    for turn in range(count + max(lag for lag, _ in stages)):
        for lag, fn in stages:
            if 0 <= turn - lag < count:
                steps.append(functools.partial(fn, turn - lag))
    return [(REACH * k / len(steps), step) for k, step in enumerate(steps)]


CHUNK = 24 * 512
BIG_CHUNK = 24 * 512
REACH = 1.0
LAG = 3
GATHER_LAG = 4


def pieces(shapes, chunk=None):
    chunks = []
    for i, (rows, n) in enumerate(shapes):
        columns = n // PAIR
        count = max(1, min(columns, -(-rows * n // (chunk or CHUNK))))
        at = 0
        for k in range(count):
            width = (columns * (k + 1) // count - columns * k // count) * PAIR
            chunks.append((i, at, width, len(chunks) % 2))
            at += width
    return chunks


def gather_job(shards, chunk=None):
    zs = lax.axis_size("ctx")
    everyone = lax.axis_size("dp") * zs
    chunks = pieces([s.shape for s in shards], chunk)
    count = len(chunks)

    def steps(ins, outs, scratch):
        send, recv, local = scratch
        dp, z, core, x, y = spot()

        def own_part(t):
            i, at, width, _ = chunks[t]
            return ins[i].at[:, pl.ds(at, width)]

        def rows_of(t, y_at, x_at, *z_at):
            i, at, width, _ = chunks[t]
            return outs[i].at[(y_at, x_at, core) + (z_at or (slice(None),)) + (slice(None), pl.ds(at, width))]

        def keep(t):
            return pltpu.make_async_copy(own_part(t), rows_of(t, y, x, z), local.at[t])

        def along_z(t, k):
            return remote(own_part(t), rows_of(t, y, x, z), send.at[t, k - 1], recv.at[t, k - 1], dp, lax.rem(z + k, zs))

        def hop(t, kind):
            near, far = dp_of(y, 1 - x, core), dp_of(1 - y, x, core)
            both = rows_of(t, y, slice(None))
            if chunks[t][3]:
                near, far, both = far, near, rows_of(t, slice(None), x)
            part, to = {
                3: (rows_of(t, y, x), near), 4: (both, far), 5: (rows_of(t, slice(None), slice(None)), dp_of(y, x, 1 - core)),
            }[kind]
            return remote(part, part, send.at[t, kind], recv.at[t, kind], to, z)

        def begin(t):
            keep(t).start()
            for k in range(1, zs):
                along_z(t, k).start()

        def first(t):
            keep(t).wait()
            for k in range(1, zs):
                along_z(t, k).wait_recv()
            hop(t, 3).start()

        def second(t):
            hop(t, 3).wait_recv()
            hop(t, 4).start()

        def third(t):
            hop(t, 4).wait_recv()
            hop(t, 5).start()

        def finish(t):
            hop(t, 5).wait_recv()
            for k in range(1, zs):
                along_z(t, k).wait_send()
            for kind in range(3, 6):
                hop(t, kind).wait_send()

        return staged(count, [(0, begin), (GATHER_LAG + 1, first), (2 * GATHER_LAG + 1, second), (3 * GATHER_LAG + 1, third), (4 * GATHER_LAG + 1, finish)])

    shapes = [jax.ShapeDtypeStruct((everyone // (4 * zs * 2) * 2, 2, 2, zs) + s.shape, s.dtype) for s in shards]
    scratch = [DMA_SEM((count, 6)), DMA_SEM((count, 6)), DMA_SEM((count,))]
    return shards, [ANY] * len(shards), shapes, [ANY] * len(shards), scratch, steps


def scatter_job(grads):
    zs, dps = lax.axis_size("ctx"), lax.axis_size("dp")
    rows = [g.shape[0] // (zs * dps) for g in grads]
    chunks = pieces([(r, g.shape[1]) for r, g in zip(rows, grads)])
    count = len(chunks)
    inputs = [g.reshape(dps // 4, 2, 2, zs * r, g.shape[1]) for r, g in zip(rows, grads)]
    scratch = [DMA_SEM((count, 6)), DMA_SEM((count, 6)), DMA_SEM((count,))]
    for i, _, width, _ in chunks:
        scratch += [
            pltpu.VMEM((2, 2, zs * rows[i], width), BRAIN),
            pltpu.VMEM((2, 2, zs * rows[i], width), BRAIN),
            pltpu.VMEM((2, zs * rows[i], width), BRAIN),
            pltpu.VMEM((zs * rows[i], width), BRAIN),
            pltpu.VMEM((zs, rows[i], width), BRAIN),
            pltpu.VMEM((zs - 1, rows[i], width), BRAIN),
        ]

    def steps(ins, outs, scratch):
        send, recv, local = scratch[:3]
        dp, z, core, x, y = spot()
        buffers = [scratch[3 + 6 * t : 9 + 6 * t] for t in range(count)]

        def source(t, core_at):
            i, at, width, _ = chunks[t]
            return ins[i].at[:, :, core_at, :, pl.ds(at, width)]

        def load(t):
            return pltpu.make_async_copy(source(t, core), buffers[t][0], local.at[t])

        def to_core(t):
            return remote(source(t, 1 - core), buffers[t][1], send.at[t, 0], recv.at[t, 0], dp_of(y, x, 1 - core), z)

        def wide(t):
            if chunks[t][3] == 0:
                part, to = buffers[t][0].at[1 - y], dp_of(1 - y, x, core)
            else:
                part, to = buffers[t][0].at[:, 1 - x], dp_of(y, 1 - x, core)
            return remote(part, buffers[t][2], send.at[t, 1], recv.at[t, 1], to, z)

        def narrow(t):
            if chunks[t][3] == 0:
                part, to = buffers[t][0].at[y, 1 - x], dp_of(y, 1 - x, core)
            else:
                part, to = buffers[t][0].at[1 - y, x], dp_of(1 - y, x, core)
            return remote(part, buffers[t][3], send.at[t, 2], recv.at[t, 2], to, z)

        def along_z(t, k):
            z_to = lax.rem(z + k, zs)
            return remote(buffers[t][4].at[z_to], buffers[t][5].at[k - 1], send.at[t, 2 + k], recv.at[t, 2 + k], dp, z_to)

        def add_into(target, other):
            total, width = target.shape

            def some(r, _):
                at = pl.ds(pl.multiple_of(r * 32, 32), 32)
                target[at, :] = target[at, :] + other[at, :]
                return 0

            lax.fori_loop(0, total // 32, some, 0)

        def begin(t):
            to_core(t).start()
            load(t).start()

        def first(t):
            load(t).wait()
            to_core(t).wait_recv()
            for b in range(4):
                add_into(buffers[t][0].at[b // 2, b % 2], buffers[t][1].at[b // 2, b % 2])
            wide(t).start()

        def second(t):
            wide(t).wait_recv()
            for j in range(2):
                block = (y, j) if chunks[t][3] == 0 else (j, x)
                add_into(buffers[t][0].at[block], buffers[t][2].at[j])
            narrow(t).start()

        def third(t):
            narrow(t).wait_recv()
            r = rows[chunks[t][0]]
            for s in range(zs):
                at = pl.ds(s * r, r)
                mine = buffers[t][0][y, x, at, :].astype(FLOAT)
                buffers[t][4][s] = (mine + buffers[t][3][at, :].astype(FLOAT)).astype(BRAIN)
            for k in range(1, zs):
                along_z(t, k).start()

        def finish(t):
            i, at, width, _ = chunks[t]
            total = buffers[t][4][z].astype(FLOAT)
            for k in range(1, zs):
                along_z(t, k).wait_recv()
                total = total + buffers[t][5][k - 1].astype(FLOAT)
            outs[i][:, pl.ds(at, width)] = total
            to_core(t).wait_send()
            wide(t).wait_send()
            narrow(t).wait_send()
            for k in range(1, zs):
                along_z(t, k).wait_send()

        return staged(count, [(0, begin), (LAG, first), (2 * LAG, second), (3 * LAG, third), (4 * LAG, finish)])

    shapes = [jax.ShapeDtypeStruct((r, g.shape[1]), FLOAT) for r, g in zip(rows, grads)]
    out_specs = [pl.BlockSpec(s.shape, lambda *_: (0, 0)) for s in shapes]
    return inputs, [ANY] * len(grads), shapes, out_specs, scratch, steps


def spread_job(tokens, ints=(), start=0.0):
    zs, count, int_count = lax.axis_size("ctx"), len(tokens), len(ints)

    def steps(ins, outs, scratch):
        send, recv, local, int_send, int_recv = scratch
        dp, z, core = place()
        pair = dp - core

        def swap(i):
            return remote(ins[count + i], outs[count + i], int_send.at[i], int_recv.at[i], pair + 1 - core, z)

        def each(t, what):
            for i in range(2):
                for h in range(2):
                    z_to, core_to = 2 * core + i, lax.rem(h + z, 2)
                    source, target = ins[t].at[i, pl.ds(h * BLOCK, BLOCK)], outs[t].at[z]
                    stays = jnp.logical_and(z_to == z, core_to == core)

                    @pl.when(stays)
                    def _():
                        what(pltpu.make_async_copy(source, target, local.at[t]), False)

                    @pl.when(jnp.logical_not(stays))
                    def _():
                        what(remote(source, target, send.at[t, 2 * i + h], recv.at[t, z], pair + core_to, z_to), True)

        def begin(t):
            if t == 0:
                for i in range(int_count):
                    swap(i).start()
            each(t, lambda copy, far: copy.start())

        def finish(t):
            each(t, lambda copy, far: copy.wait_send() if far else copy.wait())
            for s in range(zs):

                @pl.when(jnp.logical_not(jnp.logical_and(s == z, z // 2 == core)))
                def _():
                    remote(outs[t].at[s], outs[t].at[s], send.at[t, 0], recv.at[t, s], pair + 1 - core, z).wait_recv()

            if t == 0:
                for i in range(int_count):
                    swap(i).wait()

        return [(start, functools.partial(begin, t)) for t in range(count)] + [(1.0, functools.partial(finish, t)) for t in range(count)]

    shapes = [jax.ShapeDtypeStruct((zs, BLOCK, D), t.dtype) for t in tokens]
    shapes += [jax.ShapeDtypeStruct(i.shape, i.dtype) for i in ints]
    n = count + int_count
    scratch = [DMA_SEM((count, 4)), DMA_SEM((count, zs)), DMA_SEM((count,)), DMA_SEM((2,)), DMA_SEM((2,))]
    return list(tokens) + list(ints), [ANY] * n, shapes, [ANY] * n, scratch, steps


def collect_job(blocks):
    zs, count = lax.axis_size("ctx"), len(blocks)

    def steps(ins, outs, scratch):
        send, recv, local = scratch
        dp, z, core = place()
        pair = dp - core
        owner, inside = z // 2, lax.rem(z, 2)

        def each(t, what):
            for s in range(zs):
                half = lax.rem(core + s, 2)
                source = ins[t].at[s]
                target = outs[t].at[inside, pl.ds(half * BLOCK, BLOCK)]
                stays = jnp.logical_and(s == z, owner == core)

                @pl.when(stays)
                def _():
                    what(pltpu.make_async_copy(source, target, local.at[t]), False)

                @pl.when(jnp.logical_not(stays))
                def _():
                    what(remote(source, target, send.at[t, s], recv.at[t, 2 * inside + half], pair + owner, s), True)

        def begin(t):
            each(t, lambda copy, far: copy.start())

        def finish(t):
            each(t, lambda copy, far: copy.wait_send() if far else copy.wait())
            for i in range(2):
                for h in range(2):
                    z_from, core_from = 2 * core + i, lax.rem(h + z, 2)

                    @pl.when(jnp.logical_not(jnp.logical_and(z_from == z, core_from == core)))
                    def _():
                        target = outs[t].at[i, pl.ds(h * BLOCK, BLOCK)]
                        remote(target, target, send.at[t, 0], recv.at[t, 2 * i + h], pair + 1 - core, z).wait_recv()

        return [(0.0, functools.partial(begin, t)) for t in range(count)] + [(1.0, functools.partial(finish, t)) for t in range(count)]

    inputs = [b.reshape(zs, BLOCK, D) for b in blocks]
    shapes = [jax.ShapeDtypeStruct((2, 2 * BLOCK, D), b.dtype) for b in blocks]
    scratch = [DMA_SEM((count, zs)), DMA_SEM((count, 4)), DMA_SEM((count,))]
    return inputs, [ANY] * count, shapes, [ANY] * count, scratch, steps


def merge(lists):
    tagged = [(place, order, k, step) for order, steps in enumerate(lists) for k, (place, step) in enumerate(steps)]
    return [(t[0], t[3]) for t in sorted(tagged, key=lambda t: t[:3])]


def carry(
    jobs, collective_id, name, kernel=None, grid=1, slots=1, args=(), in_specs=(), out_shape=(), out_specs=(), scratch=(), cost=None
):
    sizes = [(len(j[0]), len(j[2]), len(j[4])) for j in jobs]

    def body(*refs):
        def take(n):
            nonlocal refs
            got, refs = refs[:n], refs[n:]
            return list(got)

        mine_in = take(len(args))
        job_in = [take(s[0]) for s in sizes]
        mine_out = take(len(out_shape))
        job_out = [take(s[1]) for s in sizes]
        mine_scratch = take(len(scratch))
        job_scratch = [take(s[2]) for s in sizes]
        steps = merge([j[5](i, o, s) for j, i, o, s in zip(jobs, job_in, job_out, job_scratch)])
        if kernel is None:
            greet()
            for _, step in steps:
                step()
            return
        turn = pl.program_id(0)
        calls = grid * slots
        called = [0]

        def poll():
            slot = called[0]
            called[0] += 1
            for g in range(grid):
                k = g * slots + slot
                some = [step for at, step in steps if k <= at * calls < k + 1]
                if some:

                    @pl.when(turn == g)
                    def _():
                        for step in some:
                            step()

        if jobs:

            @pl.when(turn == 0)
            def _():
                greet()

        kernel(poll, *mine_in, *mine_out, *mine_scratch)
        assert called[0] == slots
        last = [step for at, step in steps if at >= 1.0]
        if last:

            @pl.when(turn == grid - 1)
            def _():
                for step in last:
                    step()

    flat = lambda k: [v for j in jobs for v in j[k]]
    got = pl.pallas_call(
        body,
        grid=(grid,),
        out_shape=list(out_shape) + flat(2),
        in_specs=list(in_specs) + flat(1),
        out_specs=list(out_specs) + flat(3),
        scratch_shapes=list(scratch) + flat(4),
        compiler_params=pltpu.CompilerParams(
            collective_id=collective_id if jobs else None, has_side_effects=bool(jobs), vmem_limit_bytes=60 << 20
        ),
        cost_estimate=cost,
        name=name,
    )(*args, *flat(0))
    own, rest, parts = got[: len(out_shape)], got[len(out_shape) :], []
    for s in sizes:
        parts.append(rest[: s[1]])
        rest = rest[s[1] :]
    return own, parts


LOG2E = 1.4426950408889634


def key_chunks(rows, causal):
    if causal:
        return [(half, r, BLOCK, r) for r in range(0, rows, BLOCK) for half in range(2)]
    return [(half, r, 2 * BLOCK, 0) for half in range(2) for r in range(0, rows, 2 * BLOCK)]


def nt_dot(a, b):
    return lax.dot_general(a, b, (((1,), (1,)), ((), ())), preferred_element_type=FLOAT)


def head_lanes(values, head):
    lanes = lax.broadcasted_iota(jnp.int32, values.shape, 1)
    return jnp.where(lanes // HEAD_DIM == head, values, jnp.zeros_like(values))


def fold_rows(values, how):
    grouped = values.reshape(values.shape[0] // 8, 8, values.shape[1])
    return how(how(grouped, axis=0), axis=0, keepdims=True)


def attend_fwd_kernel(causal, poll, q_ref, k0_ref, v0_ref, k1_ref, v1_ref, bias_ref, o_ref, lse_ref, s_ref, p_ref):
    rows = q_ref.shape[0]
    k_refs = (k0_ref, k1_ref)
    v_all = jnp.concatenate([v0_ref[...], v1_ref[...]], axis=0)
    v_t = v_all.T
    factor = HEAD_DIM ** (-0.5) * LOG2E
    out_t = []
    for head in range(2):
        q = head_lanes(q_ref[...], head)
        top = jnp.full((1, rows), -3e38, FLOAT)
        for half, r, n, c in key_chunks(rows, causal):
            s = nt_dot(k_refs[half][pl.ds(r, n), :], q[c:])
            s = s * factor + bias_ref[pl.ds(half * rows + r, n), c:].astype(FLOAT)
            s_ref[pl.ds(half * rows + r, n), c:] = s
            peak = fold_rows(s, jnp.max)
            peak = jnp.maximum(top[:, c:], peak)
            top = jnp.concatenate([top[:, :c], peak], axis=1) if c else peak
        poll()
        total = jnp.zeros((1, rows), FLOAT)
        for half, r, n, c in key_chunks(rows, causal):
            p = jnp.exp2(s_ref[pl.ds(half * rows + r, n), c:] - top[:, c:])
            part = total[:, c:] + fold_rows(p, jnp.sum)
            total = jnp.concatenate([total[:, :c], part], axis=1) if c else part
            p_ref[pl.ds(half * rows + r, n), c:] = p.astype(BRAIN)
            if c:
                p_ref[pl.ds(half * rows + r, n), :c] = jnp.zeros((n, c), BRAIN)
        o_t = jnp.dot(v_t[head * HEAD_DIM : (head + 1) * HEAD_DIM], p_ref[...], preferred_element_type=FLOAT)
        out_t.append(o_t / total)
        poll()
        lse_ref[0, pl.ds(head, 1), :] = top + jnp.log(total) * LOG2E
    o_ref[...] = jnp.concatenate(out_t, axis=0).T.astype(o_ref.dtype)


def attention_forward(queries, q_col, pairs, kv_col, pairs_other, bias, causal, jobs=(), collective_id=None):
    rows = queries.shape[0]
    pair_count = D // PAIR
    block = (rows, PAIR)
    spec = lambda at: pl.BlockSpec(block, lambda p: (0, at + p))
    own, parts = carry(
        list(jobs),
        collective_id,
        "attend_fwd",
        kernel=functools.partial(attend_fwd_kernel, causal),
        grid=pair_count,
        slots=4,
        args=(queries, pairs, pairs, pairs_other, pairs_other, bias),
        in_specs=[
            spec(q_col), spec(kv_col), spec(kv_col + pair_count), spec(0), spec(pair_count),
            pl.BlockSpec((2 * rows, rows), lambda p: (0, 0)),
        ],
        out_shape=[jax.ShapeDtypeStruct((rows, D), BRAIN), jax.ShapeDtypeStruct((pair_count, 8, rows), FLOAT)],
        out_specs=[spec(0), pl.BlockSpec((1, 8, rows), lambda p: (p, 0, 0))],
        scratch=[pltpu.VMEM((2 * rows, rows), FLOAT), pltpu.VMEM((2 * rows, rows), BRAIN)],
        cost=pl.CostEstimate(flops=16 * rows * rows * D, bytes_accessed=10 * rows * D * 2, transcendentals=24 * rows * rows),
    )
    return own[0], own[1], parts


def attend_bwd_kernel(
    causal, poll, q_ref, k0_ref, v0_ref, k1_ref, v1_ref, bias_ref, o_ref, do_ref, lse_ref,
    dq_ref, dk0_ref, dv0_ref, dk1_ref, dv1_ref, ds_ref,
):
    rows = q_ref.shape[0]
    k_refs, v_refs = (k0_ref, k1_ref), (v0_ref, v1_ref)
    dk_refs, dv_refs = (dk0_ref, dk1_ref), (dv0_ref, dv1_ref)
    k_t = jnp.concatenate([k0_ref[...], k1_ref[...]], axis=0).T
    scale = HEAD_DIM ** (-0.5)
    factor = scale * LOG2E
    prod_t = (o_ref[...].astype(FLOAT) * do_ref[...].astype(FLOAT)).T
    dq_t = []
    q_heads = [head_lanes(q_ref[...], head) for head in range(2)]
    do_heads = [head_lanes(do_ref[...], head) for head in range(2)]
    lses = [lse_ref[0, pl.ds(head, 1), :] for head in range(2)]
    deltas = [fold_rows(prod_t[head * HEAD_DIM : (head + 1) * HEAD_DIM], jnp.sum) for head in range(2)]
    for half, r, n, c in key_chunks(rows, causal):
        k, v = k_refs[half][pl.ds(r, n), :], v_refs[half][pl.ds(r, n), :]
        bias = bias_ref[pl.ds(half * rows + r, n), c:].astype(FLOAT)
        dk = dv = None
        for head in range(2):
            q, do = q_heads[head][c:], do_heads[head][c:]
            p = jnp.exp2(nt_dot(k, q) * factor + bias - lses[head][:, c:])
            dv_part = jnp.dot(p.astype(BRAIN), do, preferred_element_type=FLOAT)
            ds = (p * (nt_dot(v, do) - deltas[head][:, c:])).astype(BRAIN)
            ds_ref[head, pl.ds(half * rows + r, n), c:] = ds
            if c:
                ds_ref[head, pl.ds(half * rows + r, n), :c] = jnp.zeros((n, c), BRAIN)
            dk_part = jnp.dot(ds, q, preferred_element_type=FLOAT)
            dk = dk_part if dk is None else dk + dk_part
            dv = dv_part if dv is None else dv + dv_part
        dk_refs[half][pl.ds(r, n), :] = (dk * scale).astype(dk_refs[half].dtype)
        dv_refs[half][pl.ds(r, n), :] = dv.astype(dv_refs[half].dtype)
        poll()
    for head in range(2):
        dq_t.append(jnp.dot(k_t[head * HEAD_DIM : (head + 1) * HEAD_DIM], ds_ref[head], preferred_element_type=FLOAT))
    dq_ref[...] = (jnp.concatenate(dq_t, axis=0) * scale).T.astype(dq_ref.dtype)


def attention_backward(
    queries, q_col, pairs, kv_col, pairs_other, bias, causal, attended, grad_attended, lse, jobs=(), collective_id=None
):
    rows = queries.shape[0]
    pair_count = D // PAIR
    block = (rows, PAIR)
    spec = lambda at: pl.BlockSpec(block, lambda p: (0, at + p))
    own, parts = carry(
        list(jobs),
        collective_id,
        "attend_bwd",
        kernel=functools.partial(attend_bwd_kernel, causal),
        grid=pair_count,
        slots=len(key_chunks(rows, causal)),
        args=(queries, pairs, pairs, pairs_other, pairs_other, bias, attended, grad_attended, lse),
        in_specs=[
            spec(q_col), spec(kv_col), spec(kv_col + pair_count), spec(0), spec(pair_count),
            pl.BlockSpec((2 * rows, rows), lambda p: (0, 0)), spec(0), spec(0),
            pl.BlockSpec((1, 8, rows), lambda p: (p, 0, 0)),
        ],
        out_shape=[jax.ShapeDtypeStruct((rows, D), t) for t in (BRAIN, FLOAT, FLOAT, BRAIN, BRAIN)],
        out_specs=[spec(0)] * 5,
        scratch=[pltpu.VMEM((2, 2 * rows, rows), BRAIN)],
        cost=pl.CostEstimate(flops=40 * rows * rows * D, bytes_accessed=18 * rows * D * 2, transcendentals=24 * rows * rows),
    )
    return own, parts


def to_sibling(values):
    count = lax.axis_size("dp")
    return lax.ppermute(values, "dp", [(i, i ^ 1) for i in range(count)])


ERF_TOP = (
    -2.72614225801306e-10, 2.77068142495902e-08, -2.10102402082508e-06, -5.69250639462346e-05,
    -7.34990630326855e-04, -2.95459980854025e-03, -1.60960333262415e-02,
)
ERF_LOW = (-1.45660718464996e-05, -2.13374055278905e-04, -1.68282697438203e-03, -7.37332916720468e-03, -1.42647390514189e-02)
FF_TILE = 512


def horner(values, factors):
    total = jnp.full_like(values, factors[0])
    for factor in factors[1:]:
        total = total * values + factor
    return total


def gelu_pair(x):
    arg = jnp.clip(x * 0.7071067811865476, -4.0, 4.0)
    square = arg * arg
    below = 0.5 + 0.5 * (arg * horner(square, ERF_TOP) / horner(square, ERF_LOW))
    return x * below, below + x * (0.3989422804014327 * jnp.exp(-0.5 * x * x))


def tn_dot(a, b):
    return lax.dot_general(a, b, (((0,), (0,)), ((), ())), preferred_element_type=FLOAT)


def ffn_end(residual, branch, gain, shift):
    summed = residual + branch
    return summed, layer_norm(summed, gain, shift)


def ffn_fwd_kernel(
    tiles, poll, first_ref, up_ref, ub_ref, down_ref, db_ref, gain_ref, shift_ref,
    act_ref, slope_ref, sum_ref, out_ref, acc, low,
):
    g = pl.program_id(0)

    @pl.when(g == 0)
    def _():
        low[...] = first_ref[...].astype(BRAIN)
        acc[...] = jnp.zeros_like(acc)

    lifted = jnp.dot(low[...], up_ref[...], preferred_element_type=FLOAT) + ub_ref[...]
    poll()
    act, slope = gelu_pair(lifted)
    act = act.astype(BRAIN)
    act_ref[...], slope_ref[...] = act, slope.astype(BRAIN)
    poll()
    acc[...] += jnp.dot(act, down_ref[...], preferred_element_type=FLOAT)
    poll()

    @pl.when(g == tiles - 1)
    def _():
        summed, final = ffn_end(first_ref[...], acc[...] + db_ref[...], gain_ref[...], shift_ref[...])
        sum_ref[...] = summed
        out_ref[...] = final.astype(BRAIN)


def ffn_bwd_start(grad, summed, gain, acc, branch, dgain_ref, dshift_ref, ddb_ref):
    grad_summed, dgain, dshift = norm_grad(grad, summed, gain)
    acc[...] = grad_summed
    branch[...] = grad_summed.astype(BRAIN)
    dgain_ref[...], dshift_ref[...] = dgain, dshift
    ddb_ref[...] = sums(branch[...])


def ffn_bwd_tile(poll, first, up, down, act, slope, branch, acc, dup_ref, dub_ref, ddown_ref):
    lift = (nt_dot(branch, down) * slope.astype(FLOAT)).astype(BRAIN)
    dub_ref[...] = sums(lift)
    poll()
    ddown_ref[...] = tn_dot(act, branch).astype(BRAIN)
    poll()
    dup_ref[...] = tn_dot(first, lift).astype(BRAIN)
    acc[...] += nt_dot(lift, up)
    poll()


def ffn_bwd_kernel(
    tiles, poll, first_ref, up_ref, down_ref, gain_ref, grad_ref, act_ref, slope_ref, sum_ref,
    dfirst_ref, dup_ref, dub_ref, ddown_ref, ddb_ref, dgain_ref, dshift_ref, acc, branch, low,
):
    g = pl.program_id(0)

    @pl.when(g == 0)
    def _():
        low[...] = first_ref[...].astype(BRAIN)
        ffn_bwd_start(grad_ref[...], sum_ref[...], gain_ref[...], acc, branch, dgain_ref, dshift_ref, ddb_ref)

    ffn_bwd_tile(
        poll, low[...], up_ref[...], down_ref[...], act_ref[...], slope_ref[...], branch[...], acc, dup_ref, dub_ref, ddown_ref
    )

    @pl.when(g == tiles - 1)
    def _():
        dfirst_ref[...] = acc[...]


def ffn_both_kernel(
    tiles, poll, first_ref, up_ref, ub_ref, down_ref, db_ref, gain_ref, shift_ref, cot_ref,
    out_ref, dfirst_ref, dup_ref, dub_ref, ddown_ref, ddb_ref, dgain_ref, dshift_ref, acc, branch, low, act_sc, slope_sc,
):
    g = pl.program_id(0)

    @pl.when(g == 0)
    def _():
        low[...] = first_ref[...].astype(BRAIN)
        acc[...] = jnp.zeros_like(acc)

    poll()

    @pl.when(g < tiles)
    def _():
        lifted = jnp.dot(low[...], up_ref[...], preferred_element_type=FLOAT) + ub_ref[...]
        act, slope = gelu_pair(lifted)
        act = act.astype(BRAIN)
        act_sc[g], slope_sc[g] = act, slope.astype(BRAIN)
        acc[...] += jnp.dot(act, down_ref[...], preferred_element_type=FLOAT)

    @pl.when(g == tiles - 1)
    def _():
        summed, final = ffn_end(first_ref[...], acc[...] + db_ref[...], gain_ref[...], shift_ref[...])
        out_ref[...] = final.astype(BRAIN)
        ffn_bwd_start(cot_ref[...].astype(FLOAT), summed, gain_ref[...], acc, branch, dgain_ref, dshift_ref, ddb_ref)

    poll()

    @pl.when(g >= tiles)
    def _():
        ffn_bwd_tile(
            lambda: None, low[...], up_ref[...], down_ref[...], act_sc[g - tiles], slope_sc[g - tiles], branch[...], acc,
            dup_ref, dub_ref, ddown_ref,
        )

    @pl.when(g == 2 * tiles - 1)
    def _():
        dfirst_ref[...] = acc[...]

    poll()


def ffn_call(mode, jobs, collective_id, first, up, ub, down, db, gain, shift, extra):
    rows, width = first.shape
    tiles = up.shape[1] // FF_TILE
    grid = 2 * tiles if mode == "both" else tiles
    at = (lambda g: lax.rem(g, tiles)) if mode == "both" else (lambda g: g)
    late = (lambda g: jnp.maximum(g - tiles, 0)) if mode == "both" else (lambda g: g)
    whole = lambda r: pl.BlockSpec((r, width), lambda g: (0, 0))
    column = lambda r, to: pl.BlockSpec((r, FF_TILE), lambda g: (0, to(g)))
    row = lambda to: pl.BlockSpec((FF_TILE, width), lambda g: (to(g), 0))
    shape = jax.ShapeDtypeStruct
    acc, low = pltpu.VMEM((rows, width), FLOAT), pltpu.VMEM((rows, width), BRAIN)
    up_spec, ub_spec, down_spec = column(width, at), column(1, at), row(at)
    grad_shapes = [shape((rows, width), FLOAT), shape(up.shape, BRAIN), shape(ub.shape, FLOAT), shape(down.shape, BRAIN)]
    grad_shapes += [shape((1, width), FLOAT)] * 3
    grad_specs = [whole(rows), column(width, late), column(1, late), row(late), whole(1), whole(1), whole(1)]
    if mode == "fwd":
        kernel, args = ffn_fwd_kernel, (first, up, ub, down, db, gain, shift)
        in_specs = [whole(rows), up_spec, ub_spec, down_spec, whole(1), whole(1), whole(1)]
        out_shape = [shape((rows, up.shape[1]), BRAIN)] * 2 + [shape((rows, width), FLOAT), shape((rows, width), BRAIN)]
        out_specs = [column(rows, at), column(rows, at), whole(rows), whole(rows)]
        scratch = [acc, low]
    elif mode == "bwd":
        grad, act, slope, summed = extra
        kernel, args = ffn_bwd_kernel, (first, up, down, gain, grad, act, slope, summed)
        in_specs = [whole(rows), up_spec, down_spec, whole(1), whole(rows), column(rows, at), column(rows, at), whole(rows)]
        out_shape, out_specs, scratch = grad_shapes, grad_specs, [acc, low, low]
    else:
        kernel, args = ffn_both_kernel, (first, up, ub, down, db, gain, shift) + tuple(extra)
        in_specs = [whole(rows), up_spec, ub_spec, down_spec, whole(1), whole(1), whole(1), whole(rows)]
        out_shape, out_specs = [shape((rows, width), BRAIN)] + grad_shapes, [whole(rows)] + grad_specs
        kept = pltpu.VMEM((tiles, rows, FF_TILE), BRAIN)
        scratch = [acc, low, low, kept, kept]
    flops = 4 * rows * width * up.shape[1] * {"fwd": 1, "bwd": 2, "both": 3}[mode]
    return carry(
        list(jobs), collective_id, "ffn_" + mode,
        kernel=functools.partial(kernel, tiles), grid=grid, slots=3, args=args, in_specs=in_specs, out_shape=out_shape,
        out_specs=out_specs, scratch=scratch,
        cost=pl.CostEstimate(flops=flops, bytes_accessed=4 * width * up.shape[1] + 16 * rows * width, transcendentals=rows * up.shape[1]),
    )


def own_blocks(per_block, core):
    zs = per_block.shape[0] // 2
    both = per_block.reshape((zs, 2) + per_block.shape[1:])
    flip = lax.rem(jnp.arange(zs, dtype=jnp.int32) + core, 2).reshape((zs,) + (1,) * (per_block.ndim - 1))
    own = jnp.where(flip == 0, both[:, 0], both[:, 1])
    return own, jnp.where(flip == 0, both[:, 1], both[:, 0])


def ordered_keys(per_token, core):
    own, other = own_blocks(per_token.reshape(-1, BLOCK), core)
    return own.reshape(-1), jnp.concatenate([own.reshape(-1), other.reshape(-1)])


SMALL = 32


def pack_small(enc_bias, dec_bias, enc_gain, dec_gain, enc_up_bias, dec_up_bias):
    rows = enc_bias.shape[0]
    parts = [enc_bias, dec_bias, enc_gain, dec_gain]
    left = jnp.pad(jnp.concatenate(parts, axis=1), ((0, 0), (0, SMALL - sum(p.shape[1] for p in parts))))
    right = jnp.pad(jnp.stack([enc_up_bias, dec_up_bias]), ((0, rows - 2), (0, PAIR - SMALL - enc_up_bias.shape[0])))
    return jnp.concatenate([left, right], axis=1)


def unpack_small(packed, width):
    cuts, at = [], 0
    for count in (6, 10, 2, 3):
        cuts.append(packed[..., at : at + count])
        at += count
    return cuts + [packed[..., 0, SMALL : SMALL + width], packed[..., 1, SMALL : SMALL + width]]


def small_grads(rows, enc_up_bias, dec_up_bias, shards):
    left = jnp.pad(jnp.concatenate(rows, axis=0), ((0, SMALL - len(rows)), (0, 0))).T.reshape(shards, -1, SMALL)
    up = jnp.stack([v.reshape(shards, -1) for v in (enc_up_bias, dec_up_bias)], axis=1)
    right = jnp.pad(up, ((0, 0), (0, left.shape[1] - 2), (0, PAIR - SMALL - up.shape[2])))
    return jnp.concatenate([left, right], axis=2).reshape(-1, PAIR)


def sums(values):
    return jnp.sum(values, axis=0, keepdims=True, dtype=FLOAT)


def norm_grad(grad, summed, gain_row):
    center = summed - jnp.mean(summed, axis=-1, keepdims=True)
    inverse = lax.rsqrt(jnp.mean(center * center, axis=-1, keepdims=True) + EPS)
    unit = center * inverse
    scaled = grad * gain_row
    back = scaled - jnp.mean(scaled, axis=-1, keepdims=True) - unit * jnp.mean(scaled * unit, axis=-1, keepdims=True)
    return inverse * back, sums(grad * unit), sums(grad)


def project_grad(grad_norm, attended, summed, out_w, gain_row):
    grad_summed, grad_gain, grad_shift = norm_grad(grad_norm, summed, gain_row)
    grad_branch = grad_summed.astype(BRAIN)
    return (
        grad_summed,
        matmul_right(grad_branch, out_w).astype(BRAIN),
        (matmul_left(attended, grad_branch), sums(grad_branch), grad_gain, grad_shift),
    )


def with_sibling(own_keys, own_values, other_keys, other_values):
    got = to_sibling(jnp.concatenate([other_keys, other_values], axis=1)).astype(FLOAT)
    return (jnp.concatenate([own_keys, own_values], axis=1) + got).astype(BRAIN)


def matrix(gathered):
    return gathered.reshape(-1, gathered.shape[-1])


def fast_body(
    enc_in, segments, dec_in, retrieved, enc_cot, dec_cot,
    enc_qkv, enc_out, enc_up, enc_down, enc_bias, enc_up_bias, enc_gain,
    dec_qkv, dec_out, cross_q, cross_kv, cross_out, dec_up, dec_down, dec_bias, dec_up_bias, dec_gain,
):
    dp, z, core = place()
    small = pack_small(enc_bias, dec_bias, enc_gain, dec_gain, enc_up_bias, dec_up_bias)
    weights = [enc_qkv, enc_out, small, enc_up, enc_down, dec_qkv, dec_out, cross_kv, cross_q, cross_out, dec_up, dec_down]
    _, ((enc_t, dec_t, seg_other, ret_other), near) = carry(
        [spread_job([enc_in, dec_in], [segments, retrieved], 0.3), gather_job(weights, BIG_CHUNK)], 0, "begin"
    )
    (
        w_enc_qkv, w_enc_out, _, w_enc_up, w_enc_down, w_dec_qkv,
        w_dec_out, w_cross_kv, w_cross_q, w_cross_out, w_dec_up, w_dec_down,
    ) = map(matrix, near)
    zs = enc_t.shape[0]
    rows = zs * BLOCK
    enc_t, dec_t = enc_t.reshape(rows, D), dec_t.reshape(rows, D)
    here = z // 2 == core
    seg = lax.dynamic_index_in_dim(jnp.where(here, segments, seg_other), lax.rem(z, 2), 0, keepdims=False)
    ret = lax.dynamic_index_in_dim(jnp.where(here, retrieved, ret_other), lax.rem(z, 2), 0, keepdims=False)
    seg_q, seg_k = ordered_keys(seg, core)
    pos_q, pos_k = ordered_keys(jnp.arange(2 * rows, dtype=jnp.int32), core)
    enc_mask = jnp.where(seg_k[:, None] == seg_q[None, :], 0.0, NEG).astype(FLOAT)
    dec_mask = jnp.where(pos_k[:, None] <= pos_q[None, :], 0.0, NEG).astype(FLOAT)
    ret_own, _ = own_blocks(ret, core)
    member = jnp.any(pos_k[:, None, None] == ret_own[None], axis=-1)
    cross_mask = jnp.broadcast_to(jnp.where(member, 0.0, NEG).astype(FLOAT)[:, :, None], (2 * rows, zs, BLOCK)).reshape(2 * rows, rows)

    near_small = near[2].reshape((-1,) + near[2].shape[-2:])
    shards = near_small.shape[0]
    b_enc, b_dec, g_enc, g_dec, enc_ub, dec_ub = unpack_small(near_small, enc_up_bias.shape[0])
    across = lambda v: jnp.swapaxes(v.reshape(D, -1), 0, 1).astype(FLOAT)
    eb, db, eg, dg = ([row[i : i + 1] for i in range(row.shape[0])] for row in map(across, (b_enc, b_dec, g_enc, g_dec)))
    enc_ub, dec_ub = (v.reshape(1, -1).astype(FLOAT) for v in (enc_ub, dec_ub))
    zero_row = jnp.zeros((1, D), FLOAT)

    e_proj = (matmul(enc_t, w_enc_qkv) + jnp.concatenate([eb[0], zero_row, eb[1]], axis=1)).astype(BRAIN)
    e_other = to_sibling(e_proj[:, D:])
    e_att, e_lse, _ = attention_forward(
        e_proj, 0, e_proj, D // PAIR, e_other, enc_mask, False
    )
    d_proj = (matmul(dec_t, w_dec_qkv) + jnp.concatenate([db[0], zero_row, db[1]], axis=1)).astype(BRAIN)
    d_other = to_sibling(d_proj[:, D:])
    d_att, d_lse, _ = attention_forward(
        d_proj, 0, d_proj, D // PAIR, d_other, dec_mask, True
    )
    e_first, e_sum = project_forward(e_att, enc_t.astype(FLOAT), w_enc_out, eb[2], eg[0], eb[4])
    (e_act, e_slope, e_sum2, memory), ((dec_c,),) = ffn_call(
        "fwd", [spread_job([dec_cot])], 8, e_first, w_enc_up, enc_ub, w_enc_down, eb[3], eg[1], eb[5], ()
    )
    dec_c = dec_c.reshape(rows, D)
    d_first, d_sum = project_forward(d_att, dec_t.astype(FLOAT), w_dec_out, db[2], dg[0], db[7])
    first_bf = d_first.astype(BRAIN)
    cross_queries = (matmul(first_bf, w_cross_q) + db[3]).astype(BRAIN)
    mem_pairs = (matmul(memory, w_cross_kv) + jnp.concatenate([zero_row, db[4]], axis=1)).astype(BRAIN)
    mem_other = to_sibling(mem_pairs)
    crossed, cross_lse, _ = attention_forward(
        cross_queries, 0, mem_pairs, 0, mem_other, cross_mask, False
    )
    second, second_sum = project_forward(crossed, d_first, w_cross_out, db[5], dg[1], db[8])
    low = lambda *grads: [g.astype(BRAIN) for g in grads]
    (dec_low, grad_second, g_dec_up, g_dec_ub, g_dec_down, g_db6, g_dg2, g_db9), ((enc_c,), (enc_hidden,)) = ffn_call(
        "both", [spread_job([enc_cot]), collect_job([memory])], 9,
        second, w_dec_up, dec_ub, w_dec_down, db[6], dg[2], db[9], (dec_c,),
    )
    enc_c = enc_c.reshape(rows, D)
    grad_first, grad_crossed, (g_cross_out, g_db5, g_dg1, g_db8) = project_grad(
        grad_second, crossed, second_sum, w_cross_out, dg[1]
    )
    (g_cq, dk, dv, dk_o, dv_o), ((dec_hidden,), (r_dec_down,)) = attention_backward(
        cross_queries, 0, mem_pairs, 0, mem_other, cross_mask, False, crossed, grad_crossed, cross_lse,
        [collect_job([dec_low]), scatter_job(low(g_dec_down))], 4,
    )
    own_memory = with_sibling(dk, dv, dk_o, dv_o)
    g_cross_q, g_db3 = matmul_left(first_bf, g_cq), sums(g_cq)
    grad_first = grad_first + matmul_right(g_cq, w_cross_q)
    memory_grad = matmul_right(own_memory, w_cross_kv)
    g_cross_kv, g_db4 = matmul_left(memory, own_memory), sums(own_memory[:, D:])
    grad_dec, grad_d_att, (g_dec_out, g_db2, g_dg0, g_db7) = project_grad(grad_first, d_att, d_sum, w_dec_out, dg[0])
    (dq, dk, dv, dk_o, dv_o), ((r_dec_up, r_cross_out, r_cross_q),) = attention_backward(
        d_proj, 0, d_proj, D // PAIR, d_other, dec_mask, True, d_att, grad_d_att, d_lse,
        [scatter_job(low(g_dec_up, g_cross_out, g_cross_q))], 5,
    )
    d_slope = jnp.concatenate([dq, with_sibling(dk, dv, dk_o, dv_o)], axis=1)
    grad_dec = grad_dec + matmul_right(d_slope, w_dec_qkv)
    g_dec_qkv, d_slope_sum = matmul_left(dec_t, d_slope), sums(d_slope)
    (grad_e_first, g_enc_up, g_enc_ub, g_enc_down, g_eb3, g_eg1, g_eb5), ((dec_home,), (r_cross_kv, r_dec_out, r_dec_qkv)) = ffn_call(
        "bwd", [collect_job(low(grad_dec)), scatter_job(low(g_cross_kv, g_dec_out, g_dec_qkv))], 10,
        e_first, w_enc_up, enc_ub, w_enc_down, eb[3], eg[1], eb[5], (enc_c.astype(FLOAT) + memory_grad, e_act, e_slope, e_sum2),
    )
    grad_enc, grad_e_att, (g_enc_out, g_eb2, g_eg0, g_eb4) = project_grad(grad_e_first, e_att, e_sum, w_enc_out, eg[0])
    (dq, dk, dv, dk_o, dv_o), ((r_enc_up, r_enc_down),) = attention_backward(
        e_proj, 0, e_proj, D // PAIR, e_other, enc_mask, False, e_att, grad_e_att, e_lse,
        [scatter_job(low(g_enc_up, g_enc_down))], 6,
    )
    e_pull = jnp.concatenate([dq, with_sibling(dk, dv, dk_o, dv_o)], axis=1)
    grad_enc = grad_enc + matmul_right(e_pull, w_enc_qkv)
    g_enc_qkv, e_slope_sum = matmul_left(enc_t, e_pull), sums(e_pull)

    g_small = small_grads(
        [e_slope_sum[:, :D], e_slope_sum[:, 2 * D :], g_eb2, g_eb3, g_eb4, g_eb5]
        + [d_slope_sum[:, :D], d_slope_sum[:, 2 * D :], g_db2, g_db3, g_db4, g_db5, g_db6, g_db7, g_db8, g_db9]
        + [g_eg0, g_eg1, g_dg0, g_dg1, g_dg2],
        g_enc_ub, g_dec_ub, shards,
    )
    _, ((enc_home,), (r_enc_out, r_enc_qkv, r_small)) = carry(
        [collect_job(low(grad_enc)), scatter_job(low(g_enc_out, g_enc_qkv, g_small))], 7, "end"
    )
    r_eb, r_db, r_eg, r_dg, r_enc_ub, r_dec_ub = unpack_small(r_small, enc_up_bias.shape[0])
    return (
        enc_hidden, dec_hidden, enc_home.astype(FLOAT), dec_home.astype(FLOAT),
        r_enc_qkv, r_enc_out, r_enc_up, r_enc_down, r_eb, r_enc_ub, r_eg,
        r_dec_qkv, r_dec_out, r_cross_q, r_cross_kv, r_cross_out, r_dec_up, r_dec_down, r_db, r_dec_ub, r_dg,
    )


def solution(mesh):
    in_specs = (
        P("dp", "ctx", None),
        P("dp", None),
        P("dp", "ctx", None),
        P("dp", None, None),
        P("dp", "ctx", None),
        P("dp", "ctx", None),
        P(("dp", "ctx"), None),
        P(("dp", "ctx"), None),
        P(("dp", "ctx"), None),
        P(("dp", "ctx"), None),
        P(("dp", "ctx"), None),
        P(("dp", "ctx")),
        P(("dp", "ctx"), None),
        P(("dp", "ctx"), None),
        P(("dp", "ctx"), None),
        P(("dp", "ctx"), None),
        P(("dp", "ctx"), None),
        P(("dp", "ctx"), None),
        P(("dp", "ctx"), None),
        P(("dp", "ctx"), None),
        P(("dp", "ctx"), None),
        P(("dp", "ctx")),
        P(("dp", "ctx"), None),
    )
    out_specs = (
        P("dp", "ctx", None),
        P("dp", "ctx", None),
        P("dp", "ctx", None),
        P("dp", "ctx", None),
        P(("dp", "ctx"), None),
        P(("dp", "ctx"), None),
        P(("dp", "ctx"), None),
        P(("dp", "ctx"), None),
        P(("dp", "ctx"), None),
        P(("dp", "ctx")),
        P(("dp", "ctx"), None),
        P(("dp", "ctx"), None),
        P(("dp", "ctx"), None),
        P(("dp", "ctx"), None),
        P(("dp", "ctx"), None),
        P(("dp", "ctx"), None),
        P(("dp", "ctx"), None),
        P(("dp", "ctx"), None),
        P(("dp", "ctx"), None),
        P(("dp", "ctx")),
        P(("dp", "ctx"), None),
    )

    def run(*args):
        sequences, tokens = args[0].shape[:2]
        fits = (
            mesh.shape["dp"] % 2 == 0
            and sequences == 2 * mesh.shape["dp"]
            and mesh.shape["ctx"] == 4
            and tokens == 2 * BLOCK * mesh.shape["ctx"]
            and args[2].shape == args[0].shape
            and D % (mesh.shape["dp"] * mesh.shape["ctx"] * 8) == 0
        )
        chosen = fast_body if fits else body
        return jax.shard_map(chosen, mesh=mesh, in_specs=in_specs, out_specs=out_specs, check_vma=False)(*args)

    return run
```
